512 devices in a mesh: seq: 32 (over y, z_lo, core), row: 4 (over x), col: 4 (over z_hi).
Axes of the slice: x: 4, y: 8, z: 8 (z_hi: 4, z_lo: 2; z = z_hi * 2 + z_lo), core: 2. Of those that a mesh axis runs over, the one named last changes fastest.
Arguments:
- hidden_in: bfloat16 [4, 16384, 1024], P('row', 'seq')
- qkv_weight: bfloat16 [1024, 16, 192], P(None, 'col'), may hold values from -0.1875 to 0.1875
- qkv_global_weight: bfloat16 [1024, 16, 192], P('row', 'col'), may hold values from -0.1875 to 0.1875
- out_weight: bfloat16 [1024, 1024], P('col'), may hold values from -0.75 to 0.75
- ln_gain: float32 [1024], replicated, may hold values from 0.1 to 1.9
- ln_bias: float32 [1024], replicated, may hold values from -3 to 3
- ffn_in: bfloat16 [1024, 4096], P('row', 'col'), may hold values from -0.1875 to 0.1875
- ffn_out: bfloat16 [4096, 1024], P('col', 'row'), may hold values from -0.09375 to 0.09375
- ln2_gain: float32 [1024], replicated, may hold values from 0.1 to 1.9
- ln2_bias: float32 [1024], replicated, may hold values from -3 to 3
- segment_ids: int32 [4, 16384], P('row'), may hold values from 0 to 63, never falling along the last dimension, each value on 1 to 9216 neighbouring positions
- global_pos: int32 [4, 128], P('row'), may hold values from 0 to 16383, as said below
- page_owner: int32 [4, 1024, 1], P('row', 'seq'), may hold values from 0 to 31; in each aligned block of 32 rows (0 to 31, 32 to 63, ..., all dimensions but the last counted through in order) at most 2 rows name the same one
Outputs:
- hidden_out: bfloat16 [4, 16384, 1024], P('row', ('seq', 'col'))
- page_pool: bfloat16 [4, 32, 32, 2, 16, 16, 128], P('row', 'seq', None, None, None, 'col')
The draws below stay inside these ranges and needn't reach their ends.
Inputs may be any that keep to these rules, and one draw needn't show every extreme that they name: `segment_ids`: in each stream, prompt numbers never fall along positions and every prompt has 1 to 9216 tokens, one exactly 9216. `global_pos`: in each stream, exactly 4 distinct global positions lie in each block of 512 consecutive tokens, listed in increasing order. `page_owner`: among the 32 pages of one shard of a stream, at most 2 have the same owner.
All inputs are finite; a program needn't handle non-finite values.
Results may differ from the reference program's by a relative error of at most 0.014.
The reference program's roundings to bfloat16 on the way count: a program that leaves them out, or rounds other values in their place, can miss the bound.
Values may be sent and summed in bfloat16 or wider, within the bound.
A program may use at most 64 MiB of HBM per device.

```python
import math
import jax
import jax.numpy as jnp
import numpy as np
from jax import lax

D = 1024
H = 16
HD = 64
FF = 4096
HALF = 256
PAGE = 16
GL = 4
TS = 512
STREAMS = 4
L = 16384
PAGES_DEV = 32
CAP = 2
PROMPTS = 64
PROMPT_MOST = 9216
N_SEQ = 32


def draw_hidden_in(key, part):
    second = jax.random.fold_in(jax.random.fold_in(key, 11), 1)
    return jnp.clip(jax.random.normal(second, (STREAMS, L, D), jnp.float32), -6.0, 6.0).astype(jnp.bfloat16)


def draw_global_pos(key, part):
    keys = jax.random.split(jax.random.fold_in(key, 23), STREAMS * N_SEQ)

    def pick(one):
        return jnp.sort(jax.random.permutation(one, TS)[:GL].astype(jnp.int32))
    offsets = jax.vmap(pick)(keys).reshape(STREAMS, N_SEQ, GL)
    starts = (jnp.arange(N_SEQ, dtype=jnp.int32) * TS)[None, :, None]
    return (offsets + starts).reshape(STREAMS, N_SEQ * GL).astype(jnp.int32)


def block_scale(own_key, dims, cuts, smallest, largest):
    level = 1.0
    for dim, blocks in cuts:
        draws = jax.random.uniform(jax.random.fold_in(jax.random.fold_in(own_key, 6), dim), (blocks,), jnp.float32, smallest / len(cuts), largest / len(cuts))
        level = level * jnp.repeat(jnp.exp(draws), dims[dim] // blocks).reshape((-1,) + (1,) * (len(dims) - 1 - dim))
    return level


def profile(amount, total, limit, slope):
    portions = [(1 << 20) // math.isqrt(rank ** slope) + 1 for rank in range(2, amount + 1)]
    surplus, given = total - limit - (amount - 1), [1] * (amount - 1)
    while surplus > 0:
        candidates = [i for i in range(amount - 1) if given[i] < limit]
        mass, remaining = sum([portions[i] for i in candidates]), surplus
        for i in candidates:
            addition = min(limit - given[i], max(1, remaining * portions[i] // mass), surplus)
            given[i] = given[i] + addition
            surplus = surplus - addition
    return np.array([limit] + given)


def uneven_parts(rng, count, total, limit, slope):
    if count == 2:
        one = jax.random.randint(rng, (), max(1, total - limit), min(limit, total - 1) + 1)
        return jnp.stack([one, total - one])
    sizes = jnp.asarray(profile(count, total, limit, slope), jnp.int32)
    twos = (count - 1) // 2
    source_of, sink = sizes[1:1 + 2 * twos:2], sizes[2:2 + 2 * twos:2]
    slack = jnp.minimum(source_of - 1, limit - sink)
    passed = jax.random.randint(jax.random.fold_in(rng, 1), (twos,), 0, 1 << 20) % (slack + 1)
    sizes = sizes.at[1:1 + 2 * twos:2].set(source_of - passed).at[2:2 + 2 * twos:2].set(sink + passed)
    return sizes[jax.random.permutation(jax.random.fold_in(rng, 2), count)]


def deal_out(stream_key, own, number, rows, amount, top, bound, lean):
    ranking = jax.random.permutation(stream_key, amount)
    heavy_load, common = portions_of(amount, rows * top, bound, lean, True), portions_of(amount, rows * top, bound, lean, False)
    places = jnp.arange(amount)

    def named(tallies, turn):
        used = int((tallies > 0).sum())
        fixed = max(1, used // 4)
        shifted = fixed + (places - fixed + turn * (used - fixed)) % max(1, amount - fixed)
        return jnp.zeros((amount,), jnp.int32).at[ranking[jnp.where(places < fixed, places, shifted)]].set(jnp.asarray(tallies, jnp.int32))

    tallies = jnp.where(number % 4 == 0, named(heavy_load, number // 4), named(common, number - number // 4 - 1))
    mixed = jax.random.permutation(jax.random.fold_in(own, 3), amount)
    donor, taker = mixed[0:amount // 2 * 2:2], mixed[1:amount // 2 * 2:2]
    margin = jnp.minimum(tallies[donor] - 1, bound - tallies[taker]) // 2
    margin = jnp.where((donor == ranking[0]) | (taker == ranking[0]) | (tallies[taker] == 0), 0, jnp.maximum(margin, 0))
    shifted = jax.random.randint(jax.random.fold_in(own, 4), (amount // 2,), 0, 1 << 20) % (margin + 1)
    tallies = tallies.at[donor].add(-shifted).at[taker].add(shifted)
    items = jnp.searchsorted(jnp.cumsum(tallies), jnp.arange(rows * top), side="right").astype(jnp.int32)
    listing = items.reshape(top, rows).T
    listing = listing[jax.random.permutation(jax.random.fold_in(own, 1), rows)]
    turn = jax.random.randint(jax.random.fold_in(own, 2), (rows, 1), 0, top)
    return jnp.take_along_axis(listing, (jnp.arange(top)[None, :] + turn) % top, axis=1)


def portions_of(count, total, most, lean, full):
    portions = [(1 << 20) // math.isqrt(rank ** lean) + 1 for rank in range(1, count + 1)]
    largest = most if full else min(most, max(-(-total // count), total * portions[0] // sum(portions)))
    least = 1 if total - largest >= count - 1 else 0
    holding, surplus = [largest] + [least] * (count - 1), total - largest - least * (count - 1)
    while surplus > 0:
        free = [i for i in range(1, count) if holding[i] < largest] or [i for i in range(1, count) if holding[i] < most]
        mass, remaining = sum([portions[i] for i in free]), surplus
        for i in free:
            extra = min(most - holding[i], max(1, remaining * portions[i] // mass), surplus)
            holding[i] = holding[i] + extra
            surplus = surplus - extra
    return np.array(holding)


def gaussian(own_key, extent, scale, limit, cuts=(), kind=jnp.bfloat16):
    loudness = block_scale(own_key, extent, cuts, -0.22, 0.18) if cuts else 1.0
    drawn = jax.random.normal(own_key, extent, jnp.float32) * scale * loudness
    return jnp.minimum(jnp.maximum(drawn, -limit), limit).astype(kind)


def setup_inputs(seed: int = 0) -> dict:
    key_list = jax.random.split(jax.random.key(seed), 14)
    hidden_in = draw_hidden_in(jax.random.fold_in(key_list[13], 71), 0)
    qkv_weight = gaussian(key_list[1], (D, H, 3 * HD), D ** -0.5, 0.1875, ((1, 4),))
    qkv_global_weight = gaussian(key_list[2], (D, H, 3 * HD), D ** -0.5, 0.1875, ((0, 4), (1, 4)))
    out_weight = gaussian(key_list[3], (H * HD, D), HD ** -0.5, 0.75, ((0, 4),))
    ln_gain = jnp.clip(1.0 + 0.18 * jax.random.normal(key_list[4], (D,), jnp.float32), 0.1, 1.9)
    ln_bias = gaussian(key_list[5], (D,), 0.5, 3.0, (), jnp.float32)
    ffn_in = gaussian(key_list[6], (D, FF), D ** -0.5, 0.1875, ((0, 4), (1, 4)))
    ffn_out = gaussian(key_list[7], (FF, D), FF ** -0.5, 0.09375, ((0, 4), (1, 4)))
    ln2_gain = jnp.clip(1.0 + 0.18 * jax.random.normal(key_list[8], (D,), jnp.float32), 0.1, 1.9)
    ln2_bias = gaussian(key_list[9], (D,), 0.5, 3.0, (), jnp.float32)
    segment_ids = jax.vmap(lambda own: jnp.searchsorted(jnp.cumsum(uneven_parts(own, PROMPTS, L, PROMPT_MOST, 2)), jnp.arange(L), side="right"))(jax.random.split(key_list[10], STREAMS)).reshape((STREAMS, L)).astype(jnp.int32)
    global_pos = draw_global_pos(jax.random.fold_in(key_list[13], 71), 0)
    page_owner_keys = jax.random.split(jax.random.fold_in(key_list[12], 1), STREAMS * (N_SEQ * PAGES_DEV) // PAGES_DEV)
    page_owner_turns = jax.random.permutation(jax.random.fold_in(key_list[12], 3), STREAMS * (N_SEQ * PAGES_DEV) // PAGES_DEV)
    page_owner = jax.vmap(lambda own, number: deal_out(jax.random.fold_in(key_list[12], 2), own, number, PAGES_DEV, N_SEQ, 1, CAP, 2))(page_owner_keys, page_owner_turns).reshape((STREAMS, N_SEQ * PAGES_DEV, 1))
    return {"hidden_in": hidden_in, "qkv_weight": qkv_weight, "qkv_global_weight": qkv_global_weight, "out_weight": out_weight, "ln_gain": ln_gain, "ln_bias": ln_bias, "ffn_in": ffn_in, "ffn_out": ffn_out, "ln2_gain": ln2_gain, "ln2_bias": ln2_bias, "segment_ids": segment_ids, "global_pos": global_pos, "page_owner": page_owner}


def layer_norm(values, gain, bias):
    center = values - lax.optimization_barrier(jnp.mean(values, axis=1, keepdims=True))
    spread = lax.optimization_barrier(jnp.mean(center * center, axis=1, keepdims=True))
    return center * lax.rsqrt(spread + 1e-05) * gain + bias

def reference(hidden_in, qkv_weight, qkv_global_weight, out_weight, ln_gain, ln_bias, ffn_in, ffn_out, ln2_gain, ln2_bias, segment_ids, global_pos, page_owner):
    scale = 1.0 / math.sqrt(HD)
    neg = -1e+30
    high = lax.Precision.HIGHEST
    flat_weight = qkv_weight.reshape(D, H * 3 * HD)
    flat_global = qkv_global_weight.reshape(D, H * 3 * HD)
    out_list = []
    pool_list = []
    for stream in range(STREAMS):
        tokens = hidden_in[stream]
        qkv = jnp.dot(tokens, flat_weight, preferred_element_type=jnp.float32).astype(jnp.bfloat16)
        qkv = lax.optimization_barrier(qkv).reshape(L, H, 3 * HD)
        qkv_glob = jnp.dot(tokens, flat_global, preferred_element_type=jnp.float32).astype(jnp.bfloat16)
        qkv_glob = lax.optimization_barrier(qkv_glob).reshape(L, H, 3 * HD)
        queries = qkv[:, :, :HD].astype(jnp.float32)
        keys = qkv[:, :, HD:2 * HD].astype(jnp.float32)
        values = qkv[:, :, 2 * HD:].astype(jnp.float32)
        keys_g = qkv_glob[:, :, HD:2 * HD].astype(jnp.float32)
        values_g = qkv_glob[:, :, 2 * HD:].astype(jnp.float32)
        seg = segment_ids[stream]
        gpos = global_pos[stream]
        flag = jnp.zeros((L,), jnp.int32).at[gpos].set(1)
        glob_seg = seg[gpos]
        glob_k = keys[gpos]
        glob_v = values[gpos]
        key_pad = jnp.pad(keys, ((HALF, HALF), (0, 0), (0, 0)))
        value_pad = jnp.pad(values, ((HALF, HALF), (0, 0), (0, 0)))
        seg_pad = jnp.pad(seg, (HALF, HALF), constant_values=-1)
        flag_pad = jnp.pad(flag, (HALF, HALF), constant_values=1)

        def window_block(index):
            start = (index * TS).astype(jnp.int32)
            q_blk = lax.dynamic_slice_in_dim(queries, start, TS, 0)
            k_blk = lax.dynamic_slice_in_dim(key_pad, start, TS + 2 * HALF, 0)
            v_blk = lax.dynamic_slice_in_dim(value_pad, start, TS + 2 * HALF, 0)
            q_seg = lax.dynamic_slice_in_dim(seg, start, TS, 0)
            k_seg = lax.dynamic_slice_in_dim(seg_pad, start, TS + 2 * HALF, 0)
            k_flag = lax.dynamic_slice_in_dim(flag_pad, start, TS + 2 * HALF, 0)
            q_pos = start + jnp.arange(TS, dtype=jnp.int32)
            k_pos = start - HALF + jnp.arange(TS + 2 * HALF, dtype=jnp.int32)
            s_win = jnp.einsum('qhd,khd->hqk', q_blk, k_blk, precision=high) * scale
            s_glob = jnp.einsum('qhd,ghd->hqg', q_blk, glob_k, precision=high) * scale
            m_win = (jnp.abs(q_pos[:, None] - k_pos[None, :]) <= HALF) & (q_seg[:, None] == k_seg[None, :]) & (k_flag[None, :] == 0)
            m_glob = q_seg[:, None] == glob_seg[None, :]
            top = jnp.maximum(lax.optimization_barrier(jnp.max(jnp.where(m_win, s_win, neg), axis=2)), lax.optimization_barrier(jnp.max(jnp.where(m_glob, s_glob, neg), axis=2)))
            e_win = jnp.where(m_win, jnp.exp(s_win - top[:, :, None]), 0.0)
            e_glob = jnp.where(m_glob, jnp.exp(s_glob - top[:, :, None]), 0.0)
            total = lax.optimization_barrier(jnp.sum(e_win, axis=2)) + lax.optimization_barrier(jnp.sum(e_glob, axis=2))
            w_win = lax.optimization_barrier(e_win.astype(jnp.bfloat16)).astype(jnp.float32)
            w_glob = lax.optimization_barrier(e_glob.astype(jnp.bfloat16)).astype(jnp.float32)
            numer = jnp.einsum('hqk,khd->hqd', w_win, v_blk, precision=high) + jnp.einsum('hqg,ghd->hqd', w_glob, glob_v, precision=high)
            return (numer / total[:, :, None]).astype(jnp.bfloat16)
        blocks = lax.map(window_block, jnp.arange(N_SEQ, dtype=jnp.int32))
        attn = jnp.transpose(blocks, (0, 2, 1, 3)).reshape(L, H, HD)
        glob_q = qkv_glob[:, :, :HD].astype(jnp.float32)[gpos]
        s_all = jnp.einsum('ghd,khd->hgk', glob_q, keys_g, precision=high) * scale
        m_all = glob_seg[:, None] == seg[None, :]
        top_all = lax.optimization_barrier(jnp.max(jnp.where(m_all, s_all, neg), axis=2))
        e_all = jnp.where(m_all, jnp.exp(s_all - top_all[:, :, None]), 0.0)
        total_all = lax.optimization_barrier(jnp.sum(e_all, axis=2))
        acc_all = jnp.einsum('hgk,khd->hgd', e_all, values_g, precision=high)
        glob_out = (acc_all / total_all[:, :, None]).astype(jnp.bfloat16)
        attn = attn.at[gpos].set(jnp.transpose(glob_out, (1, 0, 2)))
        proj = jnp.dot(attn.reshape(L, H * HD), out_weight, preferred_element_type=jnp.float32)
        summed = tokens.astype(jnp.float32) + proj
        middle = layer_norm(summed, ln_gain, ln_bias).astype(jnp.bfloat16)
        ffn_pre = jnp.dot(middle, ffn_in, preferred_element_type=jnp.float32)
        ffn_act = jax.nn.gelu(ffn_pre, approximate=False).astype(jnp.bfloat16)
        second = middle.astype(jnp.float32) + jnp.dot(ffn_act, ffn_out, preferred_element_type=jnp.float32)
        out_list.append(layer_norm(second, ln2_gain, ln2_bias).astype(jnp.bfloat16))
        kv_pages = qkv[:, :, HD:].reshape(N_SEQ, PAGES_DEV, PAGE, H, 2 * HD)
        owners = page_owner[stream, :, 0].reshape(N_SEQ, PAGES_DEV)
        order = jnp.arange(PAGES_DEV, dtype=jnp.int32)
        earlier = (owners[:, :, None] == owners[:, None, :]) & (order[None, None, :] < order[None, :, None])
        slot = lax.optimization_barrier(jnp.sum(earlier.astype(jnp.int32), axis=2)).astype(jnp.int32)
        source = jnp.broadcast_to(jnp.arange(N_SEQ, dtype=jnp.int32)[:, None], (N_SEQ, PAGES_DEV))
        pool = jnp.zeros((N_SEQ, N_SEQ, CAP, PAGE, H, 2 * HD), jnp.bfloat16).at[owners, source, slot].set(kv_pages)
        pool_list.append(pool)
    return (jnp.stack(out_list), jnp.stack(pool_list))
```

```python
import math

import jax
import jax.numpy as jnp
from jax import lax
from jax.sharding import PartitionSpec as P

HALF = 256


def padded(block, sides, width):
    for axis, dim in sides:
        count = lax.axis_size(axis)
        forward = [(i, i + 1) for i in range(count - 1)]
        backward = [(target, source) for source, target in forward]
        low = lax.ppermute(
            lax.slice_in_dim(block, block.shape[dim] - width, None, axis=dim), axis, forward
        )
        high = lax.ppermute(lax.slice_in_dim(block, 0, width, axis=dim), axis, backward)
        block = jnp.concatenate([low, block, high], axis=dim)
    return block


def layer_norm(values, gain, bias):
    center = values - jnp.mean(values, axis=1, keepdims=True)
    spread = jnp.mean(center * center, axis=1, keepdims=True)
    return center * lax.rsqrt(spread + 1e-05) * gain + bias


def per_device(
    hidden_in,
    qkv_weight,
    qkv_global_weight,
    out_weight,
    ln_gain,
    ln_bias,
    ffn_in,
    ffn_out,
    ln2_gain,
    ln2_bias,
    segment_ids,
    global_pos,
    page_owner,
):
    neg = -1e30
    tokens = hidden_in[0]
    shard_len, width = tokens.shape
    heads_here = qkv_weight.shape[1]
    triple = qkv_weight.shape[2]
    head_dim = triple // 3
    n_seq = lax.axis_size("seq")
    n_row = lax.axis_size("row")
    n_col = lax.axis_size("col")
    seq_index = lax.axis_index("seq")
    col_index = lax.axis_index("col")
    base = seq_index * shard_len
    scale = 1.0 / math.sqrt(head_dim)

    all_pos = global_pos[0]
    n_glob = all_pos.shape[0]
    per_shard = n_glob // n_seq
    own_pos = lax.dynamic_slice_in_dim(all_pos, seq_index * per_shard, per_shard, 0)
    local_order = jnp.arange(shard_len, dtype=jnp.int32)
    own_match = (own_pos - base)[:, None] == local_order[None, :]
    picker = own_match.astype(jnp.bfloat16)
    own_rows = jnp.dot(picker, tokens, preferred_element_type=jnp.float32).astype(jnp.bfloat16)
    glob_rows = lax.all_gather(own_rows, "seq", axis=0, tiled=True)

    wg_rows = qkv_global_weight.shape[0]
    fi_rows, units = ffn_in.shape
    wg_flat = qkv_global_weight.reshape(-1)
    fi_flat = ffn_in.reshape(-1)
    fo_flat = ffn_out.reshape(-1)
    n_wg, n_fi = wg_flat.shape[0], fi_flat.shape[0]
    everything = lax.all_gather(jnp.concatenate([wg_flat, fi_flat, fo_flat]), "row", axis=0)
    w_global = everything[:, :n_wg].reshape(n_row * wg_rows, heads_here * triple)
    f_in = everything[:, n_wg : n_wg + n_fi].reshape(n_row * fi_rows, units)
    f_out = jnp.transpose(
        everything[:, n_wg + n_fi :].reshape(n_row, units, ffn_out.shape[1]), (1, 0, 2)
    ).reshape(units, n_row * ffn_out.shape[1])
    w_out = lax.all_gather(out_weight, "col", axis=0, tiled=True)

    flat_weight = qkv_weight.reshape(width, heads_here * triple)
    qkv = jnp.dot(tokens, flat_weight, preferred_element_type=jnp.float32).astype(jnp.bfloat16)
    qkv_heads = qkv.reshape(shard_len, heads_here, triple)
    queries = qkv_heads[:, :, :head_dim]
    kv_local = qkv_heads[:, :, head_dim:]

    owners = page_owner[0, :, 0]
    n_pages = owners.shape[0]
    page_len = shard_len // n_pages
    capacity = max(2, n_pages // n_seq)
    page_order = jnp.arange(n_pages, dtype=jnp.int32)
    slot = jnp.sum(
        ((owners[:, None] == owners[None, :]) & (page_order[None, :] < page_order[:, None])).astype(
            jnp.int32
        ),
        axis=1,
    )
    target = owners * capacity + slot
    placing = (target[None, :] == jnp.arange(n_seq * capacity, dtype=jnp.int32)[:, None]).astype(
        jnp.bfloat16
    )
    outgoing = jnp.dot(
        placing,
        kv_local.reshape(n_pages, page_len * heads_here * 2 * head_dim),
        preferred_element_type=jnp.float32,
    ).astype(jnp.bfloat16)
    outgoing = outgoing.reshape(n_seq, capacity, page_len, heads_here, 2 * head_dim)
    arrived = lax.all_to_all(outgoing, "seq", split_axis=0, concat_axis=0, tiled=True)
    page_pool = arrived[None, None]

    kv_ext = padded(kv_local, (("seq", 0),), HALF)

    glob_qkv = jnp.dot(glob_rows, flat_weight, preferred_element_type=jnp.float32).astype(
        jnp.bfloat16
    )
    glob_kv = glob_qkv.reshape(n_glob, heads_here, triple)[:, :, head_dim:]
    glob_k = glob_kv[:, :, :head_dim]
    glob_v = glob_kv[:, :, head_dim:]
    glob_q = (
        jnp.dot(glob_rows, w_global, preferred_element_type=jnp.float32)
        .astype(jnp.bfloat16)
        .reshape(n_glob, heads_here, triple)[:, :, :head_dim]
    )
    global_kv_local = (
        jnp.dot(tokens, w_global, preferred_element_type=jnp.float32)
        .astype(jnp.bfloat16)
        .reshape(shard_len, heads_here, triple)[:, :, head_dim:]
    )

    seg_all = segment_ids[0]
    glob_seg = jnp.take(seg_all, all_pos)
    seg_pad = jnp.pad(seg_all, (HALF, HALF), constant_values=-1)
    query_seg = lax.dynamic_slice_in_dim(seg_all, base, shard_len, 0)
    key_seg = lax.dynamic_slice_in_dim(seg_pad, base, shard_len + 2 * HALF, 0)
    key_pos = base - HALF + jnp.arange(shard_len + 2 * HALF, dtype=jnp.int32)
    key_flag = jnp.any(key_pos[:, None] == all_pos[None, :], axis=1)
    query_pos = base + local_order

    s_part = (
        jnp.einsum(
            "ghd,khd->hgk",
            glob_q,
            global_kv_local[:, :, :head_dim],
            preferred_element_type=jnp.float32,
        )
        * scale
    )
    part_mask = glob_seg[:, None] == query_seg[None, :]
    part_top = jnp.max(jnp.where(part_mask, s_part, neg), axis=2)
    glob_top = lax.pmax(part_top, "seq")
    e_part = jnp.where(part_mask, jnp.exp(s_part - glob_top[:, :, None]), 0.0)
    part_total = jnp.sum(e_part, axis=2)
    part_acc = jnp.einsum(
        "hgk,khd->hgd",
        e_part,
        global_kv_local[:, :, head_dim:].astype(jnp.float32),
        precision=lax.Precision.HIGHEST,
    )
    summed = lax.psum(jnp.concatenate([part_acc, part_total[:, :, None]], axis=2), "seq")
    glob_out = (summed[:, :, :head_dim] / summed[:, :, head_dim:]).astype(jnp.bfloat16)

    glob_mask = query_seg[:, None] == glob_seg[None, :]
    k_blk = kv_ext[:, :, :head_dim]
    v_blk = kv_ext[:, :, head_dim:]
    s_win = jnp.einsum("qhd,khd->hqk", queries, k_blk, preferred_element_type=jnp.float32) * scale
    s_glob = jnp.einsum("qhd,ghd->hqg", queries, glob_k, preferred_element_type=jnp.float32) * scale
    m_win = (
        (jnp.abs(query_pos[:, None] - key_pos[None, :]) <= HALF)
        & (query_seg[:, None] == key_seg[None, :])
        & jnp.logical_not(key_flag[None, :])
    )
    top = jnp.maximum(
        jnp.max(jnp.where(m_win, s_win, neg), axis=2),
        jnp.max(jnp.where(glob_mask, s_glob, neg), axis=2),
    )
    e_win = jnp.where(m_win, jnp.exp(s_win - top[:, :, None]), 0.0)
    e_glob = jnp.where(glob_mask, jnp.exp(s_glob - top[:, :, None]), 0.0)
    total = jnp.sum(e_win, axis=2) + jnp.sum(e_glob, axis=2)
    numer = jnp.einsum(
        "hqk,khd->qhd", e_win.astype(jnp.bfloat16), v_blk, preferred_element_type=jnp.float32
    )
    numer = numer + jnp.einsum(
        "hqg,ghd->qhd", e_glob.astype(jnp.bfloat16), glob_v, preferred_element_type=jnp.float32
    )
    pieces = (numer / jnp.transpose(total)[:, :, None]).astype(jnp.bfloat16)

    own_out = lax.dynamic_slice_in_dim(glob_out, seq_index * per_shard, per_shard, 1)
    placed = jnp.einsum("gt,hgd->thd", picker, own_out, preferred_element_type=jnp.float32).astype(
        jnp.bfloat16
    )
    is_own = jnp.any(own_match, axis=0)
    attention = jnp.where(is_own[:, None, None], placed, pieces).reshape(
        shard_len, heads_here * head_dim
    )

    attn_all = lax.all_gather(attention, "col", axis=0)
    attn_full = jnp.transpose(attn_all, (1, 0, 2)).reshape(shard_len, n_col * heads_here * head_dim)
    proj = jnp.dot(attn_full, w_out, preferred_element_type=jnp.float32)
    middle = layer_norm(tokens.astype(jnp.float32) + proj, ln_gain, ln_bias).astype(jnp.bfloat16)
    ffn_pre = jnp.dot(middle, f_in, preferred_element_type=jnp.float32)
    ffn_hidden = jax.nn.gelu(ffn_pre, approximate=False).astype(jnp.bfloat16)
    ffn_part = lax.psum_scatter(
        jnp.dot(ffn_hidden, f_out, preferred_element_type=jnp.float32),
        "col",
        scatter_dimension=0,
        tiled=True,
    )
    out_rows = shard_len // n_col
    mine = lax.dynamic_slice_in_dim(middle, col_index * out_rows, out_rows, 0).astype(jnp.float32)
    normed = layer_norm(mine + ffn_part, ln2_gain, ln2_bias)
    return (normed.astype(jnp.bfloat16)[None], page_pool)


def solution(mesh):
    in_specs = (
        P("row", "seq", None),
        P(None, "col", None),
        P("row", "col", None),
        P("col", None),
        P(),
        P(),
        P("row", "col"),
        P("col", "row"),
        P(),
        P(),
        P("row", None),
        P("row", None),
        P("row", "seq", None),
    )
    out_specs = (P("row", ("seq", "col"), None), P("row", "seq", None, None, None, "col", None))
    return jax.shard_map(
        per_device, mesh=mesh, in_specs=in_specs, out_specs=out_specs, check_vma=False
    )
```

```python
import functools
import math

import jax
import jax.numpy as jnp
from jax import lax
from jax.experimental import pallas as pl
from jax.experimental.pallas import tpu as pltpu
from jax.sharding import PartitionSpec as P

MESH = pl.DeviceIdType.MESH

HALF = 256


def padded(block, sides, width):
    for axis, dim in sides:
        count = lax.axis_size(axis)
        forward = [(i, i + 1) for i in range(count - 1)]
        backward = [(target, source) for source, target in forward]
        low = lax.ppermute(
            lax.slice_in_dim(block, block.shape[dim] - width, None, axis=dim), axis, forward
        )
        high = lax.ppermute(lax.slice_in_dim(block, 0, width, axis=dim), axis, backward)
        block = jnp.concatenate([low, block, high], axis=dim)
    return block


def butterfly_partners(n):
    me = lax.axis_index("seq")
    partners = []
    step = 1
    while step < n:
        bit = (me // step) % 2
        partners.append(me + step - 2 * step * bit)
        step *= 2
    return me, partners


def enter(partners):
    row, col = lax.axis_index("row"), lax.axis_index("col")
    barrier = pltpu.get_barrier_semaphore()
    for partner in partners:
        pl.semaphore_signal(barrier, inc=1, device_id=(partner, row, col), device_id_type=MESH)
    pl.semaphore_wait(barrier, len(partners))
    return row, col


def gather_kernel(n, x_ref, out_ref, self_sem, send_sem, recv_sem):
    me, partners = butterfly_partners(n)
    row, col = enter(partners)
    own = pltpu.make_async_copy(x_ref, out_ref.at[me], self_sem)
    own.start()
    own.wait()
    size = 1
    for k, partner in enumerate(partners):
        start = (me // size) * size
        copy = pltpu.make_async_remote_copy(
            src_ref=out_ref.at[pl.ds(start, size)],
            dst_ref=out_ref.at[pl.ds(start, size)],
            send_sem=send_sem.at[k],
            recv_sem=recv_sem.at[k],
            device_id=(partner, row, col),
            device_id_type=MESH,
        )
        copy.start()
        copy.wait()
        size *= 2


def seq_gather(block):
    n = lax.axis_size("seq")
    rounds = n.bit_length() - 1
    return pl.pallas_call(
        functools.partial(gather_kernel, n),
        out_shape=jax.ShapeDtypeStruct((n,) + block.shape, block.dtype),
        in_specs=[pl.BlockSpec(memory_space=pltpu.VMEM)],
        out_specs=pl.BlockSpec(memory_space=pltpu.VMEM),
        scratch_shapes=[
            pltpu.SemaphoreType.DMA(()),
            pltpu.SemaphoreType.DMA((rounds,)),
            pltpu.SemaphoreType.DMA((rounds,)),
        ],
        compiler_params=pltpu.CompilerParams(collective_id=0, has_side_effects=True),
    )(block)


def merge_parts(mine, theirs, top_lane):
    lane = lax.broadcasted_iota(jnp.int32, mine.shape, 1)
    is_top = lane == top_lane
    top_a = jnp.max(jnp.where(is_top, mine, -jnp.inf), axis=1, keepdims=True)
    top_b = jnp.max(jnp.where(is_top, theirs, -jnp.inf), axis=1, keepdims=True)
    top = jnp.maximum(top_a, top_b)
    merged = mine * jnp.exp(top_a - top) + theirs * jnp.exp(top_b - top)
    return jnp.where(is_top, top, merged)


def combine_kernel(n, top_lane, x_ref, out_ref, cur, got, send_sem, recv_sem):
    me, partners = butterfly_partners(n)
    row, col = enter(partners)
    source = x_ref
    value = x_ref[...]
    for k, partner in enumerate(partners):
        copy = pltpu.make_async_remote_copy(
            src_ref=source,
            dst_ref=got.at[k],
            send_sem=send_sem.at[k],
            recv_sem=recv_sem.at[k],
            device_id=(partner, row, col),
            device_id_type=MESH,
        )
        copy.start()
        copy.wait()
        value = merge_parts(value, got[k], top_lane)
        if k + 1 < len(partners):
            cur[k] = value
            source = cur.at[k]
    out_ref[...] = value


def seq_softmax_combine(parts, top_lane):
    n = lax.axis_size("seq")
    rounds = n.bit_length() - 1
    return pl.pallas_call(
        functools.partial(combine_kernel, n, top_lane),
        out_shape=jax.ShapeDtypeStruct(parts.shape, parts.dtype),
        in_specs=[pl.BlockSpec(memory_space=pltpu.VMEM)],
        out_specs=pl.BlockSpec(memory_space=pltpu.VMEM),
        scratch_shapes=[
            pltpu.VMEM((max(rounds - 1, 1),) + parts.shape, parts.dtype),
            pltpu.VMEM((rounds,) + parts.shape, parts.dtype),
            pltpu.SemaphoreType.DMA((rounds,)),
            pltpu.SemaphoreType.DMA((rounds,)),
        ],
        compiler_params=pltpu.CompilerParams(collective_id=1, has_side_effects=True),
    )(parts)


def layer_norm(values, gain, bias):
    center = values - jnp.mean(values, axis=1, keepdims=True)
    spread = jnp.mean(center * center, axis=1, keepdims=True)
    return center * lax.rsqrt(spread + 1e-05) * gain + bias


def per_device(
    hidden_in,
    qkv_weight,
    qkv_global_weight,
    out_weight,
    ln_gain,
    ln_bias,
    ffn_in,
    ffn_out,
    ln2_gain,
    ln2_bias,
    segment_ids,
    global_pos,
    page_owner,
):
    neg = -1e30
    tokens = hidden_in[0]
    shard_len, width = tokens.shape
    heads_here = qkv_weight.shape[1]
    triple = qkv_weight.shape[2]
    head_dim = triple // 3
    n_seq = lax.axis_size("seq")
    n_row = lax.axis_size("row")
    n_col = lax.axis_size("col")
    seq_index = lax.axis_index("seq")
    col_index = lax.axis_index("col")
    base = seq_index * shard_len
    scale = 1.0 / math.sqrt(head_dim)

    all_pos = global_pos[0]
    n_glob = all_pos.shape[0]
    per_shard = n_glob // n_seq
    own_pos = lax.dynamic_slice_in_dim(all_pos, seq_index * per_shard, per_shard, 0)
    local_order = jnp.arange(shard_len, dtype=jnp.int32)
    own_match = (own_pos - base)[:, None] == local_order[None, :]
    picker = own_match.astype(jnp.bfloat16)
    own_rows = jnp.dot(picker, tokens, preferred_element_type=jnp.float32).astype(jnp.bfloat16)
    glob_rows = seq_gather(own_rows.reshape(-1, 128)).reshape(n_glob, width)

    wg_rows = qkv_global_weight.shape[0]
    fi_rows, units = ffn_in.shape
    wg_flat = qkv_global_weight.reshape(-1)
    fi_flat = ffn_in.reshape(-1)
    fo_flat = ffn_out.reshape(-1)
    n_wg, n_fi = wg_flat.shape[0], fi_flat.shape[0]
    everything = lax.all_gather(jnp.concatenate([wg_flat, fi_flat, fo_flat]), "row", axis=0)
    w_global = everything[:, :n_wg].reshape(n_row * wg_rows, heads_here * triple)
    f_in = everything[:, n_wg : n_wg + n_fi].reshape(n_row * fi_rows, units)
    f_out = jnp.transpose(
        everything[:, n_wg + n_fi :].reshape(n_row, units, ffn_out.shape[1]), (1, 0, 2)
    ).reshape(units, n_row * ffn_out.shape[1])
    w_out = lax.all_gather(out_weight, "col", axis=0, tiled=True)

    flat_weight = qkv_weight.reshape(width, heads_here * triple)
    qkv = jnp.dot(tokens, flat_weight, preferred_element_type=jnp.float32).astype(jnp.bfloat16)
    qkv_heads = qkv.reshape(shard_len, heads_here, triple)
    queries = qkv_heads[:, :, :head_dim]
    kv_local = qkv_heads[:, :, head_dim:]

    owners = page_owner[0, :, 0]
    n_pages = owners.shape[0]
    page_len = shard_len // n_pages
    capacity = max(2, n_pages // n_seq)
    page_order = jnp.arange(n_pages, dtype=jnp.int32)
    slot = jnp.sum(
        ((owners[:, None] == owners[None, :]) & (page_order[None, :] < page_order[:, None])).astype(
            jnp.int32
        ),
        axis=1,
    )
    target = owners * capacity + slot
    placing = (target[None, :] == jnp.arange(n_seq * capacity, dtype=jnp.int32)[:, None]).astype(
        jnp.bfloat16
    )
    outgoing = jnp.dot(
        placing,
        kv_local.reshape(n_pages, page_len * heads_here * 2 * head_dim),
        preferred_element_type=jnp.float32,
    ).astype(jnp.bfloat16)
    outgoing = outgoing.reshape(n_seq, capacity, page_len, heads_here, 2 * head_dim)
    arrived = lax.all_to_all(outgoing, "seq", split_axis=0, concat_axis=0, tiled=True)
    page_pool = arrived[None, None]

    kv_ext = padded(kv_local, (("seq", 0),), HALF)

    glob_qkv = jnp.dot(glob_rows, flat_weight, preferred_element_type=jnp.float32).astype(
        jnp.bfloat16
    )
    glob_kv = glob_qkv.reshape(n_glob, heads_here, triple)[:, :, head_dim:]
    glob_k = glob_kv[:, :, :head_dim]
    glob_v = glob_kv[:, :, head_dim:]
    glob_q = (
        jnp.dot(glob_rows, w_global, preferred_element_type=jnp.float32)
        .astype(jnp.bfloat16)
        .reshape(n_glob, heads_here, triple)[:, :, :head_dim]
    )
    global_kv_local = (
        jnp.dot(tokens, w_global, preferred_element_type=jnp.float32)
        .astype(jnp.bfloat16)
        .reshape(shard_len, heads_here, triple)[:, :, head_dim:]
    )

    seg_all = segment_ids[0]
    glob_seg = jnp.take(seg_all, all_pos)
    seg_pad = jnp.pad(seg_all, (HALF, HALF), constant_values=-1)
    query_seg = lax.dynamic_slice_in_dim(seg_all, base, shard_len, 0)
    key_seg = lax.dynamic_slice_in_dim(seg_pad, base, shard_len + 2 * HALF, 0)
    key_pos = base - HALF + jnp.arange(shard_len + 2 * HALF, dtype=jnp.int32)
    key_flag = jnp.any(key_pos[:, None] == all_pos[None, :], axis=1)
    query_pos = base + local_order

    s_part = (
        jnp.einsum(
            "ghd,khd->hgk",
            glob_q,
            global_kv_local[:, :, :head_dim],
            preferred_element_type=jnp.float32,
        )
        * scale
    )
    part_mask = glob_seg[:, None] == query_seg[None, :]
    part_top = jnp.max(jnp.where(part_mask, s_part, neg), axis=2)
    e_part = jnp.where(part_mask, jnp.exp(s_part - part_top[:, :, None]), 0.0)
    part_total = jnp.sum(e_part, axis=2)
    part_acc = jnp.einsum(
        "hgk,khd->hgd",
        e_part,
        global_kv_local[:, :, head_dim:].astype(jnp.float32),
        precision=lax.Precision.HIGHEST,
    )
    packed = jnp.concatenate(
        [
            part_acc,
            part_total[:, :, None],
            jnp.broadcast_to(part_top[:, :, None], part_top.shape + (128 - head_dim - 1,)),
        ],
        axis=2,
    ).reshape(heads_here * n_glob, 128)
    merged = seq_softmax_combine(packed, head_dim + 1).reshape(heads_here, n_glob, 128)
    glob_out = (merged[:, :, :head_dim] / merged[:, :, head_dim : head_dim + 1]).astype(
        jnp.bfloat16
    )

    glob_mask = query_seg[:, None] == glob_seg[None, :]
    k_blk = kv_ext[:, :, :head_dim]
    v_blk = kv_ext[:, :, head_dim:]
    s_win = jnp.einsum("qhd,khd->hqk", queries, k_blk, preferred_element_type=jnp.float32) * scale
    s_glob = jnp.einsum("qhd,ghd->hqg", queries, glob_k, preferred_element_type=jnp.float32) * scale
    m_win = (
        (jnp.abs(query_pos[:, None] - key_pos[None, :]) <= HALF)
        & (query_seg[:, None] == key_seg[None, :])
        & jnp.logical_not(key_flag[None, :])
    )
    top = jnp.maximum(
        jnp.max(jnp.where(m_win, s_win, neg), axis=2),
        jnp.max(jnp.where(glob_mask, s_glob, neg), axis=2),
    )
    e_win = jnp.where(m_win, jnp.exp(s_win - top[:, :, None]), 0.0)
    e_glob = jnp.where(glob_mask, jnp.exp(s_glob - top[:, :, None]), 0.0)
    total = jnp.sum(e_win, axis=2) + jnp.sum(e_glob, axis=2)
    numer = jnp.einsum(
        "hqk,khd->qhd", e_win.astype(jnp.bfloat16), v_blk, preferred_element_type=jnp.float32
    )
    numer = numer + jnp.einsum(
        "hqg,ghd->qhd", e_glob.astype(jnp.bfloat16), glob_v, preferred_element_type=jnp.float32
    )
    pieces = (numer / jnp.transpose(total)[:, :, None]).astype(jnp.bfloat16)

    own_out = lax.dynamic_slice_in_dim(glob_out, seq_index * per_shard, per_shard, 1)
    placed = jnp.einsum("gt,hgd->thd", picker, own_out, preferred_element_type=jnp.float32).astype(
        jnp.bfloat16
    )
    is_own = jnp.any(own_match, axis=0)
    attention = jnp.where(is_own[:, None, None], placed, pieces).reshape(
        shard_len, heads_here * head_dim
    )

    attn_all = lax.all_gather(attention, "col", axis=0)
    attn_full = jnp.transpose(attn_all, (1, 0, 2)).reshape(shard_len, n_col * heads_here * head_dim)
    proj = jnp.dot(attn_full, w_out, preferred_element_type=jnp.float32)
    middle = layer_norm(tokens.astype(jnp.float32) + proj, ln_gain, ln_bias).astype(jnp.bfloat16)
    ffn_pre = jnp.dot(middle, f_in, preferred_element_type=jnp.float32)
    ffn_hidden = jax.nn.gelu(ffn_pre, approximate=False).astype(jnp.bfloat16)
    ffn_part = lax.psum_scatter(
        jnp.dot(ffn_hidden, f_out, preferred_element_type=jnp.float32),
        "col",
        scatter_dimension=0,
        tiled=True,
    )
    out_rows = shard_len // n_col
    mine = lax.dynamic_slice_in_dim(middle, col_index * out_rows, out_rows, 0).astype(jnp.float32)
    normed = layer_norm(mine + ffn_part, ln2_gain, ln2_bias)
    return (normed.astype(jnp.bfloat16)[None], page_pool)


def solution(mesh):
    in_specs = (
        P("row", "seq", None),
        P(None, "col", None),
        P("row", "col", None),
        P("col", None),
        P(),
        P(),
        P("row", "col"),
        P("col", "row"),
        P(),
        P(),
        P("row", None),
        P("row", None),
        P("row", "seq", None),
    )
    out_specs = (P("row", ("seq", "col"), None), P("row", "seq", None, None, None, "col", None))
    return jax.shard_map(
        per_device, mesh=mesh, in_specs=in_specs, out_specs=out_specs, check_vma=False
    )
```

```python
import functools
import math

import jax
import jax.numpy as jnp
from jax import lax
from jax.experimental import pallas as pl
from jax.experimental.pallas import tpu as pltpu
from jax.sharding import PartitionSpec as P

MESH = pl.DeviceIdType.MESH

HALF = 256


def padded(block, sides, width):
    for axis, dim in sides:
        count = lax.axis_size(axis)
        forward = [(i, i + 1) for i in range(count - 1)]
        backward = [(target, source) for source, target in forward]
        low = lax.ppermute(
            lax.slice_in_dim(block, block.shape[dim] - width, None, axis=dim), axis, forward
        )
        high = lax.ppermute(lax.slice_in_dim(block, 0, width, axis=dim), axis, backward)
        block = jnp.concatenate([low, block, high], axis=dim)
    return block


def butterfly_partners(n):
    me = lax.axis_index("seq")
    partners = []
    step = 1
    while step < n:
        bit = (me // step) % 2
        partners.append(me + step - 2 * step * bit)
        step *= 2
    return me, partners


def enter(partners):
    row, col = lax.axis_index("row"), lax.axis_index("col")
    barrier = pltpu.get_barrier_semaphore()
    for partner in partners:
        pl.semaphore_signal(barrier, inc=1, device_id=(partner, row, col), device_id_type=MESH)
    pl.semaphore_wait(barrier, len(partners))
    return row, col


def gather_kernel(n, x_ref, out_ref, self_sem, send_sem, recv_sem):
    me, partners = butterfly_partners(n)
    row, col = enter(partners)
    own = pltpu.make_async_copy(x_ref, out_ref.at[me], self_sem)
    own.start()
    own.wait()
    size = 1
    for k, partner in enumerate(partners):
        start = (me // size) * size
        copy = pltpu.make_async_remote_copy(
            src_ref=out_ref.at[pl.ds(start, size)],
            dst_ref=out_ref.at[pl.ds(start, size)],
            send_sem=send_sem.at[k],
            recv_sem=recv_sem.at[k],
            device_id=(partner, row, col),
            device_id_type=MESH,
        )
        copy.start()
        copy.wait()
        size *= 2


def seq_gather(block):
    n = lax.axis_size("seq")
    rounds = n.bit_length() - 1
    return pl.pallas_call(
        functools.partial(gather_kernel, n),
        out_shape=jax.ShapeDtypeStruct((n,) + block.shape, block.dtype),
        in_specs=[pl.BlockSpec(memory_space=pltpu.VMEM)],
        out_specs=pl.BlockSpec(memory_space=pltpu.VMEM),
        scratch_shapes=[
            pltpu.SemaphoreType.DMA(()),
            pltpu.SemaphoreType.DMA((rounds,)),
            pltpu.SemaphoreType.DMA((rounds,)),
        ],
        compiler_params=pltpu.CompilerParams(collective_id=0, has_side_effects=True),
    )(block)


def merge_parts(mine, theirs, top_lane):
    lane = lax.broadcasted_iota(jnp.int32, mine.shape, 1)
    is_top = lane == top_lane
    top_a = jnp.max(jnp.where(is_top, mine, -jnp.inf), axis=1, keepdims=True)
    top_b = jnp.max(jnp.where(is_top, theirs, -jnp.inf), axis=1, keepdims=True)
    top = jnp.maximum(top_a, top_b)
    merged = mine * jnp.exp(top_a - top) + theirs * jnp.exp(top_b - top)
    return jnp.where(is_top, top, merged)


def halving_kernel(n, top_lane, x_ref, out_ref, *scratch):
    rounds = len(scratch) // 3
    kept, got, sems = scratch[:rounds], scratch[rounds : 2 * rounds], scratch[2 * rounds :]
    me = lax.axis_index("seq")
    steps = []
    step = n // 2
    while step >= 1:
        bit = (me // step) % 2
        steps.append((me + step - 2 * step * bit, bit))
        step //= 2
    row, col = enter([partner for partner, _ in steps])
    source = x_ref
    for k, (partner, bit) in enumerate(steps):
        half = source.shape[0] // 2
        send_at = pl.multiple_of((1 - bit) * half, 8)
        keep_at = pl.multiple_of(bit * half, 8)
        copy = pltpu.make_async_remote_copy(
            src_ref=source.at[pl.ds(send_at, half)],
            dst_ref=got[k],
            send_sem=sems[k].at[0],
            recv_sem=sems[k].at[1],
            device_id=(partner, row, col),
            device_id_type=MESH,
        )
        copy.start()
        copy.wait()
        value = merge_parts(source[pl.ds(keep_at, half)], got[k][...], top_lane)
        if k + 1 < rounds:
            kept[k][...] = value
            source = kept[k]
        else:
            out_ref[...] = value


def seq_softmax_combine(parts, top_lane):
    n = lax.axis_size("seq")
    rounds = n.bit_length() - 1
    rows, lanes = parts.shape
    scratch = []
    for k in range(rounds):
        scratch.append(pltpu.VMEM((rows >> (k + 1), lanes), parts.dtype))
    for k in range(rounds):
        scratch.append(pltpu.VMEM((rows >> (k + 1), lanes), parts.dtype))
    for k in range(rounds):
        scratch.append(pltpu.SemaphoreType.DMA((2,)))
    return pl.pallas_call(
        functools.partial(halving_kernel, n, top_lane),
        out_shape=jax.ShapeDtypeStruct((rows // n, lanes), parts.dtype),
        in_specs=[pl.BlockSpec(memory_space=pltpu.VMEM)],
        out_specs=pl.BlockSpec(memory_space=pltpu.VMEM),
        scratch_shapes=scratch,
        compiler_params=pltpu.CompilerParams(collective_id=1, has_side_effects=True),
    )(parts)


def layer_norm(values, gain, bias):
    center = values - jnp.mean(values, axis=1, keepdims=True)
    spread = jnp.mean(center * center, axis=1, keepdims=True)
    return center * lax.rsqrt(spread + 1e-05) * gain + bias


def per_device(
    hidden_in,
    qkv_weight,
    qkv_global_weight,
    out_weight,
    ln_gain,
    ln_bias,
    ffn_in,
    ffn_out,
    ln2_gain,
    ln2_bias,
    segment_ids,
    global_pos,
    page_owner,
):
    neg = -1e30
    tokens = hidden_in[0]
    shard_len, width = tokens.shape
    heads_here = qkv_weight.shape[1]
    triple = qkv_weight.shape[2]
    head_dim = triple // 3
    n_seq = lax.axis_size("seq")
    n_row = lax.axis_size("row")
    n_col = lax.axis_size("col")
    seq_index = lax.axis_index("seq")
    col_index = lax.axis_index("col")
    base = seq_index * shard_len
    scale = 1.0 / math.sqrt(head_dim)

    all_pos = global_pos[0]
    n_glob = all_pos.shape[0]
    per_shard = n_glob // n_seq
    own_pos = lax.dynamic_slice_in_dim(all_pos, seq_index * per_shard, per_shard, 0)
    local_order = jnp.arange(shard_len, dtype=jnp.int32)
    own_match = (own_pos - base)[:, None] == local_order[None, :]
    picker = own_match.astype(jnp.bfloat16)
    own_rows = jnp.dot(picker, tokens, preferred_element_type=jnp.float32).astype(jnp.bfloat16)
    glob_rows = seq_gather(own_rows.reshape(-1, 128)).reshape(n_glob, width)

    w_global = lax.all_gather(
        qkv_global_weight.reshape(qkv_global_weight.shape[0], -1), "row", axis=0, tiled=True
    )
    fi_rows, units = ffn_in.shape
    fi_flat = ffn_in.reshape(-1)
    n_fi = fi_flat.shape[0]
    everything = lax.all_gather(
        jnp.concatenate([fi_flat, ffn_out.reshape(-1)]), "row", axis=0
    )
    f_in = everything[:, :n_fi].reshape(n_row * fi_rows, units)
    f_out = jnp.transpose(
        everything[:, n_fi:].reshape(n_row, units, ffn_out.shape[1]), (1, 0, 2)
    ).reshape(units, n_row * ffn_out.shape[1])
    w_out = lax.all_gather(out_weight, "col", axis=0, tiled=True)

    flat_weight = qkv_weight.reshape(width, heads_here * triple)
    qkv = jnp.dot(tokens, flat_weight, preferred_element_type=jnp.float32).astype(jnp.bfloat16)
    qkv_heads = qkv.reshape(shard_len, heads_here, triple)
    queries = qkv_heads[:, :, :head_dim]
    kv_local = qkv_heads[:, :, head_dim:]

    owners = page_owner[0, :, 0]
    n_pages = owners.shape[0]
    page_len = shard_len // n_pages
    capacity = max(2, n_pages // n_seq)
    page_order = jnp.arange(n_pages, dtype=jnp.int32)
    slot = jnp.sum(
        ((owners[:, None] == owners[None, :]) & (page_order[None, :] < page_order[:, None])).astype(
            jnp.int32
        ),
        axis=1,
    )
    target = owners * capacity + slot
    placing = (target[None, :] == jnp.arange(n_seq * capacity, dtype=jnp.int32)[:, None]).astype(
        jnp.bfloat16
    )
    outgoing = jnp.dot(
        placing,
        kv_local.reshape(n_pages, page_len * heads_here * 2 * head_dim),
        preferred_element_type=jnp.float32,
    ).astype(jnp.bfloat16)
    outgoing = outgoing.reshape(n_seq, capacity, page_len, heads_here, 2 * head_dim)
    arrived = lax.all_to_all(outgoing, "seq", split_axis=0, concat_axis=0, tiled=True)
    page_pool = arrived[None, None]
    page_pool, glob_rows = lax.optimization_barrier((page_pool, glob_rows))

    kv_ext = padded(kv_local, (("seq", 0),), HALF)

    glob_qkv = jnp.dot(glob_rows, flat_weight, preferred_element_type=jnp.float32).astype(
        jnp.bfloat16
    )
    glob_kv = glob_qkv.reshape(n_glob, heads_here, triple)[:, :, head_dim:]
    glob_k = glob_kv[:, :, :head_dim]
    glob_v = glob_kv[:, :, head_dim:]
    glob_q = (
        jnp.dot(glob_rows, w_global, preferred_element_type=jnp.float32)
        .astype(jnp.bfloat16)
        .reshape(n_glob, heads_here, triple)[:, :, :head_dim]
    )
    global_kv_local = (
        jnp.dot(tokens, w_global, preferred_element_type=jnp.float32)
        .astype(jnp.bfloat16)
        .reshape(shard_len, heads_here, triple)[:, :, head_dim:]
    )

    seg_all = segment_ids[0]
    glob_seg = jnp.take(seg_all, all_pos)
    seg_pad = jnp.pad(seg_all, (HALF, HALF), constant_values=-1)
    query_seg = lax.dynamic_slice_in_dim(seg_all, base, shard_len, 0)
    key_seg = lax.dynamic_slice_in_dim(seg_pad, base, shard_len + 2 * HALF, 0)
    key_pos = base - HALF + jnp.arange(shard_len + 2 * HALF, dtype=jnp.int32)
    key_flag = jnp.any(key_pos[:, None] == all_pos[None, :], axis=1)
    query_pos = base + local_order

    s_part = (
        jnp.einsum(
            "ghd,khd->hgk",
            glob_q,
            global_kv_local[:, :, :head_dim],
            preferred_element_type=jnp.float32,
        )
        * scale
    )
    part_mask = glob_seg[:, None] == query_seg[None, :]
    part_top = jnp.max(jnp.where(part_mask, s_part, neg), axis=2)
    e_part = jnp.where(part_mask, jnp.exp(s_part - part_top[:, :, None]), 0.0)
    part_total = jnp.sum(e_part, axis=2)
    part_acc = jnp.einsum(
        "hgk,khd->hgd",
        e_part,
        global_kv_local[:, :, head_dim:].astype(jnp.float32),
        precision=lax.Precision.HIGHEST,
    )
    packed = jnp.concatenate(
        [
            part_acc,
            part_total[:, :, None],
            jnp.broadcast_to(part_top[:, :, None], part_top.shape + (128 - head_dim - 1,)),
        ],
        axis=2,
    )
    packed = jnp.transpose(packed, (1, 0, 2)).reshape(n_glob * heads_here, 128)
    merged = seq_softmax_combine(packed, head_dim + 1).reshape(per_shard, heads_here, 128)
    own_out = jnp.transpose(
        (merged[:, :, :head_dim] / merged[:, :, head_dim : head_dim + 1]).astype(jnp.bfloat16),
        (1, 0, 2),
    )

    glob_mask = query_seg[:, None] == glob_seg[None, :]
    k_blk = kv_ext[:, :, :head_dim]
    v_blk = kv_ext[:, :, head_dim:]
    s_win = jnp.einsum("qhd,khd->hqk", queries, k_blk, preferred_element_type=jnp.float32) * scale
    s_glob = jnp.einsum("qhd,ghd->hqg", queries, glob_k, preferred_element_type=jnp.float32) * scale
    m_win = (
        (jnp.abs(query_pos[:, None] - key_pos[None, :]) <= HALF)
        & (query_seg[:, None] == key_seg[None, :])
        & jnp.logical_not(key_flag[None, :])
    )
    top = jnp.maximum(
        jnp.max(jnp.where(m_win, s_win, neg), axis=2),
        jnp.max(jnp.where(glob_mask, s_glob, neg), axis=2),
    )
    e_win = jnp.where(m_win, jnp.exp(s_win - top[:, :, None]), 0.0)
    e_glob = jnp.where(glob_mask, jnp.exp(s_glob - top[:, :, None]), 0.0)
    total = jnp.sum(e_win, axis=2) + jnp.sum(e_glob, axis=2)
    numer = jnp.einsum(
        "hqk,khd->qhd", e_win.astype(jnp.bfloat16), v_blk, preferred_element_type=jnp.float32
    )
    numer = numer + jnp.einsum(
        "hqg,ghd->qhd", e_glob.astype(jnp.bfloat16), glob_v, preferred_element_type=jnp.float32
    )
    pieces = (numer / jnp.transpose(total)[:, :, None]).astype(jnp.bfloat16)

    placed = jnp.einsum("gt,hgd->thd", picker, own_out, preferred_element_type=jnp.float32).astype(
        jnp.bfloat16
    )
    is_own = jnp.any(own_match, axis=0)
    attention = jnp.where(is_own[:, None, None], placed, pieces).reshape(
        shard_len, heads_here * head_dim
    )

    attn_all = lax.all_gather(attention, "col", axis=0)
    attn_full = jnp.transpose(attn_all, (1, 0, 2)).reshape(shard_len, n_col * heads_here * head_dim)
    proj = jnp.dot(attn_full, w_out, preferred_element_type=jnp.float32)
    middle = layer_norm(tokens.astype(jnp.float32) + proj, ln_gain, ln_bias).astype(jnp.bfloat16)
    ffn_pre = jnp.dot(middle, f_in, preferred_element_type=jnp.float32)
    ffn_hidden = jax.nn.gelu(ffn_pre, approximate=False).astype(jnp.bfloat16)
    ffn_part = lax.psum_scatter(
        jnp.dot(ffn_hidden, f_out, preferred_element_type=jnp.float32),
        "col",
        scatter_dimension=0,
        tiled=True,
    )
    out_rows = shard_len // n_col
    mine = lax.dynamic_slice_in_dim(middle, col_index * out_rows, out_rows, 0).astype(jnp.float32)
    normed = layer_norm(mine + ffn_part, ln2_gain, ln2_bias)
    return (normed.astype(jnp.bfloat16)[None], page_pool)


def solution(mesh):
    in_specs = (
        P("row", "seq", None),
        P(None, "col", None),
        P("row", "col", None),
        P("col", None),
        P(),
        P(),
        P("row", "col"),
        P("col", "row"),
        P(),
        P(),
        P("row", None),
        P("row", None),
        P("row", "seq", None),
    )
    out_specs = (P("row", ("seq", "col"), None), P("row", "seq", None, None, None, "col", None))
    return jax.shard_map(
        per_device, mesh=mesh, in_specs=in_specs, out_specs=out_specs, check_vma=False
    )
```

```python
import functools
import math

import jax
import jax.numpy as jnp
from jax import lax
from jax.experimental import pallas as pl
from jax.experimental.pallas import tpu as pltpu
from jax.sharding import PartitionSpec as P

MESH = pl.DeviceIdType.MESH

HALF = 256


def padded(block, sides, width):
    for axis, dim in sides:
        count = lax.axis_size(axis)
        forward = [(i, i + 1) for i in range(count - 1)]
        backward = [(target, source) for source, target in forward]
        low = lax.ppermute(
            lax.slice_in_dim(block, block.shape[dim] - width, None, axis=dim), axis, forward
        )
        high = lax.ppermute(lax.slice_in_dim(block, 0, width, axis=dim), axis, backward)
        block = jnp.concatenate([low, block, high], axis=dim)
    return block


def butterfly_partners(n):
    me = lax.axis_index("seq")
    partners = []
    step = 1
    while step < n:
        bit = (me // step) % 2
        partners.append(me + step - 2 * step * bit)
        step *= 2
    return me, partners


def enter(partners):
    row, col = lax.axis_index("row"), lax.axis_index("col")
    barrier = pltpu.get_barrier_semaphore()
    for partner in partners:
        pl.semaphore_signal(barrier, inc=1, device_id=(partner, row, col), device_id_type=MESH)
    pl.semaphore_wait(barrier, len(partners))
    return row, col


def gather_kernel(n, x_ref, out_ref, self_sem, send_sem, recv_sem):
    me, partners = butterfly_partners(n)
    row, col = enter(partners)
    own = pltpu.make_async_copy(x_ref, out_ref.at[me], self_sem)
    own.start()
    own.wait()
    size = 1
    for k, partner in enumerate(partners):
        start = (me // size) * size
        copy = pltpu.make_async_remote_copy(
            src_ref=out_ref.at[pl.ds(start, size)],
            dst_ref=out_ref.at[pl.ds(start, size)],
            send_sem=send_sem.at[k],
            recv_sem=recv_sem.at[k],
            device_id=(partner, row, col),
            device_id_type=MESH,
        )
        copy.start()
        copy.wait()
        size *= 2


def seq_gather(block):
    n = lax.axis_size("seq")
    rounds = n.bit_length() - 1
    return pl.pallas_call(
        functools.partial(gather_kernel, n),
        out_shape=jax.ShapeDtypeStruct((n,) + block.shape, block.dtype),
        in_specs=[pl.BlockSpec(memory_space=pltpu.VMEM)],
        out_specs=pl.BlockSpec(memory_space=pltpu.VMEM),
        scratch_shapes=[
            pltpu.SemaphoreType.DMA(()),
            pltpu.SemaphoreType.DMA((rounds,)),
            pltpu.SemaphoreType.DMA((rounds,)),
        ],
        compiler_params=pltpu.CompilerParams(collective_id=0, has_side_effects=True),
    )(block)


def merge_parts(mine, theirs, top_lane):
    lane = lax.broadcasted_iota(jnp.int32, mine.shape, 1)
    is_top = lane == top_lane
    top_a = jnp.max(jnp.where(is_top, mine, -jnp.inf), axis=1, keepdims=True)
    top_b = jnp.max(jnp.where(is_top, theirs, -jnp.inf), axis=1, keepdims=True)
    top = jnp.maximum(top_a, top_b)
    merged = mine * jnp.exp(top_a - top) + theirs * jnp.exp(top_b - top)
    return jnp.where(is_top, top, merged)


def halving_kernel(n, top_lane, x_ref, out_ref, *scratch):
    rounds = len(scratch) // 3
    kept, got, sems = scratch[:rounds], scratch[rounds : 2 * rounds], scratch[2 * rounds :]
    me = lax.axis_index("seq")
    steps = []
    step = n // 2
    while step >= 1:
        bit = (me // step) % 2
        steps.append((me + step - 2 * step * bit, bit))
        step //= 2
    row, col = enter([partner for partner, _ in steps])
    source = x_ref
    for k, (partner, bit) in enumerate(steps):
        half = source.shape[0] // 2
        send_at = pl.multiple_of((1 - bit) * half, 8)
        keep_at = pl.multiple_of(bit * half, 8)
        copy = pltpu.make_async_remote_copy(
            src_ref=source.at[pl.ds(send_at, half)],
            dst_ref=got[k],
            send_sem=sems[k].at[0],
            recv_sem=sems[k].at[1],
            device_id=(partner, row, col),
            device_id_type=MESH,
        )
        copy.start()
        copy.wait()
        value = merge_parts(source[pl.ds(keep_at, half)], got[k][...], top_lane)
        if k + 1 < rounds:
            kept[k][...] = value
            source = kept[k]
        else:
            out_ref[...] = value


def seq_softmax_combine(parts, top_lane):
    n = lax.axis_size("seq")
    rounds = n.bit_length() - 1
    rows, lanes = parts.shape
    scratch = []
    for k in range(rounds):
        scratch.append(pltpu.VMEM((rows >> (k + 1), lanes), parts.dtype))
    for k in range(rounds):
        scratch.append(pltpu.VMEM((rows >> (k + 1), lanes), parts.dtype))
    for k in range(rounds):
        scratch.append(pltpu.SemaphoreType.DMA((2,)))
    return pl.pallas_call(
        functools.partial(halving_kernel, n, top_lane),
        out_shape=jax.ShapeDtypeStruct((rows // n, lanes), parts.dtype),
        in_specs=[pl.BlockSpec(memory_space=pltpu.VMEM)],
        out_specs=pl.BlockSpec(memory_space=pltpu.VMEM),
        scratch_shapes=scratch,
        compiler_params=pltpu.CompilerParams(collective_id=1, has_side_effects=True),
    )(parts)


def col_peers():
    me, m = lax.axis_index("col"), lax.axis_size("col")
    seq, row = lax.axis_index("seq"), lax.axis_index("row")
    peers = [lax.rem(me + j, m) for j in range(1, m)]
    barrier = pltpu.get_barrier_semaphore()
    for peer in peers:
        pl.semaphore_signal(barrier, inc=1, device_id=(seq, row, peer), device_id_type=MESH)
    pl.semaphore_wait(barrier, len(peers))
    return me, [(seq, row, peer) for peer in peers]


def col_gather_kernel(x_ref, out_ref, self_sem, send_sem, recv_sem):
    me, peers = col_peers()
    own = pltpu.make_async_copy(x_ref, out_ref.at[me], self_sem)
    own.start()
    copies = []
    for j, peer in enumerate(peers):
        copy = pltpu.make_async_remote_copy(
            src_ref=x_ref,
            dst_ref=out_ref.at[me],
            send_sem=send_sem.at[j],
            recv_sem=recv_sem.at[j],
            device_id=peer,
            device_id_type=MESH,
        )
        copy.start()
        copies.append(copy)
    own.wait()
    for copy in copies:
        copy.wait()


def col_gather(block):
    m = lax.axis_size("col")
    return pl.pallas_call(
        col_gather_kernel,
        out_shape=jax.ShapeDtypeStruct((m,) + block.shape, block.dtype),
        in_specs=[pl.BlockSpec(memory_space=pltpu.VMEM)],
        out_specs=pl.BlockSpec(memory_space=pltpu.VMEM),
        scratch_shapes=[
            pltpu.SemaphoreType.DMA(()),
            pltpu.SemaphoreType.DMA((m - 1,)),
            pltpu.SemaphoreType.DMA((m - 1,)),
        ],
        compiler_params=pltpu.CompilerParams(collective_id=2, has_side_effects=True),
    )(block)


def col_sum_kernel(x_ref, own_ref, out_ref, got, send_sem, recv_sem):
    me, peers = col_peers()
    copies = []
    for j, peer in enumerate(peers):
        copy = pltpu.make_async_remote_copy(
            src_ref=x_ref.at[peer[2]],
            dst_ref=got.at[j],
            send_sem=send_sem.at[j],
            recv_sem=recv_sem.at[j],
            device_id=peer,
            device_id_type=MESH,
        )
        copy.start()
        copies.append(copy)
    for copy in copies:
        copy.wait()
    chunk = 32

    def body(i, carry):
        rows = pl.ds(pl.multiple_of(i * chunk, chunk), chunk)
        total = own_ref[rows, :]
        for j in range(len(copies)):
            total = total + got[j, rows, :].astype(jnp.float32)
        out_ref[rows, :] = total
        return carry

    lax.fori_loop(0, out_ref.shape[0] // chunk, body, 0)


def col_reduce_scatter(parts, own):
    m = lax.axis_size("col")
    return pl.pallas_call(
        col_sum_kernel,
        out_shape=jax.ShapeDtypeStruct(own.shape, jnp.float32),
        in_specs=[pl.BlockSpec(memory_space=pltpu.VMEM)] * 2,
        out_specs=pl.BlockSpec(memory_space=pltpu.VMEM),
        scratch_shapes=[
            pltpu.VMEM((m - 1,) + parts.shape[1:], parts.dtype),
            pltpu.SemaphoreType.DMA((m - 1,)),
            pltpu.SemaphoreType.DMA((m - 1,)),
        ],
        compiler_params=pltpu.CompilerParams(collective_id=3, has_side_effects=True),
    )(parts, own)


def layer_norm(values, gain, bias):
    center = values - jnp.mean(values, axis=1, keepdims=True)
    spread = jnp.mean(center * center, axis=1, keepdims=True)
    return center * lax.rsqrt(spread + 1e-05) * gain + bias


def per_device(
    hidden_in,
    qkv_weight,
    qkv_global_weight,
    out_weight,
    ln_gain,
    ln_bias,
    ffn_in,
    ffn_out,
    ln2_gain,
    ln2_bias,
    segment_ids,
    global_pos,
    page_owner,
):
    neg = -1e30
    tokens = hidden_in[0]
    shard_len, width = tokens.shape
    heads_here = qkv_weight.shape[1]
    triple = qkv_weight.shape[2]
    head_dim = triple // 3
    n_seq = lax.axis_size("seq")
    n_row = lax.axis_size("row")
    n_col = lax.axis_size("col")
    seq_index = lax.axis_index("seq")
    col_index = lax.axis_index("col")
    base = seq_index * shard_len
    scale = 1.0 / math.sqrt(head_dim)

    all_pos = global_pos[0]
    n_glob = all_pos.shape[0]
    per_shard = n_glob // n_seq
    own_pos = lax.dynamic_slice_in_dim(all_pos, seq_index * per_shard, per_shard, 0)
    local_order = jnp.arange(shard_len, dtype=jnp.int32)
    own_match = (own_pos - base)[:, None] == local_order[None, :]
    picker = own_match.astype(jnp.bfloat16)
    own_rows = jnp.dot(picker, tokens, preferred_element_type=jnp.float32).astype(jnp.bfloat16)
    glob_rows = seq_gather(own_rows.reshape(-1, 128)).reshape(n_glob, width)

    w_global = lax.all_gather(
        qkv_global_weight.reshape(qkv_global_weight.shape[0], -1), "row", axis=0, tiled=True
    )
    fi_rows, units = ffn_in.shape
    fi_flat = ffn_in.reshape(-1)
    n_fi = fi_flat.shape[0]
    everything = lax.all_gather(
        jnp.concatenate([fi_flat, ffn_out.reshape(-1)]), "row", axis=0
    )
    f_in = everything[:, :n_fi].reshape(n_row * fi_rows, units)
    f_out = jnp.transpose(
        everything[:, n_fi:].reshape(n_row, units, ffn_out.shape[1]), (1, 0, 2)
    ).reshape(units, n_row * ffn_out.shape[1])
    w_out = lax.all_gather(out_weight, "col", axis=0, tiled=True)

    flat_weight = qkv_weight.reshape(width, heads_here * triple)
    qkv = jnp.dot(tokens, flat_weight, preferred_element_type=jnp.float32).astype(jnp.bfloat16)
    qkv_heads = qkv.reshape(shard_len, heads_here, triple)
    queries = qkv_heads[:, :, :head_dim]
    kv_local = qkv_heads[:, :, head_dim:]

    owners = page_owner[0, :, 0]
    n_pages = owners.shape[0]
    page_len = shard_len // n_pages
    capacity = max(2, n_pages // n_seq)
    page_order = jnp.arange(n_pages, dtype=jnp.int32)
    slot = jnp.sum(
        ((owners[:, None] == owners[None, :]) & (page_order[None, :] < page_order[:, None])).astype(
            jnp.int32
        ),
        axis=1,
    )
    target = owners * capacity + slot
    placing = (target[None, :] == jnp.arange(n_seq * capacity, dtype=jnp.int32)[:, None]).astype(
        jnp.bfloat16
    )
    outgoing = jnp.dot(
        placing,
        kv_local.reshape(n_pages, page_len * heads_here * 2 * head_dim),
        preferred_element_type=jnp.float32,
    ).astype(jnp.bfloat16)
    outgoing = outgoing.reshape(n_seq, capacity, page_len, heads_here, 2 * head_dim)
    arrived = lax.all_to_all(outgoing, "seq", split_axis=0, concat_axis=0, tiled=True)
    page_pool = arrived[None, None]
    page_pool, glob_rows = lax.optimization_barrier((page_pool, glob_rows))

    kv_ext = padded(kv_local, (("seq", 0),), HALF)

    glob_qkv = jnp.dot(glob_rows, flat_weight, preferred_element_type=jnp.float32).astype(
        jnp.bfloat16
    )
    glob_kv = glob_qkv.reshape(n_glob, heads_here, triple)[:, :, head_dim:]
    glob_k = glob_kv[:, :, :head_dim]
    glob_v = glob_kv[:, :, head_dim:]
    glob_q = (
        jnp.dot(glob_rows, w_global, preferred_element_type=jnp.float32)
        .astype(jnp.bfloat16)
        .reshape(n_glob, heads_here, triple)[:, :, :head_dim]
    )
    global_kv_local = (
        jnp.dot(tokens, w_global, preferred_element_type=jnp.float32)
        .astype(jnp.bfloat16)
        .reshape(shard_len, heads_here, triple)[:, :, head_dim:]
    )

    seg_all = segment_ids[0]
    glob_seg = jnp.take(seg_all, all_pos)
    seg_pad = jnp.pad(seg_all, (HALF, HALF), constant_values=-1)
    query_seg = lax.dynamic_slice_in_dim(seg_all, base, shard_len, 0)
    key_seg = lax.dynamic_slice_in_dim(seg_pad, base, shard_len + 2 * HALF, 0)
    key_pos = base - HALF + jnp.arange(shard_len + 2 * HALF, dtype=jnp.int32)
    key_flag = jnp.any(key_pos[:, None] == all_pos[None, :], axis=1)
    query_pos = base + local_order

    s_part = (
        jnp.einsum(
            "ghd,khd->hgk",
            glob_q,
            global_kv_local[:, :, :head_dim],
            preferred_element_type=jnp.float32,
        )
        * scale
    )
    part_mask = glob_seg[:, None] == query_seg[None, :]
    part_top = jnp.max(jnp.where(part_mask, s_part, neg), axis=2)
    e_part = jnp.where(part_mask, jnp.exp(s_part - part_top[:, :, None]), 0.0)
    part_total = jnp.sum(e_part, axis=2)
    part_acc = jnp.einsum(
        "hgk,khd->hgd",
        e_part,
        global_kv_local[:, :, head_dim:].astype(jnp.float32),
        precision=lax.Precision.HIGHEST,
    )
    packed = jnp.concatenate(
        [
            part_acc,
            part_total[:, :, None],
            jnp.broadcast_to(part_top[:, :, None], part_top.shape + (128 - head_dim - 1,)),
        ],
        axis=2,
    )
    packed = jnp.transpose(packed, (1, 0, 2)).reshape(n_glob * heads_here, 128)
    packed, everything = lax.optimization_barrier((packed, everything))
    merged = seq_softmax_combine(packed, head_dim + 1).reshape(per_shard, heads_here, 128)
    own_out = jnp.transpose(
        (merged[:, :, :head_dim] / merged[:, :, head_dim : head_dim + 1]).astype(jnp.bfloat16),
        (1, 0, 2),
    )

    glob_mask = query_seg[:, None] == glob_seg[None, :]
    k_blk = kv_ext[:, :, :head_dim]
    v_blk = kv_ext[:, :, head_dim:]
    s_win = jnp.einsum("qhd,khd->hqk", queries, k_blk, preferred_element_type=jnp.float32) * scale
    s_glob = jnp.einsum("qhd,ghd->hqg", queries, glob_k, preferred_element_type=jnp.float32) * scale
    m_win = (
        (jnp.abs(query_pos[:, None] - key_pos[None, :]) <= HALF)
        & (query_seg[:, None] == key_seg[None, :])
        & jnp.logical_not(key_flag[None, :])
    )
    top = jnp.maximum(
        jnp.max(jnp.where(m_win, s_win, neg), axis=2),
        jnp.max(jnp.where(glob_mask, s_glob, neg), axis=2),
    )
    e_win = jnp.where(m_win, jnp.exp(s_win - top[:, :, None]), 0.0)
    e_glob = jnp.where(glob_mask, jnp.exp(s_glob - top[:, :, None]), 0.0)
    total = jnp.sum(e_win, axis=2) + jnp.sum(e_glob, axis=2)
    numer = jnp.einsum(
        "hqk,khd->qhd", e_win.astype(jnp.bfloat16), v_blk, preferred_element_type=jnp.float32
    )
    numer = numer + jnp.einsum(
        "hqg,ghd->qhd", e_glob.astype(jnp.bfloat16), glob_v, preferred_element_type=jnp.float32
    )
    pieces = (numer / jnp.transpose(total)[:, :, None]).astype(jnp.bfloat16)

    placed = jnp.einsum("gt,hgd->thd", picker, own_out, preferred_element_type=jnp.float32).astype(
        jnp.bfloat16
    )
    is_own = jnp.any(own_match, axis=0)
    attention = jnp.where(is_own[:, None, None], placed, pieces).reshape(
        shard_len, heads_here * head_dim
    )

    attention, w_out = lax.optimization_barrier((attention, w_out))
    attn_all = col_gather(attention)
    attn_full = jnp.transpose(attn_all, (1, 0, 2)).reshape(shard_len, n_col * heads_here * head_dim)
    proj = jnp.dot(attn_full, w_out, preferred_element_type=jnp.float32)
    middle = layer_norm(tokens.astype(jnp.float32) + proj, ln_gain, ln_bias).astype(jnp.bfloat16)
    ffn_pre = jnp.dot(middle, f_in, preferred_element_type=jnp.float32)
    ffn_hidden = jax.nn.gelu(ffn_pre, approximate=False).astype(jnp.bfloat16)
    out_rows = shard_len // n_col
    ffn_full = jnp.dot(ffn_hidden, f_out, preferred_element_type=jnp.float32)
    ffn_own = lax.dynamic_slice_in_dim(ffn_full, col_index * out_rows, out_rows, 0)
    mine = lax.dynamic_slice_in_dim(middle, col_index * out_rows, out_rows, 0).astype(jnp.float32)
    second = col_reduce_scatter(
        ffn_full.astype(jnp.bfloat16).reshape(n_col, out_rows, width), mine + ffn_own
    )
    normed = layer_norm(second, ln2_gain, ln2_bias)
    return (normed.astype(jnp.bfloat16)[None], page_pool)


def solution(mesh):
    in_specs = (
        P("row", "seq", None),
        P(None, "col", None),
        P("row", "col", None),
        P("col", None),
        P(),
        P(),
        P("row", "col"),
        P("col", "row"),
        P(),
        P(),
        P("row", None),
        P("row", None),
        P("row", "seq", None),
    )
    out_specs = (P("row", ("seq", "col"), None), P("row", "seq", None, None, None, "col", None))
    return jax.shard_map(
        per_device, mesh=mesh, in_specs=in_specs, out_specs=out_specs, check_vma=False
    )
```

```python
import functools
import math

import jax
import jax.numpy as jnp
from jax import lax
from jax.experimental import pallas as pl
from jax.experimental.pallas import tpu as pltpu
from jax.sharding import PartitionSpec as P

MESH = pl.DeviceIdType.MESH

HALF = 256


def padded(block, sides, width):
    for axis, dim in sides:
        count = lax.axis_size(axis)
        forward = [(i, i + 1) for i in range(count - 1)]
        backward = [(target, source) for source, target in forward]
        low = lax.ppermute(
            lax.slice_in_dim(block, block.shape[dim] - width, None, axis=dim), axis, forward
        )
        high = lax.ppermute(lax.slice_in_dim(block, 0, width, axis=dim), axis, backward)
        block = jnp.concatenate([low, block, high], axis=dim)
    return block


def butterfly_partners(n):
    me = lax.axis_index("seq")
    partners = []
    step = 1
    while step < n:
        bit = (me // step) % 2
        partners.append(me + step - 2 * step * bit)
        step *= 2
    return me, partners


def enter(partners):
    row, col = lax.axis_index("row"), lax.axis_index("col")
    barrier = pltpu.get_barrier_semaphore()
    for partner in partners:
        pl.semaphore_signal(barrier, inc=1, device_id=(partner, row, col), device_id_type=MESH)
    pl.semaphore_wait(barrier, len(partners))
    return row, col


def gather_kernel(n, x_ref, out_ref, self_sem, send_sem, recv_sem):
    me, partners = butterfly_partners(n)
    row, col = enter(partners)
    own = pltpu.make_async_copy(x_ref, out_ref.at[me], self_sem)
    own.start()
    own.wait()
    size = 1
    for k, partner in enumerate(partners):
        start = (me // size) * size
        copy = pltpu.make_async_remote_copy(
            src_ref=out_ref.at[pl.ds(start, size)],
            dst_ref=out_ref.at[pl.ds(start, size)],
            send_sem=send_sem.at[k],
            recv_sem=recv_sem.at[k],
            device_id=(partner, row, col),
            device_id_type=MESH,
        )
        copy.start()
        copy.wait()
        size *= 2


def seq_gather(block):
    n = lax.axis_size("seq")
    rounds = n.bit_length() - 1
    return pl.pallas_call(
        functools.partial(gather_kernel, n),
        out_shape=jax.ShapeDtypeStruct((n,) + block.shape, block.dtype),
        in_specs=[pl.BlockSpec(memory_space=pltpu.VMEM)],
        out_specs=pl.BlockSpec(memory_space=pltpu.VMEM),
        scratch_shapes=[
            pltpu.SemaphoreType.DMA(()),
            pltpu.SemaphoreType.DMA((rounds,)),
            pltpu.SemaphoreType.DMA((rounds,)),
        ],
        compiler_params=pltpu.CompilerParams(collective_id=0, has_side_effects=True),
    )(block)


def merge_parts(mine, theirs, top_lane):
    lane = lax.broadcasted_iota(jnp.int32, mine.shape, 1)
    is_top = lane == top_lane
    top_a = jnp.max(jnp.where(is_top, mine, -jnp.inf), axis=1, keepdims=True)
    top_b = jnp.max(jnp.where(is_top, theirs, -jnp.inf), axis=1, keepdims=True)
    top = jnp.maximum(top_a, top_b)
    merged = mine * jnp.exp(top_a - top) + theirs * jnp.exp(top_b - top)
    return jnp.where(is_top, top, merged)


def halving_kernel(n, top_lane, x_ref, out_ref, *scratch):
    rounds = len(scratch) // 3
    kept, got, sems = scratch[:rounds], scratch[rounds : 2 * rounds], scratch[2 * rounds :]
    me = lax.axis_index("seq")
    steps = []
    step = n // 2
    while step >= 1:
        bit = (me // step) % 2
        steps.append((me + step - 2 * step * bit, bit))
        step //= 2
    row, col = enter([partner for partner, _ in steps])
    source = x_ref
    for k, (partner, bit) in enumerate(steps):
        half = source.shape[0] // 2
        send_at = pl.multiple_of((1 - bit) * half, 8)
        keep_at = pl.multiple_of(bit * half, 8)
        copy = pltpu.make_async_remote_copy(
            src_ref=source.at[pl.ds(send_at, half)],
            dst_ref=got[k],
            send_sem=sems[k].at[0],
            recv_sem=sems[k].at[1],
            device_id=(partner, row, col),
            device_id_type=MESH,
        )
        copy.start()
        copy.wait()
        value = merge_parts(source[pl.ds(keep_at, half)], got[k][...], top_lane)
        if k + 1 < rounds:
            kept[k][...] = value
            source = kept[k]
        else:
            out_ref[...] = value


def seq_softmax_combine(parts, top_lane):
    n = lax.axis_size("seq")
    rounds = n.bit_length() - 1
    rows, lanes = parts.shape
    scratch = []
    for k in range(rounds):
        scratch.append(pltpu.VMEM((rows >> (k + 1), lanes), parts.dtype))
    for k in range(rounds):
        scratch.append(pltpu.VMEM((rows >> (k + 1), lanes), parts.dtype))
    for k in range(rounds):
        scratch.append(pltpu.SemaphoreType.DMA((2,)))
    return pl.pallas_call(
        functools.partial(halving_kernel, n, top_lane),
        out_shape=jax.ShapeDtypeStruct((rows // n, lanes), parts.dtype),
        in_specs=[pl.BlockSpec(memory_space=pltpu.VMEM)],
        out_specs=pl.BlockSpec(memory_space=pltpu.VMEM),
        scratch_shapes=scratch,
        compiler_params=pltpu.CompilerParams(collective_id=1, has_side_effects=True),
    )(parts)


def seq_peers():
    me, n = lax.axis_index("seq"), lax.axis_size("seq")
    row, col = lax.axis_index("row"), lax.axis_index("col")
    peers = [lax.rem(me + j, n) for j in range(1, n)]
    barrier = pltpu.get_barrier_semaphore()
    for peer in peers:
        pl.semaphore_signal(barrier, inc=1, device_id=(peer, row, col), device_id_type=MESH)
    pl.semaphore_wait(barrier, len(peers))
    return me, [(peer, row, col) for peer in peers]


def seq_direct_gather_kernel(x_ref, out_ref, self_sem, send_sem, recv_sem):
    me, peers = seq_peers()
    own = pltpu.make_async_copy(x_ref, out_ref.at[me], self_sem)
    own.start()
    copies = []
    for j, peer in enumerate(peers):
        copy = pltpu.make_async_remote_copy(
            src_ref=x_ref,
            dst_ref=out_ref.at[me],
            send_sem=send_sem.at[j],
            recv_sem=recv_sem.at[j],
            device_id=peer,
            device_id_type=MESH,
        )
        copy.start()
        copies.append(copy)
    own.wait()
    for copy in copies:
        copy.wait()


def seq_direct_gather(block):
    n = lax.axis_size("seq")
    return pl.pallas_call(
        seq_direct_gather_kernel,
        out_shape=jax.ShapeDtypeStruct((n,) + block.shape, block.dtype),
        in_specs=[pl.BlockSpec(memory_space=pltpu.VMEM)],
        out_specs=pl.BlockSpec(memory_space=pltpu.VMEM),
        scratch_shapes=[
            pltpu.SemaphoreType.DMA(()),
            pltpu.SemaphoreType.DMA((n - 1,)),
            pltpu.SemaphoreType.DMA((n - 1,)),
        ],
        compiler_params=pltpu.CompilerParams(collective_id=4, has_side_effects=True),
    )(block)


def seq_merge_kernel(top_lane, x_ref, out_ref, got, send_sem, recv_sem):
    me, peers = seq_peers()
    copies = []
    for j, peer in enumerate(peers):
        copy = pltpu.make_async_remote_copy(
            src_ref=x_ref.at[peer[0]],
            dst_ref=got.at[j],
            send_sem=send_sem.at[j],
            recv_sem=recv_sem.at[j],
            device_id=peer,
            device_id_type=MESH,
        )
        copy.start()
        copies.append(copy)
    for copy in copies:
        copy.wait()
    value = x_ref[me]
    for j in range(len(copies)):
        value = merge_parts(value, got[j], top_lane)
    out_ref[...] = value


def seq_direct_merge(parts, top_lane):
    n = parts.shape[0]
    return pl.pallas_call(
        functools.partial(seq_merge_kernel, top_lane),
        out_shape=jax.ShapeDtypeStruct(parts.shape[1:], parts.dtype),
        in_specs=[pl.BlockSpec(memory_space=pltpu.VMEM)],
        out_specs=pl.BlockSpec(memory_space=pltpu.VMEM),
        scratch_shapes=[
            pltpu.VMEM((n - 1,) + parts.shape[1:], parts.dtype),
            pltpu.SemaphoreType.DMA((n - 1,)),
            pltpu.SemaphoreType.DMA((n - 1,)),
        ],
        compiler_params=pltpu.CompilerParams(collective_id=5, has_side_effects=True),
    )(parts)


def col_peers():
    me, m = lax.axis_index("col"), lax.axis_size("col")
    seq, row = lax.axis_index("seq"), lax.axis_index("row")
    peers = [lax.rem(me + j, m) for j in range(1, m)]
    barrier = pltpu.get_barrier_semaphore()
    for peer in peers:
        pl.semaphore_signal(barrier, inc=1, device_id=(seq, row, peer), device_id_type=MESH)
    pl.semaphore_wait(barrier, len(peers))
    return me, [(seq, row, peer) for peer in peers]


def col_gather_kernel(x_ref, out_ref, self_sem, send_sem, recv_sem):
    me, peers = col_peers()
    own = pltpu.make_async_copy(x_ref, out_ref.at[me], self_sem)
    own.start()
    copies = []
    for j, peer in enumerate(peers):
        copy = pltpu.make_async_remote_copy(
            src_ref=x_ref,
            dst_ref=out_ref.at[me],
            send_sem=send_sem.at[j],
            recv_sem=recv_sem.at[j],
            device_id=peer,
            device_id_type=MESH,
        )
        copy.start()
        copies.append(copy)
    own.wait()
    for copy in copies:
        copy.wait()


def col_gather(block):
    m = lax.axis_size("col")
    return pl.pallas_call(
        col_gather_kernel,
        out_shape=jax.ShapeDtypeStruct((m,) + block.shape, block.dtype),
        in_specs=[pl.BlockSpec(memory_space=pltpu.VMEM)],
        out_specs=pl.BlockSpec(memory_space=pltpu.VMEM),
        scratch_shapes=[
            pltpu.SemaphoreType.DMA(()),
            pltpu.SemaphoreType.DMA((m - 1,)),
            pltpu.SemaphoreType.DMA((m - 1,)),
        ],
        compiler_params=pltpu.CompilerParams(collective_id=2, has_side_effects=True),
    )(block)


def col_sum_kernel(x_ref, own_ref, out_ref, got, send_sem, recv_sem):
    me, peers = col_peers()
    copies = []
    for j, peer in enumerate(peers):
        copy = pltpu.make_async_remote_copy(
            src_ref=x_ref.at[peer[2]],
            dst_ref=got.at[j],
            send_sem=send_sem.at[j],
            recv_sem=recv_sem.at[j],
            device_id=peer,
            device_id_type=MESH,
        )
        copy.start()
        copies.append(copy)
    for copy in copies:
        copy.wait()
    chunk = 32

    def body(i, carry):
        rows = pl.ds(pl.multiple_of(i * chunk, chunk), chunk)
        total = own_ref[rows, :]
        for j in range(len(copies)):
            total = total + got[j, rows, :].astype(jnp.float32)
        out_ref[rows, :] = total
        return carry

    lax.fori_loop(0, out_ref.shape[0] // chunk, body, 0)


def col_reduce_scatter(parts, own):
    m = lax.axis_size("col")
    return pl.pallas_call(
        col_sum_kernel,
        out_shape=jax.ShapeDtypeStruct(own.shape, jnp.float32),
        in_specs=[pl.BlockSpec(memory_space=pltpu.VMEM)] * 2,
        out_specs=pl.BlockSpec(memory_space=pltpu.VMEM),
        scratch_shapes=[
            pltpu.VMEM((m - 1,) + parts.shape[1:], parts.dtype),
            pltpu.SemaphoreType.DMA((m - 1,)),
            pltpu.SemaphoreType.DMA((m - 1,)),
        ],
        compiler_params=pltpu.CompilerParams(collective_id=3, has_side_effects=True),
    )(parts, own)


def layer_norm(values, gain, bias):
    center = values - jnp.mean(values, axis=1, keepdims=True)
    spread = jnp.mean(center * center, axis=1, keepdims=True)
    return center * lax.rsqrt(spread + 1e-05) * gain + bias


def per_device(
    hidden_in,
    qkv_weight,
    qkv_global_weight,
    out_weight,
    ln_gain,
    ln_bias,
    ffn_in,
    ffn_out,
    ln2_gain,
    ln2_bias,
    segment_ids,
    global_pos,
    page_owner,
):
    neg = -1e30
    tokens = hidden_in[0]
    shard_len, width = tokens.shape
    heads_here = qkv_weight.shape[1]
    triple = qkv_weight.shape[2]
    head_dim = triple // 3
    n_seq = lax.axis_size("seq")
    n_row = lax.axis_size("row")
    n_col = lax.axis_size("col")
    seq_index = lax.axis_index("seq")
    col_index = lax.axis_index("col")
    base = seq_index * shard_len
    scale = 1.0 / math.sqrt(head_dim)

    all_pos = global_pos[0]
    n_glob = all_pos.shape[0]
    per_shard = n_glob // n_seq
    own_pos = lax.dynamic_slice_in_dim(all_pos, seq_index * per_shard, per_shard, 0)
    local_order = jnp.arange(shard_len, dtype=jnp.int32)
    own_match = (own_pos - base)[:, None] == local_order[None, :]
    picker = own_match.astype(jnp.bfloat16)
    own_rows = jnp.dot(picker, tokens, preferred_element_type=jnp.float32).astype(jnp.bfloat16)
    glob_rows = seq_direct_gather(own_rows.reshape(-1, 128)).reshape(n_glob, width)

    w_global = lax.all_gather(
        qkv_global_weight.reshape(qkv_global_weight.shape[0], -1), "row", axis=0, tiled=True
    )
    fi_rows, units = ffn_in.shape
    fi_flat = ffn_in.reshape(-1)
    n_fi = fi_flat.shape[0]
    everything = lax.all_gather(
        jnp.concatenate([fi_flat, ffn_out.reshape(-1)]), "row", axis=0
    )
    f_in = everything[:, :n_fi].reshape(n_row * fi_rows, units)
    f_out = jnp.transpose(
        everything[:, n_fi:].reshape(n_row, units, ffn_out.shape[1]), (1, 0, 2)
    ).reshape(units, n_row * ffn_out.shape[1])
    w_out = lax.all_gather(out_weight, "col", axis=0, tiled=True)

    flat_weight = qkv_weight.reshape(width, heads_here * triple)
    qkv = jnp.dot(tokens, flat_weight, preferred_element_type=jnp.float32).astype(jnp.bfloat16)
    qkv_heads = qkv.reshape(shard_len, heads_here, triple)
    queries = qkv_heads[:, :, :head_dim]
    kv_local = qkv_heads[:, :, head_dim:]

    owners = page_owner[0, :, 0]
    n_pages = owners.shape[0]
    page_len = shard_len // n_pages
    capacity = max(2, n_pages // n_seq)
    page_order = jnp.arange(n_pages, dtype=jnp.int32)
    slot = jnp.sum(
        ((owners[:, None] == owners[None, :]) & (page_order[None, :] < page_order[:, None])).astype(
            jnp.int32
        ),
        axis=1,
    )
    target = owners * capacity + slot
    placing = (target[None, :] == jnp.arange(n_seq * capacity, dtype=jnp.int32)[:, None]).astype(
        jnp.bfloat16
    )
    outgoing = jnp.dot(
        placing,
        kv_local.reshape(n_pages, page_len * heads_here * 2 * head_dim),
        preferred_element_type=jnp.float32,
    ).astype(jnp.bfloat16)
    outgoing = outgoing.reshape(n_seq, capacity, page_len, heads_here, 2 * head_dim)
    arrived = lax.all_to_all(outgoing, "seq", split_axis=0, concat_axis=0, tiled=True)
    page_pool = arrived[None, None]
    page_pool, glob_rows = lax.optimization_barrier((page_pool, glob_rows))

    kv_ext = padded(kv_local, (("seq", 0),), HALF)

    glob_qkv = jnp.dot(glob_rows, flat_weight, preferred_element_type=jnp.float32).astype(
        jnp.bfloat16
    )
    glob_kv = glob_qkv.reshape(n_glob, heads_here, triple)[:, :, head_dim:]
    glob_k = glob_kv[:, :, :head_dim]
    glob_v = glob_kv[:, :, head_dim:]
    glob_q = (
        jnp.dot(glob_rows, w_global, preferred_element_type=jnp.float32)
        .astype(jnp.bfloat16)
        .reshape(n_glob, heads_here, triple)[:, :, :head_dim]
    )
    global_kv_local = (
        jnp.dot(tokens, w_global, preferred_element_type=jnp.float32)
        .astype(jnp.bfloat16)
        .reshape(shard_len, heads_here, triple)[:, :, head_dim:]
    )

    seg_all = segment_ids[0]
    glob_seg = jnp.take(seg_all, all_pos)
    seg_pad = jnp.pad(seg_all, (HALF, HALF), constant_values=-1)
    query_seg = lax.dynamic_slice_in_dim(seg_all, base, shard_len, 0)
    key_seg = lax.dynamic_slice_in_dim(seg_pad, base, shard_len + 2 * HALF, 0)
    key_pos = base - HALF + jnp.arange(shard_len + 2 * HALF, dtype=jnp.int32)
    key_flag = jnp.any(key_pos[:, None] == all_pos[None, :], axis=1)
    query_pos = base + local_order

    s_part = (
        jnp.einsum(
            "ghd,khd->hgk",
            glob_q,
            global_kv_local[:, :, :head_dim],
            preferred_element_type=jnp.float32,
        )
        * scale
    )
    part_mask = glob_seg[:, None] == query_seg[None, :]
    part_top = jnp.max(jnp.where(part_mask, s_part, neg), axis=2)
    e_part = jnp.where(part_mask, jnp.exp(s_part - part_top[:, :, None]), 0.0)
    part_total = jnp.sum(e_part, axis=2)
    part_acc = jnp.einsum(
        "hgk,khd->hgd",
        e_part,
        global_kv_local[:, :, head_dim:].astype(jnp.float32),
        precision=lax.Precision.HIGHEST,
    )
    packed = jnp.concatenate(
        [
            part_acc,
            part_total[:, :, None],
            jnp.broadcast_to(part_top[:, :, None], part_top.shape + (128 - head_dim - 1,)),
        ],
        axis=2,
    )
    packed = jnp.transpose(packed, (1, 0, 2)).reshape(n_glob * heads_here, 128)
    packed, w_out = lax.optimization_barrier((packed, w_out))
    merged = seq_direct_merge(packed.reshape(n_seq, -1, 128), head_dim + 1).reshape(
        per_shard, heads_here, 128
    )
    own_out = jnp.transpose(
        (merged[:, :, :head_dim] / merged[:, :, head_dim : head_dim + 1]).astype(jnp.bfloat16),
        (1, 0, 2),
    )

    glob_mask = query_seg[:, None] == glob_seg[None, :]
    k_blk = kv_ext[:, :, :head_dim]
    v_blk = kv_ext[:, :, head_dim:]
    s_win = jnp.einsum("qhd,khd->hqk", queries, k_blk, preferred_element_type=jnp.float32) * scale
    s_glob = jnp.einsum("qhd,ghd->hqg", queries, glob_k, preferred_element_type=jnp.float32) * scale
    m_win = (
        (jnp.abs(query_pos[:, None] - key_pos[None, :]) <= HALF)
        & (query_seg[:, None] == key_seg[None, :])
        & jnp.logical_not(key_flag[None, :])
    )
    top = jnp.maximum(
        jnp.max(jnp.where(m_win, s_win, neg), axis=2),
        jnp.max(jnp.where(glob_mask, s_glob, neg), axis=2),
    )
    e_win = jnp.where(m_win, jnp.exp(s_win - top[:, :, None]), 0.0)
    e_glob = jnp.where(glob_mask, jnp.exp(s_glob - top[:, :, None]), 0.0)
    total = jnp.sum(e_win, axis=2) + jnp.sum(e_glob, axis=2)
    numer = jnp.einsum(
        "hqk,khd->qhd", e_win.astype(jnp.bfloat16), v_blk, preferred_element_type=jnp.float32
    )
    numer = numer + jnp.einsum(
        "hqg,ghd->qhd", e_glob.astype(jnp.bfloat16), glob_v, preferred_element_type=jnp.float32
    )
    pieces = (numer / jnp.transpose(total)[:, :, None]).astype(jnp.bfloat16)

    placed = jnp.einsum("gt,hgd->thd", picker, own_out, preferred_element_type=jnp.float32).astype(
        jnp.bfloat16
    )
    is_own = jnp.any(own_match, axis=0)
    attention = jnp.where(is_own[:, None, None], placed, pieces).reshape(
        shard_len, heads_here * head_dim
    )

    attention, everything = lax.optimization_barrier((attention, everything))
    attn_all = col_gather(attention)
    proj = jnp.einsum(
        "ctk,ckn->tn",
        attn_all,
        w_out.reshape(n_col, heads_here * head_dim, width),
        preferred_element_type=jnp.float32,
    )
    middle = layer_norm(tokens.astype(jnp.float32) + proj, ln_gain, ln_bias).astype(jnp.bfloat16)
    ffn_pre = jnp.dot(middle, f_in, preferred_element_type=jnp.float32)
    ffn_hidden = jax.nn.gelu(ffn_pre, approximate=False).astype(jnp.bfloat16)
    out_rows = shard_len // n_col
    ffn_full = jnp.dot(ffn_hidden, f_out, preferred_element_type=jnp.float32)
    ffn_own = lax.dynamic_slice_in_dim(ffn_full, col_index * out_rows, out_rows, 0)
    mine = lax.dynamic_slice_in_dim(middle, col_index * out_rows, out_rows, 0).astype(jnp.float32)
    second = col_reduce_scatter(
        ffn_full.astype(jnp.bfloat16).reshape(n_col, out_rows, width), mine + ffn_own
    )
    normed = layer_norm(second, ln2_gain, ln2_bias)
    return (normed.astype(jnp.bfloat16)[None], page_pool)


def solution(mesh):
    in_specs = (
        P("row", "seq", None),
        P(None, "col", None),
        P("row", "col", None),
        P("col", None),
        P(),
        P(),
        P("row", "col"),
        P("col", "row"),
        P(),
        P(),
        P("row", None),
        P("row", None),
        P("row", "seq", None),
    )
    out_specs = (P("row", ("seq", "col"), None), P("row", "seq", None, None, None, "col", None))
    return jax.shard_map(
        per_device, mesh=mesh, in_specs=in_specs, out_specs=out_specs, check_vma=False
    )
```

```python
import functools
import math

import jax
import jax.numpy as jnp
from jax import lax
from jax.experimental import pallas as pl
from jax.experimental.pallas import tpu as pltpu
from jax.sharding import PartitionSpec as P

MESH = pl.DeviceIdType.MESH

HALF = 256


def padded(block, sides, width):
    for axis, dim in sides:
        count = lax.axis_size(axis)
        forward = [(i, i + 1) for i in range(count - 1)]
        backward = [(target, source) for source, target in forward]
        low = lax.ppermute(
            lax.slice_in_dim(block, block.shape[dim] - width, None, axis=dim), axis, forward
        )
        high = lax.ppermute(lax.slice_in_dim(block, 0, width, axis=dim), axis, backward)
        block = jnp.concatenate([low, block, high], axis=dim)
    return block


def butterfly_partners(n):
    me = lax.axis_index("seq")
    partners = []
    step = 1
    while step < n:
        bit = (me // step) % 2
        partners.append(me + step - 2 * step * bit)
        step *= 2
    return me, partners


def enter(partners):
    row, col = lax.axis_index("row"), lax.axis_index("col")
    barrier = pltpu.get_barrier_semaphore()
    for partner in partners:
        pl.semaphore_signal(barrier, inc=1, device_id=(partner, row, col), device_id_type=MESH)
    pl.semaphore_wait(barrier, len(partners))
    return row, col


def gather_kernel(n, x_ref, out_ref, self_sem, send_sem, recv_sem):
    me, partners = butterfly_partners(n)
    row, col = enter(partners)
    own = pltpu.make_async_copy(x_ref, out_ref.at[me], self_sem)
    own.start()
    own.wait()
    size = 1
    for k, partner in enumerate(partners):
        start = (me // size) * size
        copy = pltpu.make_async_remote_copy(
            src_ref=out_ref.at[pl.ds(start, size)],
            dst_ref=out_ref.at[pl.ds(start, size)],
            send_sem=send_sem.at[k],
            recv_sem=recv_sem.at[k],
            device_id=(partner, row, col),
            device_id_type=MESH,
        )
        copy.start()
        copy.wait()
        size *= 2


def seq_gather(block):
    n = lax.axis_size("seq")
    rounds = n.bit_length() - 1
    return pl.pallas_call(
        functools.partial(gather_kernel, n),
        out_shape=jax.ShapeDtypeStruct((n,) + block.shape, block.dtype),
        in_specs=[pl.BlockSpec(memory_space=pltpu.VMEM)],
        out_specs=pl.BlockSpec(memory_space=pltpu.VMEM),
        scratch_shapes=[
            pltpu.SemaphoreType.DMA(()),
            pltpu.SemaphoreType.DMA((rounds,)),
            pltpu.SemaphoreType.DMA((rounds,)),
        ],
        compiler_params=pltpu.CompilerParams(collective_id=0, has_side_effects=True),
    )(block)


def merge_parts(mine, theirs, top_lane):
    lane = lax.broadcasted_iota(jnp.int32, mine.shape, 1)
    is_top = lane == top_lane
    top_a = jnp.max(jnp.where(is_top, mine, -jnp.inf), axis=1, keepdims=True)
    top_b = jnp.max(jnp.where(is_top, theirs, -jnp.inf), axis=1, keepdims=True)
    top = jnp.maximum(top_a, top_b)
    merged = mine * jnp.exp(top_a - top) + theirs * jnp.exp(top_b - top)
    return jnp.where(is_top, top, merged)


def halving_kernel(n, top_lane, x_ref, out_ref, *scratch):
    rounds = len(scratch) // 3
    kept, got, sems = scratch[:rounds], scratch[rounds : 2 * rounds], scratch[2 * rounds :]
    me = lax.axis_index("seq")
    steps = []
    step = n // 2
    while step >= 1:
        bit = (me // step) % 2
        steps.append((me + step - 2 * step * bit, bit))
        step //= 2
    row, col = enter([partner for partner, _ in steps])
    source = x_ref
    for k, (partner, bit) in enumerate(steps):
        half = source.shape[0] // 2
        send_at = pl.multiple_of((1 - bit) * half, 8)
        keep_at = pl.multiple_of(bit * half, 8)
        copy = pltpu.make_async_remote_copy(
            src_ref=source.at[pl.ds(send_at, half)],
            dst_ref=got[k],
            send_sem=sems[k].at[0],
            recv_sem=sems[k].at[1],
            device_id=(partner, row, col),
            device_id_type=MESH,
        )
        copy.start()
        copy.wait()
        value = merge_parts(source[pl.ds(keep_at, half)], got[k][...], top_lane)
        if k + 1 < rounds:
            kept[k][...] = value
            source = kept[k]
        else:
            out_ref[...] = value


def seq_softmax_combine(parts, top_lane):
    n = lax.axis_size("seq")
    rounds = n.bit_length() - 1
    rows, lanes = parts.shape
    scratch = []
    for k in range(rounds):
        scratch.append(pltpu.VMEM((rows >> (k + 1), lanes), parts.dtype))
    for k in range(rounds):
        scratch.append(pltpu.VMEM((rows >> (k + 1), lanes), parts.dtype))
    for k in range(rounds):
        scratch.append(pltpu.SemaphoreType.DMA((2,)))
    return pl.pallas_call(
        functools.partial(halving_kernel, n, top_lane),
        out_shape=jax.ShapeDtypeStruct((rows // n, lanes), parts.dtype),
        in_specs=[pl.BlockSpec(memory_space=pltpu.VMEM)],
        out_specs=pl.BlockSpec(memory_space=pltpu.VMEM),
        scratch_shapes=scratch,
        compiler_params=pltpu.CompilerParams(collective_id=1, has_side_effects=True),
    )(parts)


def seq_peers():
    me, n = lax.axis_index("seq"), lax.axis_size("seq")
    row, col = lax.axis_index("row"), lax.axis_index("col")
    peers = [lax.rem(me + j, n) for j in range(1, n)]
    barrier = pltpu.get_barrier_semaphore()
    for peer in peers:
        pl.semaphore_signal(barrier, inc=1, device_id=(peer, row, col), device_id_type=MESH)
    pl.semaphore_wait(barrier, len(peers))
    return me, [(peer, row, col) for peer in peers]


def seq_direct_gather_kernel(x_ref, out_ref, self_sem, send_sem, recv_sem):
    me, peers = seq_peers()
    own = pltpu.make_async_copy(x_ref, out_ref.at[me], self_sem)
    own.start()
    copies = []
    for j, peer in enumerate(peers):
        copy = pltpu.make_async_remote_copy(
            src_ref=x_ref,
            dst_ref=out_ref.at[me],
            send_sem=send_sem.at[j],
            recv_sem=recv_sem.at[j],
            device_id=peer,
            device_id_type=MESH,
        )
        copy.start()
        copies.append(copy)
    own.wait()
    for copy in copies:
        copy.wait()


def seq_direct_gather(block):
    n = lax.axis_size("seq")
    return pl.pallas_call(
        seq_direct_gather_kernel,
        out_shape=jax.ShapeDtypeStruct((n,) + block.shape, block.dtype),
        in_specs=[pl.BlockSpec(memory_space=pltpu.VMEM)],
        out_specs=pl.BlockSpec(memory_space=pltpu.VMEM),
        scratch_shapes=[
            pltpu.SemaphoreType.DMA(()),
            pltpu.SemaphoreType.DMA((n - 1,)),
            pltpu.SemaphoreType.DMA((n - 1,)),
        ],
        compiler_params=pltpu.CompilerParams(collective_id=4, has_side_effects=True),
    )(block)


def seq_merge_kernel(top_lane, x_ref, out_ref, got, send_sem, recv_sem):
    me, peers = seq_peers()
    copies = []
    for j, peer in enumerate(peers):
        copy = pltpu.make_async_remote_copy(
            src_ref=x_ref.at[peer[0]],
            dst_ref=got.at[j],
            send_sem=send_sem.at[j],
            recv_sem=recv_sem.at[j],
            device_id=peer,
            device_id_type=MESH,
        )
        copy.start()
        copies.append(copy)
    for copy in copies:
        copy.wait()
    value = x_ref[me]
    for j in range(len(copies)):
        value = merge_parts(value, got[j], top_lane)
    out_ref[...] = value


def seq_direct_merge(parts, top_lane):
    n = parts.shape[0]
    return pl.pallas_call(
        functools.partial(seq_merge_kernel, top_lane),
        out_shape=jax.ShapeDtypeStruct(parts.shape[1:], parts.dtype),
        in_specs=[pl.BlockSpec(memory_space=pltpu.VMEM)],
        out_specs=pl.BlockSpec(memory_space=pltpu.VMEM),
        scratch_shapes=[
            pltpu.VMEM((n - 1,) + parts.shape[1:], parts.dtype),
            pltpu.SemaphoreType.DMA((n - 1,)),
            pltpu.SemaphoreType.DMA((n - 1,)),
        ],
        compiler_params=pltpu.CompilerParams(collective_id=5, has_side_effects=True),
    )(parts)


def col_peers():
    me, m = lax.axis_index("col"), lax.axis_size("col")
    seq, row = lax.axis_index("seq"), lax.axis_index("row")
    peers = [lax.rem(me + j, m) for j in range(1, m)]
    barrier = pltpu.get_barrier_semaphore()
    for peer in peers:
        pl.semaphore_signal(barrier, inc=1, device_id=(seq, row, peer), device_id_type=MESH)
    pl.semaphore_wait(barrier, len(peers))
    return me, [(seq, row, peer) for peer in peers]


def col_gather_kernel(x_ref, out_ref, self_sem, send_sem, recv_sem):
    me, peers = col_peers()
    own = pltpu.make_async_copy(x_ref, out_ref.at[me], self_sem)
    own.start()
    copies = []
    for j, peer in enumerate(peers):
        copy = pltpu.make_async_remote_copy(
            src_ref=x_ref,
            dst_ref=out_ref.at[me],
            send_sem=send_sem.at[j],
            recv_sem=recv_sem.at[j],
            device_id=peer,
            device_id_type=MESH,
        )
        copy.start()
        copies.append(copy)
    own.wait()
    for copy in copies:
        copy.wait()


def col_gather(block):
    m = lax.axis_size("col")
    return pl.pallas_call(
        col_gather_kernel,
        out_shape=jax.ShapeDtypeStruct((m,) + block.shape, block.dtype),
        in_specs=[pl.BlockSpec(memory_space=pltpu.VMEM)],
        out_specs=pl.BlockSpec(memory_space=pltpu.VMEM),
        scratch_shapes=[
            pltpu.SemaphoreType.DMA(()),
            pltpu.SemaphoreType.DMA((m - 1,)),
            pltpu.SemaphoreType.DMA((m - 1,)),
        ],
        compiler_params=pltpu.CompilerParams(collective_id=2, has_side_effects=True),
    )(block)


def col_sum_kernel(x_ref, own_ref, out_ref, got, send_sem, recv_sem):
    me, peers = col_peers()
    copies = []
    for j, peer in enumerate(peers):
        copy = pltpu.make_async_remote_copy(
            src_ref=x_ref.at[peer[2]],
            dst_ref=got.at[j],
            send_sem=send_sem.at[j],
            recv_sem=recv_sem.at[j],
            device_id=peer,
            device_id_type=MESH,
        )
        copy.start()
        copies.append(copy)
    for copy in copies:
        copy.wait()
    chunk = 32

    def body(i, carry):
        rows = pl.ds(pl.multiple_of(i * chunk, chunk), chunk)
        total = own_ref[rows, :]
        for j in range(len(copies)):
            total = total + got[j, rows, :].astype(jnp.float32)
        out_ref[rows, :] = total
        return carry

    lax.fori_loop(0, out_ref.shape[0] // chunk, body, 0)


def col_reduce_scatter(parts, own, collective_id):
    m = lax.axis_size("col")
    return pl.pallas_call(
        col_sum_kernel,
        out_shape=jax.ShapeDtypeStruct(own.shape, jnp.float32),
        in_specs=[pl.BlockSpec(memory_space=pltpu.VMEM)] * 2,
        out_specs=pl.BlockSpec(memory_space=pltpu.VMEM),
        scratch_shapes=[
            pltpu.VMEM((m - 1,) + parts.shape[1:], parts.dtype),
            pltpu.SemaphoreType.DMA((m - 1,)),
            pltpu.SemaphoreType.DMA((m - 1,)),
        ],
        compiler_params=pltpu.CompilerParams(collective_id=collective_id, has_side_effects=True),
    )(parts, own)


def layer_norm(values, gain, bias):
    center = values - jnp.mean(values, axis=1, keepdims=True)
    spread = jnp.mean(center * center, axis=1, keepdims=True)
    return center * lax.rsqrt(spread + 1e-05) * gain + bias


def per_device(
    hidden_in,
    qkv_weight,
    qkv_global_weight,
    out_weight,
    ln_gain,
    ln_bias,
    ffn_in,
    ffn_out,
    ln2_gain,
    ln2_bias,
    segment_ids,
    global_pos,
    page_owner,
):
    neg = -1e30
    tokens = hidden_in[0]
    shard_len, width = tokens.shape
    heads_here = qkv_weight.shape[1]
    triple = qkv_weight.shape[2]
    head_dim = triple // 3
    n_seq = lax.axis_size("seq")
    n_row = lax.axis_size("row")
    n_col = lax.axis_size("col")
    seq_index = lax.axis_index("seq")
    col_index = lax.axis_index("col")
    base = seq_index * shard_len
    scale = 1.0 / math.sqrt(head_dim)

    all_pos = global_pos[0]
    n_glob = all_pos.shape[0]
    per_shard = n_glob // n_seq
    own_pos = lax.dynamic_slice_in_dim(all_pos, seq_index * per_shard, per_shard, 0)
    local_order = jnp.arange(shard_len, dtype=jnp.int32)
    own_match = (own_pos - base)[:, None] == local_order[None, :]
    picker = own_match.astype(jnp.bfloat16)
    own_rows = jnp.dot(picker, tokens, preferred_element_type=jnp.float32).astype(jnp.bfloat16)
    glob_rows = seq_direct_gather(own_rows.reshape(-1, 128)).reshape(n_glob, width)

    w_global = lax.all_gather(
        qkv_global_weight.reshape(qkv_global_weight.shape[0], -1), "row", axis=0, tiled=True
    )
    f_in = lax.all_gather(ffn_in, "row", axis=0, tiled=True)
    f_out = lax.all_gather(ffn_out, "row", axis=1, tiled=True)

    flat_weight = qkv_weight.reshape(width, heads_here * triple)
    qkv = jnp.dot(tokens, flat_weight, preferred_element_type=jnp.float32).astype(jnp.bfloat16)
    qkv_heads = qkv.reshape(shard_len, heads_here, triple)
    queries = qkv_heads[:, :, :head_dim]
    kv_local = qkv_heads[:, :, head_dim:]

    owners = page_owner[0, :, 0]
    n_pages = owners.shape[0]
    page_len = shard_len // n_pages
    capacity = max(2, n_pages // n_seq)
    page_order = jnp.arange(n_pages, dtype=jnp.int32)
    slot = jnp.sum(
        ((owners[:, None] == owners[None, :]) & (page_order[None, :] < page_order[:, None])).astype(
            jnp.int32
        ),
        axis=1,
    )
    target = owners * capacity + slot
    placing = (target[None, :] == jnp.arange(n_seq * capacity, dtype=jnp.int32)[:, None]).astype(
        jnp.bfloat16
    )
    outgoing = jnp.dot(
        placing,
        kv_local.reshape(n_pages, page_len * heads_here * 2 * head_dim),
        preferred_element_type=jnp.float32,
    ).astype(jnp.bfloat16)
    outgoing = outgoing.reshape(n_seq, capacity, page_len, heads_here, 2 * head_dim)
    arrived = lax.all_to_all(outgoing, "seq", split_axis=0, concat_axis=0, tiled=True)
    page_pool = arrived[None, None]
    page_pool, glob_rows = lax.optimization_barrier((page_pool, glob_rows))

    kv_ext = padded(kv_local, (("seq", 0),), HALF)

    glob_qkv = jnp.dot(glob_rows, flat_weight, preferred_element_type=jnp.float32).astype(
        jnp.bfloat16
    )
    glob_kv = glob_qkv.reshape(n_glob, heads_here, triple)[:, :, head_dim:]
    glob_k = glob_kv[:, :, :head_dim]
    glob_v = glob_kv[:, :, head_dim:]
    glob_q = (
        jnp.dot(glob_rows, w_global, preferred_element_type=jnp.float32)
        .astype(jnp.bfloat16)
        .reshape(n_glob, heads_here, triple)[:, :, :head_dim]
    )
    global_kv_local = (
        jnp.dot(tokens, w_global, preferred_element_type=jnp.float32)
        .astype(jnp.bfloat16)
        .reshape(shard_len, heads_here, triple)[:, :, head_dim:]
    )

    seg_all = segment_ids[0]
    glob_seg = jnp.take(seg_all, all_pos)
    seg_pad = jnp.pad(seg_all, (HALF, HALF), constant_values=-1)
    query_seg = lax.dynamic_slice_in_dim(seg_all, base, shard_len, 0)
    key_seg = lax.dynamic_slice_in_dim(seg_pad, base, shard_len + 2 * HALF, 0)
    key_pos = base - HALF + jnp.arange(shard_len + 2 * HALF, dtype=jnp.int32)
    key_flag = jnp.any(key_pos[:, None] == all_pos[None, :], axis=1)
    query_pos = base + local_order

    s_part = (
        jnp.einsum(
            "ghd,khd->hgk",
            glob_q,
            global_kv_local[:, :, :head_dim],
            preferred_element_type=jnp.float32,
        )
        * scale
    )
    part_mask = glob_seg[:, None] == query_seg[None, :]
    part_top = jnp.max(jnp.where(part_mask, s_part, neg), axis=2)
    e_part = jnp.where(part_mask, jnp.exp(s_part - part_top[:, :, None]), 0.0)
    part_total = jnp.sum(e_part, axis=2)
    part_acc = jnp.einsum(
        "hgk,khd->hgd",
        e_part,
        global_kv_local[:, :, head_dim:].astype(jnp.float32),
        precision=lax.Precision.HIGHEST,
    )
    packed = jnp.concatenate(
        [
            part_acc,
            part_total[:, :, None],
            jnp.broadcast_to(part_top[:, :, None], part_top.shape + (128 - head_dim - 1,)),
        ],
        axis=2,
    )
    packed = jnp.transpose(packed, (1, 0, 2)).reshape(n_glob * heads_here, 128)
    packed, f_in = lax.optimization_barrier((packed, f_in))
    merged = seq_direct_merge(packed.reshape(n_seq, -1, 128), head_dim + 1).reshape(
        per_shard, heads_here, 128
    )
    own_out = jnp.transpose(
        (merged[:, :, :head_dim] / merged[:, :, head_dim : head_dim + 1]).astype(jnp.bfloat16),
        (1, 0, 2),
    )

    glob_mask = query_seg[:, None] == glob_seg[None, :]
    k_blk = kv_ext[:, :, :head_dim]
    v_blk = kv_ext[:, :, head_dim:]
    s_win = jnp.einsum("qhd,khd->hqk", queries, k_blk, preferred_element_type=jnp.float32) * scale
    s_glob = jnp.einsum("qhd,ghd->hqg", queries, glob_k, preferred_element_type=jnp.float32) * scale
    m_win = (
        (jnp.abs(query_pos[:, None] - key_pos[None, :]) <= HALF)
        & (query_seg[:, None] == key_seg[None, :])
        & jnp.logical_not(key_flag[None, :])
    )
    top = jnp.maximum(
        jnp.max(jnp.where(m_win, s_win, neg), axis=2),
        jnp.max(jnp.where(glob_mask, s_glob, neg), axis=2),
    )
    e_win = jnp.where(m_win, jnp.exp(s_win - top[:, :, None]), 0.0)
    e_glob = jnp.where(glob_mask, jnp.exp(s_glob - top[:, :, None]), 0.0)
    total = jnp.sum(e_win, axis=2) + jnp.sum(e_glob, axis=2)
    numer = jnp.einsum(
        "hqk,khd->qhd", e_win.astype(jnp.bfloat16), v_blk, preferred_element_type=jnp.float32
    )
    numer = numer + jnp.einsum(
        "hqg,ghd->qhd", e_glob.astype(jnp.bfloat16), glob_v, preferred_element_type=jnp.float32
    )
    pieces = (numer / jnp.transpose(total)[:, :, None]).astype(jnp.bfloat16)

    placed = jnp.einsum("gt,hgd->thd", picker, own_out, preferred_element_type=jnp.float32).astype(
        jnp.bfloat16
    )
    is_own = jnp.any(own_match, axis=0)
    attention = jnp.where(is_own[:, None, None], placed, pieces).reshape(
        shard_len, heads_here * head_dim
    )

    attention, f_out = lax.optimization_barrier((attention, f_out))

    out_rows = shard_len // n_col
    proj = jnp.dot(attention, out_weight, preferred_element_type=jnp.float32)
    proj_own = lax.dynamic_slice_in_dim(proj, col_index * out_rows, out_rows, 0)
    token_own = lax.dynamic_slice_in_dim(tokens, col_index * out_rows, out_rows, 0)
    summed = col_reduce_scatter(
        proj.astype(jnp.bfloat16).reshape(n_col, out_rows, width),
        token_own.astype(jnp.float32) + proj_own,
        3,
    )
    mine = layer_norm(summed, ln_gain, ln_bias).astype(jnp.bfloat16)
    middle = col_gather(mine).reshape(shard_len, width)
    ffn_pre = jnp.dot(middle, f_in, preferred_element_type=jnp.float32)
    ffn_hidden = jax.nn.gelu(ffn_pre, approximate=False).astype(jnp.bfloat16)
    ffn_full = jnp.dot(ffn_hidden, f_out, preferred_element_type=jnp.float32)
    ffn_own = lax.dynamic_slice_in_dim(ffn_full, col_index * out_rows, out_rows, 0)
    second = col_reduce_scatter(
        ffn_full.astype(jnp.bfloat16).reshape(n_col, out_rows, width),
        mine.astype(jnp.float32) + ffn_own,
        6,
    )
    normed = layer_norm(second, ln2_gain, ln2_bias)
    return (normed.astype(jnp.bfloat16)[None], page_pool)


def solution(mesh):
    in_specs = (
        P("row", "seq", None),
        P(None, "col", None),
        P("row", "col", None),
        P("col", None),
        P(),
        P(),
        P("row", "col"),
        P("col", "row"),
        P(),
        P(),
        P("row", None),
        P("row", None),
        P("row", "seq", None),
    )
    out_specs = (P("row", ("seq", "col"), None), P("row", "seq", None, None, None, "col", None))
    return jax.shard_map(
        per_device, mesh=mesh, in_specs=in_specs, out_specs=out_specs, check_vma=False
    )
```

```python
import functools
import math

import jax
import jax.numpy as jnp
from jax import lax
from jax.experimental import pallas as pl
from jax.experimental.pallas import tpu as pltpu
from jax.sharding import PartitionSpec as P

MESH = pl.DeviceIdType.MESH

HALF = 256


def padded(block, sides, width):
    for axis, dim in sides:
        count = lax.axis_size(axis)
        forward = [(i, i + 1) for i in range(count - 1)]
        backward = [(target, source) for source, target in forward]
        low = lax.ppermute(
            lax.slice_in_dim(block, block.shape[dim] - width, None, axis=dim), axis, forward
        )
        high = lax.ppermute(lax.slice_in_dim(block, 0, width, axis=dim), axis, backward)
        block = jnp.concatenate([low, block, high], axis=dim)
    return block


def butterfly_partners(n):
    me = lax.axis_index("seq")
    partners = []
    step = 1
    while step < n:
        bit = (me // step) % 2
        partners.append(me + step - 2 * step * bit)
        step *= 2
    return me, partners


def enter(partners):
    row, col = lax.axis_index("row"), lax.axis_index("col")
    barrier = pltpu.get_barrier_semaphore()
    for partner in partners:
        pl.semaphore_signal(barrier, inc=1, device_id=(partner, row, col), device_id_type=MESH)
    pl.semaphore_wait(barrier, len(partners))
    return row, col


def gather_kernel(n, x_ref, out_ref, self_sem, send_sem, recv_sem):
    me, partners = butterfly_partners(n)
    row, col = enter(partners)
    own = pltpu.make_async_copy(x_ref, out_ref.at[me], self_sem)
    own.start()
    own.wait()
    size = 1
    for k, partner in enumerate(partners):
        start = (me // size) * size
        copy = pltpu.make_async_remote_copy(
            src_ref=out_ref.at[pl.ds(start, size)],
            dst_ref=out_ref.at[pl.ds(start, size)],
            send_sem=send_sem.at[k],
            recv_sem=recv_sem.at[k],
            device_id=(partner, row, col),
            device_id_type=MESH,
        )
        copy.start()
        copy.wait()
        size *= 2


def seq_gather(block):
    n = lax.axis_size("seq")
    rounds = n.bit_length() - 1
    return pl.pallas_call(
        functools.partial(gather_kernel, n),
        out_shape=jax.ShapeDtypeStruct((n,) + block.shape, block.dtype),
        in_specs=[pl.BlockSpec(memory_space=pltpu.VMEM)],
        out_specs=pl.BlockSpec(memory_space=pltpu.VMEM),
        scratch_shapes=[
            pltpu.SemaphoreType.DMA(()),
            pltpu.SemaphoreType.DMA((rounds,)),
            pltpu.SemaphoreType.DMA((rounds,)),
        ],
        compiler_params=pltpu.CompilerParams(collective_id=0, has_side_effects=True),
    )(block)


def merge_parts(mine, theirs, top_lane):
    lane = lax.broadcasted_iota(jnp.int32, mine.shape, 1)
    is_top = lane == top_lane
    top_a = jnp.max(jnp.where(is_top, mine, -jnp.inf), axis=1, keepdims=True)
    top_b = jnp.max(jnp.where(is_top, theirs, -jnp.inf), axis=1, keepdims=True)
    top = jnp.maximum(top_a, top_b)
    merged = mine * jnp.exp(top_a - top) + theirs * jnp.exp(top_b - top)
    return jnp.where(is_top, top, merged)


def halving_kernel(n, top_lane, x_ref, out_ref, *scratch):
    rounds = len(scratch) // 3
    kept, got, sems = scratch[:rounds], scratch[rounds : 2 * rounds], scratch[2 * rounds :]
    me = lax.axis_index("seq")
    steps = []
    step = n // 2
    while step >= 1:
        bit = (me // step) % 2
        steps.append((me + step - 2 * step * bit, bit))
        step //= 2
    row, col = enter([partner for partner, _ in steps])
    source = x_ref
    for k, (partner, bit) in enumerate(steps):
        half = source.shape[0] // 2
        send_at = pl.multiple_of((1 - bit) * half, 8)
        keep_at = pl.multiple_of(bit * half, 8)
        copy = pltpu.make_async_remote_copy(
            src_ref=source.at[pl.ds(send_at, half)],
            dst_ref=got[k],
            send_sem=sems[k].at[0],
            recv_sem=sems[k].at[1],
            device_id=(partner, row, col),
            device_id_type=MESH,
        )
        copy.start()
        copy.wait()
        value = merge_parts(source[pl.ds(keep_at, half)], got[k][...], top_lane)
        if k + 1 < rounds:
            kept[k][...] = value
            source = kept[k]
        else:
            out_ref[...] = value


def seq_softmax_combine(parts, top_lane):
    n = lax.axis_size("seq")
    rounds = n.bit_length() - 1
    rows, lanes = parts.shape
    scratch = []
    for k in range(rounds):
        scratch.append(pltpu.VMEM((rows >> (k + 1), lanes), parts.dtype))
    for k in range(rounds):
        scratch.append(pltpu.VMEM((rows >> (k + 1), lanes), parts.dtype))
    for k in range(rounds):
        scratch.append(pltpu.SemaphoreType.DMA((2,)))
    return pl.pallas_call(
        functools.partial(halving_kernel, n, top_lane),
        out_shape=jax.ShapeDtypeStruct((rows // n, lanes), parts.dtype),
        in_specs=[pl.BlockSpec(memory_space=pltpu.VMEM)],
        out_specs=pl.BlockSpec(memory_space=pltpu.VMEM),
        scratch_shapes=scratch,
        compiler_params=pltpu.CompilerParams(collective_id=1, has_side_effects=True),
    )(parts)


def seq_peers():
    me, n = lax.axis_index("seq"), lax.axis_size("seq")
    row, col = lax.axis_index("row"), lax.axis_index("col")
    peers = [lax.rem(me + j, n) for j in range(1, n)]
    barrier = pltpu.get_barrier_semaphore()
    for peer in peers:
        pl.semaphore_signal(barrier, inc=1, device_id=(peer, row, col), device_id_type=MESH)
    pl.semaphore_wait(barrier, len(peers))
    return me, [(peer, row, col) for peer in peers]


def seq_direct_gather_kernel(x_ref, out_ref, self_sem, send_sem, recv_sem):
    me, peers = seq_peers()
    own = pltpu.make_async_copy(x_ref, out_ref.at[me], self_sem)
    own.start()
    copies = []
    for j, peer in enumerate(peers):
        copy = pltpu.make_async_remote_copy(
            src_ref=x_ref,
            dst_ref=out_ref.at[me],
            send_sem=send_sem.at[j],
            recv_sem=recv_sem.at[j],
            device_id=peer,
            device_id_type=MESH,
        )
        copy.start()
        copies.append(copy)
    own.wait()
    for copy in copies:
        copy.wait()


def seq_direct_gather(block):
    n = lax.axis_size("seq")
    return pl.pallas_call(
        seq_direct_gather_kernel,
        out_shape=jax.ShapeDtypeStruct((n,) + block.shape, block.dtype),
        in_specs=[pl.BlockSpec(memory_space=pltpu.VMEM)],
        out_specs=pl.BlockSpec(memory_space=pltpu.VMEM),
        scratch_shapes=[
            pltpu.SemaphoreType.DMA(()),
            pltpu.SemaphoreType.DMA((n - 1,)),
            pltpu.SemaphoreType.DMA((n - 1,)),
        ],
        compiler_params=pltpu.CompilerParams(collective_id=4, has_side_effects=True),
    )(block)


def seq_merge_kernel(top_lane, x_ref, out_ref, got, send_sem, recv_sem):
    me, peers = seq_peers()
    copies = []
    for j, peer in enumerate(peers):
        copy = pltpu.make_async_remote_copy(
            src_ref=x_ref.at[peer[0]],
            dst_ref=got.at[j],
            send_sem=send_sem.at[j],
            recv_sem=recv_sem.at[j],
            device_id=peer,
            device_id_type=MESH,
        )
        copy.start()
        copies.append(copy)
    for copy in copies:
        copy.wait()
    value = x_ref[me]
    for j in range(len(copies)):
        value = merge_parts(value, got[j], top_lane)
    out_ref[...] = value


def seq_direct_merge(parts, top_lane):
    n = parts.shape[0]
    return pl.pallas_call(
        functools.partial(seq_merge_kernel, top_lane),
        out_shape=jax.ShapeDtypeStruct(parts.shape[1:], parts.dtype),
        in_specs=[pl.BlockSpec(memory_space=pltpu.VMEM)],
        out_specs=pl.BlockSpec(memory_space=pltpu.VMEM),
        scratch_shapes=[
            pltpu.VMEM((n - 1,) + parts.shape[1:], parts.dtype),
            pltpu.SemaphoreType.DMA((n - 1,)),
            pltpu.SemaphoreType.DMA((n - 1,)),
        ],
        compiler_params=pltpu.CompilerParams(collective_id=5, has_side_effects=True),
    )(parts)


def col_peers():
    me, m = lax.axis_index("col"), lax.axis_size("col")
    seq, row = lax.axis_index("seq"), lax.axis_index("row")
    peers = [lax.rem(me + j, m) for j in range(1, m)]
    barrier = pltpu.get_barrier_semaphore()
    for peer in peers:
        pl.semaphore_signal(barrier, inc=1, device_id=(seq, row, peer), device_id_type=MESH)
    pl.semaphore_wait(barrier, len(peers))
    return me, [(seq, row, peer) for peer in peers]


def col_gather_kernel(x_ref, out_ref, self_sem, send_sem, recv_sem):
    me, peers = col_peers()
    own = pltpu.make_async_copy(x_ref, out_ref.at[me], self_sem)
    own.start()
    copies = []
    for j, peer in enumerate(peers):
        copy = pltpu.make_async_remote_copy(
            src_ref=x_ref,
            dst_ref=out_ref.at[me],
            send_sem=send_sem.at[j],
            recv_sem=recv_sem.at[j],
            device_id=peer,
            device_id_type=MESH,
        )
        copy.start()
        copies.append(copy)
    own.wait()
    for copy in copies:
        copy.wait()


def col_gather(block):
    m = lax.axis_size("col")
    return pl.pallas_call(
        col_gather_kernel,
        out_shape=jax.ShapeDtypeStruct((m,) + block.shape, block.dtype),
        in_specs=[pl.BlockSpec(memory_space=pltpu.VMEM)],
        out_specs=pl.BlockSpec(memory_space=pltpu.VMEM),
        scratch_shapes=[
            pltpu.SemaphoreType.DMA(()),
            pltpu.SemaphoreType.DMA((m - 1,)),
            pltpu.SemaphoreType.DMA((m - 1,)),
        ],
        compiler_params=pltpu.CompilerParams(collective_id=2, has_side_effects=True),
    )(block)


def col_sum_kernel(x_ref, own_ref, out_ref, got, send_sem, recv_sem):
    me, peers = col_peers()
    copies = []
    for j, peer in enumerate(peers):
        copy = pltpu.make_async_remote_copy(
            src_ref=x_ref.at[peer[2]],
            dst_ref=got.at[j],
            send_sem=send_sem.at[j],
            recv_sem=recv_sem.at[j],
            device_id=peer,
            device_id_type=MESH,
        )
        copy.start()
        copies.append(copy)
    for copy in copies:
        copy.wait()
    chunk = 32

    def body(i, carry):
        rows = pl.ds(pl.multiple_of(i * chunk, chunk), chunk)
        total = own_ref[rows, :]
        for j in range(len(copies)):
            total = total + got[j, rows, :].astype(jnp.float32)
        out_ref[rows, :] = total
        return carry

    lax.fori_loop(0, out_ref.shape[0] // chunk, body, 0)


def col_reduce_scatter(parts, own, collective_id):
    m = lax.axis_size("col")
    return pl.pallas_call(
        col_sum_kernel,
        out_shape=jax.ShapeDtypeStruct(own.shape, jnp.float32),
        in_specs=[pl.BlockSpec(memory_space=pltpu.VMEM)] * 2,
        out_specs=pl.BlockSpec(memory_space=pltpu.VMEM),
        scratch_shapes=[
            pltpu.VMEM((m - 1,) + parts.shape[1:], parts.dtype),
            pltpu.SemaphoreType.DMA((m - 1,)),
            pltpu.SemaphoreType.DMA((m - 1,)),
        ],
        compiler_params=pltpu.CompilerParams(collective_id=collective_id, has_side_effects=True),
    )(parts, own)


def layer_norm(values, gain, bias):
    center = values - jnp.mean(values, axis=1, keepdims=True)
    spread = jnp.mean(center * center, axis=1, keepdims=True)
    return center * lax.rsqrt(spread + 1e-05) * gain + bias


def per_device(
    hidden_in,
    qkv_weight,
    qkv_global_weight,
    out_weight,
    ln_gain,
    ln_bias,
    ffn_in,
    ffn_out,
    ln2_gain,
    ln2_bias,
    segment_ids,
    global_pos,
    page_owner,
):
    neg = -1e30
    tokens = hidden_in[0]
    shard_len, width = tokens.shape
    heads_here = qkv_weight.shape[1]
    triple = qkv_weight.shape[2]
    head_dim = triple // 3
    n_seq = lax.axis_size("seq")
    n_row = lax.axis_size("row")
    n_col = lax.axis_size("col")
    seq_index = lax.axis_index("seq")
    col_index = lax.axis_index("col")
    base = seq_index * shard_len
    scale = 1.0 / math.sqrt(head_dim)

    all_pos = global_pos[0]
    n_glob = all_pos.shape[0]
    per_shard = n_glob // n_seq
    own_pos = lax.dynamic_slice_in_dim(all_pos, seq_index * per_shard, per_shard, 0)
    local_order = jnp.arange(shard_len, dtype=jnp.int32)
    own_match = (own_pos - base)[:, None] == local_order[None, :]
    picker = own_match.astype(jnp.bfloat16)
    own_rows = jnp.dot(picker, tokens, preferred_element_type=jnp.float32).astype(jnp.bfloat16)
    glob_rows = seq_direct_gather(own_rows.reshape(-1, 128)).reshape(n_glob, width)

    w_global = lax.all_gather(
        qkv_global_weight.reshape(qkv_global_weight.shape[0], -1), "row", axis=0, tiled=True
    )
    f_in = lax.all_gather(ffn_in, "row", axis=0, tiled=True)
    f_out = lax.all_gather(ffn_out, "row", axis=1, tiled=True)

    flat_weight = qkv_weight.reshape(width, heads_here * triple)
    qkv = jnp.dot(tokens, flat_weight, preferred_element_type=jnp.float32).astype(jnp.bfloat16)
    qkv_heads = qkv.reshape(shard_len, heads_here, triple)
    queries = qkv_heads[:, :, :head_dim]
    kv_local = qkv_heads[:, :, head_dim:]

    owners = page_owner[0, :, 0]
    n_pages = owners.shape[0]
    page_len = shard_len // n_pages
    capacity = max(2, n_pages // n_seq)
    page_order = jnp.arange(n_pages, dtype=jnp.int32)
    slot = jnp.sum(
        ((owners[:, None] == owners[None, :]) & (page_order[None, :] < page_order[:, None])).astype(
            jnp.int32
        ),
        axis=1,
    )
    target = owners * capacity + slot
    placing = (target[None, :] == jnp.arange(n_seq * capacity, dtype=jnp.int32)[:, None]).astype(
        jnp.bfloat16
    )
    outgoing = jnp.dot(
        placing,
        kv_local.reshape(n_pages, page_len * heads_here * 2 * head_dim),
        preferred_element_type=jnp.float32,
    ).astype(jnp.bfloat16)
    outgoing = outgoing.reshape(n_seq, capacity, page_len, heads_here, 2 * head_dim)
    arrived = lax.all_to_all(outgoing, "seq", split_axis=0, concat_axis=0, tiled=True)
    arrived, glob_rows = lax.optimization_barrier((arrived, glob_rows))
    page_pool = arrived[None, None]

    kv_ext = padded(kv_local, (("seq", 0),), HALF)

    glob_qkv = jnp.dot(glob_rows, flat_weight, preferred_element_type=jnp.float32).astype(
        jnp.bfloat16
    )
    glob_kv = glob_qkv.reshape(n_glob, heads_here, triple)[:, :, head_dim:]
    glob_k = glob_kv[:, :, :head_dim]
    glob_v = glob_kv[:, :, head_dim:]
    glob_q = (
        jnp.dot(glob_rows, w_global, preferred_element_type=jnp.float32)
        .astype(jnp.bfloat16)
        .reshape(n_glob, heads_here, triple)[:, :, :head_dim]
    )
    global_kv_local = (
        jnp.dot(tokens, w_global, preferred_element_type=jnp.float32)
        .astype(jnp.bfloat16)
        .reshape(shard_len, heads_here, triple)[:, :, head_dim:]
    )

    seg_all = segment_ids[0]
    glob_seg = jnp.take(seg_all, all_pos)
    seg_pad = jnp.pad(seg_all, (HALF, HALF), constant_values=-1)
    query_seg = lax.dynamic_slice_in_dim(seg_all, base, shard_len, 0)
    key_seg = lax.dynamic_slice_in_dim(seg_pad, base, shard_len + 2 * HALF, 0)
    key_pos = base - HALF + jnp.arange(shard_len + 2 * HALF, dtype=jnp.int32)
    key_flag = jnp.any(key_pos[:, None] == all_pos[None, :], axis=1)
    query_pos = base + local_order

    s_part = (
        jnp.einsum(
            "ghd,khd->hgk",
            glob_q,
            global_kv_local[:, :, :head_dim],
            preferred_element_type=jnp.float32,
        )
        * scale
    )
    part_mask = glob_seg[:, None] == query_seg[None, :]
    part_top = jnp.max(jnp.where(part_mask, s_part, neg), axis=2)
    e_part = jnp.where(part_mask, jnp.exp(s_part - part_top[:, :, None]), 0.0)
    part_total = jnp.sum(e_part, axis=2)
    part_acc = jnp.einsum(
        "hgk,khd->hgd",
        e_part,
        global_kv_local[:, :, head_dim:].astype(jnp.float32),
        precision=lax.Precision.HIGHEST,
    )
    packed = jnp.concatenate(
        [
            part_acc,
            part_total[:, :, None],
            jnp.broadcast_to(part_top[:, :, None], part_top.shape + (128 - head_dim - 1,)),
        ],
        axis=2,
    )
    packed = jnp.transpose(packed, (1, 0, 2)).reshape(n_glob * heads_here, 128)
    packed, f_in = lax.optimization_barrier((packed, f_in))
    merged = seq_direct_merge(packed.reshape(n_seq, -1, 128), head_dim + 1).reshape(
        per_shard, heads_here, 128
    )
    own_out = jnp.transpose(
        (merged[:, :, :head_dim] / merged[:, :, head_dim : head_dim + 1]).astype(jnp.bfloat16),
        (1, 0, 2),
    )

    glob_mask = query_seg[:, None] == glob_seg[None, :]
    k_blk = kv_ext[:, :, :head_dim]
    v_blk = kv_ext[:, :, head_dim:]
    s_win = jnp.einsum("qhd,khd->hqk", queries, k_blk, preferred_element_type=jnp.float32) * scale
    s_glob = jnp.einsum("qhd,ghd->hqg", queries, glob_k, preferred_element_type=jnp.float32) * scale
    m_win = (
        (jnp.abs(query_pos[:, None] - key_pos[None, :]) <= HALF)
        & (query_seg[:, None] == key_seg[None, :])
        & jnp.logical_not(key_flag[None, :])
    )
    top = jnp.maximum(
        jnp.max(jnp.where(m_win, s_win, neg), axis=2),
        jnp.max(jnp.where(glob_mask, s_glob, neg), axis=2),
    )
    e_win = jnp.where(m_win, jnp.exp(s_win - top[:, :, None]), 0.0)
    e_glob = jnp.where(glob_mask, jnp.exp(s_glob - top[:, :, None]), 0.0)
    total = jnp.sum(e_win, axis=2) + jnp.sum(e_glob, axis=2)
    numer = jnp.einsum(
        "hqk,khd->qhd", e_win.astype(jnp.bfloat16), v_blk, preferred_element_type=jnp.float32
    )
    numer = numer + jnp.einsum(
        "hqg,ghd->qhd", e_glob.astype(jnp.bfloat16), glob_v, preferred_element_type=jnp.float32
    )
    pieces = (numer / jnp.transpose(total)[:, :, None]).astype(jnp.bfloat16)

    placed = jnp.einsum("gt,hgd->thd", picker, own_out, preferred_element_type=jnp.float32).astype(
        jnp.bfloat16
    )
    is_own = jnp.any(own_match, axis=0)
    attention = jnp.where(is_own[:, None, None], placed, pieces).reshape(
        shard_len, heads_here * head_dim
    )


    out_rows = shard_len // n_col
    proj = jnp.dot(attention, out_weight, preferred_element_type=jnp.float32)
    proj_own = lax.dynamic_slice_in_dim(proj, col_index * out_rows, out_rows, 0)
    token_own = lax.dynamic_slice_in_dim(tokens, col_index * out_rows, out_rows, 0)
    summed = col_reduce_scatter(
        proj.astype(jnp.bfloat16).reshape(n_col, out_rows, width),
        token_own.astype(jnp.float32) + proj_own,
        3,
    )
    mine = layer_norm(summed, ln_gain, ln_bias).astype(jnp.bfloat16)
    middle = col_gather(mine).reshape(shard_len, width)
    ffn_pre = jnp.dot(middle, f_in, preferred_element_type=jnp.float32)
    ffn_hidden = jax.nn.gelu(ffn_pre, approximate=False).astype(jnp.bfloat16)
    ffn_full = jnp.dot(ffn_hidden, f_out, preferred_element_type=jnp.float32)
    ffn_own = lax.dynamic_slice_in_dim(ffn_full, col_index * out_rows, out_rows, 0)
    second = col_reduce_scatter(
        ffn_full.astype(jnp.bfloat16).reshape(n_col, out_rows, width),
        mine.astype(jnp.float32) + ffn_own,
        6,
    )
    normed = layer_norm(second, ln2_gain, ln2_bias)
    return (normed.astype(jnp.bfloat16)[None], page_pool)


def solution(mesh):
    in_specs = (
        P("row", "seq", None),
        P(None, "col", None),
        P("row", "col", None),
        P("col", None),
        P(),
        P(),
        P("row", "col"),
        P("col", "row"),
        P(),
        P(),
        P("row", None),
        P("row", None),
        P("row", "seq", None),
    )
    out_specs = (P("row", ("seq", "col"), None), P("row", "seq", None, None, None, "col", None))
    return jax.shard_map(
        per_device, mesh=mesh, in_specs=in_specs, out_specs=out_specs, check_vma=False
    )
```

```python
import functools
import math

import jax
import jax.numpy as jnp
from jax import lax
from jax.experimental import pallas as pl
from jax.experimental.pallas import tpu as pltpu
from jax.sharding import PartitionSpec as P

MESH = pl.DeviceIdType.MESH

HALF = 256


def padded(block, sides, width):
    for axis, dim in sides:
        count = lax.axis_size(axis)
        forward = [(i, i + 1) for i in range(count - 1)]
        backward = [(target, source) for source, target in forward]
        low = lax.ppermute(
            lax.slice_in_dim(block, block.shape[dim] - width, None, axis=dim), axis, forward
        )
        high = lax.ppermute(lax.slice_in_dim(block, 0, width, axis=dim), axis, backward)
        block = jnp.concatenate([low, block, high], axis=dim)
    return block


def butterfly_partners(n):
    me = lax.axis_index("seq")
    partners = []
    step = 1
    while step < n:
        bit = (me // step) % 2
        partners.append(me + step - 2 * step * bit)
        step *= 2
    return me, partners


def enter(partners):
    row, col = lax.axis_index("row"), lax.axis_index("col")
    barrier = pltpu.get_barrier_semaphore()
    for partner in partners:
        pl.semaphore_signal(barrier, inc=1, device_id=(partner, row, col), device_id_type=MESH)
    pl.semaphore_wait(barrier, len(partners))
    return row, col


def gather_kernel(n, x_ref, out_ref, self_sem, send_sem, recv_sem):
    me, partners = butterfly_partners(n)
    row, col = enter(partners)
    own = pltpu.make_async_copy(x_ref, out_ref.at[me], self_sem)
    own.start()
    own.wait()
    size = 1
    for k, partner in enumerate(partners):
        start = (me // size) * size
        copy = pltpu.make_async_remote_copy(
            src_ref=out_ref.at[pl.ds(start, size)],
            dst_ref=out_ref.at[pl.ds(start, size)],
            send_sem=send_sem.at[k],
            recv_sem=recv_sem.at[k],
            device_id=(partner, row, col),
            device_id_type=MESH,
        )
        copy.start()
        copy.wait()
        size *= 2


def seq_gather(block):
    n = lax.axis_size("seq")
    rounds = n.bit_length() - 1
    return pl.pallas_call(
        functools.partial(gather_kernel, n),
        out_shape=jax.ShapeDtypeStruct((n,) + block.shape, block.dtype),
        in_specs=[pl.BlockSpec(memory_space=pltpu.VMEM)],
        out_specs=pl.BlockSpec(memory_space=pltpu.VMEM),
        scratch_shapes=[
            pltpu.SemaphoreType.DMA(()),
            pltpu.SemaphoreType.DMA((rounds,)),
            pltpu.SemaphoreType.DMA((rounds,)),
        ],
        compiler_params=pltpu.CompilerParams(collective_id=0, has_side_effects=True),
    )(block)


def merge_parts(mine, theirs, top_lane):
    lane = lax.broadcasted_iota(jnp.int32, mine.shape, 1)
    is_top = lane == top_lane
    top_a = jnp.max(jnp.where(is_top, mine, -jnp.inf), axis=1, keepdims=True)
    top_b = jnp.max(jnp.where(is_top, theirs, -jnp.inf), axis=1, keepdims=True)
    top = jnp.maximum(top_a, top_b)
    merged = mine * jnp.exp(top_a - top) + theirs * jnp.exp(top_b - top)
    return jnp.where(is_top, top, merged)


def halving_kernel(n, top_lane, x_ref, out_ref, *scratch):
    rounds = len(scratch) // 3
    kept, got, sems = scratch[:rounds], scratch[rounds : 2 * rounds], scratch[2 * rounds :]
    me = lax.axis_index("seq")
    steps = []
    step = n // 2
    while step >= 1:
        bit = (me // step) % 2
        steps.append((me + step - 2 * step * bit, bit))
        step //= 2
    row, col = enter([partner for partner, _ in steps])
    source = x_ref
    for k, (partner, bit) in enumerate(steps):
        half = source.shape[0] // 2
        send_at = pl.multiple_of((1 - bit) * half, 8)
        keep_at = pl.multiple_of(bit * half, 8)
        copy = pltpu.make_async_remote_copy(
            src_ref=source.at[pl.ds(send_at, half)],
            dst_ref=got[k],
            send_sem=sems[k].at[0],
            recv_sem=sems[k].at[1],
            device_id=(partner, row, col),
            device_id_type=MESH,
        )
        copy.start()
        copy.wait()
        value = merge_parts(source[pl.ds(keep_at, half)], got[k][...], top_lane)
        if k + 1 < rounds:
            kept[k][...] = value
            source = kept[k]
        else:
            out_ref[...] = value


def seq_softmax_combine(parts, top_lane):
    n = lax.axis_size("seq")
    rounds = n.bit_length() - 1
    rows, lanes = parts.shape
    scratch = []
    for k in range(rounds):
        scratch.append(pltpu.VMEM((rows >> (k + 1), lanes), parts.dtype))
    for k in range(rounds):
        scratch.append(pltpu.VMEM((rows >> (k + 1), lanes), parts.dtype))
    for k in range(rounds):
        scratch.append(pltpu.SemaphoreType.DMA((2,)))
    return pl.pallas_call(
        functools.partial(halving_kernel, n, top_lane),
        out_shape=jax.ShapeDtypeStruct((rows // n, lanes), parts.dtype),
        in_specs=[pl.BlockSpec(memory_space=pltpu.VMEM)],
        out_specs=pl.BlockSpec(memory_space=pltpu.VMEM),
        scratch_shapes=scratch,
        compiler_params=pltpu.CompilerParams(collective_id=1, has_side_effects=True),
    )(parts)


def seq_peers():
    me, n = lax.axis_index("seq"), lax.axis_size("seq")
    row, col = lax.axis_index("row"), lax.axis_index("col")
    peers = [lax.rem(me + j, n) for j in range(1, n)]
    barrier = pltpu.get_barrier_semaphore()
    for peer in peers:
        pl.semaphore_signal(barrier, inc=1, device_id=(peer, row, col), device_id_type=MESH)
    pl.semaphore_wait(barrier, len(peers))
    return me, [(peer, row, col) for peer in peers]


def seq_direct_gather_kernel(x_ref, out_ref, self_sem, send_sem, recv_sem):
    me, peers = seq_peers()
    own = pltpu.make_async_copy(x_ref, out_ref.at[me], self_sem)
    own.start()
    copies = []
    for j, peer in enumerate(peers):
        copy = pltpu.make_async_remote_copy(
            src_ref=x_ref,
            dst_ref=out_ref.at[me],
            send_sem=send_sem.at[j],
            recv_sem=recv_sem.at[j],
            device_id=peer,
            device_id_type=MESH,
        )
        copy.start()
        copies.append(copy)
    own.wait()
    for copy in copies:
        copy.wait()


def seq_direct_gather(block):
    n = lax.axis_size("seq")
    return pl.pallas_call(
        seq_direct_gather_kernel,
        out_shape=jax.ShapeDtypeStruct((n,) + block.shape, block.dtype),
        in_specs=[pl.BlockSpec(memory_space=pltpu.VMEM)],
        out_specs=pl.BlockSpec(memory_space=pltpu.VMEM),
        scratch_shapes=[
            pltpu.SemaphoreType.DMA(()),
            pltpu.SemaphoreType.DMA((n - 1,)),
            pltpu.SemaphoreType.DMA((n - 1,)),
        ],
        compiler_params=pltpu.CompilerParams(collective_id=4, has_side_effects=True),
    )(block)


def seq_merge_kernel(top_lane, x_ref, out_ref, got, send_sem, recv_sem):
    me, peers = seq_peers()
    copies = []
    for j, peer in enumerate(peers):
        copy = pltpu.make_async_remote_copy(
            src_ref=x_ref.at[peer[0]],
            dst_ref=got.at[j],
            send_sem=send_sem.at[j],
            recv_sem=recv_sem.at[j],
            device_id=peer,
            device_id_type=MESH,
        )
        copy.start()
        copies.append(copy)
    for copy in copies:
        copy.wait()
    value = x_ref[me]
    for j in range(len(copies)):
        value = merge_parts(value, got[j], top_lane)
    out_ref[...] = value


def seq_direct_merge(parts, top_lane):
    n = parts.shape[0]
    return pl.pallas_call(
        functools.partial(seq_merge_kernel, top_lane),
        out_shape=jax.ShapeDtypeStruct(parts.shape[1:], parts.dtype),
        in_specs=[pl.BlockSpec(memory_space=pltpu.VMEM)],
        out_specs=pl.BlockSpec(memory_space=pltpu.VMEM),
        scratch_shapes=[
            pltpu.VMEM((n - 1,) + parts.shape[1:], parts.dtype),
            pltpu.SemaphoreType.DMA((n - 1,)),
            pltpu.SemaphoreType.DMA((n - 1,)),
        ],
        compiler_params=pltpu.CompilerParams(collective_id=5, has_side_effects=True),
    )(parts)


def col_peers():
    me, m = lax.axis_index("col"), lax.axis_size("col")
    seq, row = lax.axis_index("seq"), lax.axis_index("row")
    peers = [lax.rem(me + j, m) for j in range(1, m)]
    barrier = pltpu.get_barrier_semaphore()
    for peer in peers:
        pl.semaphore_signal(barrier, inc=1, device_id=(seq, row, peer), device_id_type=MESH)
    pl.semaphore_wait(barrier, len(peers))
    return me, [(seq, row, peer) for peer in peers]


def col_gather_kernel(x_ref, out_ref, self_sem, send_sem, recv_sem):
    me, peers = col_peers()
    own = pltpu.make_async_copy(x_ref, out_ref.at[me], self_sem)
    own.start()
    copies = []
    for j, peer in enumerate(peers):
        copy = pltpu.make_async_remote_copy(
            src_ref=x_ref,
            dst_ref=out_ref.at[me],
            send_sem=send_sem.at[j],
            recv_sem=recv_sem.at[j],
            device_id=peer,
            device_id_type=MESH,
        )
        copy.start()
        copies.append(copy)
    own.wait()
    for copy in copies:
        copy.wait()


def col_gather(block):
    m = lax.axis_size("col")
    return pl.pallas_call(
        col_gather_kernel,
        out_shape=jax.ShapeDtypeStruct((m,) + block.shape, block.dtype),
        in_specs=[pl.BlockSpec(memory_space=pltpu.VMEM)],
        out_specs=pl.BlockSpec(memory_space=pltpu.VMEM),
        scratch_shapes=[
            pltpu.SemaphoreType.DMA(()),
            pltpu.SemaphoreType.DMA((m - 1,)),
            pltpu.SemaphoreType.DMA((m - 1,)),
        ],
        compiler_params=pltpu.CompilerParams(collective_id=2, has_side_effects=True),
    )(block)


def col_sum_kernel(x_ref, own_ref, out_ref, got, send_sem, recv_sem):
    me, peers = col_peers()
    copies = []
    for j, peer in enumerate(peers):
        copy = pltpu.make_async_remote_copy(
            src_ref=x_ref.at[peer[2]],
            dst_ref=got.at[j],
            send_sem=send_sem.at[j],
            recv_sem=recv_sem.at[j],
            device_id=peer,
            device_id_type=MESH,
        )
        copy.start()
        copies.append(copy)
    for copy in copies:
        copy.wait()
    chunk = 32

    def body(i, carry):
        rows = pl.ds(pl.multiple_of(i * chunk, chunk), chunk)
        total = own_ref[rows, :]
        for j in range(len(copies)):
            total = total + got[j, rows, :].astype(jnp.float32)
        out_ref[rows, :] = total
        return carry

    lax.fori_loop(0, out_ref.shape[0] // chunk, body, 0)


def col_reduce_scatter(parts, own, collective_id):
    m = lax.axis_size("col")
    return pl.pallas_call(
        col_sum_kernel,
        out_shape=jax.ShapeDtypeStruct(own.shape, jnp.float32),
        in_specs=[pl.BlockSpec(memory_space=pltpu.VMEM)] * 2,
        out_specs=pl.BlockSpec(memory_space=pltpu.VMEM),
        scratch_shapes=[
            pltpu.VMEM((m - 1,) + parts.shape[1:], parts.dtype),
            pltpu.SemaphoreType.DMA((m - 1,)),
            pltpu.SemaphoreType.DMA((m - 1,)),
        ],
        compiler_params=pltpu.CompilerParams(collective_id=collective_id, has_side_effects=True),
    )(parts, own)


def col_mid_kernel(x_ref, own_ref, gain_ref, bias_ref, out_ref, got, rs_send, rs_recv, g_send, g_recv):
    me, peers = col_peers()
    copies = []
    for j, peer in enumerate(peers):
        copy = pltpu.make_async_remote_copy(
            src_ref=x_ref.at[peer[2]],
            dst_ref=got.at[j],
            send_sem=rs_send.at[j],
            recv_sem=rs_recv.at[j],
            device_id=peer,
            device_id_type=MESH,
        )
        copy.start()
        copies.append(copy)
    for copy in copies:
        copy.wait()
    chunk = 32
    width = out_ref.shape[2]

    def body(i, carry):
        rows = pl.ds(pl.multiple_of(i * chunk, chunk), chunk)
        total = own_ref[rows, :]
        for j in range(len(copies)):
            total = total + got[j, rows, :].astype(jnp.float32)
        center = total - jnp.sum(total, axis=1, keepdims=True) / width
        spread = jnp.sum(center * center, axis=1, keepdims=True) / width
        normed = center / jnp.sqrt(spread + 1e-05) * gain_ref[...] + bias_ref[...]
        out_ref[me, rows, :] = normed.astype(out_ref.dtype)
        return carry

    lax.fori_loop(0, out_ref.shape[1] // chunk, body, 0)
    sends = []
    for j, peer in enumerate(peers):
        copy = pltpu.make_async_remote_copy(
            src_ref=out_ref.at[me],
            dst_ref=out_ref.at[me],
            send_sem=g_send.at[j],
            recv_sem=g_recv.at[j],
            device_id=peer,
            device_id_type=MESH,
        )
        copy.start()
        sends.append(copy)
    for copy in sends:
        copy.wait()


def col_sum_norm_gather(parts, own, gain, bias):
    m = lax.axis_size("col")
    rows, width = own.shape
    return pl.pallas_call(
        col_mid_kernel,
        out_shape=jax.ShapeDtypeStruct((m, rows, width), jnp.bfloat16),
        in_specs=[pl.BlockSpec(memory_space=pltpu.VMEM)] * 4,
        out_specs=pl.BlockSpec(memory_space=pltpu.VMEM),
        scratch_shapes=[
            pltpu.VMEM((m - 1,) + parts.shape[1:], parts.dtype),
            pltpu.SemaphoreType.DMA((m - 1,)),
            pltpu.SemaphoreType.DMA((m - 1,)),
            pltpu.SemaphoreType.DMA((m - 1,)),
            pltpu.SemaphoreType.DMA((m - 1,)),
        ],
        compiler_params=pltpu.CompilerParams(collective_id=7, has_side_effects=True),
    )(parts, own, gain.reshape(1, width), bias.reshape(1, width))


def layer_norm(values, gain, bias):
    center = values - jnp.mean(values, axis=1, keepdims=True)
    spread = jnp.mean(center * center, axis=1, keepdims=True)
    return center * lax.rsqrt(spread + 1e-05) * gain + bias


def per_device(
    hidden_in,
    qkv_weight,
    qkv_global_weight,
    out_weight,
    ln_gain,
    ln_bias,
    ffn_in,
    ffn_out,
    ln2_gain,
    ln2_bias,
    segment_ids,
    global_pos,
    page_owner,
):
    neg = -1e30
    tokens = hidden_in[0]
    shard_len, width = tokens.shape
    heads_here = qkv_weight.shape[1]
    triple = qkv_weight.shape[2]
    head_dim = triple // 3
    n_seq = lax.axis_size("seq")
    n_row = lax.axis_size("row")
    n_col = lax.axis_size("col")
    seq_index = lax.axis_index("seq")
    col_index = lax.axis_index("col")
    base = seq_index * shard_len
    scale = 1.0 / math.sqrt(head_dim)

    all_pos = global_pos[0]
    n_glob = all_pos.shape[0]
    per_shard = n_glob // n_seq
    own_pos = lax.dynamic_slice_in_dim(all_pos, seq_index * per_shard, per_shard, 0)
    local_order = jnp.arange(shard_len, dtype=jnp.int32)
    own_match = (own_pos - base)[:, None] == local_order[None, :]
    picker = own_match.astype(jnp.bfloat16)
    own_rows = jnp.dot(picker, tokens, preferred_element_type=jnp.float32).astype(jnp.bfloat16)
    glob_rows = seq_direct_gather(own_rows.reshape(-1, 128)).reshape(n_glob, width)

    w_global = lax.all_gather(
        qkv_global_weight.reshape(qkv_global_weight.shape[0], -1), "row", axis=0, tiled=True
    )
    f_in = lax.all_gather(ffn_in, "row", axis=0, tiled=True)
    f_out = lax.all_gather(ffn_out, "row", axis=1, tiled=True)

    flat_weight = qkv_weight.reshape(width, heads_here * triple)
    qkv = jnp.dot(tokens, flat_weight, preferred_element_type=jnp.float32).astype(jnp.bfloat16)
    qkv_heads = qkv.reshape(shard_len, heads_here, triple)
    queries = qkv_heads[:, :, :head_dim]
    kv_local = qkv_heads[:, :, head_dim:]

    owners = page_owner[0, :, 0]
    n_pages = owners.shape[0]
    page_len = shard_len // n_pages
    capacity = max(2, n_pages // n_seq)
    page_order = jnp.arange(n_pages, dtype=jnp.int32)
    slot = jnp.sum(
        ((owners[:, None] == owners[None, :]) & (page_order[None, :] < page_order[:, None])).astype(
            jnp.int32
        ),
        axis=1,
    )
    target = owners * capacity + slot
    placing = (target[None, :] == jnp.arange(n_seq * capacity, dtype=jnp.int32)[:, None]).astype(
        jnp.bfloat16
    )
    outgoing = jnp.dot(
        placing,
        kv_local.reshape(n_pages, page_len * heads_here * 2 * head_dim),
        preferred_element_type=jnp.float32,
    ).astype(jnp.bfloat16)
    outgoing = outgoing.reshape(n_seq, capacity, page_len, heads_here, 2 * head_dim)
    arrived = lax.all_to_all(outgoing, "seq", split_axis=0, concat_axis=0, tiled=True)
    arrived, glob_rows = lax.optimization_barrier((arrived, glob_rows))
    page_pool = arrived[None, None]

    kv_ext = padded(kv_local, (("seq", 0),), HALF)

    glob_qkv = jnp.dot(glob_rows, flat_weight, preferred_element_type=jnp.float32).astype(
        jnp.bfloat16
    )
    glob_kv = glob_qkv.reshape(n_glob, heads_here, triple)[:, :, head_dim:]
    glob_k = glob_kv[:, :, :head_dim]
    glob_v = glob_kv[:, :, head_dim:]
    glob_q = (
        jnp.dot(glob_rows, w_global, preferred_element_type=jnp.float32)
        .astype(jnp.bfloat16)
        .reshape(n_glob, heads_here, triple)[:, :, :head_dim]
    )
    global_kv_local = (
        jnp.dot(tokens, w_global, preferred_element_type=jnp.float32)
        .astype(jnp.bfloat16)
        .reshape(shard_len, heads_here, triple)[:, :, head_dim:]
    )

    seg_all = segment_ids[0]
    glob_seg = jnp.take(seg_all, all_pos)
    seg_pad = jnp.pad(seg_all, (HALF, HALF), constant_values=-1)
    query_seg = lax.dynamic_slice_in_dim(seg_all, base, shard_len, 0)
    key_seg = lax.dynamic_slice_in_dim(seg_pad, base, shard_len + 2 * HALF, 0)
    key_pos = base - HALF + jnp.arange(shard_len + 2 * HALF, dtype=jnp.int32)
    key_flag = jnp.any(key_pos[:, None] == all_pos[None, :], axis=1)
    query_pos = base + local_order

    s_part = (
        jnp.einsum(
            "ghd,khd->hgk",
            glob_q,
            global_kv_local[:, :, :head_dim],
            preferred_element_type=jnp.float32,
        )
        * scale
    )
    part_mask = glob_seg[:, None] == query_seg[None, :]
    part_top = jnp.max(jnp.where(part_mask, s_part, neg), axis=2)
    e_part = jnp.where(part_mask, jnp.exp(s_part - part_top[:, :, None]), 0.0)
    part_total = jnp.sum(e_part, axis=2)
    part_acc = jnp.einsum(
        "hgk,khd->hgd",
        e_part,
        global_kv_local[:, :, head_dim:].astype(jnp.float32),
        precision=lax.Precision.HIGHEST,
    )
    packed = jnp.concatenate(
        [
            part_acc,
            part_total[:, :, None],
            jnp.broadcast_to(part_top[:, :, None], part_top.shape + (128 - head_dim - 1,)),
        ],
        axis=2,
    )
    packed = jnp.transpose(packed, (1, 0, 2)).reshape(n_glob * heads_here, 128)
    packed, f_in = lax.optimization_barrier((packed, f_in))
    merged = seq_direct_merge(packed.reshape(n_seq, -1, 128), head_dim + 1).reshape(
        per_shard, heads_here, 128
    )
    own_out = jnp.transpose(
        (merged[:, :, :head_dim] / merged[:, :, head_dim : head_dim + 1]).astype(jnp.bfloat16),
        (1, 0, 2),
    )

    glob_mask = query_seg[:, None] == glob_seg[None, :]
    k_blk = kv_ext[:, :, :head_dim]
    v_blk = kv_ext[:, :, head_dim:]
    s_win = jnp.einsum("qhd,khd->hqk", queries, k_blk, preferred_element_type=jnp.float32) * scale
    s_glob = jnp.einsum("qhd,ghd->hqg", queries, glob_k, preferred_element_type=jnp.float32) * scale
    m_win = (
        (jnp.abs(query_pos[:, None] - key_pos[None, :]) <= HALF)
        & (query_seg[:, None] == key_seg[None, :])
        & jnp.logical_not(key_flag[None, :])
    )
    top = jnp.maximum(
        jnp.max(jnp.where(m_win, s_win, neg), axis=2),
        jnp.max(jnp.where(glob_mask, s_glob, neg), axis=2),
    )
    e_win = jnp.where(m_win, jnp.exp(s_win - top[:, :, None]), 0.0)
    e_glob = jnp.where(glob_mask, jnp.exp(s_glob - top[:, :, None]), 0.0)
    total = jnp.sum(e_win, axis=2) + jnp.sum(e_glob, axis=2)
    numer = jnp.einsum(
        "hqk,khd->qhd", e_win.astype(jnp.bfloat16), v_blk, preferred_element_type=jnp.float32
    )
    numer = numer + jnp.einsum(
        "hqg,ghd->qhd", e_glob.astype(jnp.bfloat16), glob_v, preferred_element_type=jnp.float32
    )
    pieces = (numer / jnp.transpose(total)[:, :, None]).astype(jnp.bfloat16)

    placed = jnp.einsum("gt,hgd->thd", picker, own_out, preferred_element_type=jnp.float32).astype(
        jnp.bfloat16
    )
    is_own = jnp.any(own_match, axis=0)
    attention = jnp.where(is_own[:, None, None], placed, pieces).reshape(
        shard_len, heads_here * head_dim
    )


    out_rows = shard_len // n_col
    proj = jnp.dot(attention, out_weight, preferred_element_type=jnp.float32)
    proj_own = lax.dynamic_slice_in_dim(proj, col_index * out_rows, out_rows, 0)
    token_own = lax.dynamic_slice_in_dim(tokens, col_index * out_rows, out_rows, 0)
    middle_all = col_sum_norm_gather(
        proj.astype(jnp.bfloat16).reshape(n_col, out_rows, width),
        token_own.astype(jnp.float32) + proj_own,
        ln_gain,
        ln_bias,
    )
    mine = middle_all[col_index]
    middle = middle_all.reshape(shard_len, width)
    ffn_pre = jnp.dot(middle, f_in, preferred_element_type=jnp.float32)
    ffn_hidden = jax.nn.gelu(ffn_pre, approximate=False).astype(jnp.bfloat16)
    ffn_full = jnp.dot(ffn_hidden, f_out, preferred_element_type=jnp.float32)
    ffn_own = lax.dynamic_slice_in_dim(ffn_full, col_index * out_rows, out_rows, 0)
    second = col_reduce_scatter(
        ffn_full.astype(jnp.bfloat16).reshape(n_col, out_rows, width),
        mine.astype(jnp.float32) + ffn_own,
        6,
    )
    normed = layer_norm(second, ln2_gain, ln2_bias)
    return (normed.astype(jnp.bfloat16)[None], page_pool)


def solution(mesh):
    in_specs = (
        P("row", "seq", None),
        P(None, "col", None),
        P("row", "col", None),
        P("col", None),
        P(),
        P(),
        P("row", "col"),
        P("col", "row"),
        P(),
        P(),
        P("row", None),
        P("row", None),
        P("row", "seq", None),
    )
    out_specs = (P("row", ("seq", "col"), None), P("row", "seq", None, None, None, "col", None))
    return jax.shard_map(
        per_device, mesh=mesh, in_specs=in_specs, out_specs=out_specs, check_vma=False
    )
```

```python
import functools
import math

import jax
import jax.numpy as jnp
from jax import lax
from jax.experimental import pallas as pl
from jax.experimental.pallas import tpu as pltpu
from jax.sharding import PartitionSpec as P

MESH = pl.DeviceIdType.MESH

HALF = 256


def padded(block, sides, width):
    for axis, dim in sides:
        count = lax.axis_size(axis)
        forward = [(i, i + 1) for i in range(count - 1)]
        backward = [(target, source) for source, target in forward]
        low = lax.ppermute(
            lax.slice_in_dim(block, block.shape[dim] - width, None, axis=dim), axis, forward
        )
        high = lax.ppermute(lax.slice_in_dim(block, 0, width, axis=dim), axis, backward)
        block = jnp.concatenate([low, block, high], axis=dim)
    return block


def butterfly_partners(n):
    me = lax.axis_index("seq")
    partners = []
    step = 1
    while step < n:
        bit = (me // step) % 2
        partners.append(me + step - 2 * step * bit)
        step *= 2
    return me, partners


def enter(partners):
    row, col = lax.axis_index("row"), lax.axis_index("col")
    barrier = pltpu.get_barrier_semaphore()
    for partner in partners:
        pl.semaphore_signal(barrier, inc=1, device_id=(partner, row, col), device_id_type=MESH)
    pl.semaphore_wait(barrier, len(partners))
    return row, col


def gather_kernel(n, x_ref, out_ref, self_sem, send_sem, recv_sem):
    me, partners = butterfly_partners(n)
    row, col = enter(partners)
    own = pltpu.make_async_copy(x_ref, out_ref.at[me], self_sem)
    own.start()
    own.wait()
    size = 1
    for k, partner in enumerate(partners):
        start = (me // size) * size
        copy = pltpu.make_async_remote_copy(
            src_ref=out_ref.at[pl.ds(start, size)],
            dst_ref=out_ref.at[pl.ds(start, size)],
            send_sem=send_sem.at[k],
            recv_sem=recv_sem.at[k],
            device_id=(partner, row, col),
            device_id_type=MESH,
        )
        copy.start()
        copy.wait()
        size *= 2


def seq_gather(block):
    n = lax.axis_size("seq")
    rounds = n.bit_length() - 1
    return pl.pallas_call(
        functools.partial(gather_kernel, n),
        out_shape=jax.ShapeDtypeStruct((n,) + block.shape, block.dtype),
        in_specs=[pl.BlockSpec(memory_space=pltpu.VMEM)],
        out_specs=pl.BlockSpec(memory_space=pltpu.VMEM),
        scratch_shapes=[
            pltpu.SemaphoreType.DMA(()),
            pltpu.SemaphoreType.DMA((rounds,)),
            pltpu.SemaphoreType.DMA((rounds,)),
        ],
        compiler_params=pltpu.CompilerParams(collective_id=0, has_side_effects=True),
    )(block)


def merge_parts(mine, theirs, top_lane):
    lane = lax.broadcasted_iota(jnp.int32, mine.shape, 1)
    is_top = lane == top_lane
    top_a = jnp.max(jnp.where(is_top, mine, -jnp.inf), axis=1, keepdims=True)
    top_b = jnp.max(jnp.where(is_top, theirs, -jnp.inf), axis=1, keepdims=True)
    top = jnp.maximum(top_a, top_b)
    merged = mine * jnp.exp(top_a - top) + theirs * jnp.exp(top_b - top)
    return jnp.where(is_top, top, merged)


def halving_kernel(n, top_lane, x_ref, out_ref, *scratch):
    rounds = len(scratch) // 3
    kept, got, sems = scratch[:rounds], scratch[rounds : 2 * rounds], scratch[2 * rounds :]
    me = lax.axis_index("seq")
    steps = []
    step = n // 2
    while step >= 1:
        bit = (me // step) % 2
        steps.append((me + step - 2 * step * bit, bit))
        step //= 2
    row, col = enter([partner for partner, _ in steps])
    source = x_ref
    for k, (partner, bit) in enumerate(steps):
        half = source.shape[0] // 2
        send_at = pl.multiple_of((1 - bit) * half, 8)
        keep_at = pl.multiple_of(bit * half, 8)
        copy = pltpu.make_async_remote_copy(
            src_ref=source.at[pl.ds(send_at, half)],
            dst_ref=got[k],
            send_sem=sems[k].at[0],
            recv_sem=sems[k].at[1],
            device_id=(partner, row, col),
            device_id_type=MESH,
        )
        copy.start()
        copy.wait()
        value = merge_parts(source[pl.ds(keep_at, half)], got[k][...], top_lane)
        if k + 1 < rounds:
            kept[k][...] = value
            source = kept[k]
        else:
            out_ref[...] = value


def seq_softmax_combine(parts, top_lane):
    n = lax.axis_size("seq")
    rounds = n.bit_length() - 1
    rows, lanes = parts.shape
    scratch = []
    for k in range(rounds):
        scratch.append(pltpu.VMEM((rows >> (k + 1), lanes), parts.dtype))
    for k in range(rounds):
        scratch.append(pltpu.VMEM((rows >> (k + 1), lanes), parts.dtype))
    for k in range(rounds):
        scratch.append(pltpu.SemaphoreType.DMA((2,)))
    return pl.pallas_call(
        functools.partial(halving_kernel, n, top_lane),
        out_shape=jax.ShapeDtypeStruct((rows // n, lanes), parts.dtype),
        in_specs=[pl.BlockSpec(memory_space=pltpu.VMEM)],
        out_specs=pl.BlockSpec(memory_space=pltpu.VMEM),
        scratch_shapes=scratch,
        compiler_params=pltpu.CompilerParams(collective_id=1, has_side_effects=True),
    )(parts)


def seq_peers():
    me, n = lax.axis_index("seq"), lax.axis_size("seq")
    row, col = lax.axis_index("row"), lax.axis_index("col")
    peers = [lax.rem(me + j, n) for j in range(1, n)]
    barrier = pltpu.get_barrier_semaphore()
    for peer in peers:
        pl.semaphore_signal(barrier, inc=1, device_id=(peer, row, col), device_id_type=MESH)
    pl.semaphore_wait(barrier, len(peers))
    return me, [(peer, row, col) for peer in peers]


def seq_direct_gather_kernel(x_ref, out_ref, self_sem, send_sem, recv_sem):
    me, peers = seq_peers()
    own = pltpu.make_async_copy(x_ref, out_ref.at[me], self_sem)
    own.start()
    copies = []
    for j, peer in enumerate(peers):
        copy = pltpu.make_async_remote_copy(
            src_ref=x_ref,
            dst_ref=out_ref.at[me],
            send_sem=send_sem.at[j],
            recv_sem=recv_sem.at[j],
            device_id=peer,
            device_id_type=MESH,
        )
        copy.start()
        copies.append(copy)
    own.wait()
    for copy in copies:
        copy.wait()


def seq_direct_gather(block):
    n = lax.axis_size("seq")
    return pl.pallas_call(
        seq_direct_gather_kernel,
        out_shape=jax.ShapeDtypeStruct((n,) + block.shape, block.dtype),
        in_specs=[pl.BlockSpec(memory_space=pltpu.VMEM)],
        out_specs=pl.BlockSpec(memory_space=pltpu.VMEM),
        scratch_shapes=[
            pltpu.SemaphoreType.DMA(()),
            pltpu.SemaphoreType.DMA((n - 1,)),
            pltpu.SemaphoreType.DMA((n - 1,)),
        ],
        compiler_params=pltpu.CompilerParams(collective_id=4, has_side_effects=True),
    )(block)


def seq_merge_kernel(top_lane, x_ref, out_ref, got, send_sem, recv_sem):
    me, peers = seq_peers()
    copies = []
    for j, peer in enumerate(peers):
        copy = pltpu.make_async_remote_copy(
            src_ref=x_ref.at[peer[0]],
            dst_ref=got.at[j],
            send_sem=send_sem.at[j],
            recv_sem=recv_sem.at[j],
            device_id=peer,
            device_id_type=MESH,
        )
        copy.start()
        copies.append(copy)
    for copy in copies:
        copy.wait()
    value = x_ref[me]
    for j in range(len(copies)):
        value = merge_parts(value, got[j], top_lane)
    out_ref[...] = value


def seq_direct_merge(parts, top_lane):
    n = parts.shape[0]
    return pl.pallas_call(
        functools.partial(seq_merge_kernel, top_lane),
        out_shape=jax.ShapeDtypeStruct(parts.shape[1:], parts.dtype),
        in_specs=[pl.BlockSpec(memory_space=pltpu.VMEM)],
        out_specs=pl.BlockSpec(memory_space=pltpu.VMEM),
        scratch_shapes=[
            pltpu.VMEM((n - 1,) + parts.shape[1:], parts.dtype),
            pltpu.SemaphoreType.DMA((n - 1,)),
            pltpu.SemaphoreType.DMA((n - 1,)),
        ],
        compiler_params=pltpu.CompilerParams(collective_id=5, has_side_effects=True),
    )(parts)


def seq_two_level_peers(group):
    me, n = lax.axis_index("seq"), lax.axis_size("seq")
    row, col = lax.axis_index("row"), lax.axis_index("col")
    first = (me // group) * group
    near = [first + lax.rem(me - first + j, group) for j in range(1, group)]
    far = [lax.rem(me + group * j, n) for j in range(1, n // group)]
    barrier = pltpu.get_barrier_semaphore()
    for peer in near + far:
        pl.semaphore_signal(barrier, inc=1, device_id=(peer, row, col), device_id_type=MESH)
    pl.semaphore_wait(barrier, len(near) + len(far))
    return me, first, [(p, row, col) for p in near], [(p, row, col) for p in far]


def seq_gather2_kernel(group, x_ref, out_ref, self_sem, near_send, near_recv, far_send, far_recv):
    me, first, near, far = seq_two_level_peers(group)
    own = pltpu.make_async_copy(x_ref, out_ref.at[me], self_sem)
    own.start()
    copies = []
    for j, peer in enumerate(near):
        copy = pltpu.make_async_remote_copy(
            src_ref=x_ref,
            dst_ref=out_ref.at[me],
            send_sem=near_send.at[j],
            recv_sem=near_recv.at[j],
            device_id=peer,
            device_id_type=MESH,
        )
        copy.start()
        copies.append(copy)
    own.wait()
    for copy in copies:
        copy.wait()
    block = out_ref.at[pl.ds(first, group)]
    copies = []
    for j, peer in enumerate(far):
        copy = pltpu.make_async_remote_copy(
            src_ref=block,
            dst_ref=block,
            send_sem=far_send.at[j],
            recv_sem=far_recv.at[j],
            device_id=peer,
            device_id_type=MESH,
        )
        copy.start()
        copies.append(copy)
    for copy in copies:
        copy.wait()


def seq_gather2(block, group):
    n = lax.axis_size("seq")
    return pl.pallas_call(
        functools.partial(seq_gather2_kernel, group),
        out_shape=jax.ShapeDtypeStruct((n,) + block.shape, block.dtype),
        in_specs=[pl.BlockSpec(memory_space=pltpu.VMEM)],
        out_specs=pl.BlockSpec(memory_space=pltpu.VMEM),
        scratch_shapes=[
            pltpu.SemaphoreType.DMA(()),
            pltpu.SemaphoreType.DMA((group - 1,)),
            pltpu.SemaphoreType.DMA((group - 1,)),
            pltpu.SemaphoreType.DMA((n // group - 1,)),
            pltpu.SemaphoreType.DMA((n // group - 1,)),
        ],
        compiler_params=pltpu.CompilerParams(collective_id=8, has_side_effects=True),
    )(block)


def seq_merge2_kernel(
    group, top_lane, x_ref, out_ref, got_far, partial, got_near, far_send, far_recv, near_send, near_recv
):
    me, first, near, far = seq_two_level_peers(group)
    copies = []
    for j, peer in enumerate(far):
        start = pl.multiple_of((peer[0] // group) * group, group)
        copy = pltpu.make_async_remote_copy(
            src_ref=x_ref.at[pl.ds(start, group)],
            dst_ref=got_far.at[j],
            send_sem=far_send.at[j],
            recv_sem=far_recv.at[j],
            device_id=peer,
            device_id_type=MESH,
        )
        copy.start()
        copies.append(copy)
    for copy in copies:
        copy.wait()
    for k in range(group):
        value = x_ref[first + k]
        for j in range(len(far)):
            value = merge_parts(value, got_far[j, k], top_lane)
        partial[k] = value
    copies = []
    for j, peer in enumerate(near):
        copy = pltpu.make_async_remote_copy(
            src_ref=partial.at[peer[0] - first],
            dst_ref=got_near.at[j],
            send_sem=near_send.at[j],
            recv_sem=near_recv.at[j],
            device_id=peer,
            device_id_type=MESH,
        )
        copy.start()
        copies.append(copy)
    for copy in copies:
        copy.wait()
    value = partial[me - first]
    for j in range(len(near)):
        value = merge_parts(value, got_near[j], top_lane)
    out_ref[...] = value


def seq_merge2(parts, top_lane, group):
    n = parts.shape[0]
    blk = parts.shape[1:]
    return pl.pallas_call(
        functools.partial(seq_merge2_kernel, group, top_lane),
        out_shape=jax.ShapeDtypeStruct(blk, parts.dtype),
        in_specs=[pl.BlockSpec(memory_space=pltpu.VMEM)],
        out_specs=pl.BlockSpec(memory_space=pltpu.VMEM),
        scratch_shapes=[
            pltpu.VMEM((n // group - 1, group) + blk, parts.dtype),
            pltpu.VMEM((group,) + blk, parts.dtype),
            pltpu.VMEM((group - 1,) + blk, parts.dtype),
            pltpu.SemaphoreType.DMA((n // group - 1,)),
            pltpu.SemaphoreType.DMA((n // group - 1,)),
            pltpu.SemaphoreType.DMA((group - 1,)),
            pltpu.SemaphoreType.DMA((group - 1,)),
        ],
        compiler_params=pltpu.CompilerParams(collective_id=9, has_side_effects=True),
    )(parts)


def col_peers():
    me, m = lax.axis_index("col"), lax.axis_size("col")
    seq, row = lax.axis_index("seq"), lax.axis_index("row")
    peers = [lax.rem(me + j, m) for j in range(1, m)]
    barrier = pltpu.get_barrier_semaphore()
    for peer in peers:
        pl.semaphore_signal(barrier, inc=1, device_id=(seq, row, peer), device_id_type=MESH)
    pl.semaphore_wait(barrier, len(peers))
    return me, [(seq, row, peer) for peer in peers]


def col_gather_kernel(x_ref, out_ref, self_sem, send_sem, recv_sem):
    me, peers = col_peers()
    own = pltpu.make_async_copy(x_ref, out_ref.at[me], self_sem)
    own.start()
    copies = []
    for j, peer in enumerate(peers):
        copy = pltpu.make_async_remote_copy(
            src_ref=x_ref,
            dst_ref=out_ref.at[me],
            send_sem=send_sem.at[j],
            recv_sem=recv_sem.at[j],
            device_id=peer,
            device_id_type=MESH,
        )
        copy.start()
        copies.append(copy)
    own.wait()
    for copy in copies:
        copy.wait()


def col_gather(block):
    m = lax.axis_size("col")
    return pl.pallas_call(
        col_gather_kernel,
        out_shape=jax.ShapeDtypeStruct((m,) + block.shape, block.dtype),
        in_specs=[pl.BlockSpec(memory_space=pltpu.VMEM)],
        out_specs=pl.BlockSpec(memory_space=pltpu.VMEM),
        scratch_shapes=[
            pltpu.SemaphoreType.DMA(()),
            pltpu.SemaphoreType.DMA((m - 1,)),
            pltpu.SemaphoreType.DMA((m - 1,)),
        ],
        compiler_params=pltpu.CompilerParams(collective_id=2, has_side_effects=True),
    )(block)


def col_sum_kernel(x_ref, own_ref, out_ref, got, send_sem, recv_sem):
    me, peers = col_peers()
    copies = []
    for j, peer in enumerate(peers):
        copy = pltpu.make_async_remote_copy(
            src_ref=x_ref.at[peer[2]],
            dst_ref=got.at[j],
            send_sem=send_sem.at[j],
            recv_sem=recv_sem.at[j],
            device_id=peer,
            device_id_type=MESH,
        )
        copy.start()
        copies.append(copy)
    for copy in copies:
        copy.wait()
    chunk = 32

    def body(i, carry):
        rows = pl.ds(pl.multiple_of(i * chunk, chunk), chunk)
        total = own_ref[rows, :]
        for j in range(len(copies)):
            total = total + got[j, rows, :].astype(jnp.float32)
        out_ref[rows, :] = total
        return carry

    lax.fori_loop(0, out_ref.shape[0] // chunk, body, 0)


def col_reduce_scatter(parts, own, collective_id):
    m = lax.axis_size("col")
    return pl.pallas_call(
        col_sum_kernel,
        out_shape=jax.ShapeDtypeStruct(own.shape, jnp.float32),
        in_specs=[pl.BlockSpec(memory_space=pltpu.VMEM)] * 2,
        out_specs=pl.BlockSpec(memory_space=pltpu.VMEM),
        scratch_shapes=[
            pltpu.VMEM((m - 1,) + parts.shape[1:], parts.dtype),
            pltpu.SemaphoreType.DMA((m - 1,)),
            pltpu.SemaphoreType.DMA((m - 1,)),
        ],
        compiler_params=pltpu.CompilerParams(collective_id=collective_id, has_side_effects=True),
    )(parts, own)


def col_mid_kernel(x_ref, own_ref, gain_ref, bias_ref, out_ref, got, rs_send, rs_recv, g_send, g_recv):
    me, peers = col_peers()
    copies = []
    for j, peer in enumerate(peers):
        copy = pltpu.make_async_remote_copy(
            src_ref=x_ref.at[peer[2]],
            dst_ref=got.at[j],
            send_sem=rs_send.at[j],
            recv_sem=rs_recv.at[j],
            device_id=peer,
            device_id_type=MESH,
        )
        copy.start()
        copies.append(copy)
    for copy in copies:
        copy.wait()
    chunk = 32
    width = out_ref.shape[2]

    def body(i, carry):
        rows = pl.ds(pl.multiple_of(i * chunk, chunk), chunk)
        total = own_ref[rows, :]
        for j in range(len(copies)):
            total = total + got[j, rows, :].astype(jnp.float32)
        center = total - jnp.sum(total, axis=1, keepdims=True) / width
        spread = jnp.sum(center * center, axis=1, keepdims=True) / width
        normed = center / jnp.sqrt(spread + 1e-05) * gain_ref[...] + bias_ref[...]
        out_ref[me, rows, :] = normed.astype(out_ref.dtype)
        return carry

    lax.fori_loop(0, out_ref.shape[1] // chunk, body, 0)
    sends = []
    for j, peer in enumerate(peers):
        copy = pltpu.make_async_remote_copy(
            src_ref=out_ref.at[me],
            dst_ref=out_ref.at[me],
            send_sem=g_send.at[j],
            recv_sem=g_recv.at[j],
            device_id=peer,
            device_id_type=MESH,
        )
        copy.start()
        sends.append(copy)
    for copy in sends:
        copy.wait()


def col_sum_norm_gather(parts, own, gain, bias):
    m = lax.axis_size("col")
    rows, width = own.shape
    return pl.pallas_call(
        col_mid_kernel,
        out_shape=jax.ShapeDtypeStruct((m, rows, width), jnp.bfloat16),
        in_specs=[pl.BlockSpec(memory_space=pltpu.VMEM)] * 4,
        out_specs=pl.BlockSpec(memory_space=pltpu.VMEM),
        scratch_shapes=[
            pltpu.VMEM((m - 1,) + parts.shape[1:], parts.dtype),
            pltpu.SemaphoreType.DMA((m - 1,)),
            pltpu.SemaphoreType.DMA((m - 1,)),
            pltpu.SemaphoreType.DMA((m - 1,)),
            pltpu.SemaphoreType.DMA((m - 1,)),
        ],
        compiler_params=pltpu.CompilerParams(collective_id=7, has_side_effects=True),
    )(parts, own, gain.reshape(1, width), bias.reshape(1, width))


def layer_norm(values, gain, bias):
    center = values - jnp.mean(values, axis=1, keepdims=True)
    spread = jnp.mean(center * center, axis=1, keepdims=True)
    return center * lax.rsqrt(spread + 1e-05) * gain + bias


def per_device(
    hidden_in,
    qkv_weight,
    qkv_global_weight,
    out_weight,
    ln_gain,
    ln_bias,
    ffn_in,
    ffn_out,
    ln2_gain,
    ln2_bias,
    segment_ids,
    global_pos,
    page_owner,
):
    neg = -1e30
    tokens = hidden_in[0]
    shard_len, width = tokens.shape
    heads_here = qkv_weight.shape[1]
    triple = qkv_weight.shape[2]
    head_dim = triple // 3
    n_seq = lax.axis_size("seq")
    n_row = lax.axis_size("row")
    n_col = lax.axis_size("col")
    seq_index = lax.axis_index("seq")
    col_index = lax.axis_index("col")
    base = seq_index * shard_len
    scale = 1.0 / math.sqrt(head_dim)

    all_pos = global_pos[0]
    n_glob = all_pos.shape[0]
    per_shard = n_glob // n_seq
    own_pos = lax.dynamic_slice_in_dim(all_pos, seq_index * per_shard, per_shard, 0)
    local_order = jnp.arange(shard_len, dtype=jnp.int32)
    own_match = (own_pos - base)[:, None] == local_order[None, :]
    picker = own_match.astype(jnp.bfloat16)
    own_rows = jnp.dot(picker, tokens, preferred_element_type=jnp.float32).astype(jnp.bfloat16)
    group = 4 if n_seq % 4 == 0 and n_seq > 4 else 1
    if group > 1:
        glob_rows = seq_gather2(own_rows.reshape(-1, 128), group).reshape(n_glob, width)
    else:
        glob_rows = seq_direct_gather(own_rows.reshape(-1, 128)).reshape(n_glob, width)

    w_global = lax.all_gather(
        qkv_global_weight.reshape(qkv_global_weight.shape[0], -1), "row", axis=0, tiled=True
    )
    f_in = lax.all_gather(ffn_in, "row", axis=0, tiled=True)
    f_out = lax.all_gather(ffn_out, "row", axis=1, tiled=True)

    flat_weight = qkv_weight.reshape(width, heads_here * triple)
    qkv = jnp.dot(tokens, flat_weight, preferred_element_type=jnp.float32).astype(jnp.bfloat16)
    qkv_heads = qkv.reshape(shard_len, heads_here, triple)
    queries = qkv_heads[:, :, :head_dim]
    kv_local = qkv_heads[:, :, head_dim:]

    owners = page_owner[0, :, 0]
    n_pages = owners.shape[0]
    page_len = shard_len // n_pages
    capacity = max(2, n_pages // n_seq)
    page_order = jnp.arange(n_pages, dtype=jnp.int32)
    slot = jnp.sum(
        ((owners[:, None] == owners[None, :]) & (page_order[None, :] < page_order[:, None])).astype(
            jnp.int32
        ),
        axis=1,
    )
    target = owners * capacity + slot
    placing = (target[None, :] == jnp.arange(n_seq * capacity, dtype=jnp.int32)[:, None]).astype(
        jnp.bfloat16
    )
    outgoing = jnp.dot(
        placing,
        kv_local.reshape(n_pages, page_len * heads_here * 2 * head_dim),
        preferred_element_type=jnp.float32,
    ).astype(jnp.bfloat16)
    outgoing = outgoing.reshape(n_seq, capacity, page_len, heads_here, 2 * head_dim)
    arrived = lax.all_to_all(outgoing, "seq", split_axis=0, concat_axis=0, tiled=True)
    arrived, glob_rows = lax.optimization_barrier((arrived, glob_rows))
    page_pool = arrived[None, None]

    kv_ext = padded(kv_local, (("seq", 0),), HALF)

    glob_qkv = jnp.dot(glob_rows, flat_weight, preferred_element_type=jnp.float32).astype(
        jnp.bfloat16
    )
    glob_kv = glob_qkv.reshape(n_glob, heads_here, triple)[:, :, head_dim:]
    glob_k = glob_kv[:, :, :head_dim]
    glob_v = glob_kv[:, :, head_dim:]
    glob_q = (
        jnp.dot(glob_rows, w_global, preferred_element_type=jnp.float32)
        .astype(jnp.bfloat16)
        .reshape(n_glob, heads_here, triple)[:, :, :head_dim]
    )
    global_kv_local = (
        jnp.dot(tokens, w_global, preferred_element_type=jnp.float32)
        .astype(jnp.bfloat16)
        .reshape(shard_len, heads_here, triple)[:, :, head_dim:]
    )

    seg_all = segment_ids[0]
    glob_seg = jnp.take(seg_all, all_pos)
    seg_pad = jnp.pad(seg_all, (HALF, HALF), constant_values=-1)
    query_seg = lax.dynamic_slice_in_dim(seg_all, base, shard_len, 0)
    key_seg = lax.dynamic_slice_in_dim(seg_pad, base, shard_len + 2 * HALF, 0)
    key_pos = base - HALF + jnp.arange(shard_len + 2 * HALF, dtype=jnp.int32)
    key_flag = jnp.any(key_pos[:, None] == all_pos[None, :], axis=1)
    query_pos = base + local_order

    s_part = (
        jnp.einsum(
            "ghd,khd->hgk",
            glob_q,
            global_kv_local[:, :, :head_dim],
            preferred_element_type=jnp.float32,
        )
        * scale
    )
    part_mask = glob_seg[:, None] == query_seg[None, :]
    part_top = jnp.max(jnp.where(part_mask, s_part, neg), axis=2)
    e_part = jnp.where(part_mask, jnp.exp(s_part - part_top[:, :, None]), 0.0)
    part_total = jnp.sum(e_part, axis=2)
    part_acc = jnp.einsum(
        "hgk,khd->hgd",
        e_part,
        global_kv_local[:, :, head_dim:].astype(jnp.float32),
        precision=lax.Precision.HIGHEST,
    )
    packed = jnp.concatenate(
        [
            part_acc,
            part_total[:, :, None],
            jnp.broadcast_to(part_top[:, :, None], part_top.shape + (128 - head_dim - 1,)),
        ],
        axis=2,
    )
    packed = jnp.transpose(packed, (1, 0, 2)).reshape(n_glob * heads_here, 128)
    packed, f_in = lax.optimization_barrier((packed, f_in))
    if group > 1:
        merged = seq_merge2(packed.reshape(n_seq, -1, 128), head_dim + 1, group)
    else:
        merged = seq_direct_merge(packed.reshape(n_seq, -1, 128), head_dim + 1)
    merged = merged.reshape(
        per_shard, heads_here, 128
    )
    own_out = jnp.transpose(
        (merged[:, :, :head_dim] / merged[:, :, head_dim : head_dim + 1]).astype(jnp.bfloat16),
        (1, 0, 2),
    )

    glob_mask = query_seg[:, None] == glob_seg[None, :]
    k_blk = kv_ext[:, :, :head_dim]
    v_blk = kv_ext[:, :, head_dim:]
    s_win = jnp.einsum("qhd,khd->hqk", queries, k_blk, preferred_element_type=jnp.float32) * scale
    s_glob = jnp.einsum("qhd,ghd->hqg", queries, glob_k, preferred_element_type=jnp.float32) * scale
    m_win = (
        (jnp.abs(query_pos[:, None] - key_pos[None, :]) <= HALF)
        & (query_seg[:, None] == key_seg[None, :])
        & jnp.logical_not(key_flag[None, :])
    )
    top = jnp.maximum(
        jnp.max(jnp.where(m_win, s_win, neg), axis=2),
        jnp.max(jnp.where(glob_mask, s_glob, neg), axis=2),
    )
    e_win = jnp.where(m_win, jnp.exp(s_win - top[:, :, None]), 0.0)
    e_glob = jnp.where(glob_mask, jnp.exp(s_glob - top[:, :, None]), 0.0)
    total = jnp.sum(e_win, axis=2) + jnp.sum(e_glob, axis=2)
    numer = jnp.einsum(
        "hqk,khd->qhd", e_win.astype(jnp.bfloat16), v_blk, preferred_element_type=jnp.float32
    )
    numer = numer + jnp.einsum(
        "hqg,ghd->qhd", e_glob.astype(jnp.bfloat16), glob_v, preferred_element_type=jnp.float32
    )
    pieces = (numer / jnp.transpose(total)[:, :, None]).astype(jnp.bfloat16)

    placed = jnp.einsum("gt,hgd->thd", picker, own_out, preferred_element_type=jnp.float32).astype(
        jnp.bfloat16
    )
    is_own = jnp.any(own_match, axis=0)
    attention = jnp.where(is_own[:, None, None], placed, pieces).reshape(
        shard_len, heads_here * head_dim
    )


    out_rows = shard_len // n_col
    proj = jnp.dot(attention, out_weight, preferred_element_type=jnp.float32)
    proj_own = lax.dynamic_slice_in_dim(proj, col_index * out_rows, out_rows, 0)
    token_own = lax.dynamic_slice_in_dim(tokens, col_index * out_rows, out_rows, 0)
    middle_all = col_sum_norm_gather(
        proj.astype(jnp.bfloat16).reshape(n_col, out_rows, width),
        token_own.astype(jnp.float32) + proj_own,
        ln_gain,
        ln_bias,
    )
    mine = middle_all[col_index]
    middle = middle_all.reshape(shard_len, width)
    ffn_pre = jnp.dot(middle, f_in, preferred_element_type=jnp.float32)
    ffn_hidden = jax.nn.gelu(ffn_pre, approximate=False).astype(jnp.bfloat16)
    ffn_full = jnp.dot(ffn_hidden, f_out, preferred_element_type=jnp.float32)
    ffn_own = lax.dynamic_slice_in_dim(ffn_full, col_index * out_rows, out_rows, 0)
    second = col_reduce_scatter(
        ffn_full.astype(jnp.bfloat16).reshape(n_col, out_rows, width),
        mine.astype(jnp.float32) + ffn_own,
        6,
    )
    normed = layer_norm(second, ln2_gain, ln2_bias)
    return (normed.astype(jnp.bfloat16)[None], page_pool)


def solution(mesh):
    in_specs = (
        P("row", "seq", None),
        P(None, "col", None),
        P("row", "col", None),
        P("col", None),
        P(),
        P(),
        P("row", "col"),
        P("col", "row"),
        P(),
        P(),
        P("row", None),
        P("row", None),
        P("row", "seq", None),
    )
    out_specs = (P("row", ("seq", "col"), None), P("row", "seq", None, None, None, "col", None))
    return jax.shard_map(
        per_device, mesh=mesh, in_specs=in_specs, out_specs=out_specs, check_vma=False
    )
```

```python
import functools
import math

import jax
import jax.numpy as jnp
from jax import lax
from jax.experimental import pallas as pl
from jax.experimental.pallas import tpu as pltpu
from jax.sharding import PartitionSpec as P

MESH = pl.DeviceIdType.MESH

HALF = 256


def padded(block, sides, width):
    for axis, dim in sides:
        count = lax.axis_size(axis)
        forward = [(i, i + 1) for i in range(count - 1)]
        backward = [(target, source) for source, target in forward]
        low = lax.ppermute(
            lax.slice_in_dim(block, block.shape[dim] - width, None, axis=dim), axis, forward
        )
        high = lax.ppermute(lax.slice_in_dim(block, 0, width, axis=dim), axis, backward)
        block = jnp.concatenate([low, block, high], axis=dim)
    return block


def butterfly_partners(n):
    me = lax.axis_index("seq")
    partners = []
    step = 1
    while step < n:
        bit = (me // step) % 2
        partners.append(me + step - 2 * step * bit)
        step *= 2
    return me, partners


def enter(partners):
    row, col = lax.axis_index("row"), lax.axis_index("col")
    barrier = pltpu.get_barrier_semaphore()
    for partner in partners:
        pl.semaphore_signal(barrier, inc=1, device_id=(partner, row, col), device_id_type=MESH)
    pl.semaphore_wait(barrier, len(partners))
    return row, col


def gather_kernel(n, x_ref, out_ref, self_sem, send_sem, recv_sem):
    me, partners = butterfly_partners(n)
    row, col = enter(partners)
    own = pltpu.make_async_copy(x_ref, out_ref.at[me], self_sem)
    own.start()
    own.wait()
    size = 1
    for k, partner in enumerate(partners):
        start = (me // size) * size
        copy = pltpu.make_async_remote_copy(
            src_ref=out_ref.at[pl.ds(start, size)],
            dst_ref=out_ref.at[pl.ds(start, size)],
            send_sem=send_sem.at[k],
            recv_sem=recv_sem.at[k],
            device_id=(partner, row, col),
            device_id_type=MESH,
        )
        copy.start()
        copy.wait()
        size *= 2


def seq_gather(block):
    n = lax.axis_size("seq")
    rounds = n.bit_length() - 1
    return pl.pallas_call(
        functools.partial(gather_kernel, n),
        out_shape=jax.ShapeDtypeStruct((n,) + block.shape, block.dtype),
        in_specs=[pl.BlockSpec(memory_space=pltpu.VMEM)],
        out_specs=pl.BlockSpec(memory_space=pltpu.VMEM),
        scratch_shapes=[
            pltpu.SemaphoreType.DMA(()),
            pltpu.SemaphoreType.DMA((rounds,)),
            pltpu.SemaphoreType.DMA((rounds,)),
        ],
        compiler_params=pltpu.CompilerParams(collective_id=0, has_side_effects=True),
    )(block)


def merge_parts(mine, theirs, top_lane):
    lane = lax.broadcasted_iota(jnp.int32, mine.shape, 1)
    is_top = lane == top_lane
    top_a = jnp.max(jnp.where(is_top, mine, -jnp.inf), axis=1, keepdims=True)
    top_b = jnp.max(jnp.where(is_top, theirs, -jnp.inf), axis=1, keepdims=True)
    top = jnp.maximum(top_a, top_b)
    merged = mine * jnp.exp(top_a - top) + theirs * jnp.exp(top_b - top)
    return jnp.where(is_top, top, merged)


def halving_kernel(n, top_lane, x_ref, out_ref, *scratch):
    rounds = len(scratch) // 3
    kept, got, sems = scratch[:rounds], scratch[rounds : 2 * rounds], scratch[2 * rounds :]
    me = lax.axis_index("seq")
    steps = []
    step = n // 2
    while step >= 1:
        bit = (me // step) % 2
        steps.append((me + step - 2 * step * bit, bit))
        step //= 2
    row, col = enter([partner for partner, _ in steps])
    source = x_ref
    for k, (partner, bit) in enumerate(steps):
        half = source.shape[0] // 2
        send_at = pl.multiple_of((1 - bit) * half, 8)
        keep_at = pl.multiple_of(bit * half, 8)
        copy = pltpu.make_async_remote_copy(
            src_ref=source.at[pl.ds(send_at, half)],
            dst_ref=got[k],
            send_sem=sems[k].at[0],
            recv_sem=sems[k].at[1],
            device_id=(partner, row, col),
            device_id_type=MESH,
        )
        copy.start()
        copy.wait()
        value = merge_parts(source[pl.ds(keep_at, half)], got[k][...], top_lane)
        if k + 1 < rounds:
            kept[k][...] = value
            source = kept[k]
        else:
            out_ref[...] = value


def seq_softmax_combine(parts, top_lane):
    n = lax.axis_size("seq")
    rounds = n.bit_length() - 1
    rows, lanes = parts.shape
    scratch = []
    for k in range(rounds):
        scratch.append(pltpu.VMEM((rows >> (k + 1), lanes), parts.dtype))
    for k in range(rounds):
        scratch.append(pltpu.VMEM((rows >> (k + 1), lanes), parts.dtype))
    for k in range(rounds):
        scratch.append(pltpu.SemaphoreType.DMA((2,)))
    return pl.pallas_call(
        functools.partial(halving_kernel, n, top_lane),
        out_shape=jax.ShapeDtypeStruct((rows // n, lanes), parts.dtype),
        in_specs=[pl.BlockSpec(memory_space=pltpu.VMEM)],
        out_specs=pl.BlockSpec(memory_space=pltpu.VMEM),
        scratch_shapes=scratch,
        compiler_params=pltpu.CompilerParams(collective_id=1, has_side_effects=True),
    )(parts)


def seq_peers():
    me, n = lax.axis_index("seq"), lax.axis_size("seq")
    row, col = lax.axis_index("row"), lax.axis_index("col")
    peers = [lax.rem(me + j, n) for j in range(1, n)]
    barrier = pltpu.get_barrier_semaphore()
    for peer in peers:
        pl.semaphore_signal(barrier, inc=1, device_id=(peer, row, col), device_id_type=MESH)
    pl.semaphore_wait(barrier, len(peers))
    return me, [(peer, row, col) for peer in peers]


def seq_direct_gather_kernel(x_ref, out_ref, self_sem, send_sem, recv_sem):
    me, peers = seq_peers()
    own = pltpu.make_async_copy(x_ref, out_ref.at[me], self_sem)
    own.start()
    copies = []
    for j, peer in enumerate(peers):
        copy = pltpu.make_async_remote_copy(
            src_ref=x_ref,
            dst_ref=out_ref.at[me],
            send_sem=send_sem.at[j],
            recv_sem=recv_sem.at[j],
            device_id=peer,
            device_id_type=MESH,
        )
        copy.start()
        copies.append(copy)
    own.wait()
    for copy in copies:
        copy.wait()


def seq_direct_gather(block):
    n = lax.axis_size("seq")
    return pl.pallas_call(
        seq_direct_gather_kernel,
        out_shape=jax.ShapeDtypeStruct((n,) + block.shape, block.dtype),
        in_specs=[pl.BlockSpec(memory_space=pltpu.VMEM)],
        out_specs=pl.BlockSpec(memory_space=pltpu.VMEM),
        scratch_shapes=[
            pltpu.SemaphoreType.DMA(()),
            pltpu.SemaphoreType.DMA((n - 1,)),
            pltpu.SemaphoreType.DMA((n - 1,)),
        ],
        compiler_params=pltpu.CompilerParams(collective_id=4, has_side_effects=True),
    )(block)


def seq_merge_kernel(top_lane, x_ref, out_ref, got, send_sem, recv_sem):
    me, peers = seq_peers()
    copies = []
    for j, peer in enumerate(peers):
        copy = pltpu.make_async_remote_copy(
            src_ref=x_ref.at[peer[0]],
            dst_ref=got.at[j],
            send_sem=send_sem.at[j],
            recv_sem=recv_sem.at[j],
            device_id=peer,
            device_id_type=MESH,
        )
        copy.start()
        copies.append(copy)
    for copy in copies:
        copy.wait()
    value = x_ref[me]
    for j in range(len(copies)):
        value = merge_parts(value, got[j], top_lane)
    out_ref[...] = value


def seq_direct_merge(parts, top_lane):
    n = parts.shape[0]
    return pl.pallas_call(
        functools.partial(seq_merge_kernel, top_lane),
        out_shape=jax.ShapeDtypeStruct(parts.shape[1:], parts.dtype),
        in_specs=[pl.BlockSpec(memory_space=pltpu.VMEM)],
        out_specs=pl.BlockSpec(memory_space=pltpu.VMEM),
        scratch_shapes=[
            pltpu.VMEM((n - 1,) + parts.shape[1:], parts.dtype),
            pltpu.SemaphoreType.DMA((n - 1,)),
            pltpu.SemaphoreType.DMA((n - 1,)),
        ],
        compiler_params=pltpu.CompilerParams(collective_id=5, has_side_effects=True),
    )(parts)


def seq_two_level_peers(group):
    me, n = lax.axis_index("seq"), lax.axis_size("seq")
    row, col = lax.axis_index("row"), lax.axis_index("col")
    first = (me // group) * group
    near = [first + lax.rem(me - first + j, group) for j in range(1, group)]
    far = [lax.rem(me + group * j, n) for j in range(1, n // group)]
    barrier = pltpu.get_barrier_semaphore()
    for peer in near + far:
        pl.semaphore_signal(barrier, inc=1, device_id=(peer, row, col), device_id_type=MESH)
    pl.semaphore_wait(barrier, len(near) + len(far))
    return me, first, [(p, row, col) for p in near], [(p, row, col) for p in far]


def seq_gather2_kernel(group, x_ref, out_ref, self_sem, near_send, near_recv, far_send, far_recv):
    me, first, near, far = seq_two_level_peers(group)
    own = pltpu.make_async_copy(x_ref, out_ref.at[me], self_sem)
    own.start()
    copies = []
    for j, peer in enumerate(near):
        copy = pltpu.make_async_remote_copy(
            src_ref=x_ref,
            dst_ref=out_ref.at[me],
            send_sem=near_send.at[j],
            recv_sem=near_recv.at[j],
            device_id=peer,
            device_id_type=MESH,
        )
        copy.start()
        copies.append(copy)
    own.wait()
    for copy in copies:
        copy.wait()
    block = out_ref.at[pl.ds(first, group)]
    copies = []
    for j, peer in enumerate(far):
        copy = pltpu.make_async_remote_copy(
            src_ref=block,
            dst_ref=block,
            send_sem=far_send.at[j],
            recv_sem=far_recv.at[j],
            device_id=peer,
            device_id_type=MESH,
        )
        copy.start()
        copies.append(copy)
    for copy in copies:
        copy.wait()


def seq_gather2(block, group):
    n = lax.axis_size("seq")
    return pl.pallas_call(
        functools.partial(seq_gather2_kernel, group),
        out_shape=jax.ShapeDtypeStruct((n,) + block.shape, block.dtype),
        in_specs=[pl.BlockSpec(memory_space=pltpu.VMEM)],
        out_specs=pl.BlockSpec(memory_space=pltpu.VMEM),
        scratch_shapes=[
            pltpu.SemaphoreType.DMA(()),
            pltpu.SemaphoreType.DMA((group - 1,)),
            pltpu.SemaphoreType.DMA((group - 1,)),
            pltpu.SemaphoreType.DMA((n // group - 1,)),
            pltpu.SemaphoreType.DMA((n // group - 1,)),
        ],
        compiler_params=pltpu.CompilerParams(collective_id=8, has_side_effects=True),
    )(block)


def seq_merge2_kernel(
    group, top_lane, x_ref, out_ref, got_far, partial, got_near, far_send, far_recv, near_send, near_recv
):
    me, first, near, far = seq_two_level_peers(group)
    copies = []
    for j, peer in enumerate(far):
        start = pl.multiple_of((peer[0] // group) * group, group)
        copy = pltpu.make_async_remote_copy(
            src_ref=x_ref.at[pl.ds(start, group)],
            dst_ref=got_far.at[j],
            send_sem=far_send.at[j],
            recv_sem=far_recv.at[j],
            device_id=peer,
            device_id_type=MESH,
        )
        copy.start()
        copies.append(copy)
    for copy in copies:
        copy.wait()
    for k in range(group):
        value = x_ref[first + k]
        for j in range(len(far)):
            value = merge_parts(value, got_far[j, k], top_lane)
        partial[k] = value
    copies = []
    for j, peer in enumerate(near):
        copy = pltpu.make_async_remote_copy(
            src_ref=partial.at[peer[0] - first],
            dst_ref=got_near.at[j],
            send_sem=near_send.at[j],
            recv_sem=near_recv.at[j],
            device_id=peer,
            device_id_type=MESH,
        )
        copy.start()
        copies.append(copy)
    for copy in copies:
        copy.wait()
    value = partial[me - first]
    for j in range(len(near)):
        value = merge_parts(value, got_near[j], top_lane)
    out_ref[...] = value


def seq_merge2(parts, top_lane, group):
    n = parts.shape[0]
    blk = parts.shape[1:]
    return pl.pallas_call(
        functools.partial(seq_merge2_kernel, group, top_lane),
        out_shape=jax.ShapeDtypeStruct(blk, parts.dtype),
        in_specs=[pl.BlockSpec(memory_space=pltpu.VMEM)],
        out_specs=pl.BlockSpec(memory_space=pltpu.VMEM),
        scratch_shapes=[
            pltpu.VMEM((n // group - 1, group) + blk, parts.dtype),
            pltpu.VMEM((group,) + blk, parts.dtype),
            pltpu.VMEM((group - 1,) + blk, parts.dtype),
            pltpu.SemaphoreType.DMA((n // group - 1,)),
            pltpu.SemaphoreType.DMA((n // group - 1,)),
            pltpu.SemaphoreType.DMA((group - 1,)),
            pltpu.SemaphoreType.DMA((group - 1,)),
        ],
        compiler_params=pltpu.CompilerParams(collective_id=9, has_side_effects=True),
    )(parts)


def col_peers():
    me, m = lax.axis_index("col"), lax.axis_size("col")
    seq, row = lax.axis_index("seq"), lax.axis_index("row")
    peers = [lax.rem(me + j, m) for j in range(1, m)]
    barrier = pltpu.get_barrier_semaphore()
    for peer in peers:
        pl.semaphore_signal(barrier, inc=1, device_id=(seq, row, peer), device_id_type=MESH)
    pl.semaphore_wait(barrier, len(peers))
    return me, [(seq, row, peer) for peer in peers]


def col_gather_kernel(x_ref, out_ref, self_sem, send_sem, recv_sem):
    me, peers = col_peers()
    own = pltpu.make_async_copy(x_ref, out_ref.at[me], self_sem)
    own.start()
    copies = []
    for j, peer in enumerate(peers):
        copy = pltpu.make_async_remote_copy(
            src_ref=x_ref,
            dst_ref=out_ref.at[me],
            send_sem=send_sem.at[j],
            recv_sem=recv_sem.at[j],
            device_id=peer,
            device_id_type=MESH,
        )
        copy.start()
        copies.append(copy)
    own.wait()
    for copy in copies:
        copy.wait()


def col_gather(block):
    m = lax.axis_size("col")
    return pl.pallas_call(
        col_gather_kernel,
        out_shape=jax.ShapeDtypeStruct((m,) + block.shape, block.dtype),
        in_specs=[pl.BlockSpec(memory_space=pltpu.VMEM)],
        out_specs=pl.BlockSpec(memory_space=pltpu.VMEM),
        scratch_shapes=[
            pltpu.SemaphoreType.DMA(()),
            pltpu.SemaphoreType.DMA((m - 1,)),
            pltpu.SemaphoreType.DMA((m - 1,)),
        ],
        compiler_params=pltpu.CompilerParams(collective_id=2, has_side_effects=True),
    )(block)


def col_sum_kernel(x_ref, own_ref, out_ref, got, send_sem, recv_sem):
    me, peers = col_peers()
    copies = []
    for j, peer in enumerate(peers):
        copy = pltpu.make_async_remote_copy(
            src_ref=x_ref.at[peer[2]],
            dst_ref=got.at[j],
            send_sem=send_sem.at[j],
            recv_sem=recv_sem.at[j],
            device_id=peer,
            device_id_type=MESH,
        )
        copy.start()
        copies.append(copy)
    for copy in copies:
        copy.wait()
    chunk = 32

    def body(i, carry):
        rows = pl.ds(pl.multiple_of(i * chunk, chunk), chunk)
        total = own_ref[rows, :]
        for j in range(len(copies)):
            total = total + got[j, rows, :].astype(jnp.float32)
        out_ref[rows, :] = total
        return carry

    lax.fori_loop(0, out_ref.shape[0] // chunk, body, 0)


def col_reduce_scatter(parts, own, collective_id):
    m = lax.axis_size("col")
    return pl.pallas_call(
        col_sum_kernel,
        out_shape=jax.ShapeDtypeStruct(own.shape, jnp.float32),
        in_specs=[pl.BlockSpec(memory_space=pltpu.VMEM)] * 2,
        out_specs=pl.BlockSpec(memory_space=pltpu.VMEM),
        scratch_shapes=[
            pltpu.VMEM((m - 1,) + parts.shape[1:], parts.dtype),
            pltpu.SemaphoreType.DMA((m - 1,)),
            pltpu.SemaphoreType.DMA((m - 1,)),
        ],
        compiler_params=pltpu.CompilerParams(collective_id=collective_id, has_side_effects=True),
    )(parts, own)


def col_mid_kernel(x_ref, own_ref, gain_ref, bias_ref, out_ref, got, rs_send, rs_recv, g_send, g_recv):
    me, peers = col_peers()
    copies = []
    for j, peer in enumerate(peers):
        copy = pltpu.make_async_remote_copy(
            src_ref=x_ref.at[peer[2]],
            dst_ref=got.at[j],
            send_sem=rs_send.at[j],
            recv_sem=rs_recv.at[j],
            device_id=peer,
            device_id_type=MESH,
        )
        copy.start()
        copies.append(copy)
    for copy in copies:
        copy.wait()
    chunk = 32
    width = out_ref.shape[2]

    def body(i, carry):
        rows = pl.ds(pl.multiple_of(i * chunk, chunk), chunk)
        total = own_ref[rows, :]
        for j in range(len(copies)):
            total = total + got[j, rows, :].astype(jnp.float32)
        center = total - jnp.sum(total, axis=1, keepdims=True) / width
        spread = jnp.sum(center * center, axis=1, keepdims=True) / width
        normed = center / jnp.sqrt(spread + 1e-05) * gain_ref[...] + bias_ref[...]
        out_ref[me, rows, :] = normed.astype(out_ref.dtype)
        return carry

    lax.fori_loop(0, out_ref.shape[1] // chunk, body, 0)
    sends = []
    for j, peer in enumerate(peers):
        copy = pltpu.make_async_remote_copy(
            src_ref=out_ref.at[me],
            dst_ref=out_ref.at[me],
            send_sem=g_send.at[j],
            recv_sem=g_recv.at[j],
            device_id=peer,
            device_id_type=MESH,
        )
        copy.start()
        sends.append(copy)
    for copy in sends:
        copy.wait()


def col_sum_norm_gather(parts, own, gain, bias):
    m = lax.axis_size("col")
    rows, width = own.shape
    return pl.pallas_call(
        col_mid_kernel,
        out_shape=jax.ShapeDtypeStruct((m, rows, width), jnp.bfloat16),
        in_specs=[pl.BlockSpec(memory_space=pltpu.VMEM)] * 4,
        out_specs=pl.BlockSpec(memory_space=pltpu.VMEM),
        scratch_shapes=[
            pltpu.VMEM((m - 1,) + parts.shape[1:], parts.dtype),
            pltpu.SemaphoreType.DMA((m - 1,)),
            pltpu.SemaphoreType.DMA((m - 1,)),
            pltpu.SemaphoreType.DMA((m - 1,)),
            pltpu.SemaphoreType.DMA((m - 1,)),
        ],
        compiler_params=pltpu.CompilerParams(collective_id=7, has_side_effects=True),
    )(parts, own, gain.reshape(1, width), bias.reshape(1, width))


def col_proj_kernel(x_ref, own_ref, w_ref, gain_ref, bias_ref, out_ref, got, rs_send, rs_recv, g_send, g_recv):
    me, peers = col_peers()
    m = len(peers) + 1
    heads_width = x_ref.shape[2]
    copies = []
    for j, peer in enumerate(peers):
        copy = pltpu.make_async_remote_copy(
            src_ref=x_ref.at[peer[2]],
            dst_ref=got.at[j],
            send_sem=rs_send.at[j],
            recv_sem=rs_recv.at[j],
            device_id=peer,
            device_id_type=MESH,
        )
        copy.start()
        copies.append(copy)
    for copy in copies:
        copy.wait()
    chunk = 32
    width = out_ref.shape[2]

    def body(i, carry):
        rows = pl.ds(pl.multiple_of(i * chunk, chunk), chunk)
        total = own_ref[rows, :]
        for j in range(len(copies)):
            source = lax.rem(me + m - 1 - j, m)
            weights = w_ref[pl.ds(pl.multiple_of(source * heads_width, heads_width), heads_width), :]
            total = total + jnp.dot(got[j, rows, :], weights, preferred_element_type=jnp.float32)
        center = total - jnp.sum(total, axis=1, keepdims=True) / width
        spread = jnp.sum(center * center, axis=1, keepdims=True) / width
        normed = center / jnp.sqrt(spread + 1e-05) * gain_ref[...] + bias_ref[...]
        out_ref[me, rows, :] = normed.astype(out_ref.dtype)
        return carry

    lax.fori_loop(0, out_ref.shape[1] // chunk, body, 0)
    sends = []
    for j, peer in enumerate(peers):
        copy = pltpu.make_async_remote_copy(
            src_ref=out_ref.at[me],
            dst_ref=out_ref.at[me],
            send_sem=g_send.at[j],
            recv_sem=g_recv.at[j],
            device_id=peer,
            device_id_type=MESH,
        )
        copy.start()
        sends.append(copy)
    for copy in sends:
        copy.wait()


def col_proj_norm_gather(attn_parts, own, w_full, gain, bias):
    m = lax.axis_size("col")
    rows, width = own.shape
    return pl.pallas_call(
        col_proj_kernel,
        out_shape=jax.ShapeDtypeStruct((m, rows, width), jnp.bfloat16),
        in_specs=[pl.BlockSpec(memory_space=pltpu.VMEM)] * 5,
        out_specs=pl.BlockSpec(memory_space=pltpu.VMEM),
        scratch_shapes=[
            pltpu.VMEM((m - 1,) + attn_parts.shape[1:], attn_parts.dtype),
            pltpu.SemaphoreType.DMA((m - 1,)),
            pltpu.SemaphoreType.DMA((m - 1,)),
            pltpu.SemaphoreType.DMA((m - 1,)),
            pltpu.SemaphoreType.DMA((m - 1,)),
        ],
        compiler_params=pltpu.CompilerParams(
            collective_id=10, has_side_effects=True, vmem_limit_bytes=48 * 1024 * 1024
        ),
    )(attn_parts, own, w_full, gain.reshape(1, width), bias.reshape(1, width))


def layer_norm(values, gain, bias):
    center = values - jnp.mean(values, axis=1, keepdims=True)
    spread = jnp.mean(center * center, axis=1, keepdims=True)
    return center * lax.rsqrt(spread + 1e-05) * gain + bias


def per_device(
    hidden_in,
    qkv_weight,
    qkv_global_weight,
    out_weight,
    ln_gain,
    ln_bias,
    ffn_in,
    ffn_out,
    ln2_gain,
    ln2_bias,
    segment_ids,
    global_pos,
    page_owner,
):
    neg = -1e30
    tokens = hidden_in[0]
    shard_len, width = tokens.shape
    heads_here = qkv_weight.shape[1]
    triple = qkv_weight.shape[2]
    head_dim = triple // 3
    n_seq = lax.axis_size("seq")
    n_row = lax.axis_size("row")
    n_col = lax.axis_size("col")
    seq_index = lax.axis_index("seq")
    col_index = lax.axis_index("col")
    base = seq_index * shard_len
    scale = 1.0 / math.sqrt(head_dim)

    all_pos = global_pos[0]
    n_glob = all_pos.shape[0]
    per_shard = n_glob // n_seq
    own_pos = lax.dynamic_slice_in_dim(all_pos, seq_index * per_shard, per_shard, 0)
    local_order = jnp.arange(shard_len, dtype=jnp.int32)
    own_match = (own_pos - base)[:, None] == local_order[None, :]
    picker = own_match.astype(jnp.bfloat16)
    own_rows = jnp.dot(picker, tokens, preferred_element_type=jnp.float32).astype(jnp.bfloat16)
    group = 4 if n_seq % 4 == 0 and n_seq > 4 else 1
    if group > 1:
        glob_rows = seq_gather2(own_rows.reshape(-1, 128), group).reshape(n_glob, width)
    else:
        glob_rows = seq_direct_gather(own_rows.reshape(-1, 128)).reshape(n_glob, width)

    w_global = lax.all_gather(
        qkv_global_weight.reshape(qkv_global_weight.shape[0], -1), "row", axis=0, tiled=True
    )
    f_in = lax.all_gather(ffn_in, "row", axis=0, tiled=True)
    f_out = lax.all_gather(ffn_out, "row", axis=1, tiled=True)
    w_out = lax.all_gather(out_weight, "col", axis=0, tiled=True)

    flat_weight = qkv_weight.reshape(width, heads_here * triple)
    qkv = jnp.dot(tokens, flat_weight, preferred_element_type=jnp.float32).astype(jnp.bfloat16)
    qkv_heads = qkv.reshape(shard_len, heads_here, triple)
    queries = qkv_heads[:, :, :head_dim]
    kv_local = qkv_heads[:, :, head_dim:]

    owners = page_owner[0, :, 0]
    n_pages = owners.shape[0]
    page_len = shard_len // n_pages
    capacity = max(2, n_pages // n_seq)
    page_order = jnp.arange(n_pages, dtype=jnp.int32)
    slot = jnp.sum(
        ((owners[:, None] == owners[None, :]) & (page_order[None, :] < page_order[:, None])).astype(
            jnp.int32
        ),
        axis=1,
    )
    target = owners * capacity + slot
    placing = (target[None, :] == jnp.arange(n_seq * capacity, dtype=jnp.int32)[:, None]).astype(
        jnp.bfloat16
    )
    outgoing = jnp.dot(
        placing,
        kv_local.reshape(n_pages, page_len * heads_here * 2 * head_dim),
        preferred_element_type=jnp.float32,
    ).astype(jnp.bfloat16)
    outgoing = outgoing.reshape(n_seq, capacity, page_len, heads_here, 2 * head_dim)
    arrived = lax.all_to_all(outgoing, "seq", split_axis=0, concat_axis=0, tiled=True)
    arrived, glob_rows = lax.optimization_barrier((arrived, glob_rows))
    page_pool = arrived[None, None]

    kv_ext = padded(kv_local, (("seq", 0),), HALF)

    glob_qkv = jnp.dot(glob_rows, flat_weight, preferred_element_type=jnp.float32).astype(
        jnp.bfloat16
    )
    glob_kv = glob_qkv.reshape(n_glob, heads_here, triple)[:, :, head_dim:]
    glob_k = glob_kv[:, :, :head_dim]
    glob_v = glob_kv[:, :, head_dim:]
    glob_q = (
        jnp.dot(glob_rows, w_global, preferred_element_type=jnp.float32)
        .astype(jnp.bfloat16)
        .reshape(n_glob, heads_here, triple)[:, :, :head_dim]
    )
    global_kv_local = (
        jnp.dot(tokens, w_global, preferred_element_type=jnp.float32)
        .astype(jnp.bfloat16)
        .reshape(shard_len, heads_here, triple)[:, :, head_dim:]
    )

    seg_all = segment_ids[0]
    glob_seg = jnp.take(seg_all, all_pos)
    seg_pad = jnp.pad(seg_all, (HALF, HALF), constant_values=-1)
    query_seg = lax.dynamic_slice_in_dim(seg_all, base, shard_len, 0)
    key_seg = lax.dynamic_slice_in_dim(seg_pad, base, shard_len + 2 * HALF, 0)
    key_pos = base - HALF + jnp.arange(shard_len + 2 * HALF, dtype=jnp.int32)
    key_flag = jnp.any(key_pos[:, None] == all_pos[None, :], axis=1)
    query_pos = base + local_order

    s_part = (
        jnp.einsum(
            "ghd,khd->hgk",
            glob_q,
            global_kv_local[:, :, :head_dim],
            preferred_element_type=jnp.float32,
        )
        * scale
    )
    part_mask = glob_seg[:, None] == query_seg[None, :]
    part_top = jnp.max(jnp.where(part_mask, s_part, neg), axis=2)
    e_part = jnp.where(part_mask, jnp.exp(s_part - part_top[:, :, None]), 0.0)
    part_total = jnp.sum(e_part, axis=2)
    part_acc = jnp.einsum(
        "hgk,khd->hgd",
        e_part,
        global_kv_local[:, :, head_dim:].astype(jnp.float32),
        precision=lax.Precision.HIGHEST,
    )
    packed = jnp.concatenate(
        [
            part_acc,
            part_total[:, :, None],
            jnp.broadcast_to(part_top[:, :, None], part_top.shape + (128 - head_dim - 1,)),
        ],
        axis=2,
    )
    packed = jnp.transpose(packed, (1, 0, 2)).reshape(n_glob * heads_here, 128)
    packed, w_out = lax.optimization_barrier((packed, w_out))
    if group > 1:
        merged = seq_merge2(packed.reshape(n_seq, -1, 128), head_dim + 1, group)
    else:
        merged = seq_direct_merge(packed.reshape(n_seq, -1, 128), head_dim + 1)
    merged = merged.reshape(
        per_shard, heads_here, 128
    )
    own_out = jnp.transpose(
        (merged[:, :, :head_dim] / merged[:, :, head_dim : head_dim + 1]).astype(jnp.bfloat16),
        (1, 0, 2),
    )

    glob_mask = query_seg[:, None] == glob_seg[None, :]
    k_blk = kv_ext[:, :, :head_dim]
    v_blk = kv_ext[:, :, head_dim:]
    s_win = jnp.einsum("qhd,khd->hqk", queries, k_blk, preferred_element_type=jnp.float32) * scale
    s_glob = jnp.einsum("qhd,ghd->hqg", queries, glob_k, preferred_element_type=jnp.float32) * scale
    m_win = (
        (jnp.abs(query_pos[:, None] - key_pos[None, :]) <= HALF)
        & (query_seg[:, None] == key_seg[None, :])
        & jnp.logical_not(key_flag[None, :])
    )
    top = jnp.maximum(
        jnp.max(jnp.where(m_win, s_win, neg), axis=2),
        jnp.max(jnp.where(glob_mask, s_glob, neg), axis=2),
    )
    e_win = jnp.where(m_win, jnp.exp(s_win - top[:, :, None]), 0.0)
    e_glob = jnp.where(glob_mask, jnp.exp(s_glob - top[:, :, None]), 0.0)
    total = jnp.sum(e_win, axis=2) + jnp.sum(e_glob, axis=2)
    numer = jnp.einsum(
        "hqk,khd->qhd", e_win.astype(jnp.bfloat16), v_blk, preferred_element_type=jnp.float32
    )
    numer = numer + jnp.einsum(
        "hqg,ghd->qhd", e_glob.astype(jnp.bfloat16), glob_v, preferred_element_type=jnp.float32
    )
    pieces = (numer / jnp.transpose(total)[:, :, None]).astype(jnp.bfloat16)

    placed = jnp.einsum("gt,hgd->thd", picker, own_out, preferred_element_type=jnp.float32).astype(
        jnp.bfloat16
    )
    is_own = jnp.any(own_match, axis=0)
    attention = jnp.where(is_own[:, None, None], placed, pieces).reshape(
        shard_len, heads_here * head_dim
    )


    out_rows = shard_len // n_col
    attn_own = lax.dynamic_slice_in_dim(attention, col_index * out_rows, out_rows, 0)
    token_own = lax.dynamic_slice_in_dim(tokens, col_index * out_rows, out_rows, 0)
    proj_own = jnp.dot(attn_own, out_weight, preferred_element_type=jnp.float32)
    middle_all = col_proj_norm_gather(
        attention.reshape(n_col, out_rows, heads_here * head_dim),
        token_own.astype(jnp.float32) + proj_own,
        w_out,
        ln_gain,
        ln_bias,
    )
    mine = middle_all[col_index]
    middle = middle_all.reshape(shard_len, width)
    ffn_pre = jnp.dot(middle, f_in, preferred_element_type=jnp.float32)
    ffn_hidden = jax.nn.gelu(ffn_pre, approximate=False).astype(jnp.bfloat16)
    ffn_full = jnp.dot(ffn_hidden, f_out, preferred_element_type=jnp.float32)
    ffn_own = lax.dynamic_slice_in_dim(ffn_full, col_index * out_rows, out_rows, 0)
    second = col_reduce_scatter(
        ffn_full.astype(jnp.bfloat16).reshape(n_col, out_rows, width),
        mine.astype(jnp.float32) + ffn_own,
        6,
    )
    normed = layer_norm(second, ln2_gain, ln2_bias)
    return (normed.astype(jnp.bfloat16)[None], page_pool)


def solution(mesh):
    in_specs = (
        P("row", "seq", None),
        P(None, "col", None),
        P("row", "col", None),
        P("col", None),
        P(),
        P(),
        P("row", "col"),
        P("col", "row"),
        P(),
        P(),
        P("row", None),
        P("row", None),
        P("row", "seq", None),
    )
    out_specs = (P("row", ("seq", "col"), None), P("row", "seq", None, None, None, "col", None))
    return jax.shard_map(
        per_device, mesh=mesh, in_specs=in_specs, out_specs=out_specs, check_vma=False
    )
```

```python
import functools
import math

import jax
import jax.numpy as jnp
from jax import lax
from jax.experimental import pallas as pl
from jax.experimental.pallas import tpu as pltpu
from jax.sharding import PartitionSpec as P

MESH = pl.DeviceIdType.MESH

HALF = 256


def padded(block, sides, width):
    for axis, dim in sides:
        count = lax.axis_size(axis)
        forward = [(i, i + 1) for i in range(count - 1)]
        backward = [(target, source) for source, target in forward]
        low = lax.ppermute(
            lax.slice_in_dim(block, block.shape[dim] - width, None, axis=dim), axis, forward
        )
        high = lax.ppermute(lax.slice_in_dim(block, 0, width, axis=dim), axis, backward)
        block = jnp.concatenate([low, block, high], axis=dim)
    return block


def butterfly_partners(n):
    me = lax.axis_index("seq")
    partners = []
    step = 1
    while step < n:
        bit = (me // step) % 2
        partners.append(me + step - 2 * step * bit)
        step *= 2
    return me, partners


def enter(partners):
    row, col = lax.axis_index("row"), lax.axis_index("col")
    barrier = pltpu.get_barrier_semaphore()
    for partner in partners:
        pl.semaphore_signal(barrier, inc=1, device_id=(partner, row, col), device_id_type=MESH)
    pl.semaphore_wait(barrier, len(partners))
    return row, col


def gather_kernel(n, x_ref, out_ref, self_sem, send_sem, recv_sem):
    me, partners = butterfly_partners(n)
    row, col = enter(partners)
    own = pltpu.make_async_copy(x_ref, out_ref.at[me], self_sem)
    own.start()
    own.wait()
    size = 1
    for k, partner in enumerate(partners):
        start = (me // size) * size
        copy = pltpu.make_async_remote_copy(
            src_ref=out_ref.at[pl.ds(start, size)],
            dst_ref=out_ref.at[pl.ds(start, size)],
            send_sem=send_sem.at[k],
            recv_sem=recv_sem.at[k],
            device_id=(partner, row, col),
            device_id_type=MESH,
        )
        copy.start()
        copy.wait()
        size *= 2


def seq_gather(block):
    n = lax.axis_size("seq")
    rounds = n.bit_length() - 1
    return pl.pallas_call(
        functools.partial(gather_kernel, n),
        out_shape=jax.ShapeDtypeStruct((n,) + block.shape, block.dtype),
        in_specs=[pl.BlockSpec(memory_space=pltpu.VMEM)],
        out_specs=pl.BlockSpec(memory_space=pltpu.VMEM),
        scratch_shapes=[
            pltpu.SemaphoreType.DMA(()),
            pltpu.SemaphoreType.DMA((rounds,)),
            pltpu.SemaphoreType.DMA((rounds,)),
        ],
        compiler_params=pltpu.CompilerParams(collective_id=0, has_side_effects=True),
    )(block)


def merge_parts(mine, theirs, top_lane):
    lane = lax.broadcasted_iota(jnp.int32, mine.shape, 1)
    is_top = lane == top_lane
    top_a = jnp.max(jnp.where(is_top, mine, -jnp.inf), axis=1, keepdims=True)
    top_b = jnp.max(jnp.where(is_top, theirs, -jnp.inf), axis=1, keepdims=True)
    top = jnp.maximum(top_a, top_b)
    merged = mine * jnp.exp(top_a - top) + theirs * jnp.exp(top_b - top)
    return jnp.where(is_top, top, merged)


def halving_kernel(n, top_lane, x_ref, out_ref, *scratch):
    rounds = len(scratch) // 3
    kept, got, sems = scratch[:rounds], scratch[rounds : 2 * rounds], scratch[2 * rounds :]
    me = lax.axis_index("seq")
    steps = []
    step = n // 2
    while step >= 1:
        bit = (me // step) % 2
        steps.append((me + step - 2 * step * bit, bit))
        step //= 2
    row, col = enter([partner for partner, _ in steps])
    source = x_ref
    for k, (partner, bit) in enumerate(steps):
        half = source.shape[0] // 2
        send_at = pl.multiple_of((1 - bit) * half, 8)
        keep_at = pl.multiple_of(bit * half, 8)
        copy = pltpu.make_async_remote_copy(
            src_ref=source.at[pl.ds(send_at, half)],
            dst_ref=got[k],
            send_sem=sems[k].at[0],
            recv_sem=sems[k].at[1],
            device_id=(partner, row, col),
            device_id_type=MESH,
        )
        copy.start()
        copy.wait()
        value = merge_parts(source[pl.ds(keep_at, half)], got[k][...], top_lane)
        if k + 1 < rounds:
            kept[k][...] = value
            source = kept[k]
        else:
            out_ref[...] = value


def seq_softmax_combine(parts, top_lane):
    n = lax.axis_size("seq")
    rounds = n.bit_length() - 1
    rows, lanes = parts.shape
    scratch = []
    for k in range(rounds):
        scratch.append(pltpu.VMEM((rows >> (k + 1), lanes), parts.dtype))
    for k in range(rounds):
        scratch.append(pltpu.VMEM((rows >> (k + 1), lanes), parts.dtype))
    for k in range(rounds):
        scratch.append(pltpu.SemaphoreType.DMA((2,)))
    return pl.pallas_call(
        functools.partial(halving_kernel, n, top_lane),
        out_shape=jax.ShapeDtypeStruct((rows // n, lanes), parts.dtype),
        in_specs=[pl.BlockSpec(memory_space=pltpu.VMEM)],
        out_specs=pl.BlockSpec(memory_space=pltpu.VMEM),
        scratch_shapes=scratch,
        compiler_params=pltpu.CompilerParams(collective_id=1, has_side_effects=True),
    )(parts)


def seq_peers():
    me, n = lax.axis_index("seq"), lax.axis_size("seq")
    row, col = lax.axis_index("row"), lax.axis_index("col")
    peers = [lax.rem(me + j, n) for j in range(1, n)]
    barrier = pltpu.get_barrier_semaphore()
    for peer in peers:
        pl.semaphore_signal(barrier, inc=1, device_id=(peer, row, col), device_id_type=MESH)
    pl.semaphore_wait(barrier, len(peers))
    return me, [(peer, row, col) for peer in peers]


def seq_direct_gather_kernel(x_ref, out_ref, self_sem, send_sem, recv_sem):
    me, peers = seq_peers()
    own = pltpu.make_async_copy(x_ref, out_ref.at[me], self_sem)
    own.start()
    copies = []
    for j, peer in enumerate(peers):
        copy = pltpu.make_async_remote_copy(
            src_ref=x_ref,
            dst_ref=out_ref.at[me],
            send_sem=send_sem.at[j],
            recv_sem=recv_sem.at[j],
            device_id=peer,
            device_id_type=MESH,
        )
        copy.start()
        copies.append(copy)
    own.wait()
    for copy in copies:
        copy.wait()


def seq_direct_gather(block):
    n = lax.axis_size("seq")
    return pl.pallas_call(
        seq_direct_gather_kernel,
        out_shape=jax.ShapeDtypeStruct((n,) + block.shape, block.dtype),
        in_specs=[pl.BlockSpec(memory_space=pltpu.VMEM)],
        out_specs=pl.BlockSpec(memory_space=pltpu.VMEM),
        scratch_shapes=[
            pltpu.SemaphoreType.DMA(()),
            pltpu.SemaphoreType.DMA((n - 1,)),
            pltpu.SemaphoreType.DMA((n - 1,)),
        ],
        compiler_params=pltpu.CompilerParams(collective_id=4, has_side_effects=True),
    )(block)


def seq_merge_kernel(top_lane, x_ref, out_ref, got, send_sem, recv_sem):
    me, peers = seq_peers()
    copies = []
    for j, peer in enumerate(peers):
        copy = pltpu.make_async_remote_copy(
            src_ref=x_ref.at[peer[0]],
            dst_ref=got.at[j],
            send_sem=send_sem.at[j],
            recv_sem=recv_sem.at[j],
            device_id=peer,
            device_id_type=MESH,
        )
        copy.start()
        copies.append(copy)
    for copy in copies:
        copy.wait()
    value = x_ref[me]
    for j in range(len(copies)):
        value = merge_parts(value, got[j], top_lane)
    out_ref[...] = value


def seq_direct_merge(parts, top_lane):
    n = parts.shape[0]
    return pl.pallas_call(
        functools.partial(seq_merge_kernel, top_lane),
        out_shape=jax.ShapeDtypeStruct(parts.shape[1:], parts.dtype),
        in_specs=[pl.BlockSpec(memory_space=pltpu.VMEM)],
        out_specs=pl.BlockSpec(memory_space=pltpu.VMEM),
        scratch_shapes=[
            pltpu.VMEM((n - 1,) + parts.shape[1:], parts.dtype),
            pltpu.SemaphoreType.DMA((n - 1,)),
            pltpu.SemaphoreType.DMA((n - 1,)),
        ],
        compiler_params=pltpu.CompilerParams(collective_id=5, has_side_effects=True),
    )(parts)


def seq_two_level_peers(group):
    me, n = lax.axis_index("seq"), lax.axis_size("seq")
    row, col = lax.axis_index("row"), lax.axis_index("col")
    first = (me // group) * group
    near = [first + lax.rem(me - first + j, group) for j in range(1, group)]
    far = [lax.rem(me + group * j, n) for j in range(1, n // group)]
    barrier = pltpu.get_barrier_semaphore()
    for peer in near + far:
        pl.semaphore_signal(barrier, inc=1, device_id=(peer, row, col), device_id_type=MESH)
    pl.semaphore_wait(barrier, len(near) + len(far))
    return me, first, [(p, row, col) for p in near], [(p, row, col) for p in far]


def seq_gather2_kernel(group, x_ref, out_ref, self_sem, near_send, near_recv, far_send, far_recv):
    me, first, near, far = seq_two_level_peers(group)
    own = pltpu.make_async_copy(x_ref, out_ref.at[me], self_sem)
    own.start()
    copies = []
    for j, peer in enumerate(near):
        copy = pltpu.make_async_remote_copy(
            src_ref=x_ref,
            dst_ref=out_ref.at[me],
            send_sem=near_send.at[j],
            recv_sem=near_recv.at[j],
            device_id=peer,
            device_id_type=MESH,
        )
        copy.start()
        copies.append(copy)
    own.wait()
    for copy in copies:
        copy.wait()
    block = out_ref.at[pl.ds(first, group)]
    copies = []
    for j, peer in enumerate(far):
        copy = pltpu.make_async_remote_copy(
            src_ref=block,
            dst_ref=block,
            send_sem=far_send.at[j],
            recv_sem=far_recv.at[j],
            device_id=peer,
            device_id_type=MESH,
        )
        copy.start()
        copies.append(copy)
    for copy in copies:
        copy.wait()


def seq_gather2(block, group):
    n = lax.axis_size("seq")
    return pl.pallas_call(
        functools.partial(seq_gather2_kernel, group),
        out_shape=jax.ShapeDtypeStruct((n,) + block.shape, block.dtype),
        in_specs=[pl.BlockSpec(memory_space=pltpu.VMEM)],
        out_specs=pl.BlockSpec(memory_space=pltpu.VMEM),
        scratch_shapes=[
            pltpu.SemaphoreType.DMA(()),
            pltpu.SemaphoreType.DMA((group - 1,)),
            pltpu.SemaphoreType.DMA((group - 1,)),
            pltpu.SemaphoreType.DMA((n // group - 1,)),
            pltpu.SemaphoreType.DMA((n // group - 1,)),
        ],
        compiler_params=pltpu.CompilerParams(collective_id=8, has_side_effects=True),
    )(block)


def seq_merge2_kernel(
    group, top_lane, x_ref, out_ref, got_far, partial, got_near, far_send, far_recv, near_send, near_recv
):
    me, first, near, far = seq_two_level_peers(group)
    copies = []
    for j, peer in enumerate(far):
        start = pl.multiple_of((peer[0] // group) * group, group)
        copy = pltpu.make_async_remote_copy(
            src_ref=x_ref.at[pl.ds(start, group)],
            dst_ref=got_far.at[j],
            send_sem=far_send.at[j],
            recv_sem=far_recv.at[j],
            device_id=peer,
            device_id_type=MESH,
        )
        copy.start()
        copies.append(copy)
    for copy in copies:
        copy.wait()
    for k in range(group):
        value = x_ref[first + k]
        for j in range(len(far)):
            value = merge_parts(value, got_far[j, k], top_lane)
        partial[k] = value
    copies = []
    for j, peer in enumerate(near):
        copy = pltpu.make_async_remote_copy(
            src_ref=partial.at[peer[0] - first],
            dst_ref=got_near.at[j],
            send_sem=near_send.at[j],
            recv_sem=near_recv.at[j],
            device_id=peer,
            device_id_type=MESH,
        )
        copy.start()
        copies.append(copy)
    for copy in copies:
        copy.wait()
    value = partial[me - first]
    for j in range(len(near)):
        value = merge_parts(value, got_near[j], top_lane)
    out_ref[...] = value


def seq_merge2(parts, top_lane, group):
    n = parts.shape[0]
    blk = parts.shape[1:]
    return pl.pallas_call(
        functools.partial(seq_merge2_kernel, group, top_lane),
        out_shape=jax.ShapeDtypeStruct(blk, parts.dtype),
        in_specs=[pl.BlockSpec(memory_space=pltpu.VMEM)],
        out_specs=pl.BlockSpec(memory_space=pltpu.VMEM),
        scratch_shapes=[
            pltpu.VMEM((n // group - 1, group) + blk, parts.dtype),
            pltpu.VMEM((group,) + blk, parts.dtype),
            pltpu.VMEM((group - 1,) + blk, parts.dtype),
            pltpu.SemaphoreType.DMA((n // group - 1,)),
            pltpu.SemaphoreType.DMA((n // group - 1,)),
            pltpu.SemaphoreType.DMA((group - 1,)),
            pltpu.SemaphoreType.DMA((group - 1,)),
        ],
        compiler_params=pltpu.CompilerParams(collective_id=9, has_side_effects=True),
    )(parts)


def col_peers():
    me, m = lax.axis_index("col"), lax.axis_size("col")
    seq, row = lax.axis_index("seq"), lax.axis_index("row")
    peers = [lax.rem(me + j, m) for j in range(1, m)]
    barrier = pltpu.get_barrier_semaphore()
    for peer in peers:
        pl.semaphore_signal(barrier, inc=1, device_id=(seq, row, peer), device_id_type=MESH)
    pl.semaphore_wait(barrier, len(peers))
    return me, [(seq, row, peer) for peer in peers]


def col_gather_kernel(x_ref, out_ref, self_sem, send_sem, recv_sem):
    me, peers = col_peers()
    own = pltpu.make_async_copy(x_ref, out_ref.at[me], self_sem)
    own.start()
    copies = []
    for j, peer in enumerate(peers):
        copy = pltpu.make_async_remote_copy(
            src_ref=x_ref,
            dst_ref=out_ref.at[me],
            send_sem=send_sem.at[j],
            recv_sem=recv_sem.at[j],
            device_id=peer,
            device_id_type=MESH,
        )
        copy.start()
        copies.append(copy)
    own.wait()
    for copy in copies:
        copy.wait()


def col_gather(block):
    m = lax.axis_size("col")
    return pl.pallas_call(
        col_gather_kernel,
        out_shape=jax.ShapeDtypeStruct((m,) + block.shape, block.dtype),
        in_specs=[pl.BlockSpec(memory_space=pltpu.VMEM)],
        out_specs=pl.BlockSpec(memory_space=pltpu.VMEM),
        scratch_shapes=[
            pltpu.SemaphoreType.DMA(()),
            pltpu.SemaphoreType.DMA((m - 1,)),
            pltpu.SemaphoreType.DMA((m - 1,)),
        ],
        compiler_params=pltpu.CompilerParams(collective_id=2, has_side_effects=True),
    )(block)


def col_sum_kernel(x_ref, own_ref, out_ref, got, send_sem, recv_sem):
    me, peers = col_peers()
    copies = []
    for j, peer in enumerate(peers):
        copy = pltpu.make_async_remote_copy(
            src_ref=x_ref.at[peer[2]],
            dst_ref=got.at[j],
            send_sem=send_sem.at[j],
            recv_sem=recv_sem.at[j],
            device_id=peer,
            device_id_type=MESH,
        )
        copy.start()
        copies.append(copy)
    for copy in copies:
        copy.wait()
    chunk = 32

    def body(i, carry):
        rows = pl.ds(pl.multiple_of(i * chunk, chunk), chunk)
        total = own_ref[rows, :]
        for j in range(len(copies)):
            total = total + got[j, rows, :].astype(jnp.float32)
        out_ref[rows, :] = total
        return carry

    lax.fori_loop(0, out_ref.shape[0] // chunk, body, 0)


def col_reduce_scatter(parts, own, collective_id):
    m = lax.axis_size("col")
    return pl.pallas_call(
        col_sum_kernel,
        out_shape=jax.ShapeDtypeStruct(own.shape, jnp.float32),
        in_specs=[pl.BlockSpec(memory_space=pltpu.VMEM)] * 2,
        out_specs=pl.BlockSpec(memory_space=pltpu.VMEM),
        scratch_shapes=[
            pltpu.VMEM((m - 1,) + parts.shape[1:], parts.dtype),
            pltpu.SemaphoreType.DMA((m - 1,)),
            pltpu.SemaphoreType.DMA((m - 1,)),
        ],
        compiler_params=pltpu.CompilerParams(collective_id=collective_id, has_side_effects=True),
    )(parts, own)


def col_mid_kernel(x_ref, own_ref, gain_ref, bias_ref, out_ref, got, rs_send, rs_recv, g_send, g_recv):
    me, peers = col_peers()
    copies = []
    for j, peer in enumerate(peers):
        copy = pltpu.make_async_remote_copy(
            src_ref=x_ref.at[peer[2]],
            dst_ref=got.at[j],
            send_sem=rs_send.at[j],
            recv_sem=rs_recv.at[j],
            device_id=peer,
            device_id_type=MESH,
        )
        copy.start()
        copies.append(copy)
    for copy in copies:
        copy.wait()
    chunk = 32
    width = out_ref.shape[2]

    def body(i, carry):
        rows = pl.ds(pl.multiple_of(i * chunk, chunk), chunk)
        total = own_ref[rows, :]
        for j in range(len(copies)):
            total = total + got[j, rows, :].astype(jnp.float32)
        center = total - jnp.sum(total, axis=1, keepdims=True) / width
        spread = jnp.sum(center * center, axis=1, keepdims=True) / width
        normed = center / jnp.sqrt(spread + 1e-05) * gain_ref[...] + bias_ref[...]
        out_ref[me, rows, :] = normed.astype(out_ref.dtype)
        return carry

    lax.fori_loop(0, out_ref.shape[1] // chunk, body, 0)
    sends = []
    for j, peer in enumerate(peers):
        copy = pltpu.make_async_remote_copy(
            src_ref=out_ref.at[me],
            dst_ref=out_ref.at[me],
            send_sem=g_send.at[j],
            recv_sem=g_recv.at[j],
            device_id=peer,
            device_id_type=MESH,
        )
        copy.start()
        sends.append(copy)
    for copy in sends:
        copy.wait()


def col_sum_norm_gather(parts, own, gain, bias):
    m = lax.axis_size("col")
    rows, width = own.shape
    return pl.pallas_call(
        col_mid_kernel,
        out_shape=jax.ShapeDtypeStruct((m, rows, width), jnp.bfloat16),
        in_specs=[pl.BlockSpec(memory_space=pltpu.VMEM)] * 4,
        out_specs=pl.BlockSpec(memory_space=pltpu.VMEM),
        scratch_shapes=[
            pltpu.VMEM((m - 1,) + parts.shape[1:], parts.dtype),
            pltpu.SemaphoreType.DMA((m - 1,)),
            pltpu.SemaphoreType.DMA((m - 1,)),
            pltpu.SemaphoreType.DMA((m - 1,)),
            pltpu.SemaphoreType.DMA((m - 1,)),
        ],
        compiler_params=pltpu.CompilerParams(collective_id=7, has_side_effects=True),
    )(parts, own, gain.reshape(1, width), bias.reshape(1, width))


def col_proj_kernel(x_ref, own_ref, w_ref, gain_ref, bias_ref, out_ref, got, rs_send, rs_recv, g_send, g_recv):
    me, peers = col_peers()
    m = len(peers) + 1
    heads_width = x_ref.shape[2]
    copies = []
    for j, peer in enumerate(peers):
        copy = pltpu.make_async_remote_copy(
            src_ref=x_ref.at[peer[2]],
            dst_ref=got.at[j],
            send_sem=rs_send.at[j],
            recv_sem=rs_recv.at[j],
            device_id=peer,
            device_id_type=MESH,
        )
        copy.start()
        copies.append(copy)
    for copy in copies:
        copy.wait()
    chunk = 32
    width = out_ref.shape[2]

    def body(i, carry):
        rows = pl.ds(pl.multiple_of(i * chunk, chunk), chunk)
        total = own_ref[rows, :]
        for j in range(len(copies)):
            source = lax.rem(me + m - 1 - j, m)
            weights = w_ref[pl.ds(pl.multiple_of(source * heads_width, heads_width), heads_width), :]
            total = total + jnp.dot(got[j, rows, :], weights, preferred_element_type=jnp.float32)
        center = total - jnp.sum(total, axis=1, keepdims=True) / width
        spread = jnp.sum(center * center, axis=1, keepdims=True) / width
        normed = center / jnp.sqrt(spread + 1e-05) * gain_ref[...] + bias_ref[...]
        out_ref[me, rows, :] = normed.astype(out_ref.dtype)
        return carry

    lax.fori_loop(0, out_ref.shape[1] // chunk, body, 0)
    sends = []
    for j, peer in enumerate(peers):
        copy = pltpu.make_async_remote_copy(
            src_ref=out_ref.at[me],
            dst_ref=out_ref.at[me],
            send_sem=g_send.at[j],
            recv_sem=g_recv.at[j],
            device_id=peer,
            device_id_type=MESH,
        )
        copy.start()
        sends.append(copy)
    for copy in sends:
        copy.wait()


def col_proj_norm_gather(attn_parts, own, w_full, gain, bias):
    m = lax.axis_size("col")
    rows, width = own.shape
    return pl.pallas_call(
        col_proj_kernel,
        out_shape=jax.ShapeDtypeStruct((m, rows, width), jnp.bfloat16),
        in_specs=[pl.BlockSpec(memory_space=pltpu.VMEM)] * 5,
        out_specs=pl.BlockSpec(memory_space=pltpu.VMEM),
        scratch_shapes=[
            pltpu.VMEM((m - 1,) + attn_parts.shape[1:], attn_parts.dtype),
            pltpu.SemaphoreType.DMA((m - 1,)),
            pltpu.SemaphoreType.DMA((m - 1,)),
            pltpu.SemaphoreType.DMA((m - 1,)),
            pltpu.SemaphoreType.DMA((m - 1,)),
        ],
        compiler_params=pltpu.CompilerParams(
            collective_id=10, has_side_effects=True, vmem_limit_bytes=48 * 1024 * 1024
        ),
    )(attn_parts, own, w_full, gain.reshape(1, width), bias.reshape(1, width))


def layer_norm(values, gain, bias):
    center = values - jnp.mean(values, axis=1, keepdims=True)
    spread = jnp.mean(center * center, axis=1, keepdims=True)
    return center * lax.rsqrt(spread + 1e-05) * gain + bias


def per_device(
    hidden_in,
    qkv_weight,
    qkv_global_weight,
    out_weight,
    ln_gain,
    ln_bias,
    ffn_in,
    ffn_out,
    ln2_gain,
    ln2_bias,
    segment_ids,
    global_pos,
    page_owner,
):
    neg = -1e30
    tokens = hidden_in[0]
    shard_len, width = tokens.shape
    heads_here = qkv_weight.shape[1]
    triple = qkv_weight.shape[2]
    head_dim = triple // 3
    n_seq = lax.axis_size("seq")
    n_row = lax.axis_size("row")
    n_col = lax.axis_size("col")
    seq_index = lax.axis_index("seq")
    col_index = lax.axis_index("col")
    base = seq_index * shard_len
    scale = 1.0 / math.sqrt(head_dim)

    all_pos = global_pos[0]
    n_glob = all_pos.shape[0]
    per_shard = n_glob // n_seq
    own_pos = lax.dynamic_slice_in_dim(all_pos, seq_index * per_shard, per_shard, 0)
    local_order = jnp.arange(shard_len, dtype=jnp.int32)
    own_match = (own_pos - base)[:, None] == local_order[None, :]
    picker = own_match.astype(jnp.bfloat16)
    own_rows = jnp.dot(picker, tokens, preferred_element_type=jnp.float32).astype(jnp.bfloat16)
    group = 4 if n_seq % 4 == 0 and n_seq > 4 else 1
    if group > 1:
        glob_rows = seq_gather2(own_rows.reshape(-1, 128), group).reshape(n_glob, width)
    else:
        glob_rows = seq_direct_gather(own_rows.reshape(-1, 128)).reshape(n_glob, width)

    wg_cols = qkv_global_weight.shape[1] * qkv_global_weight.shape[2]
    wg_fin = lax.all_gather(
        jnp.concatenate(
            [qkv_global_weight.reshape(qkv_global_weight.shape[0], wg_cols), ffn_in], axis=1
        ),
        "row",
        axis=0,
        tiled=True,
    )
    w_global = wg_fin[:, :wg_cols]
    f_in = wg_fin[:, wg_cols:]
    f_out = lax.all_gather(ffn_out, "row", axis=1, tiled=True)
    w_out = lax.all_gather(out_weight, "col", axis=0, tiled=True)

    flat_weight = qkv_weight.reshape(width, heads_here * triple)
    qkv = jnp.dot(tokens, flat_weight, preferred_element_type=jnp.float32).astype(jnp.bfloat16)
    qkv_heads = qkv.reshape(shard_len, heads_here, triple)
    queries = qkv_heads[:, :, :head_dim]
    kv_local = qkv_heads[:, :, head_dim:]

    owners = page_owner[0, :, 0]
    n_pages = owners.shape[0]
    page_len = shard_len // n_pages
    capacity = max(2, n_pages // n_seq)
    page_order = jnp.arange(n_pages, dtype=jnp.int32)
    slot = jnp.sum(
        ((owners[:, None] == owners[None, :]) & (page_order[None, :] < page_order[:, None])).astype(
            jnp.int32
        ),
        axis=1,
    )
    target = owners * capacity + slot
    placing = (target[None, :] == jnp.arange(n_seq * capacity, dtype=jnp.int32)[:, None]).astype(
        jnp.bfloat16
    )
    outgoing = jnp.dot(
        placing,
        kv_local.reshape(n_pages, page_len * heads_here * 2 * head_dim),
        preferred_element_type=jnp.float32,
    ).astype(jnp.bfloat16)
    outgoing = outgoing.reshape(n_seq, capacity, page_len, heads_here, 2 * head_dim)
    arrived = lax.all_to_all(outgoing, "seq", split_axis=0, concat_axis=0, tiled=True)
    arrived, glob_rows = lax.optimization_barrier((arrived, glob_rows))
    page_pool = arrived[None, None]

    kv_ext = padded(kv_local, (("seq", 0),), HALF)

    glob_qkv = jnp.dot(glob_rows, flat_weight, preferred_element_type=jnp.float32).astype(
        jnp.bfloat16
    )
    glob_kv = glob_qkv.reshape(n_glob, heads_here, triple)[:, :, head_dim:]
    glob_k = glob_kv[:, :, :head_dim]
    glob_v = glob_kv[:, :, head_dim:]
    glob_q = (
        jnp.dot(glob_rows, w_global, preferred_element_type=jnp.float32)
        .astype(jnp.bfloat16)
        .reshape(n_glob, heads_here, triple)[:, :, :head_dim]
    )
    global_kv_local = (
        jnp.dot(tokens, w_global, preferred_element_type=jnp.float32)
        .astype(jnp.bfloat16)
        .reshape(shard_len, heads_here, triple)[:, :, head_dim:]
    )

    seg_all = segment_ids[0]
    glob_seg = jnp.take(seg_all, all_pos)
    seg_pad = jnp.pad(seg_all, (HALF, HALF), constant_values=-1)
    query_seg = lax.dynamic_slice_in_dim(seg_all, base, shard_len, 0)
    key_seg = lax.dynamic_slice_in_dim(seg_pad, base, shard_len + 2 * HALF, 0)
    key_pos = base - HALF + jnp.arange(shard_len + 2 * HALF, dtype=jnp.int32)
    key_flag = jnp.any(key_pos[:, None] == all_pos[None, :], axis=1)
    query_pos = base + local_order

    s_part = (
        jnp.einsum(
            "ghd,khd->hgk",
            glob_q,
            global_kv_local[:, :, :head_dim],
            preferred_element_type=jnp.float32,
        )
        * scale
    )
    part_mask = glob_seg[:, None] == query_seg[None, :]
    part_top = jnp.max(jnp.where(part_mask, s_part, neg), axis=2)
    e_part = jnp.where(part_mask, jnp.exp(s_part - part_top[:, :, None]), 0.0)
    part_total = jnp.sum(e_part, axis=2)
    part_acc = jnp.einsum(
        "hgk,khd->hgd",
        e_part,
        global_kv_local[:, :, head_dim:].astype(jnp.float32),
        precision=lax.Precision.HIGHEST,
    )
    packed = jnp.concatenate(
        [
            part_acc,
            part_total[:, :, None],
            jnp.broadcast_to(part_top[:, :, None], part_top.shape + (128 - head_dim - 1,)),
        ],
        axis=2,
    )
    packed = jnp.transpose(packed, (1, 0, 2)).reshape(n_glob * heads_here, 128)
    if group > 1:
        merged = seq_merge2(packed.reshape(n_seq, -1, 128), head_dim + 1, group)
    else:
        merged = seq_direct_merge(packed.reshape(n_seq, -1, 128), head_dim + 1)
    merged = merged.reshape(
        per_shard, heads_here, 128
    )
    own_out = jnp.transpose(
        (merged[:, :, :head_dim] / merged[:, :, head_dim : head_dim + 1]).astype(jnp.bfloat16),
        (1, 0, 2),
    )

    glob_mask = query_seg[:, None] == glob_seg[None, :]
    k_blk = kv_ext[:, :, :head_dim]
    v_blk = kv_ext[:, :, head_dim:]
    s_win = jnp.einsum("qhd,khd->hqk", queries, k_blk, preferred_element_type=jnp.float32) * scale
    s_glob = jnp.einsum("qhd,ghd->hqg", queries, glob_k, preferred_element_type=jnp.float32) * scale
    m_win = (
        (jnp.abs(query_pos[:, None] - key_pos[None, :]) <= HALF)
        & (query_seg[:, None] == key_seg[None, :])
        & jnp.logical_not(key_flag[None, :])
    )
    top = jnp.maximum(
        jnp.max(jnp.where(m_win, s_win, neg), axis=2),
        jnp.max(jnp.where(glob_mask, s_glob, neg), axis=2),
    )
    e_win = jnp.where(m_win, jnp.exp(s_win - top[:, :, None]), 0.0)
    e_glob = jnp.where(glob_mask, jnp.exp(s_glob - top[:, :, None]), 0.0)
    total = jnp.sum(e_win, axis=2) + jnp.sum(e_glob, axis=2)
    numer = jnp.einsum(
        "hqk,khd->qhd", e_win.astype(jnp.bfloat16), v_blk, preferred_element_type=jnp.float32
    )
    numer = numer + jnp.einsum(
        "hqg,ghd->qhd", e_glob.astype(jnp.bfloat16), glob_v, preferred_element_type=jnp.float32
    )
    pieces = (numer / jnp.transpose(total)[:, :, None]).astype(jnp.bfloat16)

    placed = jnp.einsum("gt,hgd->thd", picker, own_out, preferred_element_type=jnp.float32).astype(
        jnp.bfloat16
    )
    is_own = jnp.any(own_match, axis=0)
    attention = jnp.where(is_own[:, None, None], placed, pieces).reshape(
        shard_len, heads_here * head_dim
    )


    out_rows = shard_len // n_col
    attention, w_out = lax.optimization_barrier((attention, w_out))
    attn_own = lax.dynamic_slice_in_dim(attention, col_index * out_rows, out_rows, 0)
    token_own = lax.dynamic_slice_in_dim(tokens, col_index * out_rows, out_rows, 0)
    proj_own = jnp.dot(attn_own, out_weight, preferred_element_type=jnp.float32)
    middle_all = col_proj_norm_gather(
        attention.reshape(n_col, out_rows, heads_here * head_dim),
        token_own.astype(jnp.float32) + proj_own,
        w_out,
        ln_gain,
        ln_bias,
    )
    mine = middle_all[col_index]
    middle = middle_all.reshape(shard_len, width)
    ffn_pre = jnp.dot(middle, f_in, preferred_element_type=jnp.float32)
    ffn_hidden = jax.nn.gelu(ffn_pre, approximate=False).astype(jnp.bfloat16)
    ffn_full = jnp.dot(ffn_hidden, f_out, preferred_element_type=jnp.float32)
    ffn_own = lax.dynamic_slice_in_dim(ffn_full, col_index * out_rows, out_rows, 0)
    second = col_reduce_scatter(
        ffn_full.astype(jnp.bfloat16).reshape(n_col, out_rows, width),
        mine.astype(jnp.float32) + ffn_own,
        6,
    )
    normed = layer_norm(second, ln2_gain, ln2_bias)
    return (normed.astype(jnp.bfloat16)[None], page_pool)


def solution(mesh):
    in_specs = (
        P("row", "seq", None),
        P(None, "col", None),
        P("row", "col", None),
        P("col", None),
        P(),
        P(),
        P("row", "col"),
        P("col", "row"),
        P(),
        P(),
        P("row", None),
        P("row", None),
        P("row", "seq", None),
    )
    out_specs = (P("row", ("seq", "col"), None), P("row", "seq", None, None, None, "col", None))
    return jax.shard_map(
        per_device, mesh=mesh, in_specs=in_specs, out_specs=out_specs, check_vma=False
    )
```

```python
import functools
import math

import jax
import jax.numpy as jnp
from jax import lax
from jax.experimental import pallas as pl
from jax.experimental.pallas import tpu as pltpu
from jax.sharding import PartitionSpec as P

MESH = pl.DeviceIdType.MESH

HALF = 256


def padded(block, sides, width):
    for axis, dim in sides:
        count = lax.axis_size(axis)
        forward = [(i, i + 1) for i in range(count - 1)]
        backward = [(target, source) for source, target in forward]
        low = lax.ppermute(
            lax.slice_in_dim(block, block.shape[dim] - width, None, axis=dim), axis, forward
        )
        high = lax.ppermute(lax.slice_in_dim(block, 0, width, axis=dim), axis, backward)
        block = jnp.concatenate([low, block, high], axis=dim)
    return block


def butterfly_partners(n):
    me = lax.axis_index("seq")
    partners = []
    step = 1
    while step < n:
        bit = (me // step) % 2
        partners.append(me + step - 2 * step * bit)
        step *= 2
    return me, partners


def enter(partners):
    row, col = lax.axis_index("row"), lax.axis_index("col")
    barrier = pltpu.get_barrier_semaphore()
    for partner in partners:
        pl.semaphore_signal(barrier, inc=1, device_id=(partner, row, col), device_id_type=MESH)
    pl.semaphore_wait(barrier, len(partners))
    return row, col


def gather_kernel(n, x_ref, out_ref, self_sem, send_sem, recv_sem):
    me, partners = butterfly_partners(n)
    row, col = enter(partners)
    own = pltpu.make_async_copy(x_ref, out_ref.at[me], self_sem)
    own.start()
    own.wait()
    size = 1
    for k, partner in enumerate(partners):
        start = (me // size) * size
        copy = pltpu.make_async_remote_copy(
            src_ref=out_ref.at[pl.ds(start, size)],
            dst_ref=out_ref.at[pl.ds(start, size)],
            send_sem=send_sem.at[k],
            recv_sem=recv_sem.at[k],
            device_id=(partner, row, col),
            device_id_type=MESH,
        )
        copy.start()
        copy.wait()
        size *= 2


def seq_gather(block):
    n = lax.axis_size("seq")
    rounds = n.bit_length() - 1
    return pl.pallas_call(
        functools.partial(gather_kernel, n),
        out_shape=jax.ShapeDtypeStruct((n,) + block.shape, block.dtype),
        in_specs=[pl.BlockSpec(memory_space=pltpu.VMEM)],
        out_specs=pl.BlockSpec(memory_space=pltpu.VMEM),
        scratch_shapes=[
            pltpu.SemaphoreType.DMA(()),
            pltpu.SemaphoreType.DMA((rounds,)),
            pltpu.SemaphoreType.DMA((rounds,)),
        ],
        compiler_params=pltpu.CompilerParams(collective_id=0, has_side_effects=True),
    )(block)


def merge_parts(mine, theirs, top_lane):
    lane = lax.broadcasted_iota(jnp.int32, mine.shape, 1)
    is_top = lane == top_lane
    top_a = jnp.max(jnp.where(is_top, mine, -jnp.inf), axis=1, keepdims=True)
    top_b = jnp.max(jnp.where(is_top, theirs, -jnp.inf), axis=1, keepdims=True)
    top = jnp.maximum(top_a, top_b)
    merged = mine * jnp.exp(top_a - top) + theirs * jnp.exp(top_b - top)
    return jnp.where(is_top, top, merged)


def halving_kernel(n, top_lane, x_ref, out_ref, *scratch):
    rounds = len(scratch) // 3
    kept, got, sems = scratch[:rounds], scratch[rounds : 2 * rounds], scratch[2 * rounds :]
    me = lax.axis_index("seq")
    steps = []
    step = n // 2
    while step >= 1:
        bit = (me // step) % 2
        steps.append((me + step - 2 * step * bit, bit))
        step //= 2
    row, col = enter([partner for partner, _ in steps])
    source = x_ref
    for k, (partner, bit) in enumerate(steps):
        half = source.shape[0] // 2
        send_at = pl.multiple_of((1 - bit) * half, 8)
        keep_at = pl.multiple_of(bit * half, 8)
        copy = pltpu.make_async_remote_copy(
            src_ref=source.at[pl.ds(send_at, half)],
            dst_ref=got[k],
            send_sem=sems[k].at[0],
            recv_sem=sems[k].at[1],
            device_id=(partner, row, col),
            device_id_type=MESH,
        )
        copy.start()
        copy.wait()
        value = merge_parts(source[pl.ds(keep_at, half)], got[k][...], top_lane)
        if k + 1 < rounds:
            kept[k][...] = value
            source = kept[k]
        else:
            out_ref[...] = value


def seq_softmax_combine(parts, top_lane):
    n = lax.axis_size("seq")
    rounds = n.bit_length() - 1
    rows, lanes = parts.shape
    scratch = []
    for k in range(rounds):
        scratch.append(pltpu.VMEM((rows >> (k + 1), lanes), parts.dtype))
    for k in range(rounds):
        scratch.append(pltpu.VMEM((rows >> (k + 1), lanes), parts.dtype))
    for k in range(rounds):
        scratch.append(pltpu.SemaphoreType.DMA((2,)))
    return pl.pallas_call(
        functools.partial(halving_kernel, n, top_lane),
        out_shape=jax.ShapeDtypeStruct((rows // n, lanes), parts.dtype),
        in_specs=[pl.BlockSpec(memory_space=pltpu.VMEM)],
        out_specs=pl.BlockSpec(memory_space=pltpu.VMEM),
        scratch_shapes=scratch,
        compiler_params=pltpu.CompilerParams(collective_id=1, has_side_effects=True),
    )(parts)


def seq_peers():
    me, n = lax.axis_index("seq"), lax.axis_size("seq")
    row, col = lax.axis_index("row"), lax.axis_index("col")
    peers = [lax.rem(me + j, n) for j in range(1, n)]
    barrier = pltpu.get_barrier_semaphore()
    for peer in peers:
        pl.semaphore_signal(barrier, inc=1, device_id=(peer, row, col), device_id_type=MESH)
    pl.semaphore_wait(barrier, len(peers))
    return me, [(peer, row, col) for peer in peers]


def seq_direct_gather_kernel(x_ref, out_ref, self_sem, send_sem, recv_sem):
    me, peers = seq_peers()
    own = pltpu.make_async_copy(x_ref, out_ref.at[me], self_sem)
    own.start()
    copies = []
    for j, peer in enumerate(peers):
        copy = pltpu.make_async_remote_copy(
            src_ref=x_ref,
            dst_ref=out_ref.at[me],
            send_sem=send_sem.at[j],
            recv_sem=recv_sem.at[j],
            device_id=peer,
            device_id_type=MESH,
        )
        copy.start()
        copies.append(copy)
    own.wait()
    for copy in copies:
        copy.wait()


def seq_direct_gather(block):
    n = lax.axis_size("seq")
    return pl.pallas_call(
        seq_direct_gather_kernel,
        out_shape=jax.ShapeDtypeStruct((n,) + block.shape, block.dtype),
        in_specs=[pl.BlockSpec(memory_space=pltpu.VMEM)],
        out_specs=pl.BlockSpec(memory_space=pltpu.VMEM),
        scratch_shapes=[
            pltpu.SemaphoreType.DMA(()),
            pltpu.SemaphoreType.DMA((n - 1,)),
            pltpu.SemaphoreType.DMA((n - 1,)),
        ],
        compiler_params=pltpu.CompilerParams(collective_id=4, has_side_effects=True),
    )(block)


def seq_merge_kernel(top_lane, x_ref, out_ref, got, send_sem, recv_sem):
    me, peers = seq_peers()
    copies = []
    for j, peer in enumerate(peers):
        copy = pltpu.make_async_remote_copy(
            src_ref=x_ref.at[peer[0]],
            dst_ref=got.at[j],
            send_sem=send_sem.at[j],
            recv_sem=recv_sem.at[j],
            device_id=peer,
            device_id_type=MESH,
        )
        copy.start()
        copies.append(copy)
    for copy in copies:
        copy.wait()
    value = x_ref[me]
    for j in range(len(copies)):
        value = merge_parts(value, got[j], top_lane)
    out_ref[...] = value


def seq_direct_merge(parts, top_lane):
    n = parts.shape[0]
    return pl.pallas_call(
        functools.partial(seq_merge_kernel, top_lane),
        out_shape=jax.ShapeDtypeStruct(parts.shape[1:], parts.dtype),
        in_specs=[pl.BlockSpec(memory_space=pltpu.VMEM)],
        out_specs=pl.BlockSpec(memory_space=pltpu.VMEM),
        scratch_shapes=[
            pltpu.VMEM((n - 1,) + parts.shape[1:], parts.dtype),
            pltpu.SemaphoreType.DMA((n - 1,)),
            pltpu.SemaphoreType.DMA((n - 1,)),
        ],
        compiler_params=pltpu.CompilerParams(collective_id=5, has_side_effects=True),
    )(parts)


def seq_two_level_peers(group):
    me, n = lax.axis_index("seq"), lax.axis_size("seq")
    row, col = lax.axis_index("row"), lax.axis_index("col")
    first = (me // group) * group
    near = [first + lax.rem(me - first + j, group) for j in range(1, group)]
    far = [lax.rem(me + group * j, n) for j in range(1, n // group)]
    barrier = pltpu.get_barrier_semaphore()
    for peer in near + far:
        pl.semaphore_signal(barrier, inc=1, device_id=(peer, row, col), device_id_type=MESH)
    pl.semaphore_wait(barrier, len(near) + len(far))
    return me, first, [(p, row, col) for p in near], [(p, row, col) for p in far]


def seq_gather2_kernel(group, x_ref, out_ref, self_sem, near_send, near_recv, far_send, far_recv):
    me, first, near, far = seq_two_level_peers(group)
    own = pltpu.make_async_copy(x_ref, out_ref.at[me], self_sem)
    own.start()
    copies = []
    for j, peer in enumerate(near):
        copy = pltpu.make_async_remote_copy(
            src_ref=x_ref,
            dst_ref=out_ref.at[me],
            send_sem=near_send.at[j],
            recv_sem=near_recv.at[j],
            device_id=peer,
            device_id_type=MESH,
        )
        copy.start()
        copies.append(copy)
    own.wait()
    for copy in copies:
        copy.wait()
    block = out_ref.at[pl.ds(first, group)]
    copies = []
    for j, peer in enumerate(far):
        copy = pltpu.make_async_remote_copy(
            src_ref=block,
            dst_ref=block,
            send_sem=far_send.at[j],
            recv_sem=far_recv.at[j],
            device_id=peer,
            device_id_type=MESH,
        )
        copy.start()
        copies.append(copy)
    for copy in copies:
        copy.wait()


def seq_gather2(block, group):
    n = lax.axis_size("seq")
    return pl.pallas_call(
        functools.partial(seq_gather2_kernel, group),
        out_shape=jax.ShapeDtypeStruct((n,) + block.shape, block.dtype),
        in_specs=[pl.BlockSpec(memory_space=pltpu.VMEM)],
        out_specs=pl.BlockSpec(memory_space=pltpu.VMEM),
        scratch_shapes=[
            pltpu.SemaphoreType.DMA(()),
            pltpu.SemaphoreType.DMA((group - 1,)),
            pltpu.SemaphoreType.DMA((group - 1,)),
            pltpu.SemaphoreType.DMA((n // group - 1,)),
            pltpu.SemaphoreType.DMA((n // group - 1,)),
        ],
        compiler_params=pltpu.CompilerParams(collective_id=8, has_side_effects=True),
    )(block)


def seq_merge2_kernel(
    group, top_lane, x_ref, out_ref, got_far, partial, got_near, far_send, far_recv, near_send, near_recv
):
    me, first, near, far = seq_two_level_peers(group)
    copies = []
    for j, peer in enumerate(far):
        start = pl.multiple_of((peer[0] // group) * group, group)
        copy = pltpu.make_async_remote_copy(
            src_ref=x_ref.at[pl.ds(start, group)],
            dst_ref=got_far.at[j],
            send_sem=far_send.at[j],
            recv_sem=far_recv.at[j],
            device_id=peer,
            device_id_type=MESH,
        )
        copy.start()
        copies.append(copy)
    for copy in copies:
        copy.wait()
    for k in range(group):
        value = x_ref[first + k]
        for j in range(len(far)):
            value = merge_parts(value, got_far[j, k], top_lane)
        partial[k] = value
    copies = []
    for j, peer in enumerate(near):
        copy = pltpu.make_async_remote_copy(
            src_ref=partial.at[peer[0] - first],
            dst_ref=got_near.at[j],
            send_sem=near_send.at[j],
            recv_sem=near_recv.at[j],
            device_id=peer,
            device_id_type=MESH,
        )
        copy.start()
        copies.append(copy)
    for copy in copies:
        copy.wait()
    value = partial[me - first]
    for j in range(len(near)):
        value = merge_parts(value, got_near[j], top_lane)
    out_ref[...] = value


def seq_merge2(parts, top_lane, group):
    n = parts.shape[0]
    blk = parts.shape[1:]
    return pl.pallas_call(
        functools.partial(seq_merge2_kernel, group, top_lane),
        out_shape=jax.ShapeDtypeStruct(blk, parts.dtype),
        in_specs=[pl.BlockSpec(memory_space=pltpu.VMEM)],
        out_specs=pl.BlockSpec(memory_space=pltpu.VMEM),
        scratch_shapes=[
            pltpu.VMEM((n // group - 1, group) + blk, parts.dtype),
            pltpu.VMEM((group,) + blk, parts.dtype),
            pltpu.VMEM((group - 1,) + blk, parts.dtype),
            pltpu.SemaphoreType.DMA((n // group - 1,)),
            pltpu.SemaphoreType.DMA((n // group - 1,)),
            pltpu.SemaphoreType.DMA((group - 1,)),
            pltpu.SemaphoreType.DMA((group - 1,)),
        ],
        compiler_params=pltpu.CompilerParams(collective_id=9, has_side_effects=True),
    )(parts)


def col_peers():
    me, m = lax.axis_index("col"), lax.axis_size("col")
    seq, row = lax.axis_index("seq"), lax.axis_index("row")
    peers = [lax.rem(me + j, m) for j in range(1, m)]
    barrier = pltpu.get_barrier_semaphore()
    for peer in peers:
        pl.semaphore_signal(barrier, inc=1, device_id=(seq, row, peer), device_id_type=MESH)
    pl.semaphore_wait(barrier, len(peers))
    return me, [(seq, row, peer) for peer in peers]


def col_gather_kernel(x_ref, out_ref, self_sem, send_sem, recv_sem):
    me, peers = col_peers()
    own = pltpu.make_async_copy(x_ref, out_ref.at[me], self_sem)
    own.start()
    copies = []
    for j, peer in enumerate(peers):
        copy = pltpu.make_async_remote_copy(
            src_ref=x_ref,
            dst_ref=out_ref.at[me],
            send_sem=send_sem.at[j],
            recv_sem=recv_sem.at[j],
            device_id=peer,
            device_id_type=MESH,
        )
        copy.start()
        copies.append(copy)
    own.wait()
    for copy in copies:
        copy.wait()


def col_gather(block):
    m = lax.axis_size("col")
    return pl.pallas_call(
        col_gather_kernel,
        out_shape=jax.ShapeDtypeStruct((m,) + block.shape, block.dtype),
        in_specs=[pl.BlockSpec(memory_space=pltpu.VMEM)],
        out_specs=pl.BlockSpec(memory_space=pltpu.VMEM),
        scratch_shapes=[
            pltpu.SemaphoreType.DMA(()),
            pltpu.SemaphoreType.DMA((m - 1,)),
            pltpu.SemaphoreType.DMA((m - 1,)),
        ],
        compiler_params=pltpu.CompilerParams(collective_id=2, has_side_effects=True),
    )(block)


def col_sum_kernel(x_ref, own_ref, out_ref, got, send_sem, recv_sem):
    me, peers = col_peers()
    copies = []
    for j, peer in enumerate(peers):
        copy = pltpu.make_async_remote_copy(
            src_ref=x_ref.at[peer[2]],
            dst_ref=got.at[j],
            send_sem=send_sem.at[j],
            recv_sem=recv_sem.at[j],
            device_id=peer,
            device_id_type=MESH,
        )
        copy.start()
        copies.append(copy)
    for copy in copies:
        copy.wait()
    chunk = 32

    def body(i, carry):
        rows = pl.ds(pl.multiple_of(i * chunk, chunk), chunk)
        total = own_ref[rows, :]
        for j in range(len(copies)):
            total = total + got[j, rows, :].astype(jnp.float32)
        out_ref[rows, :] = total
        return carry

    lax.fori_loop(0, out_ref.shape[0] // chunk, body, 0)


def col_reduce_scatter(parts, own, collective_id):
    m = lax.axis_size("col")
    return pl.pallas_call(
        col_sum_kernel,
        out_shape=jax.ShapeDtypeStruct(own.shape, jnp.float32),
        in_specs=[pl.BlockSpec(memory_space=pltpu.VMEM)] * 2,
        out_specs=pl.BlockSpec(memory_space=pltpu.VMEM),
        scratch_shapes=[
            pltpu.VMEM((m - 1,) + parts.shape[1:], parts.dtype),
            pltpu.SemaphoreType.DMA((m - 1,)),
            pltpu.SemaphoreType.DMA((m - 1,)),
        ],
        compiler_params=pltpu.CompilerParams(collective_id=collective_id, has_side_effects=True),
    )(parts, own)


def col_mid_kernel(x_ref, own_ref, gain_ref, bias_ref, out_ref, got, rs_send, rs_recv, g_send, g_recv):
    me, peers = col_peers()
    copies = []
    for j, peer in enumerate(peers):
        copy = pltpu.make_async_remote_copy(
            src_ref=x_ref.at[peer[2]],
            dst_ref=got.at[j],
            send_sem=rs_send.at[j],
            recv_sem=rs_recv.at[j],
            device_id=peer,
            device_id_type=MESH,
        )
        copy.start()
        copies.append(copy)
    for copy in copies:
        copy.wait()
    chunk = 32
    width = out_ref.shape[2]

    def body(i, carry):
        rows = pl.ds(pl.multiple_of(i * chunk, chunk), chunk)
        total = own_ref[rows, :]
        for j in range(len(copies)):
            total = total + got[j, rows, :].astype(jnp.float32)
        center = total - jnp.sum(total, axis=1, keepdims=True) / width
        spread = jnp.sum(center * center, axis=1, keepdims=True) / width
        normed = center / jnp.sqrt(spread + 1e-05) * gain_ref[...] + bias_ref[...]
        out_ref[me, rows, :] = normed.astype(out_ref.dtype)
        return carry

    lax.fori_loop(0, out_ref.shape[1] // chunk, body, 0)
    sends = []
    for j, peer in enumerate(peers):
        copy = pltpu.make_async_remote_copy(
            src_ref=out_ref.at[me],
            dst_ref=out_ref.at[me],
            send_sem=g_send.at[j],
            recv_sem=g_recv.at[j],
            device_id=peer,
            device_id_type=MESH,
        )
        copy.start()
        sends.append(copy)
    for copy in sends:
        copy.wait()


def col_sum_norm_gather(parts, own, gain, bias):
    m = lax.axis_size("col")
    rows, width = own.shape
    return pl.pallas_call(
        col_mid_kernel,
        out_shape=jax.ShapeDtypeStruct((m, rows, width), jnp.bfloat16),
        in_specs=[pl.BlockSpec(memory_space=pltpu.VMEM)] * 4,
        out_specs=pl.BlockSpec(memory_space=pltpu.VMEM),
        scratch_shapes=[
            pltpu.VMEM((m - 1,) + parts.shape[1:], parts.dtype),
            pltpu.SemaphoreType.DMA((m - 1,)),
            pltpu.SemaphoreType.DMA((m - 1,)),
            pltpu.SemaphoreType.DMA((m - 1,)),
            pltpu.SemaphoreType.DMA((m - 1,)),
        ],
        compiler_params=pltpu.CompilerParams(collective_id=7, has_side_effects=True),
    )(parts, own, gain.reshape(1, width), bias.reshape(1, width))


def col_proj_kernel(x_ref, own_ref, w_ref, gain_ref, bias_ref, out_ref, got, rs_send, rs_recv, g_send, g_recv):
    me, peers = col_peers()
    m = len(peers) + 1
    heads_width = x_ref.shape[2]
    copies = []
    for j, peer in enumerate(peers):
        copy = pltpu.make_async_remote_copy(
            src_ref=x_ref.at[peer[2]],
            dst_ref=got.at[j],
            send_sem=rs_send.at[j],
            recv_sem=rs_recv.at[j],
            device_id=peer,
            device_id_type=MESH,
        )
        copy.start()
        copies.append(copy)
    for copy in copies:
        copy.wait()
    chunk = 32
    width = out_ref.shape[2]

    def body(i, carry):
        rows = pl.ds(pl.multiple_of(i * chunk, chunk), chunk)
        total = own_ref[rows, :]
        for j in range(len(copies)):
            source = lax.rem(me + m - 1 - j, m)
            weights = w_ref[pl.ds(pl.multiple_of(source * heads_width, heads_width), heads_width), :]
            total = total + jnp.dot(got[j, rows, :], weights, preferred_element_type=jnp.float32)
        center = total - jnp.sum(total, axis=1, keepdims=True) / width
        spread = jnp.sum(center * center, axis=1, keepdims=True) / width
        normed = center / jnp.sqrt(spread + 1e-05) * gain_ref[...] + bias_ref[...]
        out_ref[me, rows, :] = normed.astype(out_ref.dtype)
        return carry

    lax.fori_loop(0, out_ref.shape[1] // chunk, body, 0)
    sends = []
    for j, peer in enumerate(peers):
        copy = pltpu.make_async_remote_copy(
            src_ref=out_ref.at[me],
            dst_ref=out_ref.at[me],
            send_sem=g_send.at[j],
            recv_sem=g_recv.at[j],
            device_id=peer,
            device_id_type=MESH,
        )
        copy.start()
        sends.append(copy)
    for copy in sends:
        copy.wait()


def col_proj_norm_gather(attn_parts, own, w_full, gain, bias):
    m = lax.axis_size("col")
    rows, width = own.shape
    return pl.pallas_call(
        col_proj_kernel,
        out_shape=jax.ShapeDtypeStruct((m, rows, width), jnp.bfloat16),
        in_specs=[pl.BlockSpec(memory_space=pltpu.VMEM)] * 5,
        out_specs=pl.BlockSpec(memory_space=pltpu.VMEM),
        scratch_shapes=[
            pltpu.VMEM((m - 1,) + attn_parts.shape[1:], attn_parts.dtype),
            pltpu.SemaphoreType.DMA((m - 1,)),
            pltpu.SemaphoreType.DMA((m - 1,)),
            pltpu.SemaphoreType.DMA((m - 1,)),
            pltpu.SemaphoreType.DMA((m - 1,)),
        ],
        compiler_params=pltpu.CompilerParams(
            collective_id=10, has_side_effects=True, vmem_limit_bytes=48 * 1024 * 1024
        ),
    )(attn_parts, own, w_full, gain.reshape(1, width), bias.reshape(1, width))


def layer_norm(values, gain, bias):
    center = values - jnp.mean(values, axis=1, keepdims=True)
    spread = jnp.mean(center * center, axis=1, keepdims=True)
    return center * lax.rsqrt(spread + 1e-05) * gain + bias


def per_device(
    hidden_in,
    qkv_weight,
    qkv_global_weight,
    out_weight,
    ln_gain,
    ln_bias,
    ffn_in,
    ffn_out,
    ln2_gain,
    ln2_bias,
    segment_ids,
    global_pos,
    page_owner,
):
    neg = -1e30
    tokens = hidden_in[0]
    shard_len, width = tokens.shape
    heads_here = qkv_weight.shape[1]
    triple = qkv_weight.shape[2]
    head_dim = triple // 3
    n_seq = lax.axis_size("seq")
    n_row = lax.axis_size("row")
    n_col = lax.axis_size("col")
    seq_index = lax.axis_index("seq")
    col_index = lax.axis_index("col")
    base = seq_index * shard_len
    scale = 1.0 / math.sqrt(head_dim)

    all_pos = global_pos[0]
    n_glob = all_pos.shape[0]
    per_shard = n_glob // n_seq
    own_pos = lax.dynamic_slice_in_dim(all_pos, seq_index * per_shard, per_shard, 0)
    local_order = jnp.arange(shard_len, dtype=jnp.int32)
    own_match = (own_pos - base)[:, None] == local_order[None, :]
    picker = own_match.astype(jnp.bfloat16)
    own_rows = jnp.dot(picker, tokens, preferred_element_type=jnp.float32).astype(jnp.bfloat16)
    group = 4 if n_seq % 4 == 0 and n_seq > 4 else 1
    if group > 1:
        glob_rows = seq_gather2(own_rows.reshape(-1, 128), group).reshape(n_glob, width)
    else:
        glob_rows = seq_direct_gather(own_rows.reshape(-1, 128)).reshape(n_glob, width)

    wg_cols = qkv_global_weight.shape[1] * qkv_global_weight.shape[2]
    wg_fin = lax.all_gather(
        jnp.concatenate(
            [qkv_global_weight.reshape(qkv_global_weight.shape[0], wg_cols), ffn_in], axis=1
        ),
        "row",
        axis=0,
        tiled=True,
    )
    w_global = wg_fin[:, :wg_cols]
    f_in = wg_fin[:, wg_cols:]
    f_out = lax.all_gather(ffn_out, "row", axis=1, tiled=True)
    w_out = lax.all_gather(out_weight, "col", axis=0, tiled=True)

    flat_weight = qkv_weight.reshape(width, heads_here * triple)
    qkv = jnp.dot(tokens, flat_weight, preferred_element_type=jnp.float32).astype(jnp.bfloat16)
    qkv_heads = qkv.reshape(shard_len, heads_here, triple)
    queries = qkv_heads[:, :, :head_dim]
    kv_local = qkv_heads[:, :, head_dim:]

    owners = page_owner[0, :, 0]
    n_pages = owners.shape[0]
    page_len = shard_len // n_pages
    capacity = max(2, n_pages // n_seq)
    page_order = jnp.arange(n_pages, dtype=jnp.int32)
    slot = jnp.sum(
        ((owners[:, None] == owners[None, :]) & (page_order[None, :] < page_order[:, None])).astype(
            jnp.int32
        ),
        axis=1,
    )
    target = owners * capacity + slot
    placing = (target[None, :] == jnp.arange(n_seq * capacity, dtype=jnp.int32)[:, None]).astype(
        jnp.bfloat16
    )
    outgoing = jnp.dot(
        placing,
        kv_local.reshape(n_pages, page_len * heads_here * 2 * head_dim),
        preferred_element_type=jnp.float32,
    ).astype(jnp.bfloat16)
    outgoing = outgoing.reshape(n_seq, capacity, page_len, heads_here, 2 * head_dim)
    arrived = lax.all_to_all(outgoing, "seq", split_axis=0, concat_axis=0, tiled=True)
    arrived, glob_rows = lax.optimization_barrier((arrived, glob_rows))
    page_pool = arrived[None, None]

    kv_ext = padded(kv_local, (("seq", 0),), HALF)

    glob_qkv = jnp.dot(glob_rows, flat_weight, preferred_element_type=jnp.float32).astype(
        jnp.bfloat16
    )
    glob_kv = glob_qkv.reshape(n_glob, heads_here, triple)[:, :, head_dim:]
    glob_k = glob_kv[:, :, :head_dim]
    glob_v = glob_kv[:, :, head_dim:]
    glob_q = (
        jnp.dot(glob_rows, w_global, preferred_element_type=jnp.float32)
        .astype(jnp.bfloat16)
        .reshape(n_glob, heads_here, triple)[:, :, :head_dim]
    )
    global_kv_local = (
        jnp.dot(tokens, w_global, preferred_element_type=jnp.float32)
        .astype(jnp.bfloat16)
        .reshape(shard_len, heads_here, triple)[:, :, head_dim:]
    )

    seg_all = segment_ids[0]
    glob_seg = jnp.take(seg_all, all_pos)
    seg_pad = jnp.pad(seg_all, (HALF, HALF), constant_values=-1)
    query_seg = lax.dynamic_slice_in_dim(seg_all, base, shard_len, 0)
    key_seg = lax.dynamic_slice_in_dim(seg_pad, base, shard_len + 2 * HALF, 0)
    key_pos = base - HALF + jnp.arange(shard_len + 2 * HALF, dtype=jnp.int32)
    key_flag = jnp.any(key_pos[:, None] == all_pos[None, :], axis=1)
    query_pos = base + local_order

    s_part = (
        jnp.einsum(
            "ghd,khd->hgk",
            glob_q,
            global_kv_local[:, :, :head_dim],
            preferred_element_type=jnp.float32,
        )
        * scale
    )
    part_mask = glob_seg[:, None] == query_seg[None, :]
    part_top = jnp.max(jnp.where(part_mask, s_part, neg), axis=2)
    e_part = jnp.where(part_mask, jnp.exp(s_part - part_top[:, :, None]), 0.0)
    part_total = jnp.sum(e_part, axis=2)
    part_acc = jnp.einsum(
        "hgk,khd->hgd",
        e_part,
        global_kv_local[:, :, head_dim:].astype(jnp.float32),
        precision=lax.Precision.HIGHEST,
    )
    packed = jnp.concatenate(
        [
            part_acc,
            part_total[:, :, None],
            jnp.broadcast_to(part_top[:, :, None], part_top.shape + (128 - head_dim - 1,)),
        ],
        axis=2,
    )
    packed = jnp.transpose(packed, (1, 0, 2)).reshape(n_glob * heads_here, 128)
    if group > 1:
        merged = seq_merge2(packed.reshape(n_seq, -1, 128), head_dim + 1, group)
    else:
        merged = seq_direct_merge(packed.reshape(n_seq, -1, 128), head_dim + 1)
    merged = merged.reshape(
        per_shard, heads_here, 128
    )
    own_out = jnp.transpose(
        (merged[:, :, :head_dim] / merged[:, :, head_dim : head_dim + 1]).astype(jnp.bfloat16),
        (1, 0, 2),
    )

    glob_mask = query_seg[:, None] == glob_seg[None, :]
    k_blk = kv_ext[:, :, :head_dim]
    v_blk = kv_ext[:, :, head_dim:]
    s_win = jnp.einsum("qhd,khd->hqk", queries, k_blk, preferred_element_type=jnp.float32) * scale
    s_glob = jnp.einsum("qhd,ghd->hqg", queries, glob_k, preferred_element_type=jnp.float32) * scale
    m_win = (
        (jnp.abs(query_pos[:, None] - key_pos[None, :]) <= HALF)
        & (query_seg[:, None] == key_seg[None, :])
        & jnp.logical_not(key_flag[None, :])
    )
    top = jnp.maximum(
        jnp.max(jnp.where(m_win, s_win, neg), axis=2),
        jnp.max(jnp.where(glob_mask, s_glob, neg), axis=2),
    )
    e_win = jnp.where(m_win, jnp.exp(s_win - top[:, :, None]), 0.0)
    e_glob = jnp.where(glob_mask, jnp.exp(s_glob - top[:, :, None]), 0.0)
    total = jnp.sum(e_win, axis=2) + jnp.sum(e_glob, axis=2)
    numer = jnp.einsum(
        "hqk,khd->qhd", e_win.astype(jnp.bfloat16), v_blk, preferred_element_type=jnp.float32
    )
    numer = numer + jnp.einsum(
        "hqg,ghd->qhd", e_glob.astype(jnp.bfloat16), glob_v, preferred_element_type=jnp.float32
    )
    pieces = (numer / jnp.transpose(total)[:, :, None]).astype(jnp.bfloat16)

    placed = jnp.einsum("gt,hgd->thd", picker, own_out, preferred_element_type=jnp.float32).astype(
        jnp.bfloat16
    )
    is_own = jnp.any(own_match, axis=0)
    attention = jnp.where(is_own[:, None, None], placed, pieces).reshape(
        shard_len, heads_here * head_dim
    )


    out_rows = shard_len // n_col
    attn_own = lax.dynamic_slice_in_dim(attention, col_index * out_rows, out_rows, 0)
    token_own = lax.dynamic_slice_in_dim(tokens, col_index * out_rows, out_rows, 0)
    proj_own = jnp.dot(attn_own, out_weight, preferred_element_type=jnp.float32)
    own_sum, w_out = lax.optimization_barrier((token_own.astype(jnp.float32) + proj_own, w_out))
    middle_all = col_proj_norm_gather(
        attention.reshape(n_col, out_rows, heads_here * head_dim),
        own_sum,
        w_out,
        ln_gain,
        ln_bias,
    )
    mine = middle_all[col_index]
    middle = middle_all.reshape(shard_len, width)
    ffn_pre = jnp.dot(middle, f_in, preferred_element_type=jnp.float32)
    ffn_hidden = jax.nn.gelu(ffn_pre, approximate=False).astype(jnp.bfloat16)
    ffn_full = jnp.dot(ffn_hidden, f_out, preferred_element_type=jnp.float32)
    ffn_own = lax.dynamic_slice_in_dim(ffn_full, col_index * out_rows, out_rows, 0)
    second = col_reduce_scatter(
        ffn_full.astype(jnp.bfloat16).reshape(n_col, out_rows, width),
        mine.astype(jnp.float32) + ffn_own,
        6,
    )
    normed = layer_norm(second, ln2_gain, ln2_bias)
    return (normed.astype(jnp.bfloat16)[None], page_pool)


def solution(mesh):
    in_specs = (
        P("row", "seq", None),
        P(None, "col", None),
        P("row", "col", None),
        P("col", None),
        P(),
        P(),
        P("row", "col"),
        P("col", "row"),
        P(),
        P(),
        P("row", None),
        P("row", None),
        P("row", "seq", None),
    )
    out_specs = (P("row", ("seq", "col"), None), P("row", "seq", None, None, None, "col", None))
    return jax.shard_map(
        per_device, mesh=mesh, in_specs=in_specs, out_specs=out_specs, check_vma=False
    )
```

```python
import functools
import math

import jax
import jax.numpy as jnp
from jax import lax
from jax.experimental import pallas as pl
from jax.experimental.pallas import tpu as pltpu
from jax.sharding import PartitionSpec as P

MESH = pl.DeviceIdType.MESH

HALF = 256


def padded(block, sides, width):
    for axis, dim in sides:
        count = lax.axis_size(axis)
        forward = [(i, i + 1) for i in range(count - 1)]
        backward = [(target, source) for source, target in forward]
        low = lax.ppermute(
            lax.slice_in_dim(block, block.shape[dim] - width, None, axis=dim), axis, forward
        )
        high = lax.ppermute(lax.slice_in_dim(block, 0, width, axis=dim), axis, backward)
        block = jnp.concatenate([low, block, high], axis=dim)
    return block


def butterfly_partners(n):
    me = lax.axis_index("seq")
    partners = []
    step = 1
    while step < n:
        bit = (me // step) % 2
        partners.append(me + step - 2 * step * bit)
        step *= 2
    return me, partners


def enter(partners):
    row, col = lax.axis_index("row"), lax.axis_index("col")
    barrier = pltpu.get_barrier_semaphore()
    for partner in partners:
        pl.semaphore_signal(barrier, inc=1, device_id=(partner, row, col), device_id_type=MESH)
    pl.semaphore_wait(barrier, len(partners))
    return row, col


def gather_kernel(n, x_ref, out_ref, self_sem, send_sem, recv_sem):
    me, partners = butterfly_partners(n)
    row, col = enter(partners)
    own = pltpu.make_async_copy(x_ref, out_ref.at[me], self_sem)
    own.start()
    own.wait()
    size = 1
    for k, partner in enumerate(partners):
        start = (me // size) * size
        copy = pltpu.make_async_remote_copy(
            src_ref=out_ref.at[pl.ds(start, size)],
            dst_ref=out_ref.at[pl.ds(start, size)],
            send_sem=send_sem.at[k],
            recv_sem=recv_sem.at[k],
            device_id=(partner, row, col),
            device_id_type=MESH,
        )
        copy.start()
        copy.wait()
        size *= 2


def seq_gather(block):
    n = lax.axis_size("seq")
    rounds = n.bit_length() - 1
    return pl.pallas_call(
        functools.partial(gather_kernel, n),
        out_shape=jax.ShapeDtypeStruct((n,) + block.shape, block.dtype),
        in_specs=[pl.BlockSpec(memory_space=pltpu.VMEM)],
        out_specs=pl.BlockSpec(memory_space=pltpu.VMEM),
        scratch_shapes=[
            pltpu.SemaphoreType.DMA(()),
            pltpu.SemaphoreType.DMA((rounds,)),
            pltpu.SemaphoreType.DMA((rounds,)),
        ],
        compiler_params=pltpu.CompilerParams(collective_id=0, has_side_effects=True),
    )(block)


def merge_parts(mine, theirs, top_lane):
    lane = lax.broadcasted_iota(jnp.int32, mine.shape, 1)
    is_top = lane == top_lane
    top_a = jnp.max(jnp.where(is_top, mine, -jnp.inf), axis=1, keepdims=True)
    top_b = jnp.max(jnp.where(is_top, theirs, -jnp.inf), axis=1, keepdims=True)
    top = jnp.maximum(top_a, top_b)
    merged = mine * jnp.exp(top_a - top) + theirs * jnp.exp(top_b - top)
    return jnp.where(is_top, top, merged)


def halving_kernel(n, top_lane, x_ref, out_ref, *scratch):
    rounds = len(scratch) // 3
    kept, got, sems = scratch[:rounds], scratch[rounds : 2 * rounds], scratch[2 * rounds :]
    me = lax.axis_index("seq")
    steps = []
    step = n // 2
    while step >= 1:
        bit = (me // step) % 2
        steps.append((me + step - 2 * step * bit, bit))
        step //= 2
    row, col = enter([partner for partner, _ in steps])
    source = x_ref
    for k, (partner, bit) in enumerate(steps):
        half = source.shape[0] // 2
        send_at = pl.multiple_of((1 - bit) * half, 8)
        keep_at = pl.multiple_of(bit * half, 8)
        copy = pltpu.make_async_remote_copy(
            src_ref=source.at[pl.ds(send_at, half)],
            dst_ref=got[k],
            send_sem=sems[k].at[0],
            recv_sem=sems[k].at[1],
            device_id=(partner, row, col),
            device_id_type=MESH,
        )
        copy.start()
        copy.wait()
        value = merge_parts(source[pl.ds(keep_at, half)], got[k][...], top_lane)
        if k + 1 < rounds:
            kept[k][...] = value
            source = kept[k]
        else:
            out_ref[...] = value


def seq_softmax_combine(parts, top_lane):
    n = lax.axis_size("seq")
    rounds = n.bit_length() - 1
    rows, lanes = parts.shape
    scratch = []
    for k in range(rounds):
        scratch.append(pltpu.VMEM((rows >> (k + 1), lanes), parts.dtype))
    for k in range(rounds):
        scratch.append(pltpu.VMEM((rows >> (k + 1), lanes), parts.dtype))
    for k in range(rounds):
        scratch.append(pltpu.SemaphoreType.DMA((2,)))
    return pl.pallas_call(
        functools.partial(halving_kernel, n, top_lane),
        out_shape=jax.ShapeDtypeStruct((rows // n, lanes), parts.dtype),
        in_specs=[pl.BlockSpec(memory_space=pltpu.VMEM)],
        out_specs=pl.BlockSpec(memory_space=pltpu.VMEM),
        scratch_shapes=scratch,
        compiler_params=pltpu.CompilerParams(collective_id=1, has_side_effects=True),
    )(parts)


def seq_peers():
    me, n = lax.axis_index("seq"), lax.axis_size("seq")
    row, col = lax.axis_index("row"), lax.axis_index("col")
    peers = [lax.rem(me + j, n) for j in range(1, n)]
    barrier = pltpu.get_barrier_semaphore()
    for peer in peers:
        pl.semaphore_signal(barrier, inc=1, device_id=(peer, row, col), device_id_type=MESH)
    pl.semaphore_wait(barrier, len(peers))
    return me, [(peer, row, col) for peer in peers]


def seq_direct_gather_kernel(x_ref, out_ref, self_sem, send_sem, recv_sem):
    me, peers = seq_peers()
    own = pltpu.make_async_copy(x_ref, out_ref.at[me], self_sem)
    own.start()
    copies = []
    for j, peer in enumerate(peers):
        copy = pltpu.make_async_remote_copy(
            src_ref=x_ref,
            dst_ref=out_ref.at[me],
            send_sem=send_sem.at[j],
            recv_sem=recv_sem.at[j],
            device_id=peer,
            device_id_type=MESH,
        )
        copy.start()
        copies.append(copy)
    own.wait()
    for copy in copies:
        copy.wait()


def seq_direct_gather(block):
    n = lax.axis_size("seq")
    return pl.pallas_call(
        seq_direct_gather_kernel,
        out_shape=jax.ShapeDtypeStruct((n,) + block.shape, block.dtype),
        in_specs=[pl.BlockSpec(memory_space=pltpu.VMEM)],
        out_specs=pl.BlockSpec(memory_space=pltpu.VMEM),
        scratch_shapes=[
            pltpu.SemaphoreType.DMA(()),
            pltpu.SemaphoreType.DMA((n - 1,)),
            pltpu.SemaphoreType.DMA((n - 1,)),
        ],
        compiler_params=pltpu.CompilerParams(collective_id=4, has_side_effects=True),
    )(block)


def seq_merge_kernel(top_lane, x_ref, out_ref, got, send_sem, recv_sem):
    me, peers = seq_peers()
    copies = []
    for j, peer in enumerate(peers):
        copy = pltpu.make_async_remote_copy(
            src_ref=x_ref.at[peer[0]],
            dst_ref=got.at[j],
            send_sem=send_sem.at[j],
            recv_sem=recv_sem.at[j],
            device_id=peer,
            device_id_type=MESH,
        )
        copy.start()
        copies.append(copy)
    for copy in copies:
        copy.wait()
    value = x_ref[me]
    for j in range(len(copies)):
        value = merge_parts(value, got[j], top_lane)
    out_ref[...] = value


def seq_direct_merge(parts, top_lane):
    n = parts.shape[0]
    return pl.pallas_call(
        functools.partial(seq_merge_kernel, top_lane),
        out_shape=jax.ShapeDtypeStruct(parts.shape[1:], parts.dtype),
        in_specs=[pl.BlockSpec(memory_space=pltpu.VMEM)],
        out_specs=pl.BlockSpec(memory_space=pltpu.VMEM),
        scratch_shapes=[
            pltpu.VMEM((n - 1,) + parts.shape[1:], parts.dtype),
            pltpu.SemaphoreType.DMA((n - 1,)),
            pltpu.SemaphoreType.DMA((n - 1,)),
        ],
        compiler_params=pltpu.CompilerParams(collective_id=5, has_side_effects=True),
    )(parts)


def seq_two_level_peers(group):
    me, n = lax.axis_index("seq"), lax.axis_size("seq")
    row, col = lax.axis_index("row"), lax.axis_index("col")
    first = (me // group) * group
    near = [first + lax.rem(me - first + j, group) for j in range(1, group)]
    far = [lax.rem(me + group * j, n) for j in range(1, n // group)]
    barrier = pltpu.get_barrier_semaphore()
    for peer in near + far:
        pl.semaphore_signal(barrier, inc=1, device_id=(peer, row, col), device_id_type=MESH)
    pl.semaphore_wait(barrier, len(near) + len(far))
    return me, first, [(p, row, col) for p in near], [(p, row, col) for p in far]


def seq_gather2_kernel(group, x_ref, out_ref, self_sem, near_send, near_recv, far_send, far_recv):
    me, first, near, far = seq_two_level_peers(group)
    own = pltpu.make_async_copy(x_ref, out_ref.at[me], self_sem)
    own.start()
    copies = []
    for j, peer in enumerate(near):
        copy = pltpu.make_async_remote_copy(
            src_ref=x_ref,
            dst_ref=out_ref.at[me],
            send_sem=near_send.at[j],
            recv_sem=near_recv.at[j],
            device_id=peer,
            device_id_type=MESH,
        )
        copy.start()
        copies.append(copy)
    own.wait()
    for copy in copies:
        copy.wait()
    block = out_ref.at[pl.ds(first, group)]
    copies = []
    for j, peer in enumerate(far):
        copy = pltpu.make_async_remote_copy(
            src_ref=block,
            dst_ref=block,
            send_sem=far_send.at[j],
            recv_sem=far_recv.at[j],
            device_id=peer,
            device_id_type=MESH,
        )
        copy.start()
        copies.append(copy)
    for copy in copies:
        copy.wait()


def seq_gather2(block, group):
    n = lax.axis_size("seq")
    return pl.pallas_call(
        functools.partial(seq_gather2_kernel, group),
        out_shape=jax.ShapeDtypeStruct((n,) + block.shape, block.dtype),
        in_specs=[pl.BlockSpec(memory_space=pltpu.VMEM)],
        out_specs=pl.BlockSpec(memory_space=pltpu.VMEM),
        scratch_shapes=[
            pltpu.SemaphoreType.DMA(()),
            pltpu.SemaphoreType.DMA((group - 1,)),
            pltpu.SemaphoreType.DMA((group - 1,)),
            pltpu.SemaphoreType.DMA((n // group - 1,)),
            pltpu.SemaphoreType.DMA((n // group - 1,)),
        ],
        compiler_params=pltpu.CompilerParams(collective_id=8, has_side_effects=True),
    )(block)


def seq_merge2_kernel(
    group, top_lane, x_ref, out_ref, got_far, partial, got_near, far_send, far_recv, near_send, near_recv
):
    me, first, near, far = seq_two_level_peers(group)
    copies = []
    for j, peer in enumerate(far):
        start = pl.multiple_of((peer[0] // group) * group, group)
        copy = pltpu.make_async_remote_copy(
            src_ref=x_ref.at[pl.ds(start, group)],
            dst_ref=got_far.at[j],
            send_sem=far_send.at[j],
            recv_sem=far_recv.at[j],
            device_id=peer,
            device_id_type=MESH,
        )
        copy.start()
        copies.append(copy)
    for copy in copies:
        copy.wait()
    for k in range(group):
        value = x_ref[first + k]
        for j in range(len(far)):
            value = merge_parts(value, got_far[j, k], top_lane)
        partial[k] = value
    copies = []
    for j, peer in enumerate(near):
        copy = pltpu.make_async_remote_copy(
            src_ref=partial.at[peer[0] - first],
            dst_ref=got_near.at[j],
            send_sem=near_send.at[j],
            recv_sem=near_recv.at[j],
            device_id=peer,
            device_id_type=MESH,
        )
        copy.start()
        copies.append(copy)
    for copy in copies:
        copy.wait()
    value = partial[me - first]
    for j in range(len(near)):
        value = merge_parts(value, got_near[j], top_lane)
    out_ref[...] = value


def seq_merge2(parts, top_lane, group):
    n = parts.shape[0]
    blk = parts.shape[1:]
    return pl.pallas_call(
        functools.partial(seq_merge2_kernel, group, top_lane),
        out_shape=jax.ShapeDtypeStruct(blk, parts.dtype),
        in_specs=[pl.BlockSpec(memory_space=pltpu.VMEM)],
        out_specs=pl.BlockSpec(memory_space=pltpu.VMEM),
        scratch_shapes=[
            pltpu.VMEM((n // group - 1, group) + blk, parts.dtype),
            pltpu.VMEM((group,) + blk, parts.dtype),
            pltpu.VMEM((group - 1,) + blk, parts.dtype),
            pltpu.SemaphoreType.DMA((n // group - 1,)),
            pltpu.SemaphoreType.DMA((n // group - 1,)),
            pltpu.SemaphoreType.DMA((group - 1,)),
            pltpu.SemaphoreType.DMA((group - 1,)),
        ],
        compiler_params=pltpu.CompilerParams(collective_id=9, has_side_effects=True),
    )(parts)


def col_peers():
    me, m = lax.axis_index("col"), lax.axis_size("col")
    seq, row = lax.axis_index("seq"), lax.axis_index("row")
    peers = [lax.rem(me + j, m) for j in range(1, m)]
    barrier = pltpu.get_barrier_semaphore()
    for peer in peers:
        pl.semaphore_signal(barrier, inc=1, device_id=(seq, row, peer), device_id_type=MESH)
    pl.semaphore_wait(barrier, len(peers))
    return me, [(seq, row, peer) for peer in peers]


def col_gather_kernel(x_ref, out_ref, self_sem, send_sem, recv_sem):
    me, peers = col_peers()
    own = pltpu.make_async_copy(x_ref, out_ref.at[me], self_sem)
    own.start()
    copies = []
    for j, peer in enumerate(peers):
        copy = pltpu.make_async_remote_copy(
            src_ref=x_ref,
            dst_ref=out_ref.at[me],
            send_sem=send_sem.at[j],
            recv_sem=recv_sem.at[j],
            device_id=peer,
            device_id_type=MESH,
        )
        copy.start()
        copies.append(copy)
    own.wait()
    for copy in copies:
        copy.wait()


def col_gather(block):
    m = lax.axis_size("col")
    return pl.pallas_call(
        col_gather_kernel,
        out_shape=jax.ShapeDtypeStruct((m,) + block.shape, block.dtype),
        in_specs=[pl.BlockSpec(memory_space=pltpu.VMEM)],
        out_specs=pl.BlockSpec(memory_space=pltpu.VMEM),
        scratch_shapes=[
            pltpu.SemaphoreType.DMA(()),
            pltpu.SemaphoreType.DMA((m - 1,)),
            pltpu.SemaphoreType.DMA((m - 1,)),
        ],
        compiler_params=pltpu.CompilerParams(collective_id=2, has_side_effects=True),
    )(block)


def col_sum_kernel(x_ref, own_ref, out_ref, got, send_sem, recv_sem):
    me, peers = col_peers()
    copies = []
    for j, peer in enumerate(peers):
        copy = pltpu.make_async_remote_copy(
            src_ref=x_ref.at[peer[2]],
            dst_ref=got.at[j],
            send_sem=send_sem.at[j],
            recv_sem=recv_sem.at[j],
            device_id=peer,
            device_id_type=MESH,
        )
        copy.start()
        copies.append(copy)
    for copy in copies:
        copy.wait()
    chunk = 32

    def body(i, carry):
        rows = pl.ds(pl.multiple_of(i * chunk, chunk), chunk)
        total = own_ref[rows, :]
        for j in range(len(copies)):
            total = total + got[j, rows, :].astype(jnp.float32)
        out_ref[rows, :] = total
        return carry

    lax.fori_loop(0, out_ref.shape[0] // chunk, body, 0)


def col_reduce_scatter(parts, own, collective_id):
    m = lax.axis_size("col")
    return pl.pallas_call(
        col_sum_kernel,
        out_shape=jax.ShapeDtypeStruct(own.shape, jnp.float32),
        in_specs=[pl.BlockSpec(memory_space=pltpu.VMEM)] * 2,
        out_specs=pl.BlockSpec(memory_space=pltpu.VMEM),
        scratch_shapes=[
            pltpu.VMEM((m - 1,) + parts.shape[1:], parts.dtype),
            pltpu.SemaphoreType.DMA((m - 1,)),
            pltpu.SemaphoreType.DMA((m - 1,)),
        ],
        compiler_params=pltpu.CompilerParams(collective_id=collective_id, has_side_effects=True),
    )(parts, own)


def col_mid_kernel(x_ref, own_ref, gain_ref, bias_ref, out_ref, got, rs_send, rs_recv, g_send, g_recv):
    me, peers = col_peers()
    copies = []
    for j, peer in enumerate(peers):
        copy = pltpu.make_async_remote_copy(
            src_ref=x_ref.at[peer[2]],
            dst_ref=got.at[j],
            send_sem=rs_send.at[j],
            recv_sem=rs_recv.at[j],
            device_id=peer,
            device_id_type=MESH,
        )
        copy.start()
        copies.append(copy)
    for copy in copies:
        copy.wait()
    chunk = 32
    width = out_ref.shape[2]

    def body(i, carry):
        rows = pl.ds(pl.multiple_of(i * chunk, chunk), chunk)
        total = own_ref[rows, :]
        for j in range(len(copies)):
            total = total + got[j, rows, :].astype(jnp.float32)
        center = total - jnp.sum(total, axis=1, keepdims=True) / width
        spread = jnp.sum(center * center, axis=1, keepdims=True) / width
        normed = center / jnp.sqrt(spread + 1e-05) * gain_ref[...] + bias_ref[...]
        out_ref[me, rows, :] = normed.astype(out_ref.dtype)
        return carry

    lax.fori_loop(0, out_ref.shape[1] // chunk, body, 0)
    sends = []
    for j, peer in enumerate(peers):
        copy = pltpu.make_async_remote_copy(
            src_ref=out_ref.at[me],
            dst_ref=out_ref.at[me],
            send_sem=g_send.at[j],
            recv_sem=g_recv.at[j],
            device_id=peer,
            device_id_type=MESH,
        )
        copy.start()
        sends.append(copy)
    for copy in sends:
        copy.wait()


def col_sum_norm_gather(parts, own, gain, bias):
    m = lax.axis_size("col")
    rows, width = own.shape
    return pl.pallas_call(
        col_mid_kernel,
        out_shape=jax.ShapeDtypeStruct((m, rows, width), jnp.bfloat16),
        in_specs=[pl.BlockSpec(memory_space=pltpu.VMEM)] * 4,
        out_specs=pl.BlockSpec(memory_space=pltpu.VMEM),
        scratch_shapes=[
            pltpu.VMEM((m - 1,) + parts.shape[1:], parts.dtype),
            pltpu.SemaphoreType.DMA((m - 1,)),
            pltpu.SemaphoreType.DMA((m - 1,)),
            pltpu.SemaphoreType.DMA((m - 1,)),
            pltpu.SemaphoreType.DMA((m - 1,)),
        ],
        compiler_params=pltpu.CompilerParams(collective_id=7, has_side_effects=True),
    )(parts, own, gain.reshape(1, width), bias.reshape(1, width))


def col_proj_kernel(x_ref, own_ref, w_ref, gain_ref, bias_ref, out_ref, got, rs_send, rs_recv, g_send, g_recv):
    me, peers = col_peers()
    m = len(peers) + 1
    heads_width = x_ref.shape[2]
    copies = []
    for j, peer in enumerate(peers):
        copy = pltpu.make_async_remote_copy(
            src_ref=x_ref.at[peer[2]],
            dst_ref=got.at[j],
            send_sem=rs_send.at[j],
            recv_sem=rs_recv.at[j],
            device_id=peer,
            device_id_type=MESH,
        )
        copy.start()
        copies.append(copy)
    for copy in copies:
        copy.wait()
    chunk = 32
    width = out_ref.shape[2]
    n_chunks = out_ref.shape[1] // chunk
    sends = []
    for i in range(n_chunks):
        rows = pl.ds(i * chunk, chunk)
        total = own_ref[rows, :]
        for j in range(len(copies)):
            source = lax.rem(me + m - 1 - j, m)
            weights = w_ref[pl.ds(pl.multiple_of(source * heads_width, heads_width), heads_width), :]
            total = total + jnp.dot(got[j, rows, :], weights, preferred_element_type=jnp.float32)
        center = total - jnp.sum(total, axis=1, keepdims=True) / width
        spread = jnp.sum(center * center, axis=1, keepdims=True) / width
        normed = center / jnp.sqrt(spread + 1e-05) * gain_ref[...] + bias_ref[...]
        out_ref[me, rows, :] = normed.astype(out_ref.dtype)
        for j, peer in enumerate(peers):
            copy = pltpu.make_async_remote_copy(
                src_ref=out_ref.at[me, rows],
                dst_ref=out_ref.at[me, rows],
                send_sem=g_send.at[j * n_chunks + i],
                recv_sem=g_recv.at[j * n_chunks + i],
                device_id=peer,
                device_id_type=MESH,
            )
            copy.start()
            sends.append(copy)
    for copy in sends:
        copy.wait()


def col_proj_norm_gather(attn_parts, own, w_full, gain, bias):
    m = lax.axis_size("col")
    rows, width = own.shape
    return pl.pallas_call(
        col_proj_kernel,
        out_shape=jax.ShapeDtypeStruct((m, rows, width), jnp.bfloat16),
        in_specs=[pl.BlockSpec(memory_space=pltpu.VMEM)] * 5,
        out_specs=pl.BlockSpec(memory_space=pltpu.VMEM),
        scratch_shapes=[
            pltpu.VMEM((m - 1,) + attn_parts.shape[1:], attn_parts.dtype),
            pltpu.SemaphoreType.DMA((m - 1,)),
            pltpu.SemaphoreType.DMA((m - 1,)),
            pltpu.SemaphoreType.DMA(((m - 1) * (rows // 32),)),
            pltpu.SemaphoreType.DMA(((m - 1) * (rows // 32),)),
        ],
        compiler_params=pltpu.CompilerParams(
            collective_id=10, has_side_effects=True, vmem_limit_bytes=48 * 1024 * 1024
        ),
    )(attn_parts, own, w_full, gain.reshape(1, width), bias.reshape(1, width))


def layer_norm(values, gain, bias):
    center = values - jnp.mean(values, axis=1, keepdims=True)
    spread = jnp.mean(center * center, axis=1, keepdims=True)
    return center * lax.rsqrt(spread + 1e-05) * gain + bias


def per_device(
    hidden_in,
    qkv_weight,
    qkv_global_weight,
    out_weight,
    ln_gain,
    ln_bias,
    ffn_in,
    ffn_out,
    ln2_gain,
    ln2_bias,
    segment_ids,
    global_pos,
    page_owner,
):
    neg = -1e30
    tokens = hidden_in[0]
    shard_len, width = tokens.shape
    heads_here = qkv_weight.shape[1]
    triple = qkv_weight.shape[2]
    head_dim = triple // 3
    n_seq = lax.axis_size("seq")
    n_row = lax.axis_size("row")
    n_col = lax.axis_size("col")
    seq_index = lax.axis_index("seq")
    col_index = lax.axis_index("col")
    base = seq_index * shard_len
    scale = 1.0 / math.sqrt(head_dim)

    all_pos = global_pos[0]
    n_glob = all_pos.shape[0]
    per_shard = n_glob // n_seq
    own_pos = lax.dynamic_slice_in_dim(all_pos, seq_index * per_shard, per_shard, 0)
    local_order = jnp.arange(shard_len, dtype=jnp.int32)
    own_match = (own_pos - base)[:, None] == local_order[None, :]
    picker = own_match.astype(jnp.bfloat16)
    own_rows = jnp.dot(picker, tokens, preferred_element_type=jnp.float32).astype(jnp.bfloat16)
    group = 4 if n_seq % 4 == 0 and n_seq > 4 else 1
    if group > 1:
        glob_rows = seq_gather2(own_rows.reshape(-1, 128), group).reshape(n_glob, width)
    else:
        glob_rows = seq_direct_gather(own_rows.reshape(-1, 128)).reshape(n_glob, width)

    wg_cols = qkv_global_weight.shape[1] * qkv_global_weight.shape[2]
    wg_fin = lax.all_gather(
        jnp.concatenate(
            [qkv_global_weight.reshape(qkv_global_weight.shape[0], wg_cols), ffn_in], axis=1
        ),
        "row",
        axis=0,
        tiled=True,
    )
    w_global = wg_fin[:, :wg_cols]
    f_in = wg_fin[:, wg_cols:]
    f_out = lax.all_gather(ffn_out, "row", axis=1, tiled=True)
    w_out = lax.all_gather(out_weight, "col", axis=0, tiled=True)

    flat_weight = qkv_weight.reshape(width, heads_here * triple)
    qkv = jnp.dot(tokens, flat_weight, preferred_element_type=jnp.float32).astype(jnp.bfloat16)
    qkv_heads = qkv.reshape(shard_len, heads_here, triple)
    queries = qkv_heads[:, :, :head_dim]
    kv_local = qkv_heads[:, :, head_dim:]

    owners = page_owner[0, :, 0]
    n_pages = owners.shape[0]
    page_len = shard_len // n_pages
    capacity = max(2, n_pages // n_seq)
    page_order = jnp.arange(n_pages, dtype=jnp.int32)
    slot = jnp.sum(
        ((owners[:, None] == owners[None, :]) & (page_order[None, :] < page_order[:, None])).astype(
            jnp.int32
        ),
        axis=1,
    )
    target = owners * capacity + slot
    placing = (target[None, :] == jnp.arange(n_seq * capacity, dtype=jnp.int32)[:, None]).astype(
        jnp.bfloat16
    )
    outgoing = jnp.dot(
        placing,
        kv_local.reshape(n_pages, page_len * heads_here * 2 * head_dim),
        preferred_element_type=jnp.float32,
    ).astype(jnp.bfloat16)
    outgoing = outgoing.reshape(n_seq, capacity, page_len, heads_here, 2 * head_dim)
    arrived = lax.all_to_all(outgoing, "seq", split_axis=0, concat_axis=0, tiled=True)
    arrived, glob_rows = lax.optimization_barrier((arrived, glob_rows))
    page_pool = arrived[None, None]

    kv_ext = padded(kv_local, (("seq", 0),), HALF)

    glob_qkv = jnp.dot(glob_rows, flat_weight, preferred_element_type=jnp.float32).astype(
        jnp.bfloat16
    )
    glob_kv = glob_qkv.reshape(n_glob, heads_here, triple)[:, :, head_dim:]
    glob_k = glob_kv[:, :, :head_dim]
    glob_v = glob_kv[:, :, head_dim:]
    glob_q = (
        jnp.dot(glob_rows, w_global, preferred_element_type=jnp.float32)
        .astype(jnp.bfloat16)
        .reshape(n_glob, heads_here, triple)[:, :, :head_dim]
    )
    global_kv_local = (
        jnp.dot(tokens, w_global, preferred_element_type=jnp.float32)
        .astype(jnp.bfloat16)
        .reshape(shard_len, heads_here, triple)[:, :, head_dim:]
    )

    seg_all = segment_ids[0]
    glob_seg = jnp.take(seg_all, all_pos)
    seg_pad = jnp.pad(seg_all, (HALF, HALF), constant_values=-1)
    query_seg = lax.dynamic_slice_in_dim(seg_all, base, shard_len, 0)
    key_seg = lax.dynamic_slice_in_dim(seg_pad, base, shard_len + 2 * HALF, 0)
    key_pos = base - HALF + jnp.arange(shard_len + 2 * HALF, dtype=jnp.int32)
    key_flag = jnp.any(key_pos[:, None] == all_pos[None, :], axis=1)
    query_pos = base + local_order

    s_part = (
        jnp.einsum(
            "ghd,khd->hgk",
            glob_q,
            global_kv_local[:, :, :head_dim],
            preferred_element_type=jnp.float32,
        )
        * scale
    )
    part_mask = glob_seg[:, None] == query_seg[None, :]
    part_top = jnp.max(jnp.where(part_mask, s_part, neg), axis=2)
    e_part = jnp.where(part_mask, jnp.exp(s_part - part_top[:, :, None]), 0.0)
    part_total = jnp.sum(e_part, axis=2)
    part_acc = jnp.einsum(
        "hgk,khd->hgd",
        e_part,
        global_kv_local[:, :, head_dim:].astype(jnp.float32),
        precision=lax.Precision.HIGHEST,
    )
    packed = jnp.concatenate(
        [
            part_acc,
            part_total[:, :, None],
            jnp.broadcast_to(part_top[:, :, None], part_top.shape + (128 - head_dim - 1,)),
        ],
        axis=2,
    )
    packed = jnp.transpose(packed, (1, 0, 2)).reshape(n_glob * heads_here, 128)
    if group > 1:
        merged = seq_merge2(packed.reshape(n_seq, -1, 128), head_dim + 1, group)
    else:
        merged = seq_direct_merge(packed.reshape(n_seq, -1, 128), head_dim + 1)
    merged = merged.reshape(
        per_shard, heads_here, 128
    )
    own_out = jnp.transpose(
        (merged[:, :, :head_dim] / merged[:, :, head_dim : head_dim + 1]).astype(jnp.bfloat16),
        (1, 0, 2),
    )

    glob_mask = query_seg[:, None] == glob_seg[None, :]
    k_blk = kv_ext[:, :, :head_dim]
    v_blk = kv_ext[:, :, head_dim:]
    s_win = jnp.einsum("qhd,khd->hqk", queries, k_blk, preferred_element_type=jnp.float32) * scale
    s_glob = jnp.einsum("qhd,ghd->hqg", queries, glob_k, preferred_element_type=jnp.float32) * scale
    m_win = (
        (jnp.abs(query_pos[:, None] - key_pos[None, :]) <= HALF)
        & (query_seg[:, None] == key_seg[None, :])
        & jnp.logical_not(key_flag[None, :])
    )
    top = jnp.maximum(
        jnp.max(jnp.where(m_win, s_win, neg), axis=2),
        jnp.max(jnp.where(glob_mask, s_glob, neg), axis=2),
    )
    e_win = jnp.where(m_win, jnp.exp(s_win - top[:, :, None]), 0.0)
    e_glob = jnp.where(glob_mask, jnp.exp(s_glob - top[:, :, None]), 0.0)
    total = jnp.sum(e_win, axis=2) + jnp.sum(e_glob, axis=2)
    numer = jnp.einsum(
        "hqk,khd->qhd", e_win.astype(jnp.bfloat16), v_blk, preferred_element_type=jnp.float32
    )
    numer = numer + jnp.einsum(
        "hqg,ghd->qhd", e_glob.astype(jnp.bfloat16), glob_v, preferred_element_type=jnp.float32
    )
    pieces = (numer / jnp.transpose(total)[:, :, None]).astype(jnp.bfloat16)

    placed = jnp.einsum("gt,hgd->thd", picker, own_out, preferred_element_type=jnp.float32).astype(
        jnp.bfloat16
    )
    is_own = jnp.any(own_match, axis=0)
    attention = jnp.where(is_own[:, None, None], placed, pieces).reshape(
        shard_len, heads_here * head_dim
    )


    out_rows = shard_len // n_col
    attn_own = lax.dynamic_slice_in_dim(attention, col_index * out_rows, out_rows, 0)
    token_own = lax.dynamic_slice_in_dim(tokens, col_index * out_rows, out_rows, 0)
    proj_own = jnp.dot(attn_own, out_weight, preferred_element_type=jnp.float32)
    own_sum, w_out = lax.optimization_barrier((token_own.astype(jnp.float32) + proj_own, w_out))
    middle_all = col_proj_norm_gather(
        attention.reshape(n_col, out_rows, heads_here * head_dim),
        own_sum,
        w_out,
        ln_gain,
        ln_bias,
    )
    mine = middle_all[col_index]
    middle = middle_all.reshape(shard_len, width)
    ffn_pre = jnp.dot(middle, f_in, preferred_element_type=jnp.float32)
    ffn_hidden = jax.nn.gelu(ffn_pre, approximate=False).astype(jnp.bfloat16)
    ffn_full = jnp.dot(ffn_hidden, f_out, preferred_element_type=jnp.float32)
    ffn_own = lax.dynamic_slice_in_dim(ffn_full, col_index * out_rows, out_rows, 0)
    second = col_reduce_scatter(
        ffn_full.astype(jnp.bfloat16).reshape(n_col, out_rows, width),
        mine.astype(jnp.float32) + ffn_own,
        6,
    )
    normed = layer_norm(second, ln2_gain, ln2_bias)
    return (normed.astype(jnp.bfloat16)[None], page_pool)


def solution(mesh):
    in_specs = (
        P("row", "seq", None),
        P(None, "col", None),
        P("row", "col", None),
        P("col", None),
        P(),
        P(),
        P("row", "col"),
        P("col", "row"),
        P(),
        P(),
        P("row", None),
        P("row", None),
        P("row", "seq", None),
    )
    out_specs = (P("row", ("seq", "col"), None), P("row", "seq", None, None, None, "col", None))
    return jax.shard_map(
        per_device, mesh=mesh, in_specs=in_specs, out_specs=out_specs, check_vma=False
    )
```

```python
import functools
import math

import jax
import jax.numpy as jnp
from jax import lax
from jax.experimental import pallas as pl
from jax.experimental.pallas import tpu as pltpu
from jax.sharding import PartitionSpec as P

MESH = pl.DeviceIdType.MESH

HALF = 256


def padded(block, sides, width):
    for axis, dim in sides:
        count = lax.axis_size(axis)
        forward = [(i, i + 1) for i in range(count - 1)]
        backward = [(target, source) for source, target in forward]
        low = lax.ppermute(
            lax.slice_in_dim(block, block.shape[dim] - width, None, axis=dim), axis, forward
        )
        high = lax.ppermute(lax.slice_in_dim(block, 0, width, axis=dim), axis, backward)
        block = jnp.concatenate([low, block, high], axis=dim)
    return block


def butterfly_partners(n):
    me = lax.axis_index("seq")
    partners = []
    step = 1
    while step < n:
        bit = (me // step) % 2
        partners.append(me + step - 2 * step * bit)
        step *= 2
    return me, partners


def enter(partners):
    row, col = lax.axis_index("row"), lax.axis_index("col")
    barrier = pltpu.get_barrier_semaphore()
    for partner in partners:
        pl.semaphore_signal(barrier, inc=1, device_id=(partner, row, col), device_id_type=MESH)
    pl.semaphore_wait(barrier, len(partners))
    return row, col


def gather_kernel(n, x_ref, out_ref, self_sem, send_sem, recv_sem):
    me, partners = butterfly_partners(n)
    row, col = enter(partners)
    own = pltpu.make_async_copy(x_ref, out_ref.at[me], self_sem)
    own.start()
    own.wait()
    size = 1
    for k, partner in enumerate(partners):
        start = (me // size) * size
        copy = pltpu.make_async_remote_copy(
            src_ref=out_ref.at[pl.ds(start, size)],
            dst_ref=out_ref.at[pl.ds(start, size)],
            send_sem=send_sem.at[k],
            recv_sem=recv_sem.at[k],
            device_id=(partner, row, col),
            device_id_type=MESH,
        )
        copy.start()
        copy.wait()
        size *= 2


def seq_gather(block):
    n = lax.axis_size("seq")
    rounds = n.bit_length() - 1
    return pl.pallas_call(
        functools.partial(gather_kernel, n),
        out_shape=jax.ShapeDtypeStruct((n,) + block.shape, block.dtype),
        in_specs=[pl.BlockSpec(memory_space=pltpu.VMEM)],
        out_specs=pl.BlockSpec(memory_space=pltpu.VMEM),
        scratch_shapes=[
            pltpu.SemaphoreType.DMA(()),
            pltpu.SemaphoreType.DMA((rounds,)),
            pltpu.SemaphoreType.DMA((rounds,)),
        ],
        compiler_params=pltpu.CompilerParams(collective_id=0, has_side_effects=True),
    )(block)


def merge_parts(mine, theirs, top_lane):
    lane = lax.broadcasted_iota(jnp.int32, mine.shape, 1)
    is_top = lane == top_lane
    top_a = jnp.max(jnp.where(is_top, mine, -jnp.inf), axis=1, keepdims=True)
    top_b = jnp.max(jnp.where(is_top, theirs, -jnp.inf), axis=1, keepdims=True)
    top = jnp.maximum(top_a, top_b)
    merged = mine * jnp.exp(top_a - top) + theirs * jnp.exp(top_b - top)
    return jnp.where(is_top, top, merged)


def halving_kernel(n, top_lane, x_ref, out_ref, *scratch):
    rounds = len(scratch) // 3
    kept, got, sems = scratch[:rounds], scratch[rounds : 2 * rounds], scratch[2 * rounds :]
    me = lax.axis_index("seq")
    steps = []
    step = n // 2
    while step >= 1:
        bit = (me // step) % 2
        steps.append((me + step - 2 * step * bit, bit))
        step //= 2
    row, col = enter([partner for partner, _ in steps])
    source = x_ref
    for k, (partner, bit) in enumerate(steps):
        half = source.shape[0] // 2
        send_at = pl.multiple_of((1 - bit) * half, 8)
        keep_at = pl.multiple_of(bit * half, 8)
        copy = pltpu.make_async_remote_copy(
            src_ref=source.at[pl.ds(send_at, half)],
            dst_ref=got[k],
            send_sem=sems[k].at[0],
            recv_sem=sems[k].at[1],
            device_id=(partner, row, col),
            device_id_type=MESH,
        )
        copy.start()
        copy.wait()
        value = merge_parts(source[pl.ds(keep_at, half)], got[k][...], top_lane)
        if k + 1 < rounds:
            kept[k][...] = value
            source = kept[k]
        else:
            out_ref[...] = value


def seq_softmax_combine(parts, top_lane):
    n = lax.axis_size("seq")
    rounds = n.bit_length() - 1
    rows, lanes = parts.shape
    scratch = []
    for k in range(rounds):
        scratch.append(pltpu.VMEM((rows >> (k + 1), lanes), parts.dtype))
    for k in range(rounds):
        scratch.append(pltpu.VMEM((rows >> (k + 1), lanes), parts.dtype))
    for k in range(rounds):
        scratch.append(pltpu.SemaphoreType.DMA((2,)))
    return pl.pallas_call(
        functools.partial(halving_kernel, n, top_lane),
        out_shape=jax.ShapeDtypeStruct((rows // n, lanes), parts.dtype),
        in_specs=[pl.BlockSpec(memory_space=pltpu.VMEM)],
        out_specs=pl.BlockSpec(memory_space=pltpu.VMEM),
        scratch_shapes=scratch,
        compiler_params=pltpu.CompilerParams(collective_id=1, has_side_effects=True),
    )(parts)


def seq_peers():
    me, n = lax.axis_index("seq"), lax.axis_size("seq")
    row, col = lax.axis_index("row"), lax.axis_index("col")
    peers = [lax.rem(me + j, n) for j in range(1, n)]
    barrier = pltpu.get_barrier_semaphore()
    for peer in peers:
        pl.semaphore_signal(barrier, inc=1, device_id=(peer, row, col), device_id_type=MESH)
    pl.semaphore_wait(barrier, len(peers))
    return me, [(peer, row, col) for peer in peers]


def seq_direct_gather_kernel(x_ref, out_ref, self_sem, send_sem, recv_sem):
    me, peers = seq_peers()
    own = pltpu.make_async_copy(x_ref, out_ref.at[me], self_sem)
    own.start()
    copies = []
    for j, peer in enumerate(peers):
        copy = pltpu.make_async_remote_copy(
            src_ref=x_ref,
            dst_ref=out_ref.at[me],
            send_sem=send_sem.at[j],
            recv_sem=recv_sem.at[j],
            device_id=peer,
            device_id_type=MESH,
        )
        copy.start()
        copies.append(copy)
    own.wait()
    for copy in copies:
        copy.wait()


def seq_direct_gather(block):
    n = lax.axis_size("seq")
    return pl.pallas_call(
        seq_direct_gather_kernel,
        out_shape=jax.ShapeDtypeStruct((n,) + block.shape, block.dtype),
        in_specs=[pl.BlockSpec(memory_space=pltpu.VMEM)],
        out_specs=pl.BlockSpec(memory_space=pltpu.VMEM),
        scratch_shapes=[
            pltpu.SemaphoreType.DMA(()),
            pltpu.SemaphoreType.DMA((n - 1,)),
            pltpu.SemaphoreType.DMA((n - 1,)),
        ],
        compiler_params=pltpu.CompilerParams(collective_id=4, has_side_effects=True),
    )(block)


def seq_merge_kernel(top_lane, x_ref, out_ref, got, send_sem, recv_sem):
    me, peers = seq_peers()
    copies = []
    for j, peer in enumerate(peers):
        copy = pltpu.make_async_remote_copy(
            src_ref=x_ref.at[peer[0]],
            dst_ref=got.at[j],
            send_sem=send_sem.at[j],
            recv_sem=recv_sem.at[j],
            device_id=peer,
            device_id_type=MESH,
        )
        copy.start()
        copies.append(copy)
    for copy in copies:
        copy.wait()
    value = x_ref[me]
    for j in range(len(copies)):
        value = merge_parts(value, got[j], top_lane)
    out_ref[...] = value


def seq_direct_merge(parts, top_lane):
    n = parts.shape[0]
    return pl.pallas_call(
        functools.partial(seq_merge_kernel, top_lane),
        out_shape=jax.ShapeDtypeStruct(parts.shape[1:], parts.dtype),
        in_specs=[pl.BlockSpec(memory_space=pltpu.VMEM)],
        out_specs=pl.BlockSpec(memory_space=pltpu.VMEM),
        scratch_shapes=[
            pltpu.VMEM((n - 1,) + parts.shape[1:], parts.dtype),
            pltpu.SemaphoreType.DMA((n - 1,)),
            pltpu.SemaphoreType.DMA((n - 1,)),
        ],
        compiler_params=pltpu.CompilerParams(collective_id=5, has_side_effects=True),
    )(parts)


def seq_two_level_peers(group):
    me, n = lax.axis_index("seq"), lax.axis_size("seq")
    row, col = lax.axis_index("row"), lax.axis_index("col")
    first = (me // group) * group
    near = [first + lax.rem(me - first + j, group) for j in range(1, group)]
    far = [lax.rem(me + group * j, n) for j in range(1, n // group)]
    barrier = pltpu.get_barrier_semaphore()
    for peer in near + far:
        pl.semaphore_signal(barrier, inc=1, device_id=(peer, row, col), device_id_type=MESH)
    pl.semaphore_wait(barrier, len(near) + len(far))
    return me, first, [(p, row, col) for p in near], [(p, row, col) for p in far]


def seq_gather2_kernel(group, x_ref, out_ref, self_sem, near_send, near_recv, far_send, far_recv):
    me, first, near, far = seq_two_level_peers(group)
    own = pltpu.make_async_copy(x_ref, out_ref.at[me], self_sem)
    own.start()
    copies = []
    for j, peer in enumerate(near):
        copy = pltpu.make_async_remote_copy(
            src_ref=x_ref,
            dst_ref=out_ref.at[me],
            send_sem=near_send.at[j],
            recv_sem=near_recv.at[j],
            device_id=peer,
            device_id_type=MESH,
        )
        copy.start()
        copies.append(copy)
    own.wait()
    for copy in copies:
        copy.wait()
    block = out_ref.at[pl.ds(first, group)]
    copies = []
    for j, peer in enumerate(far):
        copy = pltpu.make_async_remote_copy(
            src_ref=block,
            dst_ref=block,
            send_sem=far_send.at[j],
            recv_sem=far_recv.at[j],
            device_id=peer,
            device_id_type=MESH,
        )
        copy.start()
        copies.append(copy)
    for copy in copies:
        copy.wait()


def seq_gather2(block, group):
    n = lax.axis_size("seq")
    return pl.pallas_call(
        functools.partial(seq_gather2_kernel, group),
        out_shape=jax.ShapeDtypeStruct((n,) + block.shape, block.dtype),
        in_specs=[pl.BlockSpec(memory_space=pltpu.VMEM)],
        out_specs=pl.BlockSpec(memory_space=pltpu.VMEM),
        scratch_shapes=[
            pltpu.SemaphoreType.DMA(()),
            pltpu.SemaphoreType.DMA((group - 1,)),
            pltpu.SemaphoreType.DMA((group - 1,)),
            pltpu.SemaphoreType.DMA((n // group - 1,)),
            pltpu.SemaphoreType.DMA((n // group - 1,)),
        ],
        compiler_params=pltpu.CompilerParams(collective_id=8, has_side_effects=True),
    )(block)


def seq_merge2_kernel(
    group, top_lane, x_ref, out_ref, got_far, partial, got_near, far_send, far_recv, near_send, near_recv
):
    me, first, near, far = seq_two_level_peers(group)
    copies = []
    for j, peer in enumerate(far):
        start = pl.multiple_of((peer[0] // group) * group, group)
        copy = pltpu.make_async_remote_copy(
            src_ref=x_ref.at[pl.ds(start, group)],
            dst_ref=got_far.at[j],
            send_sem=far_send.at[j],
            recv_sem=far_recv.at[j],
            device_id=peer,
            device_id_type=MESH,
        )
        copy.start()
        copies.append(copy)
    for copy in copies:
        copy.wait()
    for k in range(group):
        value = x_ref[first + k]
        for j in range(len(far)):
            value = merge_parts(value, got_far[j, k], top_lane)
        partial[k] = value
    copies = []
    for j, peer in enumerate(near):
        copy = pltpu.make_async_remote_copy(
            src_ref=partial.at[peer[0] - first],
            dst_ref=got_near.at[j],
            send_sem=near_send.at[j],
            recv_sem=near_recv.at[j],
            device_id=peer,
            device_id_type=MESH,
        )
        copy.start()
        copies.append(copy)
    for copy in copies:
        copy.wait()
    value = partial[me - first]
    for j in range(len(near)):
        value = merge_parts(value, got_near[j], top_lane)
    out_ref[...] = value


def seq_merge2(parts, top_lane, group):
    n = parts.shape[0]
    blk = parts.shape[1:]
    return pl.pallas_call(
        functools.partial(seq_merge2_kernel, group, top_lane),
        out_shape=jax.ShapeDtypeStruct(blk, parts.dtype),
        in_specs=[pl.BlockSpec(memory_space=pltpu.VMEM)],
        out_specs=pl.BlockSpec(memory_space=pltpu.VMEM),
        scratch_shapes=[
            pltpu.VMEM((n // group - 1, group) + blk, parts.dtype),
            pltpu.VMEM((group,) + blk, parts.dtype),
            pltpu.VMEM((group - 1,) + blk, parts.dtype),
            pltpu.SemaphoreType.DMA((n // group - 1,)),
            pltpu.SemaphoreType.DMA((n // group - 1,)),
            pltpu.SemaphoreType.DMA((group - 1,)),
            pltpu.SemaphoreType.DMA((group - 1,)),
        ],
        compiler_params=pltpu.CompilerParams(collective_id=9, has_side_effects=True),
    )(parts)


def col_peers():
    me, m = lax.axis_index("col"), lax.axis_size("col")
    seq, row = lax.axis_index("seq"), lax.axis_index("row")
    peers = [lax.rem(me + j, m) for j in range(1, m)]
    barrier = pltpu.get_barrier_semaphore()
    for peer in peers:
        pl.semaphore_signal(barrier, inc=1, device_id=(seq, row, peer), device_id_type=MESH)
    pl.semaphore_wait(barrier, len(peers))
    return me, [(seq, row, peer) for peer in peers]


def col_gather_kernel(x_ref, out_ref, self_sem, send_sem, recv_sem):
    me, peers = col_peers()
    own = pltpu.make_async_copy(x_ref, out_ref.at[me], self_sem)
    own.start()
    copies = []
    for j, peer in enumerate(peers):
        copy = pltpu.make_async_remote_copy(
            src_ref=x_ref,
            dst_ref=out_ref.at[me],
            send_sem=send_sem.at[j],
            recv_sem=recv_sem.at[j],
            device_id=peer,
            device_id_type=MESH,
        )
        copy.start()
        copies.append(copy)
    own.wait()
    for copy in copies:
        copy.wait()


def col_gather(block):
    m = lax.axis_size("col")
    return pl.pallas_call(
        col_gather_kernel,
        out_shape=jax.ShapeDtypeStruct((m,) + block.shape, block.dtype),
        in_specs=[pl.BlockSpec(memory_space=pltpu.VMEM)],
        out_specs=pl.BlockSpec(memory_space=pltpu.VMEM),
        scratch_shapes=[
            pltpu.SemaphoreType.DMA(()),
            pltpu.SemaphoreType.DMA((m - 1,)),
            pltpu.SemaphoreType.DMA((m - 1,)),
        ],
        compiler_params=pltpu.CompilerParams(collective_id=2, has_side_effects=True),
    )(block)


def col_sum_kernel(x_ref, own_ref, out_ref, got, send_sem, recv_sem):
    me, peers = col_peers()
    copies = []
    for j, peer in enumerate(peers):
        copy = pltpu.make_async_remote_copy(
            src_ref=x_ref.at[peer[2]],
            dst_ref=got.at[j],
            send_sem=send_sem.at[j],
            recv_sem=recv_sem.at[j],
            device_id=peer,
            device_id_type=MESH,
        )
        copy.start()
        copies.append(copy)
    for copy in copies:
        copy.wait()
    chunk = 32

    def body(i, carry):
        rows = pl.ds(pl.multiple_of(i * chunk, chunk), chunk)
        total = own_ref[rows, :]
        for j in range(len(copies)):
            total = total + got[j, rows, :].astype(jnp.float32)
        out_ref[rows, :] = total
        return carry

    lax.fori_loop(0, out_ref.shape[0] // chunk, body, 0)


def col_reduce_scatter(parts, own, collective_id):
    m = lax.axis_size("col")
    return pl.pallas_call(
        col_sum_kernel,
        out_shape=jax.ShapeDtypeStruct(own.shape, jnp.float32),
        in_specs=[pl.BlockSpec(memory_space=pltpu.VMEM)] * 2,
        out_specs=pl.BlockSpec(memory_space=pltpu.VMEM),
        scratch_shapes=[
            pltpu.VMEM((m - 1,) + parts.shape[1:], parts.dtype),
            pltpu.SemaphoreType.DMA((m - 1,)),
            pltpu.SemaphoreType.DMA((m - 1,)),
        ],
        compiler_params=pltpu.CompilerParams(collective_id=collective_id, has_side_effects=True),
    )(parts, own)


def col_mid_kernel(x_ref, own_ref, gain_ref, bias_ref, out_ref, got, rs_send, rs_recv, g_send, g_recv):
    me, peers = col_peers()
    copies = []
    for j, peer in enumerate(peers):
        copy = pltpu.make_async_remote_copy(
            src_ref=x_ref.at[peer[2]],
            dst_ref=got.at[j],
            send_sem=rs_send.at[j],
            recv_sem=rs_recv.at[j],
            device_id=peer,
            device_id_type=MESH,
        )
        copy.start()
        copies.append(copy)
    for copy in copies:
        copy.wait()
    chunk = 32
    width = out_ref.shape[2]

    def body(i, carry):
        rows = pl.ds(pl.multiple_of(i * chunk, chunk), chunk)
        total = own_ref[rows, :]
        for j in range(len(copies)):
            total = total + got[j, rows, :].astype(jnp.float32)
        center = total - jnp.sum(total, axis=1, keepdims=True) / width
        spread = jnp.sum(center * center, axis=1, keepdims=True) / width
        normed = center / jnp.sqrt(spread + 1e-05) * gain_ref[...] + bias_ref[...]
        out_ref[me, rows, :] = normed.astype(out_ref.dtype)
        return carry

    lax.fori_loop(0, out_ref.shape[1] // chunk, body, 0)
    sends = []
    for j, peer in enumerate(peers):
        copy = pltpu.make_async_remote_copy(
            src_ref=out_ref.at[me],
            dst_ref=out_ref.at[me],
            send_sem=g_send.at[j],
            recv_sem=g_recv.at[j],
            device_id=peer,
            device_id_type=MESH,
        )
        copy.start()
        sends.append(copy)
    for copy in sends:
        copy.wait()


def col_sum_norm_gather(parts, own, gain, bias):
    m = lax.axis_size("col")
    rows, width = own.shape
    return pl.pallas_call(
        col_mid_kernel,
        out_shape=jax.ShapeDtypeStruct((m, rows, width), jnp.bfloat16),
        in_specs=[pl.BlockSpec(memory_space=pltpu.VMEM)] * 4,
        out_specs=pl.BlockSpec(memory_space=pltpu.VMEM),
        scratch_shapes=[
            pltpu.VMEM((m - 1,) + parts.shape[1:], parts.dtype),
            pltpu.SemaphoreType.DMA((m - 1,)),
            pltpu.SemaphoreType.DMA((m - 1,)),
            pltpu.SemaphoreType.DMA((m - 1,)),
            pltpu.SemaphoreType.DMA((m - 1,)),
        ],
        compiler_params=pltpu.CompilerParams(collective_id=7, has_side_effects=True),
    )(parts, own, gain.reshape(1, width), bias.reshape(1, width))


def col_proj_kernel(x_ref, own_ref, w_ref, gain_ref, bias_ref, out_ref, got, rs_send, rs_recv, g_send, g_recv):
    me, peers = col_peers()
    m = len(peers) + 1
    heads_width = x_ref.shape[2]
    copies = []
    for j, peer in enumerate(peers):
        copy = pltpu.make_async_remote_copy(
            src_ref=x_ref.at[peer[2]],
            dst_ref=got.at[j],
            send_sem=rs_send.at[j],
            recv_sem=rs_recv.at[j],
            device_id=peer,
            device_id_type=MESH,
        )
        copy.start()
        copies.append(copy)
    for copy in copies:
        copy.wait()
    chunk = 32
    width = out_ref.shape[2]
    n_chunks = out_ref.shape[1] // chunk
    sends = []
    for i in range(n_chunks):
        rows = pl.ds(i * chunk, chunk)
        total = own_ref[rows, :]
        for j in range(len(copies)):
            source = lax.rem(me + m - 1 - j, m)
            weights = w_ref[pl.ds(pl.multiple_of(source * heads_width, heads_width), heads_width), :]
            total = total + jnp.dot(got[j, rows, :], weights, preferred_element_type=jnp.float32)
        center = total - jnp.sum(total, axis=1, keepdims=True) / width
        spread = jnp.sum(center * center, axis=1, keepdims=True) / width
        normed = center / jnp.sqrt(spread + 1e-05) * gain_ref[...] + bias_ref[...]
        out_ref[me, rows, :] = normed.astype(out_ref.dtype)
        for j, peer in enumerate(peers):
            copy = pltpu.make_async_remote_copy(
                src_ref=out_ref.at[me, rows],
                dst_ref=out_ref.at[me, rows],
                send_sem=g_send.at[j * n_chunks + i],
                recv_sem=g_recv.at[j * n_chunks + i],
                device_id=peer,
                device_id_type=MESH,
            )
            copy.start()
            sends.append(copy)
    for copy in sends:
        copy.wait()


def col_proj_norm_gather(attn_parts, own, w_full, gain, bias):
    m = lax.axis_size("col")
    rows, width = own.shape
    return pl.pallas_call(
        col_proj_kernel,
        out_shape=jax.ShapeDtypeStruct((m, rows, width), jnp.bfloat16),
        in_specs=[pl.BlockSpec(memory_space=pltpu.VMEM)] * 5,
        out_specs=pl.BlockSpec(memory_space=pltpu.VMEM),
        scratch_shapes=[
            pltpu.VMEM((m - 1,) + attn_parts.shape[1:], attn_parts.dtype),
            pltpu.SemaphoreType.DMA((m - 1,)),
            pltpu.SemaphoreType.DMA((m - 1,)),
            pltpu.SemaphoreType.DMA(((m - 1) * (rows // 32),)),
            pltpu.SemaphoreType.DMA(((m - 1) * (rows // 32),)),
        ],
        compiler_params=pltpu.CompilerParams(
            collective_id=10, has_side_effects=True, vmem_limit_bytes=48 * 1024 * 1024
        ),
    )(attn_parts, own, w_full, gain.reshape(1, width), bias.reshape(1, width))


def col_sum_ln_kernel(x_ref, own_ref, gain_ref, bias_ref, out_ref, got, send_sem, recv_sem):
    me, peers = col_peers()
    copies = []
    for j, peer in enumerate(peers):
        copy = pltpu.make_async_remote_copy(
            src_ref=x_ref.at[peer[2]],
            dst_ref=got.at[j],
            send_sem=send_sem.at[j],
            recv_sem=recv_sem.at[j],
            device_id=peer,
            device_id_type=MESH,
        )
        copy.start()
        copies.append(copy)
    for copy in copies:
        copy.wait()
    chunk = 32
    width = out_ref.shape[1]

    def body(i, carry):
        rows = pl.ds(pl.multiple_of(i * chunk, chunk), chunk)
        total = own_ref[rows, :]
        for j in range(len(copies)):
            total = total + got[j, rows, :].astype(jnp.float32)
        center = total - jnp.sum(total, axis=1, keepdims=True) / width
        spread = jnp.sum(center * center, axis=1, keepdims=True) / width
        normed = center / jnp.sqrt(spread + 1e-05) * gain_ref[...] + bias_ref[...]
        out_ref[rows, :] = normed.astype(out_ref.dtype)
        return carry

    lax.fori_loop(0, out_ref.shape[0] // chunk, body, 0)


def col_sum_norm(parts, own, gain, bias):
    m = lax.axis_size("col")
    rows, width = own.shape
    return pl.pallas_call(
        col_sum_ln_kernel,
        out_shape=jax.ShapeDtypeStruct(own.shape, jnp.bfloat16),
        in_specs=[pl.BlockSpec(memory_space=pltpu.VMEM)] * 4,
        out_specs=pl.BlockSpec(memory_space=pltpu.VMEM),
        scratch_shapes=[
            pltpu.VMEM((m - 1,) + parts.shape[1:], parts.dtype),
            pltpu.SemaphoreType.DMA((m - 1,)),
            pltpu.SemaphoreType.DMA((m - 1,)),
        ],
        compiler_params=pltpu.CompilerParams(collective_id=11, has_side_effects=True),
    )(parts, own, gain.reshape(1, width), bias.reshape(1, width))


def layer_norm(values, gain, bias):
    center = values - jnp.mean(values, axis=1, keepdims=True)
    spread = jnp.mean(center * center, axis=1, keepdims=True)
    return center * lax.rsqrt(spread + 1e-05) * gain + bias


def per_device(
    hidden_in,
    qkv_weight,
    qkv_global_weight,
    out_weight,
    ln_gain,
    ln_bias,
    ffn_in,
    ffn_out,
    ln2_gain,
    ln2_bias,
    segment_ids,
    global_pos,
    page_owner,
):
    neg = -1e30
    tokens = hidden_in[0]
    shard_len, width = tokens.shape
    heads_here = qkv_weight.shape[1]
    triple = qkv_weight.shape[2]
    head_dim = triple // 3
    n_seq = lax.axis_size("seq")
    n_row = lax.axis_size("row")
    n_col = lax.axis_size("col")
    seq_index = lax.axis_index("seq")
    col_index = lax.axis_index("col")
    base = seq_index * shard_len
    scale = 1.0 / math.sqrt(head_dim)

    all_pos = global_pos[0]
    n_glob = all_pos.shape[0]
    per_shard = n_glob // n_seq
    own_pos = lax.dynamic_slice_in_dim(all_pos, seq_index * per_shard, per_shard, 0)
    local_order = jnp.arange(shard_len, dtype=jnp.int32)
    own_match = (own_pos - base)[:, None] == local_order[None, :]
    picker = own_match.astype(jnp.bfloat16)
    own_rows = jnp.dot(picker, tokens, preferred_element_type=jnp.float32).astype(jnp.bfloat16)
    group = 4 if n_seq % 4 == 0 and n_seq > 4 else 1
    if group > 1:
        glob_rows = seq_gather2(own_rows.reshape(-1, 128), group).reshape(n_glob, width)
    else:
        glob_rows = seq_direct_gather(own_rows.reshape(-1, 128)).reshape(n_glob, width)

    wg_cols = qkv_global_weight.shape[1] * qkv_global_weight.shape[2]
    wg_fin = lax.all_gather(
        jnp.concatenate(
            [qkv_global_weight.reshape(qkv_global_weight.shape[0], wg_cols), ffn_in], axis=1
        ),
        "row",
        axis=0,
        tiled=True,
    )
    w_global = wg_fin[:, :wg_cols]
    f_in = wg_fin[:, wg_cols:]
    f_out = lax.all_gather(ffn_out, "row", axis=1, tiled=True)
    w_out = lax.all_gather(out_weight, "col", axis=0, tiled=True)

    flat_weight = qkv_weight.reshape(width, heads_here * triple)
    qkv = jnp.dot(tokens, flat_weight, preferred_element_type=jnp.float32).astype(jnp.bfloat16)
    qkv_heads = qkv.reshape(shard_len, heads_here, triple)
    queries = qkv_heads[:, :, :head_dim]
    kv_local = qkv_heads[:, :, head_dim:]

    owners = page_owner[0, :, 0]
    n_pages = owners.shape[0]
    page_len = shard_len // n_pages
    capacity = max(2, n_pages // n_seq)
    page_order = jnp.arange(n_pages, dtype=jnp.int32)
    slot = jnp.sum(
        ((owners[:, None] == owners[None, :]) & (page_order[None, :] < page_order[:, None])).astype(
            jnp.int32
        ),
        axis=1,
    )
    target = owners * capacity + slot
    placing = (target[None, :] == jnp.arange(n_seq * capacity, dtype=jnp.int32)[:, None]).astype(
        jnp.bfloat16
    )
    outgoing = jnp.dot(
        placing,
        kv_local.reshape(n_pages, page_len * heads_here * 2 * head_dim),
        preferred_element_type=jnp.float32,
    ).astype(jnp.bfloat16)
    outgoing = outgoing.reshape(n_seq, capacity, page_len, heads_here, 2 * head_dim)
    arrived = lax.all_to_all(outgoing, "seq", split_axis=0, concat_axis=0, tiled=True)
    arrived, glob_rows = lax.optimization_barrier((arrived, glob_rows))
    page_pool = arrived[None, None]

    kv_ext = padded(kv_local, (("seq", 0),), HALF)

    glob_qkv = jnp.dot(glob_rows, flat_weight, preferred_element_type=jnp.float32).astype(
        jnp.bfloat16
    )
    glob_kv = glob_qkv.reshape(n_glob, heads_here, triple)[:, :, head_dim:]
    glob_k = glob_kv[:, :, :head_dim]
    glob_v = glob_kv[:, :, head_dim:]
    glob_q = (
        jnp.dot(glob_rows, w_global, preferred_element_type=jnp.float32)
        .astype(jnp.bfloat16)
        .reshape(n_glob, heads_here, triple)[:, :, :head_dim]
    )
    global_kv_local = (
        jnp.dot(tokens, w_global, preferred_element_type=jnp.float32)
        .astype(jnp.bfloat16)
        .reshape(shard_len, heads_here, triple)[:, :, head_dim:]
    )

    seg_all = segment_ids[0]
    glob_seg = jnp.take(seg_all, all_pos)
    seg_pad = jnp.pad(seg_all, (HALF, HALF), constant_values=-1)
    query_seg = lax.dynamic_slice_in_dim(seg_all, base, shard_len, 0)
    key_seg = lax.dynamic_slice_in_dim(seg_pad, base, shard_len + 2 * HALF, 0)
    key_pos = base - HALF + jnp.arange(shard_len + 2 * HALF, dtype=jnp.int32)
    key_flag = jnp.any(key_pos[:, None] == all_pos[None, :], axis=1)
    query_pos = base + local_order

    s_part = (
        jnp.einsum(
            "ghd,khd->hgk",
            glob_q,
            global_kv_local[:, :, :head_dim],
            preferred_element_type=jnp.float32,
        )
        * scale
    )
    part_mask = glob_seg[:, None] == query_seg[None, :]
    part_top = jnp.max(jnp.where(part_mask, s_part, neg), axis=2)
    e_part = jnp.where(part_mask, jnp.exp(s_part - part_top[:, :, None]), 0.0)
    part_total = jnp.sum(e_part, axis=2)
    part_acc = jnp.einsum(
        "hgk,khd->hgd",
        e_part,
        global_kv_local[:, :, head_dim:].astype(jnp.float32),
        precision=lax.Precision.HIGHEST,
    )
    packed = jnp.concatenate(
        [
            part_acc,
            part_total[:, :, None],
            jnp.broadcast_to(part_top[:, :, None], part_top.shape + (128 - head_dim - 1,)),
        ],
        axis=2,
    )
    packed = jnp.transpose(packed, (1, 0, 2)).reshape(n_glob * heads_here, 128)
    if group > 1:
        merged = seq_merge2(packed.reshape(n_seq, -1, 128), head_dim + 1, group)
    else:
        merged = seq_direct_merge(packed.reshape(n_seq, -1, 128), head_dim + 1)
    merged = merged.reshape(
        per_shard, heads_here, 128
    )
    own_out = jnp.transpose(
        (merged[:, :, :head_dim] / merged[:, :, head_dim : head_dim + 1]).astype(jnp.bfloat16),
        (1, 0, 2),
    )

    glob_mask = query_seg[:, None] == glob_seg[None, :]
    k_blk = kv_ext[:, :, :head_dim]
    v_blk = kv_ext[:, :, head_dim:]
    s_win = jnp.einsum("qhd,khd->hqk", queries, k_blk, preferred_element_type=jnp.float32) * scale
    s_glob = jnp.einsum("qhd,ghd->hqg", queries, glob_k, preferred_element_type=jnp.float32) * scale
    m_win = (
        (jnp.abs(query_pos[:, None] - key_pos[None, :]) <= HALF)
        & (query_seg[:, None] == key_seg[None, :])
        & jnp.logical_not(key_flag[None, :])
    )
    top = jnp.maximum(
        jnp.max(jnp.where(m_win, s_win, neg), axis=2),
        jnp.max(jnp.where(glob_mask, s_glob, neg), axis=2),
    )
    e_win = jnp.where(m_win, jnp.exp(s_win - top[:, :, None]), 0.0)
    e_glob = jnp.where(glob_mask, jnp.exp(s_glob - top[:, :, None]), 0.0)
    total = jnp.sum(e_win, axis=2) + jnp.sum(e_glob, axis=2)
    numer = jnp.einsum(
        "hqk,khd->qhd", e_win.astype(jnp.bfloat16), v_blk, preferred_element_type=jnp.float32
    )
    numer = numer + jnp.einsum(
        "hqg,ghd->qhd", e_glob.astype(jnp.bfloat16), glob_v, preferred_element_type=jnp.float32
    )
    pieces = (numer / jnp.transpose(total)[:, :, None]).astype(jnp.bfloat16)

    placed = jnp.einsum("gt,hgd->thd", picker, own_out, preferred_element_type=jnp.float32).astype(
        jnp.bfloat16
    )
    is_own = jnp.any(own_match, axis=0)
    attention = jnp.where(is_own[:, None, None], placed, pieces).reshape(
        shard_len, heads_here * head_dim
    )


    out_rows = shard_len // n_col
    attn_own = lax.dynamic_slice_in_dim(attention, col_index * out_rows, out_rows, 0)
    token_own = lax.dynamic_slice_in_dim(tokens, col_index * out_rows, out_rows, 0)
    proj_own = jnp.dot(attn_own, out_weight, preferred_element_type=jnp.float32)
    own_sum, w_out = lax.optimization_barrier((token_own.astype(jnp.float32) + proj_own, w_out))
    middle_all = col_proj_norm_gather(
        attention.reshape(n_col, out_rows, heads_here * head_dim),
        own_sum,
        w_out,
        ln_gain,
        ln_bias,
    )
    mine = middle_all[col_index]
    middle = middle_all.reshape(shard_len, width)
    ffn_pre = jnp.dot(middle, f_in, preferred_element_type=jnp.float32)
    ffn_hidden = jax.nn.gelu(ffn_pre, approximate=False).astype(jnp.bfloat16)
    ffn_full = jnp.dot(ffn_hidden, f_out, preferred_element_type=jnp.float32)
    ffn_own = lax.dynamic_slice_in_dim(ffn_full, col_index * out_rows, out_rows, 0)
    normed = col_sum_norm(
        ffn_full.astype(jnp.bfloat16).reshape(n_col, out_rows, width),
        mine.astype(jnp.float32) + ffn_own,
        ln2_gain,
        ln2_bias,
    )
    return (normed[None], page_pool)


def solution(mesh):
    in_specs = (
        P("row", "seq", None),
        P(None, "col", None),
        P("row", "col", None),
        P("col", None),
        P(),
        P(),
        P("row", "col"),
        P("col", "row"),
        P(),
        P(),
        P("row", None),
        P("row", None),
        P("row", "seq", None),
    )
    out_specs = (P("row", ("seq", "col"), None), P("row", "seq", None, None, None, "col", None))
    return jax.shard_map(
        per_device, mesh=mesh, in_specs=in_specs, out_specs=out_specs, check_vma=False
    )
```

```python
import functools
import math

import jax
import jax.numpy as jnp
from jax import lax
from jax.experimental import pallas as pl
from jax.experimental.pallas import tpu as pltpu
from jax.sharding import PartitionSpec as P

MESH = pl.DeviceIdType.MESH

HALF = 256


def padded(block, sides, width):
    for axis, dim in sides:
        count = lax.axis_size(axis)
        forward = [(i, i + 1) for i in range(count - 1)]
        backward = [(target, source) for source, target in forward]
        low = lax.ppermute(
            lax.slice_in_dim(block, block.shape[dim] - width, None, axis=dim), axis, forward
        )
        high = lax.ppermute(lax.slice_in_dim(block, 0, width, axis=dim), axis, backward)
        block = jnp.concatenate([low, block, high], axis=dim)
    return block


def butterfly_partners(n):
    me = lax.axis_index("seq")
    partners = []
    step = 1
    while step < n:
        bit = (me // step) % 2
        partners.append(me + step - 2 * step * bit)
        step *= 2
    return me, partners


def enter(partners):
    row, col = lax.axis_index("row"), lax.axis_index("col")
    barrier = pltpu.get_barrier_semaphore()
    for partner in partners:
        pl.semaphore_signal(barrier, inc=1, device_id=(partner, row, col), device_id_type=MESH)
    pl.semaphore_wait(barrier, len(partners))
    return row, col


def gather_kernel(n, x_ref, out_ref, self_sem, send_sem, recv_sem):
    me, partners = butterfly_partners(n)
    row, col = enter(partners)
    own = pltpu.make_async_copy(x_ref, out_ref.at[me], self_sem)
    own.start()
    own.wait()
    size = 1
    for k, partner in enumerate(partners):
        start = (me // size) * size
        copy = pltpu.make_async_remote_copy(
            src_ref=out_ref.at[pl.ds(start, size)],
            dst_ref=out_ref.at[pl.ds(start, size)],
            send_sem=send_sem.at[k],
            recv_sem=recv_sem.at[k],
            device_id=(partner, row, col),
            device_id_type=MESH,
        )
        copy.start()
        copy.wait()
        size *= 2


def seq_gather(block):
    n = lax.axis_size("seq")
    rounds = n.bit_length() - 1
    return pl.pallas_call(
        functools.partial(gather_kernel, n),
        out_shape=jax.ShapeDtypeStruct((n,) + block.shape, block.dtype),
        in_specs=[pl.BlockSpec(memory_space=pltpu.VMEM)],
        out_specs=pl.BlockSpec(memory_space=pltpu.VMEM),
        scratch_shapes=[
            pltpu.SemaphoreType.DMA(()),
            pltpu.SemaphoreType.DMA((rounds,)),
            pltpu.SemaphoreType.DMA((rounds,)),
        ],
        compiler_params=pltpu.CompilerParams(collective_id=0, has_side_effects=True),
    )(block)


def merge_parts(mine, theirs, top_lane):
    lane = lax.broadcasted_iota(jnp.int32, mine.shape, 1)
    is_top = lane == top_lane
    top_a = jnp.max(jnp.where(is_top, mine, -jnp.inf), axis=1, keepdims=True)
    top_b = jnp.max(jnp.where(is_top, theirs, -jnp.inf), axis=1, keepdims=True)
    top = jnp.maximum(top_a, top_b)
    merged = mine * jnp.exp(top_a - top) + theirs * jnp.exp(top_b - top)
    return jnp.where(is_top, top, merged)


def halving_kernel(n, top_lane, x_ref, out_ref, *scratch):
    rounds = len(scratch) // 3
    kept, got, sems = scratch[:rounds], scratch[rounds : 2 * rounds], scratch[2 * rounds :]
    me = lax.axis_index("seq")
    steps = []
    step = n // 2
    while step >= 1:
        bit = (me // step) % 2
        steps.append((me + step - 2 * step * bit, bit))
        step //= 2
    row, col = enter([partner for partner, _ in steps])
    source = x_ref
    for k, (partner, bit) in enumerate(steps):
        half = source.shape[0] // 2
        send_at = pl.multiple_of((1 - bit) * half, 8)
        keep_at = pl.multiple_of(bit * half, 8)
        copy = pltpu.make_async_remote_copy(
            src_ref=source.at[pl.ds(send_at, half)],
            dst_ref=got[k],
            send_sem=sems[k].at[0],
            recv_sem=sems[k].at[1],
            device_id=(partner, row, col),
            device_id_type=MESH,
        )
        copy.start()
        copy.wait()
        value = merge_parts(source[pl.ds(keep_at, half)], got[k][...], top_lane)
        if k + 1 < rounds:
            kept[k][...] = value
            source = kept[k]
        else:
            out_ref[...] = value


def seq_softmax_combine(parts, top_lane):
    n = lax.axis_size("seq")
    rounds = n.bit_length() - 1
    rows, lanes = parts.shape
    scratch = []
    for k in range(rounds):
        scratch.append(pltpu.VMEM((rows >> (k + 1), lanes), parts.dtype))
    for k in range(rounds):
        scratch.append(pltpu.VMEM((rows >> (k + 1), lanes), parts.dtype))
    for k in range(rounds):
        scratch.append(pltpu.SemaphoreType.DMA((2,)))
    return pl.pallas_call(
        functools.partial(halving_kernel, n, top_lane),
        out_shape=jax.ShapeDtypeStruct((rows // n, lanes), parts.dtype),
        in_specs=[pl.BlockSpec(memory_space=pltpu.VMEM)],
        out_specs=pl.BlockSpec(memory_space=pltpu.VMEM),
        scratch_shapes=scratch,
        compiler_params=pltpu.CompilerParams(collective_id=1, has_side_effects=True),
    )(parts)


def seq_peers():
    me, n = lax.axis_index("seq"), lax.axis_size("seq")
    row, col = lax.axis_index("row"), lax.axis_index("col")
    peers = [lax.rem(me + j, n) for j in range(1, n)]
    barrier = pltpu.get_barrier_semaphore()
    for peer in peers:
        pl.semaphore_signal(barrier, inc=1, device_id=(peer, row, col), device_id_type=MESH)
    pl.semaphore_wait(barrier, len(peers))
    return me, [(peer, row, col) for peer in peers]


def seq_direct_gather_kernel(x_ref, out_ref, self_sem, send_sem, recv_sem):
    me, peers = seq_peers()
    own = pltpu.make_async_copy(x_ref, out_ref.at[me], self_sem)
    own.start()
    copies = []
    for j, peer in enumerate(peers):
        copy = pltpu.make_async_remote_copy(
            src_ref=x_ref,
            dst_ref=out_ref.at[me],
            send_sem=send_sem.at[j],
            recv_sem=recv_sem.at[j],
            device_id=peer,
            device_id_type=MESH,
        )
        copy.start()
        copies.append(copy)
    own.wait()
    for copy in copies:
        copy.wait()


def seq_direct_gather(block):
    n = lax.axis_size("seq")
    return pl.pallas_call(
        seq_direct_gather_kernel,
        out_shape=jax.ShapeDtypeStruct((n,) + block.shape, block.dtype),
        in_specs=[pl.BlockSpec(memory_space=pltpu.VMEM)],
        out_specs=pl.BlockSpec(memory_space=pltpu.VMEM),
        scratch_shapes=[
            pltpu.SemaphoreType.DMA(()),
            pltpu.SemaphoreType.DMA((n - 1,)),
            pltpu.SemaphoreType.DMA((n - 1,)),
        ],
        compiler_params=pltpu.CompilerParams(collective_id=4, has_side_effects=True),
    )(block)


def seq_merge_kernel(top_lane, x_ref, out_ref, got, send_sem, recv_sem):
    me, peers = seq_peers()
    copies = []
    for j, peer in enumerate(peers):
        copy = pltpu.make_async_remote_copy(
            src_ref=x_ref.at[peer[0]],
            dst_ref=got.at[j],
            send_sem=send_sem.at[j],
            recv_sem=recv_sem.at[j],
            device_id=peer,
            device_id_type=MESH,
        )
        copy.start()
        copies.append(copy)
    for copy in copies:
        copy.wait()
    value = x_ref[me]
    for j in range(len(copies)):
        value = merge_parts(value, got[j], top_lane)
    out_ref[...] = value


def seq_direct_merge(parts, top_lane):
    n = parts.shape[0]
    return pl.pallas_call(
        functools.partial(seq_merge_kernel, top_lane),
        out_shape=jax.ShapeDtypeStruct(parts.shape[1:], parts.dtype),
        in_specs=[pl.BlockSpec(memory_space=pltpu.VMEM)],
        out_specs=pl.BlockSpec(memory_space=pltpu.VMEM),
        scratch_shapes=[
            pltpu.VMEM((n - 1,) + parts.shape[1:], parts.dtype),
            pltpu.SemaphoreType.DMA((n - 1,)),
            pltpu.SemaphoreType.DMA((n - 1,)),
        ],
        compiler_params=pltpu.CompilerParams(collective_id=5, has_side_effects=True),
    )(parts)


def seq_two_level_peers(group):
    me, n = lax.axis_index("seq"), lax.axis_size("seq")
    row, col = lax.axis_index("row"), lax.axis_index("col")
    first = (me // group) * group
    near = [first + lax.rem(me - first + j, group) for j in range(1, group)]
    far = [lax.rem(me + group * j, n) for j in range(1, n // group)]
    barrier = pltpu.get_barrier_semaphore()
    for peer in near + far:
        pl.semaphore_signal(barrier, inc=1, device_id=(peer, row, col), device_id_type=MESH)
    pl.semaphore_wait(barrier, len(near) + len(far))
    return me, first, [(p, row, col) for p in near], [(p, row, col) for p in far]


def seq_gather2_kernel(group, x_ref, out_ref, self_sem, near_send, near_recv, far_send, far_recv):
    me, first, near, far = seq_two_level_peers(group)
    own = pltpu.make_async_copy(x_ref, out_ref.at[me], self_sem)
    own.start()
    copies = []
    for j, peer in enumerate(near):
        copy = pltpu.make_async_remote_copy(
            src_ref=x_ref,
            dst_ref=out_ref.at[me],
            send_sem=near_send.at[j],
            recv_sem=near_recv.at[j],
            device_id=peer,
            device_id_type=MESH,
        )
        copy.start()
        copies.append(copy)
    own.wait()
    for copy in copies:
        copy.wait()
    block = out_ref.at[pl.ds(first, group)]
    copies = []
    for j, peer in enumerate(far):
        copy = pltpu.make_async_remote_copy(
            src_ref=block,
            dst_ref=block,
            send_sem=far_send.at[j],
            recv_sem=far_recv.at[j],
            device_id=peer,
            device_id_type=MESH,
        )
        copy.start()
        copies.append(copy)
    for copy in copies:
        copy.wait()


def seq_gather2(block, group):
    n = lax.axis_size("seq")
    return pl.pallas_call(
        functools.partial(seq_gather2_kernel, group),
        out_shape=jax.ShapeDtypeStruct((n,) + block.shape, block.dtype),
        in_specs=[pl.BlockSpec(memory_space=pltpu.VMEM)],
        out_specs=pl.BlockSpec(memory_space=pltpu.VMEM),
        scratch_shapes=[
            pltpu.SemaphoreType.DMA(()),
            pltpu.SemaphoreType.DMA((group - 1,)),
            pltpu.SemaphoreType.DMA((group - 1,)),
            pltpu.SemaphoreType.DMA((n // group - 1,)),
            pltpu.SemaphoreType.DMA((n // group - 1,)),
        ],
        compiler_params=pltpu.CompilerParams(collective_id=8, has_side_effects=True),
    )(block)


def seq_merge2_kernel(
    group, top_lane, x_ref, out_ref, got_far, partial, got_near, far_send, far_recv, near_send, near_recv
):
    me, first, near, far = seq_two_level_peers(group)
    copies = []
    for j, peer in enumerate(far):
        start = pl.multiple_of((peer[0] // group) * group, group)
        copy = pltpu.make_async_remote_copy(
            src_ref=x_ref.at[pl.ds(start, group)],
            dst_ref=got_far.at[j],
            send_sem=far_send.at[j],
            recv_sem=far_recv.at[j],
            device_id=peer,
            device_id_type=MESH,
        )
        copy.start()
        copies.append(copy)
    for copy in copies:
        copy.wait()
    for k in range(group):
        value = x_ref[first + k]
        for j in range(len(far)):
            value = merge_parts(value, got_far[j, k], top_lane)
        partial[k] = value
    copies = []
    for j, peer in enumerate(near):
        copy = pltpu.make_async_remote_copy(
            src_ref=partial.at[peer[0] - first],
            dst_ref=got_near.at[j],
            send_sem=near_send.at[j],
            recv_sem=near_recv.at[j],
            device_id=peer,
            device_id_type=MESH,
        )
        copy.start()
        copies.append(copy)
    for copy in copies:
        copy.wait()
    value = partial[me - first]
    for j in range(len(near)):
        value = merge_parts(value, got_near[j], top_lane)
    out_ref[...] = value


def seq_merge2(parts, top_lane, group):
    n = parts.shape[0]
    blk = parts.shape[1:]
    return pl.pallas_call(
        functools.partial(seq_merge2_kernel, group, top_lane),
        out_shape=jax.ShapeDtypeStruct(blk, parts.dtype),
        in_specs=[pl.BlockSpec(memory_space=pltpu.VMEM)],
        out_specs=pl.BlockSpec(memory_space=pltpu.VMEM),
        scratch_shapes=[
            pltpu.VMEM((n // group - 1, group) + blk, parts.dtype),
            pltpu.VMEM((group,) + blk, parts.dtype),
            pltpu.VMEM((group - 1,) + blk, parts.dtype),
            pltpu.SemaphoreType.DMA((n // group - 1,)),
            pltpu.SemaphoreType.DMA((n // group - 1,)),
            pltpu.SemaphoreType.DMA((group - 1,)),
            pltpu.SemaphoreType.DMA((group - 1,)),
        ],
        compiler_params=pltpu.CompilerParams(collective_id=9, has_side_effects=True),
    )(parts)


def col_peers():
    me, m = lax.axis_index("col"), lax.axis_size("col")
    seq, row = lax.axis_index("seq"), lax.axis_index("row")
    peers = [lax.rem(me + j, m) for j in range(1, m)]
    barrier = pltpu.get_barrier_semaphore()
    for peer in peers:
        pl.semaphore_signal(barrier, inc=1, device_id=(seq, row, peer), device_id_type=MESH)
    pl.semaphore_wait(barrier, len(peers))
    return me, [(seq, row, peer) for peer in peers]


def col_gather_kernel(x_ref, out_ref, self_sem, send_sem, recv_sem):
    me, peers = col_peers()
    own = pltpu.make_async_copy(x_ref, out_ref.at[me], self_sem)
    own.start()
    copies = []
    for j, peer in enumerate(peers):
        copy = pltpu.make_async_remote_copy(
            src_ref=x_ref,
            dst_ref=out_ref.at[me],
            send_sem=send_sem.at[j],
            recv_sem=recv_sem.at[j],
            device_id=peer,
            device_id_type=MESH,
        )
        copy.start()
        copies.append(copy)
    own.wait()
    for copy in copies:
        copy.wait()


def col_gather(block):
    m = lax.axis_size("col")
    return pl.pallas_call(
        col_gather_kernel,
        out_shape=jax.ShapeDtypeStruct((m,) + block.shape, block.dtype),
        in_specs=[pl.BlockSpec(memory_space=pltpu.VMEM)],
        out_specs=pl.BlockSpec(memory_space=pltpu.VMEM),
        scratch_shapes=[
            pltpu.SemaphoreType.DMA(()),
            pltpu.SemaphoreType.DMA((m - 1,)),
            pltpu.SemaphoreType.DMA((m - 1,)),
        ],
        compiler_params=pltpu.CompilerParams(collective_id=2, has_side_effects=True),
    )(block)


def col_sum_kernel(x_ref, own_ref, out_ref, got, send_sem, recv_sem):
    me, peers = col_peers()
    copies = []
    for j, peer in enumerate(peers):
        copy = pltpu.make_async_remote_copy(
            src_ref=x_ref.at[peer[2]],
            dst_ref=got.at[j],
            send_sem=send_sem.at[j],
            recv_sem=recv_sem.at[j],
            device_id=peer,
            device_id_type=MESH,
        )
        copy.start()
        copies.append(copy)
    for copy in copies:
        copy.wait()
    chunk = 32

    def body(i, carry):
        rows = pl.ds(pl.multiple_of(i * chunk, chunk), chunk)
        total = own_ref[rows, :]
        for j in range(len(copies)):
            total = total + got[j, rows, :].astype(jnp.float32)
        out_ref[rows, :] = total
        return carry

    lax.fori_loop(0, out_ref.shape[0] // chunk, body, 0)


def col_reduce_scatter(parts, own, collective_id):
    m = lax.axis_size("col")
    return pl.pallas_call(
        col_sum_kernel,
        out_shape=jax.ShapeDtypeStruct(own.shape, jnp.float32),
        in_specs=[pl.BlockSpec(memory_space=pltpu.VMEM)] * 2,
        out_specs=pl.BlockSpec(memory_space=pltpu.VMEM),
        scratch_shapes=[
            pltpu.VMEM((m - 1,) + parts.shape[1:], parts.dtype),
            pltpu.SemaphoreType.DMA((m - 1,)),
            pltpu.SemaphoreType.DMA((m - 1,)),
        ],
        compiler_params=pltpu.CompilerParams(collective_id=collective_id, has_side_effects=True),
    )(parts, own)


def col_mid_kernel(x_ref, own_ref, gain_ref, bias_ref, out_ref, got, rs_send, rs_recv, g_send, g_recv):
    me, peers = col_peers()
    copies = []
    for j, peer in enumerate(peers):
        copy = pltpu.make_async_remote_copy(
            src_ref=x_ref.at[peer[2]],
            dst_ref=got.at[j],
            send_sem=rs_send.at[j],
            recv_sem=rs_recv.at[j],
            device_id=peer,
            device_id_type=MESH,
        )
        copy.start()
        copies.append(copy)
    for copy in copies:
        copy.wait()
    chunk = 32
    width = out_ref.shape[2]

    def body(i, carry):
        rows = pl.ds(pl.multiple_of(i * chunk, chunk), chunk)
        total = own_ref[rows, :]
        for j in range(len(copies)):
            total = total + got[j, rows, :].astype(jnp.float32)
        center = total - jnp.sum(total, axis=1, keepdims=True) / width
        spread = jnp.sum(center * center, axis=1, keepdims=True) / width
        normed = center / jnp.sqrt(spread + 1e-05) * gain_ref[...] + bias_ref[...]
        out_ref[me, rows, :] = normed.astype(out_ref.dtype)
        return carry

    lax.fori_loop(0, out_ref.shape[1] // chunk, body, 0)
    sends = []
    for j, peer in enumerate(peers):
        copy = pltpu.make_async_remote_copy(
            src_ref=out_ref.at[me],
            dst_ref=out_ref.at[me],
            send_sem=g_send.at[j],
            recv_sem=g_recv.at[j],
            device_id=peer,
            device_id_type=MESH,
        )
        copy.start()
        sends.append(copy)
    for copy in sends:
        copy.wait()


def col_sum_norm_gather(parts, own, gain, bias):
    m = lax.axis_size("col")
    rows, width = own.shape
    return pl.pallas_call(
        col_mid_kernel,
        out_shape=jax.ShapeDtypeStruct((m, rows, width), jnp.bfloat16),
        in_specs=[pl.BlockSpec(memory_space=pltpu.VMEM)] * 4,
        out_specs=pl.BlockSpec(memory_space=pltpu.VMEM),
        scratch_shapes=[
            pltpu.VMEM((m - 1,) + parts.shape[1:], parts.dtype),
            pltpu.SemaphoreType.DMA((m - 1,)),
            pltpu.SemaphoreType.DMA((m - 1,)),
            pltpu.SemaphoreType.DMA((m - 1,)),
            pltpu.SemaphoreType.DMA((m - 1,)),
        ],
        compiler_params=pltpu.CompilerParams(collective_id=7, has_side_effects=True),
    )(parts, own, gain.reshape(1, width), bias.reshape(1, width))


def col_proj_kernel(
    x_ref, own_ref, w_hbm, gain_ref, bias_ref, out_ref, got, w_ref, w_sem, rs_send, rs_recv, g_send, g_recv
):
    me, peers = col_peers()
    w_copy = pltpu.make_async_copy(w_hbm, w_ref, w_sem)
    w_copy.start()
    m = len(peers) + 1
    heads_width = x_ref.shape[2]
    copies = []
    for j, peer in enumerate(peers):
        copy = pltpu.make_async_remote_copy(
            src_ref=x_ref.at[peer[2]],
            dst_ref=got.at[j],
            send_sem=rs_send.at[j],
            recv_sem=rs_recv.at[j],
            device_id=peer,
            device_id_type=MESH,
        )
        copy.start()
        copies.append(copy)
    for copy in copies:
        copy.wait()
    w_copy.wait()
    chunk = 32
    width = out_ref.shape[2]
    n_chunks = out_ref.shape[1] // chunk
    sends = []
    for i in range(n_chunks):
        rows = pl.ds(i * chunk, chunk)
        total = own_ref[rows, :]
        for j in range(len(copies)):
            source = lax.rem(me + m - 1 - j, m)
            weights = w_ref[pl.ds(pl.multiple_of(source * heads_width, heads_width), heads_width), :]
            total = total + jnp.dot(got[j, rows, :], weights, preferred_element_type=jnp.float32)
        center = total - jnp.sum(total, axis=1, keepdims=True) / width
        spread = jnp.sum(center * center, axis=1, keepdims=True) / width
        normed = center / jnp.sqrt(spread + 1e-05) * gain_ref[...] + bias_ref[...]
        out_ref[me, rows, :] = normed.astype(out_ref.dtype)
        for j, peer in enumerate(peers):
            copy = pltpu.make_async_remote_copy(
                src_ref=out_ref.at[me, rows],
                dst_ref=out_ref.at[me, rows],
                send_sem=g_send.at[j * n_chunks + i],
                recv_sem=g_recv.at[j * n_chunks + i],
                device_id=peer,
                device_id_type=MESH,
            )
            copy.start()
            sends.append(copy)
    for copy in sends:
        copy.wait()


def col_proj_norm_gather(attn_parts, own, w_full, gain, bias):
    m = lax.axis_size("col")
    rows, width = own.shape
    return pl.pallas_call(
        col_proj_kernel,
        out_shape=jax.ShapeDtypeStruct((m, rows, width), jnp.bfloat16),
        in_specs=[pl.BlockSpec(memory_space=pltpu.VMEM)] * 2
        + [pl.BlockSpec(memory_space=pl.ANY)]
        + [pl.BlockSpec(memory_space=pltpu.VMEM)] * 2,
        out_specs=pl.BlockSpec(memory_space=pltpu.VMEM),
        scratch_shapes=[
            pltpu.VMEM((m - 1,) + attn_parts.shape[1:], attn_parts.dtype),
            pltpu.VMEM(w_full.shape, w_full.dtype),
            pltpu.SemaphoreType.DMA(()),
            pltpu.SemaphoreType.DMA((m - 1,)),
            pltpu.SemaphoreType.DMA((m - 1,)),
            pltpu.SemaphoreType.DMA(((m - 1) * (rows // 32),)),
            pltpu.SemaphoreType.DMA(((m - 1) * (rows // 32),)),
        ],
        compiler_params=pltpu.CompilerParams(
            collective_id=10, has_side_effects=True, vmem_limit_bytes=48 * 1024 * 1024
        ),
    )(attn_parts, own, w_full, gain.reshape(1, width), bias.reshape(1, width))


def col_sum_ln_kernel(x_ref, own_ref, gain_ref, bias_ref, out_ref, got, send_sem, recv_sem):
    me, peers = col_peers()
    copies = []
    for j, peer in enumerate(peers):
        copy = pltpu.make_async_remote_copy(
            src_ref=x_ref.at[peer[2]],
            dst_ref=got.at[j],
            send_sem=send_sem.at[j],
            recv_sem=recv_sem.at[j],
            device_id=peer,
            device_id_type=MESH,
        )
        copy.start()
        copies.append(copy)
    for copy in copies:
        copy.wait()
    chunk = 32
    width = out_ref.shape[1]

    def body(i, carry):
        rows = pl.ds(pl.multiple_of(i * chunk, chunk), chunk)
        total = own_ref[rows, :]
        for j in range(len(copies)):
            total = total + got[j, rows, :].astype(jnp.float32)
        center = total - jnp.sum(total, axis=1, keepdims=True) / width
        spread = jnp.sum(center * center, axis=1, keepdims=True) / width
        normed = center / jnp.sqrt(spread + 1e-05) * gain_ref[...] + bias_ref[...]
        out_ref[rows, :] = normed.astype(out_ref.dtype)
        return carry

    lax.fori_loop(0, out_ref.shape[0] // chunk, body, 0)


def col_sum_norm(parts, own, gain, bias):
    m = lax.axis_size("col")
    rows, width = own.shape
    return pl.pallas_call(
        col_sum_ln_kernel,
        out_shape=jax.ShapeDtypeStruct(own.shape, jnp.bfloat16),
        in_specs=[pl.BlockSpec(memory_space=pltpu.VMEM)] * 4,
        out_specs=pl.BlockSpec(memory_space=pltpu.VMEM),
        scratch_shapes=[
            pltpu.VMEM((m - 1,) + parts.shape[1:], parts.dtype),
            pltpu.SemaphoreType.DMA((m - 1,)),
            pltpu.SemaphoreType.DMA((m - 1,)),
        ],
        compiler_params=pltpu.CompilerParams(collective_id=11, has_side_effects=True),
    )(parts, own, gain.reshape(1, width), bias.reshape(1, width))


def layer_norm(values, gain, bias):
    center = values - jnp.mean(values, axis=1, keepdims=True)
    spread = jnp.mean(center * center, axis=1, keepdims=True)
    return center * lax.rsqrt(spread + 1e-05) * gain + bias


def per_device(
    hidden_in,
    qkv_weight,
    qkv_global_weight,
    out_weight,
    ln_gain,
    ln_bias,
    ffn_in,
    ffn_out,
    ln2_gain,
    ln2_bias,
    segment_ids,
    global_pos,
    page_owner,
):
    neg = -1e30
    tokens = hidden_in[0]
    shard_len, width = tokens.shape
    heads_here = qkv_weight.shape[1]
    triple = qkv_weight.shape[2]
    head_dim = triple // 3
    n_seq = lax.axis_size("seq")
    n_row = lax.axis_size("row")
    n_col = lax.axis_size("col")
    seq_index = lax.axis_index("seq")
    col_index = lax.axis_index("col")
    base = seq_index * shard_len
    scale = 1.0 / math.sqrt(head_dim)

    all_pos = global_pos[0]
    n_glob = all_pos.shape[0]
    per_shard = n_glob // n_seq
    own_pos = lax.dynamic_slice_in_dim(all_pos, seq_index * per_shard, per_shard, 0)
    local_order = jnp.arange(shard_len, dtype=jnp.int32)
    own_match = (own_pos - base)[:, None] == local_order[None, :]
    picker = own_match.astype(jnp.bfloat16)
    own_rows = jnp.dot(picker, tokens, preferred_element_type=jnp.float32).astype(jnp.bfloat16)
    group = 4 if n_seq % 4 == 0 and n_seq > 4 else 1
    if group > 1:
        glob_rows = seq_gather2(own_rows.reshape(-1, 128), group).reshape(n_glob, width)
    else:
        glob_rows = seq_direct_gather(own_rows.reshape(-1, 128)).reshape(n_glob, width)

    wg_cols = qkv_global_weight.shape[1] * qkv_global_weight.shape[2]
    wg_fin = lax.all_gather(
        jnp.concatenate(
            [qkv_global_weight.reshape(qkv_global_weight.shape[0], wg_cols), ffn_in], axis=1
        ),
        "row",
        axis=0,
        tiled=True,
    )
    w_global = wg_fin[:, :wg_cols]
    f_in = wg_fin[:, wg_cols:]
    f_out = lax.all_gather(ffn_out, "row", axis=1, tiled=True)
    w_out = lax.all_gather(out_weight, "col", axis=0, tiled=True)

    flat_weight = qkv_weight.reshape(width, heads_here * triple)
    qkv = jnp.dot(tokens, flat_weight, preferred_element_type=jnp.float32).astype(jnp.bfloat16)
    qkv_heads = qkv.reshape(shard_len, heads_here, triple)
    queries = qkv_heads[:, :, :head_dim]
    kv_local = qkv_heads[:, :, head_dim:]

    owners = page_owner[0, :, 0]
    n_pages = owners.shape[0]
    page_len = shard_len // n_pages
    capacity = max(2, n_pages // n_seq)
    page_order = jnp.arange(n_pages, dtype=jnp.int32)
    slot = jnp.sum(
        ((owners[:, None] == owners[None, :]) & (page_order[None, :] < page_order[:, None])).astype(
            jnp.int32
        ),
        axis=1,
    )
    target = owners * capacity + slot
    placing = (target[None, :] == jnp.arange(n_seq * capacity, dtype=jnp.int32)[:, None]).astype(
        jnp.bfloat16
    )
    outgoing = jnp.dot(
        placing,
        kv_local.reshape(n_pages, page_len * heads_here * 2 * head_dim),
        preferred_element_type=jnp.float32,
    ).astype(jnp.bfloat16)
    outgoing = outgoing.reshape(n_seq, capacity, page_len, heads_here, 2 * head_dim)
    arrived = lax.all_to_all(outgoing, "seq", split_axis=0, concat_axis=0, tiled=True)
    arrived, glob_rows = lax.optimization_barrier((arrived, glob_rows))
    page_pool = arrived[None, None]

    kv_ext = padded(kv_local, (("seq", 0),), HALF)

    glob_qkv = jnp.dot(glob_rows, flat_weight, preferred_element_type=jnp.float32).astype(
        jnp.bfloat16
    )
    glob_kv = glob_qkv.reshape(n_glob, heads_here, triple)[:, :, head_dim:]
    glob_k = glob_kv[:, :, :head_dim]
    glob_v = glob_kv[:, :, head_dim:]
    glob_q = (
        jnp.dot(glob_rows, w_global, preferred_element_type=jnp.float32)
        .astype(jnp.bfloat16)
        .reshape(n_glob, heads_here, triple)[:, :, :head_dim]
    )
    global_kv_local = (
        jnp.dot(tokens, w_global, preferred_element_type=jnp.float32)
        .astype(jnp.bfloat16)
        .reshape(shard_len, heads_here, triple)[:, :, head_dim:]
    )

    seg_all = segment_ids[0]
    glob_seg = jnp.take(seg_all, all_pos)
    seg_pad = jnp.pad(seg_all, (HALF, HALF), constant_values=-1)
    query_seg = lax.dynamic_slice_in_dim(seg_all, base, shard_len, 0)
    key_seg = lax.dynamic_slice_in_dim(seg_pad, base, shard_len + 2 * HALF, 0)
    key_pos = base - HALF + jnp.arange(shard_len + 2 * HALF, dtype=jnp.int32)
    key_flag = jnp.any(key_pos[:, None] == all_pos[None, :], axis=1)
    query_pos = base + local_order

    s_part = (
        jnp.einsum(
            "ghd,khd->hgk",
            glob_q,
            global_kv_local[:, :, :head_dim],
            preferred_element_type=jnp.float32,
        )
        * scale
    )
    part_mask = glob_seg[:, None] == query_seg[None, :]
    part_top = jnp.max(jnp.where(part_mask, s_part, neg), axis=2)
    e_part = jnp.where(part_mask, jnp.exp(s_part - part_top[:, :, None]), 0.0)
    part_total = jnp.sum(e_part, axis=2)
    part_acc = jnp.einsum(
        "hgk,khd->hgd",
        e_part,
        global_kv_local[:, :, head_dim:].astype(jnp.float32),
        precision=lax.Precision.HIGHEST,
    )
    packed = jnp.concatenate(
        [
            part_acc,
            part_total[:, :, None],
            jnp.broadcast_to(part_top[:, :, None], part_top.shape + (128 - head_dim - 1,)),
        ],
        axis=2,
    )
    packed = jnp.transpose(packed, (1, 0, 2)).reshape(n_glob * heads_here, 128)
    if group > 1:
        merged = seq_merge2(packed.reshape(n_seq, -1, 128), head_dim + 1, group)
    else:
        merged = seq_direct_merge(packed.reshape(n_seq, -1, 128), head_dim + 1)
    merged = merged.reshape(
        per_shard, heads_here, 128
    )
    own_out = jnp.transpose(
        (merged[:, :, :head_dim] / merged[:, :, head_dim : head_dim + 1]).astype(jnp.bfloat16),
        (1, 0, 2),
    )

    glob_mask = query_seg[:, None] == glob_seg[None, :]
    k_blk = kv_ext[:, :, :head_dim]
    v_blk = kv_ext[:, :, head_dim:]
    s_win = jnp.einsum("qhd,khd->hqk", queries, k_blk, preferred_element_type=jnp.float32) * scale
    s_glob = jnp.einsum("qhd,ghd->hqg", queries, glob_k, preferred_element_type=jnp.float32) * scale
    m_win = (
        (jnp.abs(query_pos[:, None] - key_pos[None, :]) <= HALF)
        & (query_seg[:, None] == key_seg[None, :])
        & jnp.logical_not(key_flag[None, :])
    )
    top = jnp.maximum(
        jnp.max(jnp.where(m_win, s_win, neg), axis=2),
        jnp.max(jnp.where(glob_mask, s_glob, neg), axis=2),
    )
    e_win = jnp.where(m_win, jnp.exp(s_win - top[:, :, None]), 0.0)
    e_glob = jnp.where(glob_mask, jnp.exp(s_glob - top[:, :, None]), 0.0)
    total = jnp.sum(e_win, axis=2) + jnp.sum(e_glob, axis=2)
    numer = jnp.einsum(
        "hqk,khd->qhd", e_win.astype(jnp.bfloat16), v_blk, preferred_element_type=jnp.float32
    )
    numer = numer + jnp.einsum(
        "hqg,ghd->qhd", e_glob.astype(jnp.bfloat16), glob_v, preferred_element_type=jnp.float32
    )
    pieces = (numer / jnp.transpose(total)[:, :, None]).astype(jnp.bfloat16)

    placed = jnp.einsum("gt,hgd->thd", picker, own_out, preferred_element_type=jnp.float32).astype(
        jnp.bfloat16
    )
    is_own = jnp.any(own_match, axis=0)
    attention = jnp.where(is_own[:, None, None], placed, pieces).reshape(
        shard_len, heads_here * head_dim
    )


    out_rows = shard_len // n_col
    attn_own = lax.dynamic_slice_in_dim(attention, col_index * out_rows, out_rows, 0)
    token_own = lax.dynamic_slice_in_dim(tokens, col_index * out_rows, out_rows, 0)
    proj_own = jnp.dot(attn_own, out_weight, preferred_element_type=jnp.float32)
    own_sum, w_out = lax.optimization_barrier((token_own.astype(jnp.float32) + proj_own, w_out))
    middle_all = col_proj_norm_gather(
        attention.reshape(n_col, out_rows, heads_here * head_dim),
        own_sum,
        w_out,
        ln_gain,
        ln_bias,
    )
    mine = middle_all[col_index]
    middle = middle_all.reshape(shard_len, width)
    ffn_pre = jnp.dot(middle, f_in, preferred_element_type=jnp.float32)
    ffn_hidden = jax.nn.gelu(ffn_pre, approximate=False).astype(jnp.bfloat16)
    ffn_full = jnp.dot(ffn_hidden, f_out, preferred_element_type=jnp.float32)
    ffn_own = lax.dynamic_slice_in_dim(ffn_full, col_index * out_rows, out_rows, 0)
    normed = col_sum_norm(
        ffn_full.astype(jnp.bfloat16).reshape(n_col, out_rows, width),
        mine.astype(jnp.float32) + ffn_own,
        ln2_gain,
        ln2_bias,
    )
    return (normed[None], page_pool)


def solution(mesh):
    in_specs = (
        P("row", "seq", None),
        P(None, "col", None),
        P("row", "col", None),
        P("col", None),
        P(),
        P(),
        P("row", "col"),
        P("col", "row"),
        P(),
        P(),
        P("row", None),
        P("row", None),
        P("row", "seq", None),
    )
    out_specs = (P("row", ("seq", "col"), None), P("row", "seq", None, None, None, "col", None))
    return jax.shard_map(
        per_device, mesh=mesh, in_specs=in_specs, out_specs=out_specs, check_vma=False
    )
```

```python
import functools
import math

import jax
import jax.numpy as jnp
from jax import lax
from jax.experimental import pallas as pl
from jax.experimental.pallas import tpu as pltpu
from jax.sharding import PartitionSpec as P

MESH = pl.DeviceIdType.MESH

HALF = 256


def padded(block, sides, width):
    for axis, dim in sides:
        count = lax.axis_size(axis)
        forward = [(i, i + 1) for i in range(count - 1)]
        backward = [(target, source) for source, target in forward]
        low = lax.ppermute(
            lax.slice_in_dim(block, block.shape[dim] - width, None, axis=dim), axis, forward
        )
        high = lax.ppermute(lax.slice_in_dim(block, 0, width, axis=dim), axis, backward)
        block = jnp.concatenate([low, block, high], axis=dim)
    return block


def butterfly_partners(n):
    me = lax.axis_index("seq")
    partners = []
    step = 1
    while step < n:
        bit = (me // step) % 2
        partners.append(me + step - 2 * step * bit)
        step *= 2
    return me, partners


def enter(partners):
    row, col = lax.axis_index("row"), lax.axis_index("col")
    barrier = pltpu.get_barrier_semaphore()
    for partner in partners:
        pl.semaphore_signal(barrier, inc=1, device_id=(partner, row, col), device_id_type=MESH)
    pl.semaphore_wait(barrier, len(partners))
    return row, col


def gather_kernel(n, x_ref, out_ref, self_sem, send_sem, recv_sem):
    me, partners = butterfly_partners(n)
    row, col = enter(partners)
    own = pltpu.make_async_copy(x_ref, out_ref.at[me], self_sem)
    own.start()
    own.wait()
    size = 1
    for k, partner in enumerate(partners):
        start = (me // size) * size
        copy = pltpu.make_async_remote_copy(
            src_ref=out_ref.at[pl.ds(start, size)],
            dst_ref=out_ref.at[pl.ds(start, size)],
            send_sem=send_sem.at[k],
            recv_sem=recv_sem.at[k],
            device_id=(partner, row, col),
            device_id_type=MESH,
        )
        copy.start()
        copy.wait()
        size *= 2


def seq_gather(block):
    n = lax.axis_size("seq")
    rounds = n.bit_length() - 1
    return pl.pallas_call(
        functools.partial(gather_kernel, n),
        out_shape=jax.ShapeDtypeStruct((n,) + block.shape, block.dtype),
        in_specs=[pl.BlockSpec(memory_space=pltpu.VMEM)],
        out_specs=pl.BlockSpec(memory_space=pltpu.VMEM),
        scratch_shapes=[
            pltpu.SemaphoreType.DMA(()),
            pltpu.SemaphoreType.DMA((rounds,)),
            pltpu.SemaphoreType.DMA((rounds,)),
        ],
        compiler_params=pltpu.CompilerParams(collective_id=0, has_side_effects=True),
    )(block)


def merge_parts(mine, theirs, top_lane):
    lane = lax.broadcasted_iota(jnp.int32, mine.shape, 1)
    is_top = lane == top_lane
    top_a = jnp.max(jnp.where(is_top, mine, -jnp.inf), axis=1, keepdims=True)
    top_b = jnp.max(jnp.where(is_top, theirs, -jnp.inf), axis=1, keepdims=True)
    top = jnp.maximum(top_a, top_b)
    merged = mine * jnp.exp(top_a - top) + theirs * jnp.exp(top_b - top)
    return jnp.where(is_top, top, merged)


def halving_kernel(n, top_lane, x_ref, out_ref, *scratch):
    rounds = len(scratch) // 3
    kept, got, sems = scratch[:rounds], scratch[rounds : 2 * rounds], scratch[2 * rounds :]
    me = lax.axis_index("seq")
    steps = []
    step = n // 2
    while step >= 1:
        bit = (me // step) % 2
        steps.append((me + step - 2 * step * bit, bit))
        step //= 2
    row, col = enter([partner for partner, _ in steps])
    source = x_ref
    for k, (partner, bit) in enumerate(steps):
        half = source.shape[0] // 2
        send_at = pl.multiple_of((1 - bit) * half, 8)
        keep_at = pl.multiple_of(bit * half, 8)
        copy = pltpu.make_async_remote_copy(
            src_ref=source.at[pl.ds(send_at, half)],
            dst_ref=got[k],
            send_sem=sems[k].at[0],
            recv_sem=sems[k].at[1],
            device_id=(partner, row, col),
            device_id_type=MESH,
        )
        copy.start()
        copy.wait()
        value = merge_parts(source[pl.ds(keep_at, half)], got[k][...], top_lane)
        if k + 1 < rounds:
            kept[k][...] = value
            source = kept[k]
        else:
            out_ref[...] = value


def seq_softmax_combine(parts, top_lane):
    n = lax.axis_size("seq")
    rounds = n.bit_length() - 1
    rows, lanes = parts.shape
    scratch = []
    for k in range(rounds):
        scratch.append(pltpu.VMEM((rows >> (k + 1), lanes), parts.dtype))
    for k in range(rounds):
        scratch.append(pltpu.VMEM((rows >> (k + 1), lanes), parts.dtype))
    for k in range(rounds):
        scratch.append(pltpu.SemaphoreType.DMA((2,)))
    return pl.pallas_call(
        functools.partial(halving_kernel, n, top_lane),
        out_shape=jax.ShapeDtypeStruct((rows // n, lanes), parts.dtype),
        in_specs=[pl.BlockSpec(memory_space=pltpu.VMEM)],
        out_specs=pl.BlockSpec(memory_space=pltpu.VMEM),
        scratch_shapes=scratch,
        compiler_params=pltpu.CompilerParams(collective_id=1, has_side_effects=True),
    )(parts)


def seq_peers():
    me, n = lax.axis_index("seq"), lax.axis_size("seq")
    row, col = lax.axis_index("row"), lax.axis_index("col")
    peers = [lax.rem(me + j, n) for j in range(1, n)]
    barrier = pltpu.get_barrier_semaphore()
    for peer in peers:
        pl.semaphore_signal(barrier, inc=1, device_id=(peer, row, col), device_id_type=MESH)
    pl.semaphore_wait(barrier, len(peers))
    return me, [(peer, row, col) for peer in peers]


def seq_direct_gather_kernel(x_ref, out_ref, self_sem, send_sem, recv_sem):
    me, peers = seq_peers()
    own = pltpu.make_async_copy(x_ref, out_ref.at[me], self_sem)
    own.start()
    copies = []
    for j, peer in enumerate(peers):
        copy = pltpu.make_async_remote_copy(
            src_ref=x_ref,
            dst_ref=out_ref.at[me],
            send_sem=send_sem.at[j],
            recv_sem=recv_sem.at[j],
            device_id=peer,
            device_id_type=MESH,
        )
        copy.start()
        copies.append(copy)
    own.wait()
    for copy in copies:
        copy.wait()


def seq_direct_gather(block):
    n = lax.axis_size("seq")
    return pl.pallas_call(
        seq_direct_gather_kernel,
        out_shape=jax.ShapeDtypeStruct((n,) + block.shape, block.dtype),
        in_specs=[pl.BlockSpec(memory_space=pltpu.VMEM)],
        out_specs=pl.BlockSpec(memory_space=pltpu.VMEM),
        scratch_shapes=[
            pltpu.SemaphoreType.DMA(()),
            pltpu.SemaphoreType.DMA((n - 1,)),
            pltpu.SemaphoreType.DMA((n - 1,)),
        ],
        compiler_params=pltpu.CompilerParams(collective_id=4, has_side_effects=True),
    )(block)


def seq_merge_kernel(top_lane, x_ref, out_ref, got, send_sem, recv_sem):
    me, peers = seq_peers()
    copies = []
    for j, peer in enumerate(peers):
        copy = pltpu.make_async_remote_copy(
            src_ref=x_ref.at[peer[0]],
            dst_ref=got.at[j],
            send_sem=send_sem.at[j],
            recv_sem=recv_sem.at[j],
            device_id=peer,
            device_id_type=MESH,
        )
        copy.start()
        copies.append(copy)
    for copy in copies:
        copy.wait()
    value = x_ref[me]
    for j in range(len(copies)):
        value = merge_parts(value, got[j], top_lane)
    out_ref[...] = value


def seq_direct_merge(parts, top_lane):
    n = parts.shape[0]
    return pl.pallas_call(
        functools.partial(seq_merge_kernel, top_lane),
        out_shape=jax.ShapeDtypeStruct(parts.shape[1:], parts.dtype),
        in_specs=[pl.BlockSpec(memory_space=pltpu.VMEM)],
        out_specs=pl.BlockSpec(memory_space=pltpu.VMEM),
        scratch_shapes=[
            pltpu.VMEM((n - 1,) + parts.shape[1:], parts.dtype),
            pltpu.SemaphoreType.DMA((n - 1,)),
            pltpu.SemaphoreType.DMA((n - 1,)),
        ],
        compiler_params=pltpu.CompilerParams(collective_id=5, has_side_effects=True),
    )(parts)


def seq_two_level_peers(group):
    me, n = lax.axis_index("seq"), lax.axis_size("seq")
    row, col = lax.axis_index("row"), lax.axis_index("col")
    first = (me // group) * group
    near = [first + lax.rem(me - first + j, group) for j in range(1, group)]
    far = [lax.rem(me + group * j, n) for j in range(1, n // group)]
    barrier = pltpu.get_barrier_semaphore()
    for peer in near + far:
        pl.semaphore_signal(barrier, inc=1, device_id=(peer, row, col), device_id_type=MESH)
    pl.semaphore_wait(barrier, len(near) + len(far))
    return me, first, [(p, row, col) for p in near], [(p, row, col) for p in far]


def seq_gather2_kernel(group, x_ref, out_ref, self_sem, near_send, near_recv, far_send, far_recv):
    me, first, near, far = seq_two_level_peers(group)
    own = pltpu.make_async_copy(x_ref, out_ref.at[me], self_sem)
    own.start()
    copies = []
    for j, peer in enumerate(near):
        copy = pltpu.make_async_remote_copy(
            src_ref=x_ref,
            dst_ref=out_ref.at[me],
            send_sem=near_send.at[j],
            recv_sem=near_recv.at[j],
            device_id=peer,
            device_id_type=MESH,
        )
        copy.start()
        copies.append(copy)
    own.wait()
    for copy in copies:
        copy.wait()
    block = out_ref.at[pl.ds(first, group)]
    copies = []
    for j, peer in enumerate(far):
        copy = pltpu.make_async_remote_copy(
            src_ref=block,
            dst_ref=block,
            send_sem=far_send.at[j],
            recv_sem=far_recv.at[j],
            device_id=peer,
            device_id_type=MESH,
        )
        copy.start()
        copies.append(copy)
    for copy in copies:
        copy.wait()


def seq_gather2(block, group):
    n = lax.axis_size("seq")
    return pl.pallas_call(
        functools.partial(seq_gather2_kernel, group),
        out_shape=jax.ShapeDtypeStruct((n,) + block.shape, block.dtype),
        in_specs=[pl.BlockSpec(memory_space=pltpu.VMEM)],
        out_specs=pl.BlockSpec(memory_space=pltpu.VMEM),
        scratch_shapes=[
            pltpu.SemaphoreType.DMA(()),
            pltpu.SemaphoreType.DMA((group - 1,)),
            pltpu.SemaphoreType.DMA((group - 1,)),
            pltpu.SemaphoreType.DMA((n // group - 1,)),
            pltpu.SemaphoreType.DMA((n // group - 1,)),
        ],
        compiler_params=pltpu.CompilerParams(collective_id=8, has_side_effects=True),
    )(block)


def seq_merge2_kernel(
    group, top_lane, x_ref, out_ref, got_far, partial, got_near, far_send, far_recv, near_send, near_recv
):
    me, first, near, far = seq_two_level_peers(group)
    copies = []
    for j, peer in enumerate(far):
        start = pl.multiple_of((peer[0] // group) * group, group)
        copy = pltpu.make_async_remote_copy(
            src_ref=x_ref.at[pl.ds(start, group)],
            dst_ref=got_far.at[j],
            send_sem=far_send.at[j],
            recv_sem=far_recv.at[j],
            device_id=peer,
            device_id_type=MESH,
        )
        copy.start()
        copies.append(copy)
    for copy in copies:
        copy.wait()
    for k in range(group):
        value = x_ref[first + k]
        for j in range(len(far)):
            value = merge_parts(value, got_far[j, k], top_lane)
        partial[k] = value
    copies = []
    for j, peer in enumerate(near):
        copy = pltpu.make_async_remote_copy(
            src_ref=partial.at[peer[0] - first],
            dst_ref=got_near.at[j],
            send_sem=near_send.at[j],
            recv_sem=near_recv.at[j],
            device_id=peer,
            device_id_type=MESH,
        )
        copy.start()
        copies.append(copy)
    for copy in copies:
        copy.wait()
    value = partial[me - first]
    for j in range(len(near)):
        value = merge_parts(value, got_near[j], top_lane)
    out_ref[...] = value


def seq_merge2(parts, top_lane, group):
    n = parts.shape[0]
    blk = parts.shape[1:]
    return pl.pallas_call(
        functools.partial(seq_merge2_kernel, group, top_lane),
        out_shape=jax.ShapeDtypeStruct(blk, parts.dtype),
        in_specs=[pl.BlockSpec(memory_space=pltpu.VMEM)],
        out_specs=pl.BlockSpec(memory_space=pltpu.VMEM),
        scratch_shapes=[
            pltpu.VMEM((n // group - 1, group) + blk, parts.dtype),
            pltpu.VMEM((group,) + blk, parts.dtype),
            pltpu.VMEM((group - 1,) + blk, parts.dtype),
            pltpu.SemaphoreType.DMA((n // group - 1,)),
            pltpu.SemaphoreType.DMA((n // group - 1,)),
            pltpu.SemaphoreType.DMA((group - 1,)),
            pltpu.SemaphoreType.DMA((group - 1,)),
        ],
        compiler_params=pltpu.CompilerParams(collective_id=9, has_side_effects=True),
    )(parts)


def col_peers():
    me, m = lax.axis_index("col"), lax.axis_size("col")
    seq, row = lax.axis_index("seq"), lax.axis_index("row")
    peers = [lax.rem(me + j, m) for j in range(1, m)]
    barrier = pltpu.get_barrier_semaphore()
    for peer in peers:
        pl.semaphore_signal(barrier, inc=1, device_id=(seq, row, peer), device_id_type=MESH)
    pl.semaphore_wait(barrier, len(peers))
    return me, [(seq, row, peer) for peer in peers]


def col_gather_kernel(x_ref, out_ref, self_sem, send_sem, recv_sem):
    me, peers = col_peers()
    own = pltpu.make_async_copy(x_ref, out_ref.at[me], self_sem)
    own.start()
    copies = []
    for j, peer in enumerate(peers):
        copy = pltpu.make_async_remote_copy(
            src_ref=x_ref,
            dst_ref=out_ref.at[me],
            send_sem=send_sem.at[j],
            recv_sem=recv_sem.at[j],
            device_id=peer,
            device_id_type=MESH,
        )
        copy.start()
        copies.append(copy)
    own.wait()
    for copy in copies:
        copy.wait()


def col_gather(block):
    m = lax.axis_size("col")
    return pl.pallas_call(
        col_gather_kernel,
        out_shape=jax.ShapeDtypeStruct((m,) + block.shape, block.dtype),
        in_specs=[pl.BlockSpec(memory_space=pltpu.VMEM)],
        out_specs=pl.BlockSpec(memory_space=pltpu.VMEM),
        scratch_shapes=[
            pltpu.SemaphoreType.DMA(()),
            pltpu.SemaphoreType.DMA((m - 1,)),
            pltpu.SemaphoreType.DMA((m - 1,)),
        ],
        compiler_params=pltpu.CompilerParams(collective_id=2, has_side_effects=True),
    )(block)


def col_sum_kernel(x_ref, own_ref, out_ref, got, send_sem, recv_sem):
    me, peers = col_peers()
    copies = []
    for j, peer in enumerate(peers):
        copy = pltpu.make_async_remote_copy(
            src_ref=x_ref.at[peer[2]],
            dst_ref=got.at[j],
            send_sem=send_sem.at[j],
            recv_sem=recv_sem.at[j],
            device_id=peer,
            device_id_type=MESH,
        )
        copy.start()
        copies.append(copy)
    for copy in copies:
        copy.wait()
    chunk = 32

    def body(i, carry):
        rows = pl.ds(pl.multiple_of(i * chunk, chunk), chunk)
        total = own_ref[rows, :]
        for j in range(len(copies)):
            total = total + got[j, rows, :].astype(jnp.float32)
        out_ref[rows, :] = total
        return carry

    lax.fori_loop(0, out_ref.shape[0] // chunk, body, 0)


def col_reduce_scatter(parts, own, collective_id):
    m = lax.axis_size("col")
    return pl.pallas_call(
        col_sum_kernel,
        out_shape=jax.ShapeDtypeStruct(own.shape, jnp.float32),
        in_specs=[pl.BlockSpec(memory_space=pltpu.VMEM)] * 2,
        out_specs=pl.BlockSpec(memory_space=pltpu.VMEM),
        scratch_shapes=[
            pltpu.VMEM((m - 1,) + parts.shape[1:], parts.dtype),
            pltpu.SemaphoreType.DMA((m - 1,)),
            pltpu.SemaphoreType.DMA((m - 1,)),
        ],
        compiler_params=pltpu.CompilerParams(collective_id=collective_id, has_side_effects=True),
    )(parts, own)


def col_mid_kernel(x_ref, own_ref, gain_ref, bias_ref, out_ref, got, rs_send, rs_recv, g_send, g_recv):
    me, peers = col_peers()
    copies = []
    for j, peer in enumerate(peers):
        copy = pltpu.make_async_remote_copy(
            src_ref=x_ref.at[peer[2]],
            dst_ref=got.at[j],
            send_sem=rs_send.at[j],
            recv_sem=rs_recv.at[j],
            device_id=peer,
            device_id_type=MESH,
        )
        copy.start()
        copies.append(copy)
    for copy in copies:
        copy.wait()
    chunk = 32
    width = out_ref.shape[2]

    def body(i, carry):
        rows = pl.ds(pl.multiple_of(i * chunk, chunk), chunk)
        total = own_ref[rows, :]
        for j in range(len(copies)):
            total = total + got[j, rows, :].astype(jnp.float32)
        center = total - jnp.sum(total, axis=1, keepdims=True) / width
        spread = jnp.sum(center * center, axis=1, keepdims=True) / width
        normed = center / jnp.sqrt(spread + 1e-05) * gain_ref[...] + bias_ref[...]
        out_ref[me, rows, :] = normed.astype(out_ref.dtype)
        return carry

    lax.fori_loop(0, out_ref.shape[1] // chunk, body, 0)
    sends = []
    for j, peer in enumerate(peers):
        copy = pltpu.make_async_remote_copy(
            src_ref=out_ref.at[me],
            dst_ref=out_ref.at[me],
            send_sem=g_send.at[j],
            recv_sem=g_recv.at[j],
            device_id=peer,
            device_id_type=MESH,
        )
        copy.start()
        sends.append(copy)
    for copy in sends:
        copy.wait()


def col_sum_norm_gather(parts, own, gain, bias):
    m = lax.axis_size("col")
    rows, width = own.shape
    return pl.pallas_call(
        col_mid_kernel,
        out_shape=jax.ShapeDtypeStruct((m, rows, width), jnp.bfloat16),
        in_specs=[pl.BlockSpec(memory_space=pltpu.VMEM)] * 4,
        out_specs=pl.BlockSpec(memory_space=pltpu.VMEM),
        scratch_shapes=[
            pltpu.VMEM((m - 1,) + parts.shape[1:], parts.dtype),
            pltpu.SemaphoreType.DMA((m - 1,)),
            pltpu.SemaphoreType.DMA((m - 1,)),
            pltpu.SemaphoreType.DMA((m - 1,)),
            pltpu.SemaphoreType.DMA((m - 1,)),
        ],
        compiler_params=pltpu.CompilerParams(collective_id=7, has_side_effects=True),
    )(parts, own, gain.reshape(1, width), bias.reshape(1, width))


def col_proj_kernel(
    x_ref, own_ref, w_hbm, gain_ref, bias_ref, out_ref, got, w_ref, w_sem, rs_send, rs_recv, g_send, g_recv
):
    me, peers = col_peers()
    w_copy = pltpu.make_async_copy(w_hbm, w_ref, w_sem)
    w_copy.start()
    m = len(peers) + 1
    heads_width = x_ref.shape[2]
    copies = []
    for j, peer in enumerate(peers):
        copy = pltpu.make_async_remote_copy(
            src_ref=x_ref.at[peer[2]],
            dst_ref=got.at[j],
            send_sem=rs_send.at[j],
            recv_sem=rs_recv.at[j],
            device_id=peer,
            device_id_type=MESH,
        )
        copy.start()
        copies.append(copy)
    for copy in copies:
        copy.wait()
    w_copy.wait()
    chunk = 32
    width = out_ref.shape[2]
    n_chunks = out_ref.shape[1] // chunk
    sends = []
    for i in range(n_chunks):
        rows = pl.ds(i * chunk, chunk)
        total = own_ref[rows, :]
        for j in range(len(copies)):
            source = lax.rem(me + m - 1 - j, m)
            weights = w_ref[pl.ds(pl.multiple_of(source * heads_width, heads_width), heads_width), :]
            total = total + jnp.dot(got[j, rows, :], weights, preferred_element_type=jnp.float32)
        center = total - jnp.sum(total, axis=1, keepdims=True) / width
        spread = jnp.sum(center * center, axis=1, keepdims=True) / width
        normed = center / jnp.sqrt(spread + 1e-05) * gain_ref[...] + bias_ref[...]
        out_ref[me, rows, :] = normed.astype(out_ref.dtype)
        for j, peer in enumerate(peers):
            copy = pltpu.make_async_remote_copy(
                src_ref=out_ref.at[me, rows],
                dst_ref=out_ref.at[me, rows],
                send_sem=g_send.at[j * n_chunks + i],
                recv_sem=g_recv.at[j * n_chunks + i],
                device_id=peer,
                device_id_type=MESH,
            )
            copy.start()
            sends.append(copy)
    for copy in sends:
        copy.wait()


def col_proj_norm_gather(attn_parts, own, w_full, gain, bias):
    m = lax.axis_size("col")
    rows, width = own.shape
    return pl.pallas_call(
        col_proj_kernel,
        out_shape=jax.ShapeDtypeStruct((m, rows, width), jnp.bfloat16),
        in_specs=[pl.BlockSpec(memory_space=pltpu.VMEM)] * 2
        + [pl.BlockSpec(memory_space=pl.ANY)]
        + [pl.BlockSpec(memory_space=pltpu.VMEM)] * 2,
        out_specs=pl.BlockSpec(memory_space=pltpu.VMEM),
        scratch_shapes=[
            pltpu.VMEM((m - 1,) + attn_parts.shape[1:], attn_parts.dtype),
            pltpu.VMEM(w_full.shape, w_full.dtype),
            pltpu.SemaphoreType.DMA(()),
            pltpu.SemaphoreType.DMA((m - 1,)),
            pltpu.SemaphoreType.DMA((m - 1,)),
            pltpu.SemaphoreType.DMA(((m - 1) * (rows // 32),)),
            pltpu.SemaphoreType.DMA(((m - 1) * (rows // 32),)),
        ],
        compiler_params=pltpu.CompilerParams(
            collective_id=10, has_side_effects=True, vmem_limit_bytes=48 * 1024 * 1024
        ),
    )(attn_parts, own, w_full, gain.reshape(1, width), bias.reshape(1, width))


def col_sum_ln_kernel(x_ref, own_ref, gain_ref, bias_ref, out_ref, got, send_sem, recv_sem):
    me, peers = col_peers()
    copies = []
    for j, peer in enumerate(peers):
        copy = pltpu.make_async_remote_copy(
            src_ref=x_ref.at[peer[2]],
            dst_ref=got.at[j],
            send_sem=send_sem.at[j],
            recv_sem=recv_sem.at[j],
            device_id=peer,
            device_id_type=MESH,
        )
        copy.start()
        copies.append(copy)
    for copy in copies:
        copy.wait()
    chunk = 32
    width = out_ref.shape[1]

    def body(i, carry):
        rows = pl.ds(pl.multiple_of(i * chunk, chunk), chunk)
        total = own_ref[rows, :]
        for j in range(len(copies)):
            total = total + got[j, rows, :].astype(jnp.float32)
        center = total - jnp.sum(total, axis=1, keepdims=True) / width
        spread = jnp.sum(center * center, axis=1, keepdims=True) / width
        normed = center / jnp.sqrt(spread + 1e-05) * gain_ref[...] + bias_ref[...]
        out_ref[rows, :] = normed.astype(out_ref.dtype)
        return carry

    lax.fori_loop(0, out_ref.shape[0] // chunk, body, 0)


def col_sum_norm(parts, own, gain, bias):
    m = lax.axis_size("col")
    rows, width = own.shape
    return pl.pallas_call(
        col_sum_ln_kernel,
        out_shape=jax.ShapeDtypeStruct(own.shape, jnp.float32),
        in_specs=[pl.BlockSpec(memory_space=pltpu.VMEM)] * 4,
        out_specs=pl.BlockSpec(memory_space=pltpu.VMEM),
        scratch_shapes=[
            pltpu.VMEM((m - 1,) + parts.shape[1:], parts.dtype),
            pltpu.SemaphoreType.DMA((m - 1,)),
            pltpu.SemaphoreType.DMA((m - 1,)),
        ],
        compiler_params=pltpu.CompilerParams(collective_id=11, has_side_effects=True),
    )(parts, own, gain.reshape(1, width), bias.reshape(1, width))


def layer_norm(values, gain, bias):
    center = values - jnp.mean(values, axis=1, keepdims=True)
    spread = jnp.mean(center * center, axis=1, keepdims=True)
    return center * lax.rsqrt(spread + 1e-05) * gain + bias


def per_device(
    hidden_in,
    qkv_weight,
    qkv_global_weight,
    out_weight,
    ln_gain,
    ln_bias,
    ffn_in,
    ffn_out,
    ln2_gain,
    ln2_bias,
    segment_ids,
    global_pos,
    page_owner,
):
    neg = -1e30
    tokens = hidden_in[0]
    shard_len, width = tokens.shape
    heads_here = qkv_weight.shape[1]
    triple = qkv_weight.shape[2]
    head_dim = triple // 3
    n_seq = lax.axis_size("seq")
    n_row = lax.axis_size("row")
    n_col = lax.axis_size("col")
    seq_index = lax.axis_index("seq")
    col_index = lax.axis_index("col")
    base = seq_index * shard_len
    scale = 1.0 / math.sqrt(head_dim)

    all_pos = global_pos[0]
    n_glob = all_pos.shape[0]
    per_shard = n_glob // n_seq
    own_pos = lax.dynamic_slice_in_dim(all_pos, seq_index * per_shard, per_shard, 0)
    local_order = jnp.arange(shard_len, dtype=jnp.int32)
    own_match = (own_pos - base)[:, None] == local_order[None, :]
    picker = own_match.astype(jnp.bfloat16)
    own_rows = jnp.dot(picker, tokens, preferred_element_type=jnp.float32).astype(jnp.bfloat16)
    group = 4 if n_seq % 4 == 0 and n_seq > 4 else 1
    if group > 1:
        glob_rows = seq_gather2(own_rows.reshape(-1, 128), group).reshape(n_glob, width)
    else:
        glob_rows = seq_direct_gather(own_rows.reshape(-1, 128)).reshape(n_glob, width)

    wg_cols = qkv_global_weight.shape[1] * qkv_global_weight.shape[2]
    wg_fin = lax.all_gather(
        jnp.concatenate(
            [qkv_global_weight.reshape(qkv_global_weight.shape[0], wg_cols), ffn_in], axis=1
        ),
        "row",
        axis=0,
        tiled=True,
    )
    w_global = wg_fin[:, :wg_cols]
    f_in = wg_fin[:, wg_cols:]
    f_out = lax.all_gather(ffn_out, "row", axis=1, tiled=True)
    w_out = lax.all_gather(out_weight, "col", axis=0, tiled=True)

    flat_weight = qkv_weight.reshape(width, heads_here * triple)
    qkv = jnp.dot(tokens, flat_weight, preferred_element_type=jnp.float32).astype(jnp.bfloat16)
    qkv_heads = qkv.reshape(shard_len, heads_here, triple)
    queries = qkv_heads[:, :, :head_dim]
    kv_local = qkv_heads[:, :, head_dim:]

    owners = page_owner[0, :, 0]
    n_pages = owners.shape[0]
    page_len = shard_len // n_pages
    capacity = max(2, n_pages // n_seq)
    page_order = jnp.arange(n_pages, dtype=jnp.int32)
    slot = jnp.sum(
        ((owners[:, None] == owners[None, :]) & (page_order[None, :] < page_order[:, None])).astype(
            jnp.int32
        ),
        axis=1,
    )
    target = owners * capacity + slot
    placing = (target[None, :] == jnp.arange(n_seq * capacity, dtype=jnp.int32)[:, None]).astype(
        jnp.bfloat16
    )
    outgoing = jnp.dot(
        placing,
        kv_local.reshape(n_pages, page_len * heads_here * 2 * head_dim),
        preferred_element_type=jnp.float32,
    ).astype(jnp.bfloat16)
    outgoing = outgoing.reshape(n_seq, capacity, page_len, heads_here, 2 * head_dim)
    arrived = lax.all_to_all(outgoing, "seq", split_axis=0, concat_axis=0, tiled=True)
    arrived, glob_rows = lax.optimization_barrier((arrived, glob_rows))
    page_pool = arrived[None, None]

    kv_ext = padded(kv_local, (("seq", 0),), HALF)

    glob_qkv = jnp.dot(glob_rows, flat_weight, preferred_element_type=jnp.float32).astype(
        jnp.bfloat16
    )
    glob_kv = glob_qkv.reshape(n_glob, heads_here, triple)[:, :, head_dim:]
    glob_k = glob_kv[:, :, :head_dim]
    glob_v = glob_kv[:, :, head_dim:]
    glob_q = (
        jnp.dot(glob_rows, w_global, preferred_element_type=jnp.float32)
        .astype(jnp.bfloat16)
        .reshape(n_glob, heads_here, triple)[:, :, :head_dim]
    )
    global_kv_local = (
        jnp.dot(tokens, w_global, preferred_element_type=jnp.float32)
        .astype(jnp.bfloat16)
        .reshape(shard_len, heads_here, triple)[:, :, head_dim:]
    )

    seg_all = segment_ids[0]
    glob_seg = jnp.take(seg_all, all_pos)
    seg_pad = jnp.pad(seg_all, (HALF, HALF), constant_values=-1)
    query_seg = lax.dynamic_slice_in_dim(seg_all, base, shard_len, 0)
    key_seg = lax.dynamic_slice_in_dim(seg_pad, base, shard_len + 2 * HALF, 0)
    key_pos = base - HALF + jnp.arange(shard_len + 2 * HALF, dtype=jnp.int32)
    key_flag = jnp.any(key_pos[:, None] == all_pos[None, :], axis=1)
    query_pos = base + local_order

    s_part = (
        jnp.einsum(
            "ghd,khd->hgk",
            glob_q,
            global_kv_local[:, :, :head_dim],
            preferred_element_type=jnp.float32,
        )
        * scale
    )
    part_mask = glob_seg[:, None] == query_seg[None, :]
    part_top = jnp.max(jnp.where(part_mask, s_part, neg), axis=2)
    e_part = jnp.where(part_mask, jnp.exp(s_part - part_top[:, :, None]), 0.0)
    part_total = jnp.sum(e_part, axis=2)
    part_acc = jnp.einsum(
        "hgk,khd->hgd",
        e_part,
        global_kv_local[:, :, head_dim:].astype(jnp.float32),
        precision=lax.Precision.HIGHEST,
    )
    packed = jnp.concatenate(
        [
            part_acc,
            part_total[:, :, None],
            jnp.broadcast_to(part_top[:, :, None], part_top.shape + (128 - head_dim - 1,)),
        ],
        axis=2,
    )
    packed = jnp.transpose(packed, (1, 0, 2)).reshape(n_glob * heads_here, 128)
    if group > 1:
        merged = seq_merge2(packed.reshape(n_seq, -1, 128), head_dim + 1, group)
    else:
        merged = seq_direct_merge(packed.reshape(n_seq, -1, 128), head_dim + 1)
    merged = merged.reshape(
        per_shard, heads_here, 128
    )
    own_out = jnp.transpose(
        (merged[:, :, :head_dim] / merged[:, :, head_dim : head_dim + 1]).astype(jnp.bfloat16),
        (1, 0, 2),
    )

    glob_mask = query_seg[:, None] == glob_seg[None, :]
    k_blk = kv_ext[:, :, :head_dim]
    v_blk = kv_ext[:, :, head_dim:]
    s_win = jnp.einsum("qhd,khd->hqk", queries, k_blk, preferred_element_type=jnp.float32) * scale
    s_glob = jnp.einsum("qhd,ghd->hqg", queries, glob_k, preferred_element_type=jnp.float32) * scale
    m_win = (
        (jnp.abs(query_pos[:, None] - key_pos[None, :]) <= HALF)
        & (query_seg[:, None] == key_seg[None, :])
        & jnp.logical_not(key_flag[None, :])
    )
    top = jnp.maximum(
        jnp.max(jnp.where(m_win, s_win, neg), axis=2),
        jnp.max(jnp.where(glob_mask, s_glob, neg), axis=2),
    )
    e_win = jnp.where(m_win, jnp.exp(s_win - top[:, :, None]), 0.0)
    e_glob = jnp.where(glob_mask, jnp.exp(s_glob - top[:, :, None]), 0.0)
    total = jnp.sum(e_win, axis=2) + jnp.sum(e_glob, axis=2)
    numer = jnp.einsum(
        "hqk,khd->qhd", e_win.astype(jnp.bfloat16), v_blk, preferred_element_type=jnp.float32
    )
    numer = numer + jnp.einsum(
        "hqg,ghd->qhd", e_glob.astype(jnp.bfloat16), glob_v, preferred_element_type=jnp.float32
    )
    pieces = (numer / jnp.transpose(total)[:, :, None]).astype(jnp.bfloat16)

    placed = jnp.einsum("gt,hgd->thd", picker, own_out, preferred_element_type=jnp.float32).astype(
        jnp.bfloat16
    )
    is_own = jnp.any(own_match, axis=0)
    attention = jnp.where(is_own[:, None, None], placed, pieces).reshape(
        shard_len, heads_here * head_dim
    )


    out_rows = shard_len // n_col
    attn_own = lax.dynamic_slice_in_dim(attention, col_index * out_rows, out_rows, 0)
    token_own = lax.dynamic_slice_in_dim(tokens, col_index * out_rows, out_rows, 0)
    proj_own = jnp.dot(attn_own, out_weight, preferred_element_type=jnp.float32)
    own_sum, w_out = lax.optimization_barrier((token_own.astype(jnp.float32) + proj_own, w_out))
    middle_all = col_proj_norm_gather(
        attention.reshape(n_col, out_rows, heads_here * head_dim),
        own_sum,
        w_out,
        ln_gain,
        ln_bias,
    )
    mine = middle_all[col_index]
    middle = middle_all.reshape(shard_len, width)
    ffn_pre = jnp.dot(middle, f_in, preferred_element_type=jnp.float32)
    ffn_hidden = jax.nn.gelu(ffn_pre, approximate=False).astype(jnp.bfloat16)
    ffn_full = jnp.dot(ffn_hidden, f_out, preferred_element_type=jnp.float32)
    ffn_own = lax.dynamic_slice_in_dim(ffn_full, col_index * out_rows, out_rows, 0)
    normed = col_sum_norm(
        ffn_full.astype(jnp.bfloat16).reshape(n_col, out_rows, width),
        mine.astype(jnp.float32) + ffn_own,
        ln2_gain,
        ln2_bias,
    )
    return (normed.astype(jnp.bfloat16)[None], page_pool)


def solution(mesh):
    in_specs = (
        P("row", "seq", None),
        P(None, "col", None),
        P("row", "col", None),
        P("col", None),
        P(),
        P(),
        P("row", "col"),
        P("col", "row"),
        P(),
        P(),
        P("row", None),
        P("row", None),
        P("row", "seq", None),
    )
    out_specs = (P("row", ("seq", "col"), None), P("row", "seq", None, None, None, "col", None))
    return jax.shard_map(
        per_device, mesh=mesh, in_specs=in_specs, out_specs=out_specs, check_vma=False
    )
```
